32 devices in a mesh: dp: 8 (over y, x, core), tensor: 4 (over z).
Axes of the slice: x: 2, y: 2, z: 4, core: 2. Of those that a mesh axis runs over, the one named last changes fastest.
Arguments:
- tokens: bfloat16 [8192, 2048], P('dp'), may hold values from -6 to 6
- cotangent: bfloat16 [8192, 2048], P('dp'), may hold values from -6 to 6
- segment_ids: int32 [8, 1024], P('dp'), may hold values from 0 to 2, never falling along the last dimension, each value on 1 to 768 neighbouring positions
- step_count: int32 [1], replicated, may hold values from 2 to 4
- norm_gains: float32 [2, 2048], P(None, 'dp'), may hold values from 0.5 to 1.5
- gains_first: float32 [2, 2048], P(None, 'dp'), may hold values from -0.0004272461 to 0.0004272461
- gains_second: float32 [2, 2048], P(None, 'dp'), may hold values from 9.5358565e-09 to 1.5211961e-07
- w_query: float32 [2048, 2048], P('dp', 'tensor'), may hold values from -0.125 to 0.125
- query_first: float32 [2048, 2048], P('dp', 'tensor'), may hold values from -0.00015258789 to 0.00015258789
- query_second: float32 [2048, 2048], P('dp', 'tensor'), may hold values from 1.4757873e-09 to 2.3839641e-08
- w_keyval: float32 [2, 2048, 256], P(None, 'dp', 'tensor'), may hold values from -0.125 to 0.125
- keyval_first: float32 [2, 2048, 256], P(None, 'dp', 'tensor'), may hold values from -0.0004272461 to 0.0004272461
- keyval_second: float32 [2, 2048, 256], P(None, 'dp', 'tensor'), may hold values from 1.0353215e-08 to 1.6710453e-07
- w_out: float32 [2048, 2048], P('tensor', 'dp'), may hold values from -1.5 to 1.5
- out_first: float32 [2048, 2048], P('tensor', 'dp'), may hold values from -1.5258789e-05 to 1.5258789e-05
- out_second: float32 [2048, 2048], P('tensor', 'dp'), may hold values from 1.7709447e-11 to 2.860757e-10
- w_gateup: float32 [2, 2048, 5632], P(None, 'dp', 'tensor'), may hold values from -0.125 to 0.125
- gateup_first: float32 [2, 2048, 5632], P(None, 'dp', 'tensor'), may hold values from -5.340576e-05 to 5.340576e-05
- gateup_second: float32 [2, 2048, 5632], P(None, 'dp', 'tensor'), may hold values from 1.4757873e-10 to 2.3839641e-09
- w_down: float32 [5632, 2048], P('tensor', 'dp'), may hold values from -0.15625 to 0.15625
- down_first: float32 [5632, 2048], P('tensor', 'dp'), may hold values from -4.5776367e-05 to 4.5776367e-05
- down_second: float32 [5632, 2048], P('tensor', 'dp'), may hold values from 1.1806298e-10 to 1.9071713e-09
Outputs:
- layer_out: bfloat16 [8192, 2048], P('dp')
- input_grad: float32 [8192, 2048], P('dp')
- grad_norm: float32 [1], replicated
- gains_moment: float32 [2, 2048], P(None, 'dp')
- gains_square: float32 [2, 2048], P(None, 'dp')
- gains_new: float32 [2, 2048], P(None, 'dp')
- query_moment: float32 [2048, 2048], P('dp', 'tensor')
- query_square: float32 [2048, 2048], P('dp', 'tensor')
- query_new: float32 [2048, 2048], P('dp', 'tensor')
- keyval_moment: float32 [2, 2048, 256], P(None, 'dp', 'tensor')
- keyval_square: float32 [2, 2048, 256], P(None, 'dp', 'tensor')
- keyval_new: float32 [2, 2048, 256], P(None, 'dp', 'tensor')
- out_moment: float32 [2048, 2048], P('tensor', 'dp')
- out_square: float32 [2048, 2048], P('tensor', 'dp')
- out_new: float32 [2048, 2048], P('tensor', 'dp')
- gateup_moment: float32 [2, 2048, 5632], P(None, 'dp', 'tensor')
- gateup_square: float32 [2, 2048, 5632], P(None, 'dp', 'tensor')
- gateup_new: float32 [2, 2048, 5632], P(None, 'dp', 'tensor')
- down_moment: float32 [5632, 2048], P('tensor', 'dp')
- down_square: float32 [5632, 2048], P('tensor', 'dp')
- down_new: float32 [5632, 2048], P('tensor', 'dp')
The draws below stay inside these ranges and needn't reach their ends.
Inputs may be any that keep to these rules, and one draw needn't show every extreme that they name: `segment_ids`: in each batch row the segment ids never fall, all 3 ids occur, and the longest sequence of a row has 768 tokens; a token attends to the earlier tokens of its own sequence only.
All inputs are finite; a program needn't handle non-finite values.
Results may differ from the reference program's by a relative error of at most 0.017.
Values may be sent and summed in bfloat16 or wider, within the bound.
A program may use at most 320 MiB of HBM per device.

```python
import math
import jax
import jax.numpy as jnp
import numpy as np
from jax import lax

D = 2048
HEADS = 32
KVH = 4
HD = 64
FF = 5632
TOK_DEV = 1024
SEGS = 3
LONGEST = 768
TOKENS = 8192
PARAMS = 44044288
N_DP = 8


def block_levels(key, extent, cuts, least, top_value):
    level = 1.0
    for axis_at, shards_of in cuts:
        draws = jax.random.uniform(jax.random.fold_in(jax.random.fold_in(key, 6), axis_at), (shards_of,), jnp.float32, least / len(cuts), top_value / len(cuts))
        level = level * jnp.repeat(jnp.exp(draws), extent[axis_at] // shards_of).reshape((-1,) + (1,) * (len(extent) - 1 - axis_at))
    return level


def split_up(count, total, reach, lean):
    loads = [(1 << 20) // math.isqrt(standing ** lean) + 1 for standing in range(2, count + 1)]
    rest, holding = total - reach - (count - 1), [1] * (count - 1)
    while rest > 0:
        movable = [i for i in range(count - 1) if holding[i] < reach]
        whole, budget = sum([loads[i] for i in movable]), rest
        for i in movable:
            more = min(reach - holding[i], max(1, budget * loads[i] // whole), rest)
            holding[i] = holding[i] + more
            rest = rest - more
    return np.array([reach] + holding)


def ragged(own_key, amount, total, limit, lean):
    if amount == 2:
        one = jax.random.randint(own_key, (), max(1, total - limit), min(limit, total - 1) + 1)
        return jnp.stack([one, total - one])
    lengths = jnp.asarray(split_up(amount, total, limit, lean), jnp.int32)
    pairs = (amount - 1) // 2
    donor, sink = lengths[1:1 + 2 * pairs:2], lengths[2:2 + 2 * pairs:2]
    slack = jnp.minimum(donor - 1, limit - sink)
    moved = jax.random.randint(jax.random.fold_in(own_key, 1), (pairs,), 0, 1 << 20) % (slack + 1)
    lengths = lengths.at[1:1 + 2 * pairs:2].set(donor - moved).at[2:2 + 2 * pairs:2].set(sink + moved)
    return lengths[jax.random.permutation(jax.random.fold_in(own_key, 2), amount)]


def noise(stream_key, extent, scale, bound, cuts=(), held_as=jnp.bfloat16):
    level = block_levels(stream_key, extent, cuts, -0.22, 0.18) if cuts else 1.0
    drawn = jax.random.normal(stream_key, extent, jnp.float32) * scale * level
    return jnp.minimum(jnp.maximum(drawn, -bound), bound).astype(held_as)


def setup_inputs(seed: int = 0) -> dict:
    streams_of = jax.random.split(jax.random.key(seed), 23)
    return {
        "tokens": noise(streams_of[0], (TOKENS, D), 1.0, 6.0, ((0, 8),)),
        "cotangent": noise(streams_of[1], (TOKENS, D), 1.0, 6.0, ((0, 8),)),
        "segment_ids": jax.vmap(lambda own: jnp.searchsorted(jnp.cumsum(ragged(own, SEGS, TOK_DEV, LONGEST, 0)), jnp.arange(TOK_DEV), side="right"))(jax.random.split(streams_of[2], N_DP)).reshape((N_DP, TOK_DEV)).astype(jnp.int32),
        "step_count": jax.random.randint(streams_of[3], (1,), 2, 5).astype(jnp.int32),
        "norm_gains": jnp.clip(1.0 + 0.1 * jax.random.normal(streams_of[4], (2, D), jnp.float32), 0.5, 1.5),
        "gains_first": noise(streams_of[5], (2, D), (0.44 * PARAMS ** -0.5), 0.0004272461, ((1, 8),), jnp.float32),
        "gains_second": jnp.clip(jnp.exp(math.log(1.5211961112981953e-07) - 2.769608 * jax.random.uniform(streams_of[6], (2, D), jnp.float32) ** block_levels(streams_of[6], (2, D), ((1, 8),), -0.2, 0.2)), 9.535856548836819e-09, 1.5211961112981953e-07),
        "w_query": noise(streams_of[7], (D, HEADS * HD), D ** -0.5, 0.125, ((0, 8), (1, 4)), jnp.float32),
        "query_first": noise(streams_of[8], (D, HEADS * HD), (0.17 * PARAMS ** -0.5), 0.00015258789, ((0, 8), (1, 4)), jnp.float32),
        "query_second": jnp.clip(jnp.exp(math.log(2.3839641372092046e-08) - 2.7821582 * jax.random.uniform(streams_of[9], (D, HEADS * HD), jnp.float32) ** block_levels(streams_of[9], (D, HEADS * HD), ((0, 8), (1, 4)), -0.2, 0.2)), 1.4757872701665065e-09, 2.3839641372092046e-08),
        "w_keyval": noise(streams_of[10], (2, D, KVH * HD), D ** -0.5, 0.125, ((1, 8), (2, 4)), jnp.float32),
        "keyval_first": noise(streams_of[11], (2, D, KVH * HD), (0.16 * (HEADS / (KVH * PARAMS)) ** 0.5), 0.0004272461, ((1, 8), (2, 4)), jnp.float32),
        "keyval_second": jnp.clip(jnp.exp(math.log(1.671045311013586e-07) - 2.7813224 * jax.random.uniform(streams_of[12], (2, D, KVH * HD), jnp.float32) ** block_levels(streams_of[12], (2, D, KVH * HD), ((1, 8), (2, 4)), -0.2, 0.2)), 1.0353215174063735e-08, 1.671045311013586e-07),
        "w_out": noise(streams_of[13], (HEADS * HD, D), (max(1, HEADS * HD * 8 // TOK_DEV)) ** -0.5, 1.5, ((0, 4), (1, 8)), jnp.float32),
        "out_first": noise(streams_of[14], (HEADS * HD, D), (0.019 * PARAMS ** -0.5), 1.52587890625e-05, ((0, 4), (1, 8)), jnp.float32),
        "out_second": jnp.clip(jnp.exp(math.log(2.8607569091398943e-10) - 2.7821582 * jax.random.uniform(streams_of[15], (HEADS * HD, D), jnp.float32) ** block_levels(streams_of[15], (HEADS * HD, D), ((0, 4), (1, 8)), -0.2, 0.2)), 1.7709446756275504e-11, 2.8607569091398943e-10),
        "w_gateup": noise(streams_of[16], (2, D, FF), D ** -0.5, 0.125, ((1, 8), (2, 4)), jnp.float32),
        "gateup_first": noise(streams_of[17], (2, D, FF), (0.055 * PARAMS ** -0.5), 5.340576171875e-05, ((1, 8), (2, 4)), jnp.float32),
        "gateup_second": jnp.clip(jnp.exp(math.log(2.3839641372092046e-09) - 2.7821582 * jax.random.uniform(streams_of[18], (2, D, FF), jnp.float32) ** block_levels(streams_of[18], (2, D, FF), ((1, 8), (2, 4)), -0.2, 0.2)), 1.4757872701665065e-10, 2.3839641372092046e-09),
        "w_down": noise(streams_of[19], (FF, D), (FF // 4) ** -0.5, 0.15625, ((0, 4), (1, 8)), jnp.float32),
        "down_first": noise(streams_of[20], (FF, D), (0.049 * PARAMS ** -0.5), 4.57763671875e-05, ((0, 4), (1, 8)), jnp.float32),
        "down_second": jnp.clip(jnp.exp(math.log(1.9071713097673637e-09) - 2.7821583 * jax.random.uniform(streams_of[21], (FF, D), jnp.float32) ** block_levels(streams_of[21], (FF, D), ((0, 4), (1, 8)), -0.2, 0.2)), 1.180629760622054e-10, 1.9071713097673637e-09),
    }


@jax.custom_vjp
def low(v):
    return lax.optimization_barrier(v.astype(jnp.bfloat16)).astype(jnp.float32)

@jax.custom_vjp
def low_back(v):
    return v

def low_keep(v):
    return (low(v), None)

def low_pass(kept, grad):
    return (grad,)

def back_keep(v):
    return (v, None)

def back_low(kept, grad):
    return (low(grad),)
low.defvjp(low_keep, low_pass)
low_back.defvjp(back_keep, back_low)
norm_eps = 1e-05
beta_first = 0.9
beta_second = 0.95
adam_eps = 1e-08
weight_decay = 0.1
weight_rate = 0.02
out_rate = 0.1
gain_rate = 0.2
clip_limit = 1.0
masked_value = -1000000000.0

def norm_rows(values, gain):
    inverse = lax.rsqrt(lax.optimization_barrier(jnp.mean(values * values, axis=-1, keepdims=True)) + norm_eps)
    return values * inverse * gain

def positions(segment):
    length = segment.shape[0]
    indices = jnp.arange(length, dtype=jnp.int32)
    earlier = jnp.concatenate([segment[:1] - 1, segment[:-1]])
    begins = jnp.where(segment != earlier, indices, jnp.zeros_like(indices))
    return indices - lax.cummax(begins, axis=0)

def rotary_tables(places, width):
    half_width = width // 2
    frequency = jnp.power(10000.0, -jnp.arange(half_width, dtype=jnp.float32) * (2.0 / width))
    angles = places.astype(jnp.float32)[:, None] * frequency[None, :]
    cosine_table = jnp.concatenate([jnp.cos(angles), jnp.cos(angles)], axis=-1)
    sine_table = jnp.concatenate([jnp.sin(angles), jnp.sin(angles)], axis=-1)
    return (cosine_table, sine_table)

def rotate(values, cosine_table, sine_table):
    half_width = values.shape[-1] // 2
    turned = jnp.concatenate([-values[..., half_width:], values[..., :half_width]], axis=-1)
    return values * cosine_table[:, None, :] + turned * sine_table[:, None, :]

def layer(row_values, gain_rows, w_query, w_keyval, w_out, w_gateup, w_down, cosine_table, sine_table, allowed):
    length = row_values.shape[0]
    gain_rows = low(gain_rows)
    normed_one = low(norm_rows(row_values, gain_rows[0]))
    queries = low_back(jnp.dot(normed_one, low(w_query), precision=lax.Precision.HIGHEST, preferred_element_type=jnp.float32))
    queries = low(rotate(queries.reshape(length, HEADS, HD), cosine_table, sine_table))
    keyval = low_back(jnp.einsum('nd,sdk->snk', normed_one, low(w_keyval), precision=lax.Precision.HIGHEST))
    key_rows = low(rotate(keyval[0].reshape(length, KVH, HD), cosine_table, sine_table))
    value_rows = low(keyval[1].reshape(length, KVH, HD))
    grouped = queries.reshape(length, KVH, HEADS // KVH, HD)
    raw_scores = low_back(jnp.einsum('qkgh,pkh->kgqp', grouped, key_rows, precision=lax.Precision.HIGHEST))
    scaled = jnp.where(allowed, raw_scores * HD ** (-0.5), masked_value)
    highest = lax.optimization_barrier(jnp.max(scaled, axis=-1, keepdims=True))
    lifted = jnp.exp(scaled - highest)
    soft_weights = low(lifted / lax.optimization_barrier(jnp.sum(lifted, axis=-1, keepdims=True)))
    mixture = jnp.einsum('kgqp,pkh->qkgh', soft_weights, value_rows, precision=lax.Precision.HIGHEST)
    mixture = low(low_back(mixture.reshape(length, HEADS * HD)))
    branch = low_back(jnp.dot(mixture, low(w_out), precision=lax.Precision.HIGHEST, preferred_element_type=jnp.float32))
    middle = row_values + branch
    normed_two = low(norm_rows(middle, gain_rows[1]))
    gateup = low_back(jnp.einsum('nd,sdf->snf', normed_two, low(w_gateup), precision=lax.Precision.HIGHEST))
    hidden = low(jax.nn.silu(gateup[0]) * gateup[1])
    feed_out = low_back(jnp.dot(hidden, low(w_down), precision=lax.Precision.HIGHEST, preferred_element_type=jnp.float32))
    return middle + feed_out

def adam_step(weight, first, second, gradient, clip_factor, step_float, step_rate, decay_rate):
    gradient = gradient * clip_factor
    first = beta_first * first + (1.0 - beta_first) * gradient
    second = beta_second * second + (1.0 - beta_second) * gradient * gradient
    correct_one = 1.0 - jnp.power(beta_first, step_float)
    correct_two = 1.0 - jnp.power(beta_second, step_float)
    update = first / correct_one / (jnp.sqrt(second / correct_two) + adam_eps)
    return (first, second, weight - step_rate * (update + decay_rate * weight))

def reference(tokens, cotangent, segment_ids, step_count, norm_gains, gains_first, gains_second, w_query, query_first, query_second, w_keyval, keyval_first, keyval_second, w_out, out_first, out_second, w_gateup, gateup_first, gateup_second, w_down, down_first, down_second):
    params = (norm_gains, w_query, w_keyval, w_out, w_gateup, w_down)
    inputs = tokens.reshape(N_DP, TOK_DEV, D)
    backs = cotangent.reshape(N_DP, TOK_DEV, D)

    def one_row(totals, pieces):
        row_values, back_values, segment = pieces
        cosine_table, sine_table = rotary_tables(positions(segment), HD)
        indices = jnp.arange(TOK_DEV, dtype=jnp.int32)
        allowed = (segment[:, None] == segment[None, :]) & (indices[:, None] >= indices[None, :])

        def forward(values, *weights):
            return layer(values, *weights, cosine_table, sine_table, allowed)
        output, pullback = jax.vjp(forward, row_values.astype(jnp.float32), *params)
        gradients = pullback(back_values.astype(jnp.float32))
        totals = tuple((a + b for a, b in zip(totals, gradients[1:])))
        return (totals, (output.astype(jnp.bfloat16), gradients[0]))
    zero_grads = tuple((jnp.zeros_like(p) for p in params))
    totals, (outputs, input_grads) = lax.scan(one_row, zero_grads, (inputs, backs, segment_ids))
    square_total = sum((jnp.sum(g * g) for g in totals))
    grad_norm = jnp.sqrt(square_total)
    clip_factor = jnp.minimum(1.0, clip_limit / (grad_norm + 1e-06))
    step_float = step_count[0].astype(jnp.float32)
    states = ((gains_first, gains_second), (query_first, query_second), (keyval_first, keyval_second), (out_first, out_second), (gateup_first, gateup_second), (down_first, down_second))
    step_rates = (gain_rate, weight_rate, weight_rate, out_rate, weight_rate, weight_rate)
    decay_rates = (0.0, weight_decay, weight_decay, weight_decay, weight_decay, weight_decay)
    results = []
    for position_index in range(6):
        first, second = states[position_index]
        results.extend(adam_step(params[position_index], first, second, totals[position_index], clip_factor, step_float, step_rates[position_index], decay_rates[position_index]))
    return (outputs.reshape(TOKENS, D), input_grads.reshape(TOKENS, D), grad_norm.reshape(1), results[0], results[1], results[2], results[3], results[4], results[5], results[6], results[7], results[8], results[9], results[10], results[11], results[12], results[13], results[14], results[15], results[16], results[17])
```

```python
import functools

import jax
import jax.numpy as jnp
from jax import lax
from jax.experimental import pallas as pl
from jax.experimental.pallas import tpu as pltpu
from jax.sharding import PartitionSpec as P

HD = 64
MESH = pl.DeviceIdType.MESH


masked_value = -1e9


def dot_t(left, right):
    return lax.dot_general(left, right, (((1,), (1,)), ((), ())), preferred_element_type=jnp.float32)


def dot_n(left, right):
    return lax.dot_general(left, right, (((1,), (0,)), ((), ())), preferred_element_type=jnp.float32)


def swap_halves(values, first_half):
    return jnp.where(first_half, pltpu.roll(values, 96, 1), pltpu.roll(values, 32, 1))


def lane_tests(rows):
    lane = lax.broadcasted_iota(jnp.int32, (rows, 128), 1)
    return lane < 64, (lane % 64) < 32


def block_bias(seg_col_ref, seg_row_ref, i, j, size):
    keys = seg_col_ref[pl.ds(pl.multiple_of(j * size, size), size), :]
    rows = seg_row_ref[:, pl.ds(pl.multiple_of(i * size, size), size)]
    key_at = j * size + lax.broadcasted_iota(jnp.int32, (size, size), 0)
    row_at = i * size + lax.broadcasted_iota(jnp.int32, (size, size), 1)
    return jnp.where((keys == rows) & (key_at <= row_at), 0.0, masked_value)


def stack_pair(pair, low_lanes):
    zero = jnp.zeros_like(pair)
    return jnp.concatenate([jnp.where(low_lanes, pair, zero), jnp.where(low_lanes, zero, pair)], axis=0)


def forward_kernel(size, pairs, first_ref, raw_ref, cos_ref, sin_ref, seg_col_ref, seg_row_ref,
                   mix_ref, q_ref, k_ref, v_ref, lse_ref, bias, scores, v_turned):
    length = raw_ref.shape[0]
    low_lanes, first_half = lane_tests(size)
    low_rows = lax.broadcasted_iota(jnp.int32, (128, size), 0) < 64
    width = pairs * 128

    def prepare(i, carry):
        rows = pl.ds(pl.multiple_of(i * size, size), size)
        cosines, sines = cos_ref[rows, :], sin_ref[rows, :]
        for hp in range(pairs):
            values = raw_ref[rows, hp * 128:(hp + 1) * 128]
            turned = values * cosines + swap_halves(values, first_half) * sines
            q_ref[rows, hp * 128:(hp + 1) * 128] = (turned.astype(jnp.bfloat16).astype(jnp.float32) * 0.125).astype(jnp.bfloat16)
        both = raw_ref[rows, width:width + 128]
        other = pltpu.roll(both, 64, 1)
        keys = jnp.where(low_lanes, both, other)
        k_ref[rows, :] = (keys * cosines + swap_halves(keys, first_half) * sines).astype(jnp.bfloat16)
        values = jnp.where(low_lanes, other, both)
        v_ref[rows, :] = values.astype(jnp.bfloat16)
        v_turned[i] = values.T.astype(jnp.bfloat16)
        return carry

    lax.fori_loop(0, length // size, prepare, 0)

    def row_block(i, carry):
        rows = pl.ds(pl.multiple_of(i * size, size), size)
        begin = first_ref[i]

        def fill(j, c):
            bias[j] = block_bias(seg_col_ref, seg_row_ref, i, j, size)
            return c

        lax.fori_loop(begin, i + 1, fill, 0)

        for hp in range(pairs):
            stacked = stack_pair(q_ref[rows, hp * 128:(hp + 1) * 128], low_lanes)

            def score(j, top):
                keys = k_ref[pl.ds(pl.multiple_of(j * size, size), size), :]
                b = bias[j]
                s = dot_t(keys, stacked) + jnp.concatenate([b, b], axis=1)
                scores[j] = s
                return jnp.maximum(top, jnp.max(s, axis=0, keepdims=True))

            top = lax.fori_loop(begin, i + 1, score, jnp.full((1, 2 * size), -jnp.inf, jnp.float32))

            def mix(j, c):
                total, acc = c
                p = jnp.exp(scores[j] - top)
                total = total + jnp.sum(p, axis=0, keepdims=True)
                return total, acc + dot_n(v_turned[j], p.astype(jnp.bfloat16))

            total, acc = lax.fori_loop(begin, i + 1, mix, (
                jnp.zeros((1, 2 * size), jnp.float32), jnp.zeros((128, 2 * size), jnp.float32)))
            lse_ref[i, hp] = top + jnp.log(total)
            acc = acc / total
            acc = jnp.where(low_rows, acc[:, :size], acc[:, size:])
            mix_ref[rows, hp * 128:(hp + 1) * 128] = acc.T.astype(jnp.bfloat16)
        return carry

    lax.fori_loop(0, length // size, row_block, 0)


def attention_forward(raw, cosines, sines, seg_col, seg_row, first, size):
    length, wide = raw.shape
    width = wide - 128
    pairs = width // 128
    blocks = length // size
    vmem = pl.BlockSpec(memory_space=pltpu.VMEM)
    return pl.pallas_call(
        functools.partial(forward_kernel, size, pairs),
        out_shape=(
            jax.ShapeDtypeStruct((length, width), jnp.bfloat16),
            jax.ShapeDtypeStruct((length, width), jnp.bfloat16),
            jax.ShapeDtypeStruct((length, 128), jnp.bfloat16),
            jax.ShapeDtypeStruct((length, 128), jnp.bfloat16),
            jax.ShapeDtypeStruct((blocks, pairs, 1, 2 * size), jnp.float32),
        ),
        in_specs=[pl.BlockSpec(memory_space=pltpu.SMEM)] + [vmem] * 5,
        out_specs=(vmem,) * 5,
        scratch_shapes=[
            pltpu.VMEM((blocks, size, size), jnp.float32),
            pltpu.VMEM((blocks, size, 2 * size), jnp.float32),
            pltpu.VMEM((blocks, 128, size), jnp.bfloat16),
        ],
        compiler_params=pltpu.CompilerParams(vmem_limit_bytes=40 << 20),
        cost_estimate=pl.CostEstimate(flops=10 * length * length * width, bytes_accessed=8 * length * width,
                                      transcendentals=length * length * pairs),
    )(first, raw, cosines, sines, seg_col, seg_row)


def backward_kernel(size, pairs, first_ref, q_ref, k_ref, v_ref, mix_ref, grad_ref, lse_ref, cos_ref, sin_ref,
                    seg_col_ref, seg_row_ref, out_ref, bias, k_turned, grad_k, grad_v):
    length = q_ref.shape[0]
    width = pairs * 128
    low_lanes, first_half = lane_tests(size)
    low_rows = lax.broadcasted_iota(jnp.int32, (128, size), 0) < 64

    def prepare(i, carry):
        rows = pl.ds(pl.multiple_of(i * size, size), size)
        k_turned[i] = k_ref[rows, :].astype(jnp.float32).T.astype(jnp.bfloat16)
        grad_k[i] = jnp.zeros((size, 128), jnp.float32)
        grad_v[i] = jnp.zeros((size, 128), jnp.float32)
        return carry

    lax.fori_loop(0, length // size, prepare, 0)

    def row_block(i, carry):
        rows = pl.ds(pl.multiple_of(i * size, size), size)
        begin = first_ref[i]
        cosines, sines = cos_ref[rows, :], sin_ref[rows, :]

        def fill(j, c):
            bias[j] = block_bias(seg_col_ref, seg_row_ref, i, j, size)
            return c

        lax.fori_loop(begin, i + 1, fill, 0)

        for hp in range(pairs):
            columns = slice(hp * 128, (hp + 1) * 128)
            stacked = stack_pair(q_ref[rows, columns], low_lanes)
            grad_pair = grad_ref[rows, columns]
            grad_stacked = stack_pair(grad_pair, low_lanes)
            product = (grad_pair.astype(jnp.float32) * mix_ref[rows, columns].astype(jnp.float32)).T
            spread = jnp.concatenate([
                jnp.sum(product[:64], axis=0, keepdims=True), jnp.sum(product[64:], axis=0, keepdims=True)], axis=1)
            logsum = lse_ref[i, hp]

            def piece(j, acc):
                at = pl.ds(pl.multiple_of(j * size, size), size)
                b = bias[j]
                s = dot_t(k_ref[at, :], stacked) + jnp.concatenate([b, b], axis=1)
                p = jnp.exp(s - logsum)
                grad_p = dot_t(v_ref[at, :], grad_stacked)
                grad_s = (p * (grad_p - spread)).astype(jnp.bfloat16)
                grad_v[j] += dot_n(p.astype(jnp.bfloat16), grad_stacked)
                grad_k[j] += dot_n(grad_s, stacked)
                return acc + dot_n(k_turned[j], grad_s)

            acc = lax.fori_loop(begin, i + 1, piece, jnp.zeros((128, 2 * size), jnp.float32))
            acc = jnp.where(low_rows, acc[:, :size], acc[:, size:]).T * 0.125
            out_ref[rows, columns] = (acc * cosines - swap_halves(acc, first_half) * sines).astype(jnp.bfloat16)
        return carry

    lax.fori_loop(0, length // size, row_block, 0)

    def finish(i, carry):
        rows = pl.ds(pl.multiple_of(i * size, size), size)
        cosines, sines = cos_ref[rows, :], sin_ref[rows, :]
        dk = grad_k[i] + pltpu.roll(grad_k[i], 64, 1)
        dk = dk * cosines - swap_halves(dk, first_half) * sines
        dv = grad_v[i] + pltpu.roll(grad_v[i], 64, 1)
        out_ref[rows, width:width + 128] = jnp.where(low_lanes, dk, dv).astype(jnp.bfloat16)
        return carry

    lax.fori_loop(0, length // size, finish, 0)


def attention_backward(q, k, v, mix, grad, lse, cosines, sines, seg_col, seg_row, first, size):
    length, width = q.shape
    pairs = width // 128
    blocks = length // size
    vmem = pl.BlockSpec(memory_space=pltpu.VMEM)
    return pl.pallas_call(
        functools.partial(backward_kernel, size, pairs),
        out_shape=jax.ShapeDtypeStruct((length, width + 128), jnp.bfloat16),
        in_specs=[pl.BlockSpec(memory_space=pltpu.SMEM)] + [vmem] * 10,
        out_specs=vmem,
        scratch_shapes=[
            pltpu.VMEM((blocks, size, size), jnp.float32),
            pltpu.VMEM((blocks, 128, size), jnp.bfloat16),
            pltpu.VMEM((blocks, size, 128), jnp.float32),
            pltpu.VMEM((blocks, size, 128), jnp.float32),
        ],
        compiler_params=pltpu.CompilerParams(vmem_limit_bytes=40 << 20),
        cost_estimate=pl.CostEstimate(flops=20 * length * length * width, bytes_accessed=8 * length * width,
                                      transcendentals=length * length * pairs),
    )(first, q, k, v, mix, grad, lse, cosines, sines, seg_col, seg_row)


def line_reduce(partial, n, chunks, cid, lagk=1):
    rows, width = partial.shape
    half = rows // 2
    rc = half // chunks

    def kernel(in_ref, out_ref, got, send_a, recv_a, send_g, recv_g):
        me = lax.axis_index("tensor")
        barrier = pltpu.get_barrier_semaphore()

        @pl.when(me > 0)
        def _():
            pl.semaphore_signal(barrier, inc=1, device_id={"tensor": me - 1}, device_id_type=MESH)

        @pl.when(me < n - 1)
        def _():
            pl.semaphore_signal(barrier, inc=1, device_id={"tensor": me + 1}, device_id_type=MESH)

        @pl.when((me > 0) & (me < n - 1))
        def _():
            pl.semaphore_wait(barrier, 2)

        @pl.when((me == 0) | (me == n - 1))
        def _():
            pl.semaphore_wait(barrier, 1)

        def rs(stream, c, nxt, src):
            return pltpu.make_async_remote_copy(
                src_ref=src, dst_ref=got.at[stream, c],
                send_sem=send_a.at[stream, c], recv_sem=recv_a.at[stream, c],
                device_id={"tensor": nxt}, device_id_type=MESH)

        def ag(stream, c, nxt):
            r0 = pl.multiple_of(stream * half + c * rc, rc)
            return pltpu.make_async_remote_copy(
                src_ref=out_ref.at[pl.ds(r0, rc)], dst_ref=out_ref.at[pl.ds(r0, rc)],
                send_sem=send_g.at[stream, c], recv_sem=recv_g.at[stream, c],
                device_id={"tensor": nxt}, device_id_type=MESH)

        K = lagk
        steps = chunks + 2 * K * (n - 1)

        def body(s, carry):
            for stream in (0, 1):
                pos = me if stream == 0 else n - 1 - me
                fwd = me + 1 if stream == 0 else me - 1
                bwd = me - 1 if stream == 0 else me + 1
                c = s - K * pos

                @pl.when((c >= 0) & (c < chunks))
                def _():
                    r0 = pl.multiple_of(stream * half + c * rc, rc)

                    def summed():
                        rs(stream, c, fwd, got.at[stream, c]).wait_recv()
                        return (
                            in_ref[pl.ds(r0, rc)].astype(jnp.float32) + got[stream, c].astype(jnp.float32)
                        ).astype(out_ref.dtype)

                    @pl.when(pos == 0)
                    def _():
                        rs(stream, c, fwd, in_ref.at[pl.ds(r0, rc)]).start()

                    @pl.when((pos > 0) & (pos < n - 1))
                    def _():
                        got[stream, c] = summed()
                        rs(stream, c, fwd, got.at[stream, c]).start()

                    @pl.when(pos == n - 1)
                    def _():
                        out_ref[pl.ds(r0, rc)] = summed()
                        ag(stream, c, bwd).start()
                d = s - K * (n - 1) - K * (n - 1 - pos)

                @pl.when((d >= 0) & (d < chunks) & (pos < n - 1))
                def _():
                    ag(stream, d, bwd).wait_recv()

                    @pl.when(pos > 0)
                    def _():
                        ag(stream, d, bwd).start()
            return carry

        lax.fori_loop(0, steps, body, 0)

        def drain(c, carry):
            for stream in (0, 1):
                pos = me if stream == 0 else n - 1 - me
                fwd = me + 1 if stream == 0 else me - 1
                bwd = me - 1 if stream == 0 else me + 1

                @pl.when(pos < n - 1)
                def _():
                    rs(stream, c, fwd, got.at[stream, c]).wait_send()

                @pl.when(pos > 0)
                def _():
                    ag(stream, c, bwd).wait_send()
            return carry

        lax.fori_loop(0, chunks, drain, 0)

    return pl.pallas_call(
        kernel,
        out_shape=jax.ShapeDtypeStruct((rows, width), partial.dtype),
        in_specs=[pl.BlockSpec(memory_space=pltpu.VMEM)],
        out_specs=pl.BlockSpec(memory_space=pltpu.VMEM),
        scratch_shapes=[
            pltpu.VMEM((2, chunks, rc, width), partial.dtype),
            pltpu.SemaphoreType.DMA((2, chunks)),
            pltpu.SemaphoreType.DMA((2, chunks)),
            pltpu.SemaphoreType.DMA((2, chunks)),
            pltpu.SemaphoreType.DMA((2, chunks)),
        ],
        compiler_params=pltpu.CompilerParams(collective_id=cid, has_side_effects=True, vmem_limit_bytes=40 << 20),
        cost_estimate=pl.CostEstimate(flops=rows * width * 2, bytes_accessed=rows * width * 4 * 30, transcendentals=0),
    )(partial)


def total_kernel(n, m, in_ref, out_ref, line, got_line, got_plane, send_line, recv_line, send_plane, recv_plane):
    z = lax.axis_index("tensor")
    d = lax.axis_index("dp")
    barrier = pltpu.get_barrier_semaphore()
    for k in range(1, n):
        pl.semaphore_signal(barrier, inc=1, device_id={"tensor": lax.rem(z + k, n)}, device_id_type=MESH)
    for k in range(1, m):
        pl.semaphore_signal(barrier, inc=1, device_id={"dp": lax.rem(d + k, m)}, device_id_type=MESH)
    pl.semaphore_wait(barrier, n - 1 + m - 1)

    def along_line(k, sender):
        return pltpu.make_async_remote_copy(
            src_ref=in_ref, dst_ref=got_line.at[sender], send_sem=send_line.at[k], recv_sem=recv_line.at[sender],
            device_id={"tensor": lax.rem(z + k, n)}, device_id_type=MESH)

    def over_plane(k, sender):
        return pltpu.make_async_remote_copy(
            src_ref=line, dst_ref=got_plane.at[sender], send_sem=send_plane.at[k], recv_sem=recv_plane.at[sender],
            device_id={"dp": lax.rem(d + k, m)}, device_id_type=MESH)

    for k in range(1, n):
        along_line(k, z).start()
    got_line[z] = in_ref[...]
    for k in range(1, n):
        along_line(k, z).wait_send()
        along_line(k, lax.rem(z + n - k, n)).wait_recv()
    whole = got_line[0]
    for k in range(1, n):
        whole = whole + got_line[k]
    line[...] = whole
    for k in range(1, m):
        over_plane(k, d).start()
    got_plane[d] = line[...]
    for k in range(1, m):
        over_plane(k, d).wait_send()
        over_plane(k, lax.rem(d + m - k, m)).wait_recv()
    whole = got_plane[0]
    for k in range(1, m):
        whole = whole + got_plane[k]
    out_ref[...] = whole


def total_sum(value, n, m, cid):
    tile = jnp.broadcast_to(value.reshape(1, 1), (8, 128))
    vmem = pl.BlockSpec(memory_space=pltpu.VMEM)
    total = pl.pallas_call(
        functools.partial(total_kernel, n, m),
        out_shape=jax.ShapeDtypeStruct((8, 128), jnp.float32),
        in_specs=[vmem],
        out_specs=vmem,
        scratch_shapes=[
            pltpu.VMEM((8, 128), jnp.float32),
            pltpu.VMEM((n, 8, 128), jnp.float32),
            pltpu.VMEM((m, 8, 128), jnp.float32),
            pltpu.SemaphoreType.DMA((n,)),
            pltpu.SemaphoreType.DMA((n,)),
            pltpu.SemaphoreType.DMA((m,)),
            pltpu.SemaphoreType.DMA((m,)),
        ],
        compiler_params=pltpu.CompilerParams(collective_id=cid, has_side_effects=True),
    )(tile)
    return total[0, 0]


norm_eps = 1e-05
beta_first = 0.9
beta_second = 0.95
adam_eps = 1e-08
weight_decay = 0.1
weight_rate = 0.02
out_rate = 0.1
gain_rate = 0.2
clip_limit = 1.0


def positions(segment):
    length = segment.shape[0]
    indices = jnp.arange(length, dtype=jnp.int32)
    earlier = jnp.concatenate([segment[:1] - 1, segment[:-1]])
    begins = jnp.where(segment != earlier, indices, jnp.zeros_like(indices))
    return indices - lax.cummax(begins, axis=0)


def paired_tables(places):
    frequency = jnp.power(10000.0, -jnp.arange(HD // 2, dtype=jnp.float32) * (2.0 / HD))
    angles = places.astype(jnp.float32)[:, None] * frequency[None, :]
    cosines, sines = jnp.cos(angles), jnp.sin(angles)
    return (
        jnp.concatenate([cosines] * 4, axis=-1),
        jnp.concatenate([-sines, sines, -sines, sines], axis=-1),
    )


def over_rows(left, right):
    return lax.dot_general(
        left, right, (((0,), (0,)), ((), ())), preferred_element_type=jnp.float32
    )


def against(left, right):
    return lax.dot_general(
        left, right, (((1,), (1,)), ((), ())), preferred_element_type=jnp.float32
    )


def norm_back(grad_output, unit_rows, inverse, gain):
    scaled = grad_output * gain
    gain_grad = jnp.sum(grad_output * unit_rows, axis=0)
    inner_mean = jnp.mean(scaled * unit_rows, axis=-1, keepdims=True)
    return (inverse * (scaled - unit_rows * inner_mean), gain_grad)


def adam_step(weight, first, second, gradient, clip_factor, step_float, step_rate, decay_rate):
    gradient = gradient * clip_factor
    first = beta_first * first + (1.0 - beta_first) * gradient
    second = beta_second * second + (1.0 - beta_second) * gradient * gradient
    correct_one = 1.0 - jnp.power(beta_first, step_float)
    correct_two = 1.0 - jnp.power(beta_second, step_float)
    update = first / correct_one / (jnp.sqrt(second / correct_two) + adam_eps)
    return (first, second, weight - step_rate * (update + decay_rate * weight))


def on_device(
    n,
    m,
    tokens,
    cotangent,
    segment_ids,
    step_count,
    norm_gains,
    gains_first,
    gains_second,
    w_query,
    query_first,
    query_second,
    w_keyval,
    keyval_first,
    keyval_second,
    w_out,
    out_first,
    out_second,
    w_gateup,
    gateup_first,
    gateup_second,
    w_down,
    down_first,
    down_second,
):
    low = jnp.bfloat16
    width = w_query.shape[1]
    kv_width = w_keyval.shape[2]
    gain_rows = lax.all_gather(norm_gains.astype(low), "dp", axis=1, tiled=True)
    qkv_shard = jnp.concatenate([w_query, w_keyval[0], w_keyval[1]], axis=1).astype(low)
    qkv_weight = lax.all_gather(qkv_shard, "dp", axis=0, tiled=True)
    out_weight = lax.all_gather(w_out.astype(low), "dp", axis=1, tiled=True)
    gateup_weight = lax.all_gather(w_gateup.astype(low), "dp", axis=1, tiled=True)
    down_weight = lax.all_gather(w_down.astype(low), "dp", axis=1, tiled=True)
    gain_values = gain_rows.astype(jnp.float32)
    length = tokens.shape[0]
    size = min(256, length)
    segment = segment_ids[0]
    places = positions(segment)
    cosines, sines = paired_tables(places)
    first = (jnp.arange(length, dtype=jnp.int32) - places)[::size] // size
    seg_col, seg_row = segment[:, None], segment[None, :]

    values_in = tokens.astype(jnp.float32)
    inverse_one = lax.rsqrt(jnp.mean(values_in * values_in, axis=-1, keepdims=True) + norm_eps)
    unit_one = values_in * inverse_one
    normed_one = (unit_one * gain_values[0]).astype(low)
    raw = jnp.dot(normed_one, qkv_weight, preferred_element_type=jnp.float32)
    mixture, q, k, v, lse = attention_forward(raw, cosines, sines, seg_col, seg_row, first, size)
    branch_part = jnp.dot(mixture, out_weight, preferred_element_type=jnp.float32).astype(low)
    branch = line_reduce(branch_part, n, 16, 1, 2)
    middle = values_in + branch.astype(jnp.float32)
    inverse_two = lax.rsqrt(jnp.mean(middle * middle, axis=-1, keepdims=True) + norm_eps)
    unit_two = middle * inverse_two
    normed_two = (unit_two * gain_values[1]).astype(low)
    gateup = jnp.einsum(
        "nd,sdf->snf", normed_two, gateup_weight, preferred_element_type=jnp.float32
    )
    gate_values = gateup[0]
    up_values = gateup[1]
    sigmoid_gate = jax.nn.sigmoid(gate_values)
    silu_gate = gate_values * sigmoid_gate
    hidden = (silu_gate * up_values).astype(low)
    grad_hidden = against(cotangent, down_weight)
    grad_gate = grad_hidden * up_values * sigmoid_gate * (1.0 + gate_values * (1.0 - sigmoid_gate))
    grad_up = grad_hidden * silu_gate
    grad_gateup = jnp.stack([grad_gate, grad_up]).astype(low)
    partial_two = jnp.einsum(
        "snf,sdf->nd", grad_gateup, gateup_weight, preferred_element_type=jnp.float32
    ).astype(low)
    grad_down_weight = over_rows(hidden, cotangent).astype(low)
    grad_gateup_weight = jnp.einsum(
        "nd,snf->sdf", normed_two, grad_gateup, preferred_element_type=jnp.float32
    ).astype(low)
    partial_two, grad_gateup_weight, grad_down_weight = lax.optimization_barrier(
        (partial_two, grad_gateup_weight, grad_down_weight)
    )
    gateup_reduced = lax.psum_scatter(grad_gateup_weight, "dp", scatter_dimension=1, tiled=True)
    down_reduced = lax.psum_scatter(grad_down_weight, "dp", scatter_dimension=1, tiled=True)
    grad_normed_two = line_reduce(partial_two, n, 16, 2, 2)
    feed_part = jnp.dot(hidden, down_weight, preferred_element_type=jnp.float32).astype(low)
    feed_out = lax.psum(feed_part, "tensor").astype(jnp.float32)
    layer_out = (middle + feed_out).astype(low)
    grad_from_two, gain_grad_two = norm_back(
        grad_normed_two.astype(jnp.float32), unit_two, inverse_two, gain_values[1]
    )
    grad_middle = cotangent.astype(jnp.float32) + grad_from_two
    grad_branch = grad_middle.astype(low)
    grad_mixture = against(grad_branch, out_weight).astype(low)
    grad_qkv = attention_backward(
        q, k, v, mixture, grad_mixture, lse, cosines, sines, seg_col, seg_row, first, size
    )
    partial_one = against(grad_qkv, qkv_weight).astype(low)
    grad_out_weight = over_rows(mixture, grad_branch).astype(low)
    grad_qkv_weight = over_rows(normed_one, grad_qkv).astype(low)
    partial_one, grad_out_weight, grad_qkv_weight = lax.optimization_barrier(
        (partial_one, grad_out_weight, grad_qkv_weight)
    )
    out_reduced = lax.psum_scatter(grad_out_weight, "dp", scatter_dimension=1, tiled=True)
    qkv_reduced = lax.psum_scatter(grad_qkv_weight, "dp", scatter_dimension=0, tiled=True)
    grad_normed_one = line_reduce(partial_one, n, 16, 3, 2).astype(jnp.float32)
    grad_from_one, gain_grad_one = norm_back(grad_normed_one, unit_one, inverse_one, gain_values[0])
    input_grad = grad_middle + grad_from_one
    gain_grads = jnp.stack([gain_grad_one, gain_grad_two])
    gains_reduced = lax.psum_scatter(gain_grads, "dp", scatter_dimension=1, tiled=True)
    qkv_reduced = qkv_reduced.astype(jnp.float32)
    reduced = (
        gains_reduced,
        qkv_reduced[:, :width],
        jnp.stack([qkv_reduced[:, width : width + kv_width], qkv_reduced[:, width + kv_width :]]),
        out_reduced.astype(jnp.float32),
        gateup_reduced.astype(jnp.float32),
        down_reduced.astype(jnp.float32),
    )
    first_owner = (lax.axis_index("tensor") == 0).astype(jnp.float32)
    local_square = first_owner * jnp.sum(reduced[0] * reduced[0]) + sum(
        (jnp.sum(g * g) for g in reduced[1:])
    )
    square_total = total_sum(local_square, n, m, 4)
    grad_norm = jnp.sqrt(square_total)
    clip_factor = jnp.minimum(1.0, clip_limit / (grad_norm + 1e-06))
    step_float = step_count[0].astype(jnp.float32)
    params = (norm_gains, w_query, w_keyval, w_out, w_gateup, w_down)
    states = (
        (gains_first, gains_second),
        (query_first, query_second),
        (keyval_first, keyval_second),
        (out_first, out_second),
        (gateup_first, gateup_second),
        (down_first, down_second),
    )
    step_rates = (gain_rate, weight_rate, weight_rate, out_rate, weight_rate, weight_rate)
    decay_rates = (0.0, weight_decay, weight_decay, weight_decay, weight_decay, weight_decay)
    results = []
    for position_index in range(6):
        one, two = states[position_index]
        results.extend(
            adam_step(
                params[position_index],
                one,
                two,
                reduced[position_index],
                clip_factor,
                step_float,
                step_rates[position_index],
                decay_rates[position_index],
            )
        )
    return (layer_out, input_grad, grad_norm.reshape(1), *results)


def solution(mesh):
    rows = P("dp", None)
    gains = P(None, "dp")
    query = P("dp", "tensor")
    stacked = P(None, "dp", "tensor")
    turned = P("tensor", "dp")
    states = (gains,) * 3 + (query,) * 3 + (stacked,) * 3 + (turned,) * 3 + (stacked,) * 3 + (turned,) * 3
    return jax.shard_map(
        functools.partial(on_device, mesh.shape["tensor"], mesh.shape["dp"]),
        mesh=mesh,
        in_specs=(rows, rows, rows, P()) + states,
        out_specs=(rows, rows, P()) + states,
        check_vma=False,
    )
```

```python
import functools

import jax
import jax.numpy as jnp
from jax import lax
from jax.experimental import pallas as pl
from jax.experimental.pallas import tpu as pltpu
from jax.sharding import PartitionSpec as P

HD = 64
MESH = pl.DeviceIdType.MESH


masked_value = -1e9


def dot_t(left, right):
    return lax.dot_general(left, right, (((1,), (1,)), ((), ())), preferred_element_type=jnp.float32)


def dot_n(left, right):
    return lax.dot_general(left, right, (((1,), (0,)), ((), ())), preferred_element_type=jnp.float32)


def swap_halves(values, first_half):
    return jnp.where(first_half, pltpu.roll(values, 96, 1), pltpu.roll(values, 32, 1))


def lane_tests(rows):
    lane = lax.broadcasted_iota(jnp.int32, (rows, 128), 1)
    return lane < 64, (lane % 64) < 32


def block_bias(seg_col_ref, seg_row_ref, i, j, size):
    keys = seg_col_ref[pl.ds(pl.multiple_of(j * size, size), size), :]
    rows = seg_row_ref[:, pl.ds(pl.multiple_of(i * size, size), size)]
    key_at = j * size + lax.broadcasted_iota(jnp.int32, (size, size), 0)
    row_at = i * size + lax.broadcasted_iota(jnp.int32, (size, size), 1)
    return jnp.where((keys == rows) & (key_at <= row_at), 0.0, masked_value)


def stack_pair(pair, low_lanes):
    zero = jnp.zeros_like(pair)
    return jnp.concatenate([jnp.where(low_lanes, pair, zero), jnp.where(low_lanes, zero, pair)], axis=0)


def forward_kernel(size, pairs, first_ref, raw_ref, cos_ref, sin_ref, seg_col_ref, seg_row_ref,
                   mix_ref, q_ref, k_ref, v_ref, lse_ref, bias, scores, v_turned):
    length = raw_ref.shape[0]
    low_lanes, first_half = lane_tests(size)
    low_rows = lax.broadcasted_iota(jnp.int32, (128, size), 0) < 64
    width = pairs * 128

    def prepare(i, carry):
        rows = pl.ds(pl.multiple_of(i * size, size), size)
        cosines, sines = cos_ref[rows, :], sin_ref[rows, :]
        for hp in range(pairs):
            values = raw_ref[rows, hp * 128:(hp + 1) * 128]
            turned = values * cosines + swap_halves(values, first_half) * sines
            q_ref[rows, hp * 128:(hp + 1) * 128] = (turned.astype(jnp.bfloat16).astype(jnp.float32) * 0.125).astype(jnp.bfloat16)
        both = raw_ref[rows, width:width + 128]
        other = pltpu.roll(both, 64, 1)
        keys = jnp.where(low_lanes, both, other)
        k_ref[rows, :] = (keys * cosines + swap_halves(keys, first_half) * sines).astype(jnp.bfloat16)
        values = jnp.where(low_lanes, other, both)
        v_ref[rows, :] = values.astype(jnp.bfloat16)
        v_turned[i] = values.T.astype(jnp.bfloat16)
        return carry

    lax.fori_loop(0, length // size, prepare, 0)

    def row_block(i, carry):
        rows = pl.ds(pl.multiple_of(i * size, size), size)
        begin = first_ref[i]

        def fill(j, c):
            bias[j] = block_bias(seg_col_ref, seg_row_ref, i, j, size)
            return c

        lax.fori_loop(begin, i + 1, fill, 0)

        for hp in range(pairs):
            stacked = stack_pair(q_ref[rows, hp * 128:(hp + 1) * 128], low_lanes)

            def score(j, top):
                keys = k_ref[pl.ds(pl.multiple_of(j * size, size), size), :]
                b = bias[j]
                s = dot_t(keys, stacked) + jnp.concatenate([b, b], axis=1)
                scores[j] = s
                return jnp.maximum(top, jnp.max(s, axis=0, keepdims=True))

            top = lax.fori_loop(begin, i + 1, score, jnp.full((1, 2 * size), -jnp.inf, jnp.float32))

            def mix(j, c):
                total, acc = c
                p = jnp.exp(scores[j] - top)
                total = total + jnp.sum(p, axis=0, keepdims=True)
                return total, acc + dot_n(v_turned[j], p.astype(jnp.bfloat16))

            total, acc = lax.fori_loop(begin, i + 1, mix, (
                jnp.zeros((1, 2 * size), jnp.float32), jnp.zeros((128, 2 * size), jnp.float32)))
            lse_ref[i, hp] = top + jnp.log(total)
            acc = acc / total
            acc = jnp.where(low_rows, acc[:, :size], acc[:, size:])
            mix_ref[rows, hp * 128:(hp + 1) * 128] = acc.T.astype(jnp.bfloat16)
        return carry

    lax.fori_loop(0, length // size, row_block, 0)


def attention_forward(raw, cosines, sines, seg_col, seg_row, first, size):
    length, wide = raw.shape
    width = wide - 128
    pairs = width // 128
    blocks = length // size
    vmem = pl.BlockSpec(memory_space=pltpu.VMEM)
    return pl.pallas_call(
        functools.partial(forward_kernel, size, pairs),
        out_shape=(
            jax.ShapeDtypeStruct((length, width), jnp.bfloat16),
            jax.ShapeDtypeStruct((length, width), jnp.bfloat16),
            jax.ShapeDtypeStruct((length, 128), jnp.bfloat16),
            jax.ShapeDtypeStruct((length, 128), jnp.bfloat16),
            jax.ShapeDtypeStruct((blocks, pairs, 1, 2 * size), jnp.float32),
        ),
        in_specs=[pl.BlockSpec(memory_space=pltpu.SMEM)] + [vmem] * 5,
        out_specs=(vmem,) * 5,
        scratch_shapes=[
            pltpu.VMEM((blocks, size, size), jnp.float32),
            pltpu.VMEM((blocks, size, 2 * size), jnp.float32),
            pltpu.VMEM((blocks, 128, size), jnp.bfloat16),
        ],
        compiler_params=pltpu.CompilerParams(vmem_limit_bytes=40 << 20),
        cost_estimate=pl.CostEstimate(flops=10 * length * length * width, bytes_accessed=8 * length * width,
                                      transcendentals=length * length * pairs),
    )(first, raw, cosines, sines, seg_col, seg_row)


def backward_kernel(size, pairs, first_ref, q_ref, k_ref, v_ref, mix_ref, grad_ref, lse_ref, cos_ref, sin_ref,
                    seg_col_ref, seg_row_ref, out_ref, bias, k_turned, grad_k, grad_v):
    length = q_ref.shape[0]
    width = pairs * 128
    low_lanes, first_half = lane_tests(size)
    low_rows = lax.broadcasted_iota(jnp.int32, (128, size), 0) < 64

    def prepare(i, carry):
        rows = pl.ds(pl.multiple_of(i * size, size), size)
        k_turned[i] = k_ref[rows, :].astype(jnp.float32).T.astype(jnp.bfloat16)
        grad_k[i] = jnp.zeros((size, 128), jnp.float32)
        grad_v[i] = jnp.zeros((size, 128), jnp.float32)
        return carry

    lax.fori_loop(0, length // size, prepare, 0)

    def row_block(i, carry):
        rows = pl.ds(pl.multiple_of(i * size, size), size)
        begin = first_ref[i]
        cosines, sines = cos_ref[rows, :], sin_ref[rows, :]

        def fill(j, c):
            bias[j] = block_bias(seg_col_ref, seg_row_ref, i, j, size)
            return c

        lax.fori_loop(begin, i + 1, fill, 0)

        for hp in range(pairs):
            columns = slice(hp * 128, (hp + 1) * 128)
            stacked = stack_pair(q_ref[rows, columns], low_lanes)
            grad_pair = grad_ref[rows, columns]
            grad_stacked = stack_pair(grad_pair, low_lanes)
            product = (grad_pair.astype(jnp.float32) * mix_ref[rows, columns].astype(jnp.float32)).T
            spread = jnp.concatenate([
                jnp.sum(product[:64], axis=0, keepdims=True), jnp.sum(product[64:], axis=0, keepdims=True)], axis=1)
            logsum = lse_ref[i, hp]

            def piece(j, acc):
                at = pl.ds(pl.multiple_of(j * size, size), size)
                b = bias[j]
                s = dot_t(k_ref[at, :], stacked) + jnp.concatenate([b, b], axis=1)
                p = jnp.exp(s - logsum)
                grad_p = dot_t(v_ref[at, :], grad_stacked)
                grad_s = (p * (grad_p - spread)).astype(jnp.bfloat16)
                grad_v[j] += dot_n(p.astype(jnp.bfloat16), grad_stacked)
                grad_k[j] += dot_n(grad_s, stacked)
                return acc + dot_n(k_turned[j], grad_s)

            acc = lax.fori_loop(begin, i + 1, piece, jnp.zeros((128, 2 * size), jnp.float32))
            acc = jnp.where(low_rows, acc[:, :size], acc[:, size:]).T * 0.125
            out_ref[rows, columns] = (acc * cosines - swap_halves(acc, first_half) * sines).astype(jnp.bfloat16)
        return carry

    lax.fori_loop(0, length // size, row_block, 0)

    def finish(i, carry):
        rows = pl.ds(pl.multiple_of(i * size, size), size)
        cosines, sines = cos_ref[rows, :], sin_ref[rows, :]
        dk = grad_k[i] + pltpu.roll(grad_k[i], 64, 1)
        dk = dk * cosines - swap_halves(dk, first_half) * sines
        dv = grad_v[i] + pltpu.roll(grad_v[i], 64, 1)
        out_ref[rows, width:width + 128] = jnp.where(low_lanes, dk, dv).astype(jnp.bfloat16)
        return carry

    lax.fori_loop(0, length // size, finish, 0)


def attention_backward(q, k, v, mix, grad, lse, cosines, sines, seg_col, seg_row, first, size):
    length, width = q.shape
    pairs = width // 128
    blocks = length // size
    vmem = pl.BlockSpec(memory_space=pltpu.VMEM)
    return pl.pallas_call(
        functools.partial(backward_kernel, size, pairs),
        out_shape=jax.ShapeDtypeStruct((length, width + 128), jnp.bfloat16),
        in_specs=[pl.BlockSpec(memory_space=pltpu.SMEM)] + [vmem] * 10,
        out_specs=vmem,
        scratch_shapes=[
            pltpu.VMEM((blocks, size, size), jnp.float32),
            pltpu.VMEM((blocks, 128, size), jnp.bfloat16),
            pltpu.VMEM((blocks, size, 128), jnp.float32),
            pltpu.VMEM((blocks, size, 128), jnp.float32),
        ],
        compiler_params=pltpu.CompilerParams(vmem_limit_bytes=40 << 20),
        cost_estimate=pl.CostEstimate(flops=20 * length * length * width, bytes_accessed=8 * length * width,
                                      transcendentals=length * length * pairs),
    )(first, q, k, v, mix, grad, lse, cosines, sines, seg_col, seg_row)


def line_reduce(partial, n, chunks, cid, lagk=1):
    rows, width = partial.shape
    half = rows // 2
    rc = half // chunks

    def kernel(in_ref, out_ref, got, send_a, recv_a, send_g, recv_g):
        me = lax.axis_index("tensor")
        barrier = pltpu.get_barrier_semaphore()

        @pl.when(me > 0)
        def _():
            pl.semaphore_signal(barrier, inc=1, device_id={"tensor": me - 1}, device_id_type=MESH)

        @pl.when(me < n - 1)
        def _():
            pl.semaphore_signal(barrier, inc=1, device_id={"tensor": me + 1}, device_id_type=MESH)

        @pl.when((me > 0) & (me < n - 1))
        def _():
            pl.semaphore_wait(barrier, 2)

        @pl.when((me == 0) | (me == n - 1))
        def _():
            pl.semaphore_wait(barrier, 1)

        def rs(stream, c, nxt, src):
            return pltpu.make_async_remote_copy(
                src_ref=src, dst_ref=got.at[stream, c],
                send_sem=send_a.at[stream, c], recv_sem=recv_a.at[stream, c],
                device_id={"tensor": nxt}, device_id_type=MESH)

        def ag(stream, c, nxt):
            r0 = pl.multiple_of(stream * half + c * rc, rc)
            return pltpu.make_async_remote_copy(
                src_ref=out_ref.at[pl.ds(r0, rc)], dst_ref=out_ref.at[pl.ds(r0, rc)],
                send_sem=send_g.at[stream, c], recv_sem=recv_g.at[stream, c],
                device_id={"tensor": nxt}, device_id_type=MESH)

        K = lagk
        steps = chunks + 2 * K * (n - 1)

        def body(s, carry):
            for stream in (0, 1):
                pos = me if stream == 0 else n - 1 - me
                fwd = me + 1 if stream == 0 else me - 1
                bwd = me - 1 if stream == 0 else me + 1
                c = s - K * pos

                @pl.when((c >= 0) & (c < chunks))
                def _():
                    r0 = pl.multiple_of(stream * half + c * rc, rc)

                    def summed():
                        rs(stream, c, fwd, got.at[stream, c]).wait_recv()
                        return (
                            in_ref[pl.ds(r0, rc)].astype(jnp.float32) + got[stream, c].astype(jnp.float32)
                        ).astype(out_ref.dtype)

                    @pl.when(pos == 0)
                    def _():
                        rs(stream, c, fwd, in_ref.at[pl.ds(r0, rc)]).start()

                    @pl.when((pos > 0) & (pos < n - 1))
                    def _():
                        got[stream, c] = summed()
                        rs(stream, c, fwd, got.at[stream, c]).start()

                    @pl.when(pos == n - 1)
                    def _():
                        out_ref[pl.ds(r0, rc)] = summed()
                        ag(stream, c, bwd).start()
                d = s - K * (n - 1) - K * (n - 1 - pos)

                @pl.when((d >= 0) & (d < chunks) & (pos < n - 1))
                def _():
                    ag(stream, d, bwd).wait_recv()

                    @pl.when(pos > 0)
                    def _():
                        ag(stream, d, bwd).start()
            return carry

        lax.fori_loop(0, steps, body, 0)

        def drain(c, carry):
            for stream in (0, 1):
                pos = me if stream == 0 else n - 1 - me
                fwd = me + 1 if stream == 0 else me - 1
                bwd = me - 1 if stream == 0 else me + 1

                @pl.when(pos < n - 1)
                def _():
                    rs(stream, c, fwd, got.at[stream, c]).wait_send()

                @pl.when(pos > 0)
                def _():
                    ag(stream, c, bwd).wait_send()
            return carry

        lax.fori_loop(0, chunks, drain, 0)

    return pl.pallas_call(
        kernel,
        out_shape=jax.ShapeDtypeStruct((rows, width), partial.dtype),
        in_specs=[pl.BlockSpec(memory_space=pltpu.VMEM)],
        out_specs=pl.BlockSpec(memory_space=pltpu.VMEM),
        scratch_shapes=[
            pltpu.VMEM((2, chunks, rc, width), partial.dtype),
            pltpu.SemaphoreType.DMA((2, chunks)),
            pltpu.SemaphoreType.DMA((2, chunks)),
            pltpu.SemaphoreType.DMA((2, chunks)),
            pltpu.SemaphoreType.DMA((2, chunks)),
        ],
        compiler_params=pltpu.CompilerParams(collective_id=cid, has_side_effects=True, vmem_limit_bytes=40 << 20),
        cost_estimate=pl.CostEstimate(flops=rows * width * 2, bytes_accessed=rows * width * 4 * 30, transcendentals=0),
    )(partial)


def total_kernel(n, m, gains_ref, square_ref, total_ref, gain_ref, line, got_gains, got_line, got_plane,
                 send_gains, recv_gains, send_line, recv_line, send_plane, recv_plane):
    z = lax.axis_index("tensor")
    d = lax.axis_index("dp")
    barrier = pltpu.get_barrier_semaphore()
    for k in range(1, n):
        pl.semaphore_signal(barrier, inc=1, device_id={"tensor": lax.rem(z + k, n)}, device_id_type=MESH)
    for k in range(1, m):
        pl.semaphore_signal(barrier, inc=1, device_id={"dp": lax.rem(d + k, m)}, device_id_type=MESH)
    pl.semaphore_wait(barrier, n - 1 + m - 1)

    def gains_to(k, sender):
        peer = lax.rem(d + k, m)
        return pltpu.make_async_remote_copy(
            src_ref=gains_ref.at[peer], dst_ref=got_gains.at[sender], send_sem=send_gains.at[k],
            recv_sem=recv_gains.at[sender], device_id={"dp": peer}, device_id_type=MESH)

    def along_line(k, sender):
        return pltpu.make_async_remote_copy(
            src_ref=line.at[0], dst_ref=got_line.at[sender], send_sem=send_line.at[k], recv_sem=recv_line.at[sender],
            device_id={"tensor": lax.rem(z + k, n)}, device_id_type=MESH)

    def over_plane(k, sender):
        return pltpu.make_async_remote_copy(
            src_ref=line.at[1], dst_ref=got_plane.at[sender], send_sem=send_plane.at[k], recv_sem=recv_plane.at[sender],
            device_id={"dp": lax.rem(d + k, m)}, device_id_type=MESH)

    def summed(ref, count):
        whole = ref[0]
        for k in range(1, count):
            whole = whole + ref[k]
        return whole

    for k in range(1, m):
        gains_to(k, d).start()
    got_gains[d] = gains_ref[d]
    for k in range(1, m):
        gains_to(k, d).wait_send()
        gains_to(k, lax.rem(d + m - k, m)).wait_recv()
    gains = summed(got_gains, m)
    gain_ref[...] = gains
    own = jnp.sum(jnp.sum(gains * gains, axis=1, keepdims=True), axis=0, keepdims=True)
    own = jnp.where(z == 0, own, jnp.zeros_like(own))
    line[0] = square_ref[...] + jnp.broadcast_to(own, square_ref.shape)
    for k in range(1, n):
        along_line(k, z).start()
    got_line[z] = line[0]
    for k in range(1, n):
        along_line(k, z).wait_send()
        along_line(k, lax.rem(z + n - k, n)).wait_recv()
    line[1] = summed(got_line, n)
    for k in range(1, m):
        over_plane(k, d).start()
    got_plane[d] = line[1]
    for k in range(1, m):
        over_plane(k, d).wait_send()
        over_plane(k, lax.rem(d + m - k, m)).wait_recv()
    total_ref[...] = summed(got_plane, m)


def reduce_tail(gains, square, n, m, cid):
    share = gains.shape[1] // m
    parts = gains.reshape(2, m, share).transpose(1, 0, 2)
    tile = jnp.broadcast_to(square.reshape(1, 1), (8, 128))
    vmem = pl.BlockSpec(memory_space=pltpu.VMEM)
    dma = pltpu.SemaphoreType.DMA
    total, gain = pl.pallas_call(
        functools.partial(total_kernel, n, m),
        out_shape=(jax.ShapeDtypeStruct((8, 128), jnp.float32), jax.ShapeDtypeStruct((2, share), jnp.float32)),
        in_specs=[vmem, vmem],
        out_specs=(vmem, vmem),
        scratch_shapes=[
            pltpu.VMEM((2, 8, 128), jnp.float32),
            pltpu.VMEM((m, 2, share), jnp.float32),
            pltpu.VMEM((n, 8, 128), jnp.float32),
            pltpu.VMEM((m, 8, 128), jnp.float32),
            dma((m,)), dma((m,)), dma((n,)), dma((n,)), dma((m,)), dma((m,)),
        ],
        compiler_params=pltpu.CompilerParams(collective_id=cid, has_side_effects=True),
    )(parts, tile)
    return total[0, 0], gain


norm_eps = 1e-05
beta_first = 0.9
beta_second = 0.95
adam_eps = 1e-08
weight_decay = 0.1
weight_rate = 0.02
out_rate = 0.1
gain_rate = 0.2
clip_limit = 1.0


def positions(segment):
    length = segment.shape[0]
    indices = jnp.arange(length, dtype=jnp.int32)
    earlier = jnp.concatenate([segment[:1] - 1, segment[:-1]])
    begins = jnp.where(segment != earlier, indices, jnp.zeros_like(indices))
    return indices - lax.cummax(begins, axis=0)


def paired_tables(places):
    frequency = jnp.power(10000.0, -jnp.arange(HD // 2, dtype=jnp.float32) * (2.0 / HD))
    angles = places.astype(jnp.float32)[:, None] * frequency[None, :]
    cosines, sines = jnp.cos(angles), jnp.sin(angles)
    return (
        jnp.concatenate([cosines] * 4, axis=-1),
        jnp.concatenate([-sines, sines, -sines, sines], axis=-1),
    )


def over_rows(left, right):
    return lax.dot_general(
        left, right, (((0,), (0,)), ((), ())), preferred_element_type=jnp.float32
    )


def against(left, right):
    return lax.dot_general(
        left, right, (((1,), (1,)), ((), ())), preferred_element_type=jnp.float32
    )


def norm_back(grad_output, unit_rows, inverse, gain):
    scaled = grad_output * gain
    gain_grad = jnp.sum(grad_output * unit_rows, axis=0)
    inner_mean = jnp.mean(scaled * unit_rows, axis=-1, keepdims=True)
    return (inverse * (scaled - unit_rows * inner_mean), gain_grad)


def adam_step(weight, first, second, gradient, clip_factor, step_float, step_rate, decay_rate):
    gradient = gradient * clip_factor
    first = beta_first * first + (1.0 - beta_first) * gradient
    second = beta_second * second + (1.0 - beta_second) * gradient * gradient
    correct_one = 1.0 - jnp.power(beta_first, step_float)
    correct_two = 1.0 - jnp.power(beta_second, step_float)
    update = first / correct_one / (jnp.sqrt(second / correct_two) + adam_eps)
    return (first, second, weight - step_rate * (update + decay_rate * weight))


def on_device(
    n,
    m,
    tokens,
    cotangent,
    segment_ids,
    step_count,
    norm_gains,
    gains_first,
    gains_second,
    w_query,
    query_first,
    query_second,
    w_keyval,
    keyval_first,
    keyval_second,
    w_out,
    out_first,
    out_second,
    w_gateup,
    gateup_first,
    gateup_second,
    w_down,
    down_first,
    down_second,
):
    low = jnp.bfloat16
    width = w_query.shape[1]
    kv_width = w_keyval.shape[2]
    gain_rows = lax.all_gather(norm_gains.astype(low), "dp", axis=1, tiled=True)
    qkv_shard = jnp.concatenate([w_query, w_keyval[0], w_keyval[1]], axis=1).astype(low)
    qkv_weight = lax.all_gather(qkv_shard, "dp", axis=0, tiled=True)
    out_weight = lax.all_gather(w_out.astype(low), "dp", axis=1, tiled=True)
    gateup_weight = lax.all_gather(w_gateup.astype(low), "dp", axis=1, tiled=True)
    down_weight = lax.all_gather(w_down.astype(low), "dp", axis=1, tiled=True)
    gain_values = gain_rows.astype(jnp.float32)
    length = tokens.shape[0]
    size = min(256, length)
    segment = segment_ids[0]
    places = positions(segment)
    cosines, sines = paired_tables(places)
    first = (jnp.arange(length, dtype=jnp.int32) - places)[::size] // size
    seg_col, seg_row = segment[:, None], segment[None, :]

    values_in = tokens.astype(jnp.float32)
    inverse_one = lax.rsqrt(jnp.mean(values_in * values_in, axis=-1, keepdims=True) + norm_eps)
    unit_one = values_in * inverse_one
    normed_one = (unit_one * gain_values[0]).astype(low)
    raw = jnp.dot(normed_one, qkv_weight, preferred_element_type=jnp.float32)
    mixture, q, k, v, lse = attention_forward(raw, cosines, sines, seg_col, seg_row, first, size)
    branch_part = jnp.dot(mixture, out_weight, preferred_element_type=jnp.float32).astype(low)
    branch = line_reduce(branch_part, n, 16, 1, 2)
    middle = values_in + branch.astype(jnp.float32)
    inverse_two = lax.rsqrt(jnp.mean(middle * middle, axis=-1, keepdims=True) + norm_eps)
    unit_two = middle * inverse_two
    normed_two = (unit_two * gain_values[1]).astype(low)
    gateup = jnp.einsum(
        "nd,sdf->snf", normed_two, gateup_weight, preferred_element_type=jnp.float32
    )
    gate_values = gateup[0]
    up_values = gateup[1]
    sigmoid_gate = jax.nn.sigmoid(gate_values)
    silu_gate = gate_values * sigmoid_gate
    hidden = (silu_gate * up_values).astype(low)
    grad_hidden = against(cotangent, down_weight)
    grad_gate = grad_hidden * up_values * sigmoid_gate * (1.0 + gate_values * (1.0 - sigmoid_gate))
    grad_up = grad_hidden * silu_gate
    grad_gateup = jnp.stack([grad_gate, grad_up]).astype(low)
    partial_two = jnp.einsum(
        "snf,sdf->nd", grad_gateup, gateup_weight, preferred_element_type=jnp.float32
    ).astype(low)
    grad_down_weight = over_rows(hidden, cotangent).astype(low)
    grad_gateup_weight = jnp.einsum(
        "nd,snf->sdf", normed_two, grad_gateup, preferred_element_type=jnp.float32
    ).astype(low)
    partial_two, grad_gateup_weight, grad_down_weight = lax.optimization_barrier(
        (partial_two, grad_gateup_weight, grad_down_weight)
    )
    gateup_reduced = lax.psum_scatter(grad_gateup_weight, "dp", scatter_dimension=1, tiled=True)
    down_reduced = lax.psum_scatter(grad_down_weight, "dp", scatter_dimension=1, tiled=True)
    grad_normed_two = line_reduce(partial_two, n, 16, 2, 2)
    grad_normed_two, gateup_reduced = lax.optimization_barrier((grad_normed_two, gateup_reduced))
    feed_part = jnp.dot(hidden, down_weight, preferred_element_type=jnp.float32).astype(low)
    grad_from_two, gain_grad_two = norm_back(
        grad_normed_two.astype(jnp.float32), unit_two, inverse_two, gain_values[1]
    )
    grad_middle = cotangent.astype(jnp.float32) + grad_from_two
    grad_branch = grad_middle.astype(low)
    grad_mixture = against(grad_branch, out_weight).astype(low)
    grad_qkv = attention_backward(
        q, k, v, mixture, grad_mixture, lse, cosines, sines, seg_col, seg_row, first, size
    )
    partial_one = against(grad_qkv, qkv_weight).astype(low)
    grad_out_weight = over_rows(mixture, grad_branch).astype(low)
    grad_qkv_weight = over_rows(normed_one, grad_qkv).astype(low)
    partial_one, grad_out_weight, grad_qkv_weight, down_reduced = lax.optimization_barrier(
        (partial_one, grad_out_weight, grad_qkv_weight, down_reduced)
    )
    out_reduced = lax.psum_scatter(grad_out_weight, "dp", scatter_dimension=1, tiled=True)
    qkv_reduced = lax.psum_scatter(grad_qkv_weight, "dp", scatter_dimension=0, tiled=True)
    summed = line_reduce(jnp.concatenate([partial_one, feed_part]), n, 32, 3, 2).astype(jnp.float32)
    grad_normed_one = summed[:length]
    layer_out = (middle + summed[length:]).astype(low)
    grad_from_one, gain_grad_one = norm_back(grad_normed_one, unit_one, inverse_one, gain_values[0])
    input_grad = grad_middle + grad_from_one
    gain_grads = jnp.stack([gain_grad_one, gain_grad_two])
    qkv_reduced = qkv_reduced.astype(jnp.float32)
    reduced = (
        qkv_reduced[:, :width],
        jnp.stack([qkv_reduced[:, width : width + kv_width], qkv_reduced[:, width + kv_width :]]),
        out_reduced.astype(jnp.float32),
        gateup_reduced.astype(jnp.float32),
        down_reduced.astype(jnp.float32),
    )
    local_square = sum((jnp.sum(g * g) for g in reduced))
    square_total, gains_reduced = reduce_tail(gain_grads, local_square, n, m, 4)
    reduced = (gains_reduced, *reduced)
    grad_norm = jnp.sqrt(square_total)
    clip_factor = jnp.minimum(1.0, clip_limit / (grad_norm + 1e-06))
    step_float = step_count[0].astype(jnp.float32)
    params = (norm_gains, w_query, w_keyval, w_out, w_gateup, w_down)
    states = (
        (gains_first, gains_second),
        (query_first, query_second),
        (keyval_first, keyval_second),
        (out_first, out_second),
        (gateup_first, gateup_second),
        (down_first, down_second),
    )
    step_rates = (gain_rate, weight_rate, weight_rate, out_rate, weight_rate, weight_rate)
    decay_rates = (0.0, weight_decay, weight_decay, weight_decay, weight_decay, weight_decay)
    results = []
    for position_index in range(6):
        one, two = states[position_index]
        results.extend(
            adam_step(
                params[position_index],
                one,
                two,
                reduced[position_index],
                clip_factor,
                step_float,
                step_rates[position_index],
                decay_rates[position_index],
            )
        )
    return (layer_out, input_grad, grad_norm.reshape(1), *results)


def solution(mesh):
    rows = P("dp", None)
    gains = P(None, "dp")
    query = P("dp", "tensor")
    stacked = P(None, "dp", "tensor")
    turned = P("tensor", "dp")
    states = (gains,) * 3 + (query,) * 3 + (stacked,) * 3 + (turned,) * 3 + (stacked,) * 3 + (turned,) * 3
    return jax.shard_map(
        functools.partial(on_device, mesh.shape["tensor"], mesh.shape["dp"]),
        mesh=mesh,
        in_specs=(rows, rows, rows, P()) + states,
        out_specs=(rows, rows, P()) + states,
        check_vma=False,
    )
```

```python
import functools

import jax
import jax.numpy as jnp
from jax import lax
from jax.experimental import pallas as pl
from jax.experimental.pallas import tpu as pltpu
from jax.sharding import PartitionSpec as P

HD = 64
MESH = pl.DeviceIdType.MESH


masked_value = -1e9


def dot_t(left, right):
    return lax.dot_general(left, right, (((1,), (1,)), ((), ())), preferred_element_type=jnp.float32)


def dot_n(left, right):
    return lax.dot_general(left, right, (((1,), (0,)), ((), ())), preferred_element_type=jnp.float32)


def swap_halves(values, first_half):
    return jnp.where(first_half, pltpu.roll(values, 96, 1), pltpu.roll(values, 32, 1))


def lane_tests(rows):
    lane = lax.broadcasted_iota(jnp.int32, (rows, 128), 1)
    return lane < 64, (lane % 64) < 32


def block_bias(seg_col_ref, seg_row_ref, i, j, size):
    keys = seg_col_ref[pl.ds(pl.multiple_of(j * size, size), size), :]
    rows = seg_row_ref[:, pl.ds(pl.multiple_of(i * size, size), size)]
    key_at = j * size + lax.broadcasted_iota(jnp.int32, (size, size), 0)
    row_at = i * size + lax.broadcasted_iota(jnp.int32, (size, size), 1)
    return jnp.where((keys == rows) & (key_at <= row_at), 0.0, masked_value)


def stack_pair(pair, low_lanes):
    zero = jnp.zeros_like(pair)
    return jnp.concatenate([jnp.where(low_lanes, pair, zero), jnp.where(low_lanes, zero, pair)], axis=0)


def forward_kernel(size, pairs, first_ref, raw_ref, cos_ref, sin_ref, seg_col_ref, seg_row_ref,
                   mix_ref, q_ref, k_ref, v_ref, lse_ref, bias, scores, v_turned):
    length = raw_ref.shape[0]
    low_lanes, first_half = lane_tests(size)
    low_rows = lax.broadcasted_iota(jnp.int32, (128, size), 0) < 64
    width = pairs * 128

    def prepare(i, carry):
        rows = pl.ds(pl.multiple_of(i * size, size), size)
        cosines, sines = cos_ref[rows, :], sin_ref[rows, :]
        for hp in range(pairs):
            values = raw_ref[rows, hp * 128:(hp + 1) * 128]
            turned = values * cosines + swap_halves(values, first_half) * sines
            q_ref[rows, hp * 128:(hp + 1) * 128] = (turned.astype(jnp.bfloat16).astype(jnp.float32) * 0.125).astype(jnp.bfloat16)
        both = raw_ref[rows, width:width + 128]
        other = pltpu.roll(both, 64, 1)
        keys = jnp.where(low_lanes, both, other)
        k_ref[rows, :] = (keys * cosines + swap_halves(keys, first_half) * sines).astype(jnp.bfloat16)
        values = jnp.where(low_lanes, other, both)
        v_ref[rows, :] = values.astype(jnp.bfloat16)
        v_turned[i] = values.T.astype(jnp.bfloat16)
        return carry

    lax.fori_loop(0, length // size, prepare, 0)

    def row_block(i, carry):
        rows = pl.ds(pl.multiple_of(i * size, size), size)
        begin = first_ref[i]

        def fill(j, c):
            bias[j] = block_bias(seg_col_ref, seg_row_ref, i, j, size)
            return c

        lax.fori_loop(begin, i + 1, fill, 0)

        for hp in range(pairs):
            stacked = stack_pair(q_ref[rows, hp * 128:(hp + 1) * 128], low_lanes)

            def score(j, top):
                keys = k_ref[pl.ds(pl.multiple_of(j * size, size), size), :]
                b = bias[j]
                s = dot_t(keys, stacked) + jnp.concatenate([b, b], axis=1)
                scores[j] = s
                return jnp.maximum(top, jnp.max(s, axis=0, keepdims=True))

            top = lax.fori_loop(begin, i + 1, score, jnp.full((1, 2 * size), -jnp.inf, jnp.float32))

            def mix(j, c):
                total, acc = c
                p = jnp.exp(scores[j] - top)
                total = total + jnp.sum(p, axis=0, keepdims=True)
                return total, acc + dot_n(v_turned[j], p.astype(jnp.bfloat16))

            total, acc = lax.fori_loop(begin, i + 1, mix, (
                jnp.zeros((1, 2 * size), jnp.float32), jnp.zeros((128, 2 * size), jnp.float32)))
            lse_ref[i, hp] = top + jnp.log(total)
            acc = acc / total
            acc = jnp.where(low_rows, acc[:, :size], acc[:, size:])
            mix_ref[rows, hp * 128:(hp + 1) * 128] = acc.T.astype(jnp.bfloat16)
        return carry

    lax.fori_loop(0, length // size, row_block, 0)


def attention_forward(raw, cosines, sines, seg_col, seg_row, first, size):
    length, wide = raw.shape
    width = wide - 128
    pairs = width // 128
    blocks = length // size
    vmem = pl.BlockSpec(memory_space=pltpu.VMEM)
    return pl.pallas_call(
        functools.partial(forward_kernel, size, pairs),
        out_shape=(
            jax.ShapeDtypeStruct((length, width), jnp.bfloat16),
            jax.ShapeDtypeStruct((length, width), jnp.bfloat16),
            jax.ShapeDtypeStruct((length, 128), jnp.bfloat16),
            jax.ShapeDtypeStruct((length, 128), jnp.bfloat16),
            jax.ShapeDtypeStruct((blocks, pairs, 1, 2 * size), jnp.float32),
        ),
        in_specs=[pl.BlockSpec(memory_space=pltpu.SMEM)] + [vmem] * 5,
        out_specs=(vmem,) * 5,
        scratch_shapes=[
            pltpu.VMEM((blocks, size, size), jnp.float32),
            pltpu.VMEM((blocks, size, 2 * size), jnp.float32),
            pltpu.VMEM((blocks, 128, size), jnp.bfloat16),
        ],
        compiler_params=pltpu.CompilerParams(vmem_limit_bytes=40 << 20),
        cost_estimate=pl.CostEstimate(flops=10 * length * length * width, bytes_accessed=8 * length * width,
                                      transcendentals=length * length * pairs),
    )(first, raw, cosines, sines, seg_col, seg_row)


def backward_kernel(size, pairs, first_ref, q_ref, k_ref, v_ref, mix_ref, grad_ref, lse_ref, cos_ref, sin_ref,
                    seg_col_ref, seg_row_ref, out_ref, bias, k_turned, grad_k, grad_v):
    length = q_ref.shape[0]
    width = pairs * 128
    low_lanes, first_half = lane_tests(size)
    low_rows = lax.broadcasted_iota(jnp.int32, (128, size), 0) < 64

    def prepare(i, carry):
        rows = pl.ds(pl.multiple_of(i * size, size), size)
        k_turned[i] = k_ref[rows, :].astype(jnp.float32).T.astype(jnp.bfloat16)
        grad_k[i] = jnp.zeros((size, 128), jnp.float32)
        grad_v[i] = jnp.zeros((size, 128), jnp.float32)
        return carry

    lax.fori_loop(0, length // size, prepare, 0)

    def row_block(i, carry):
        rows = pl.ds(pl.multiple_of(i * size, size), size)
        begin = first_ref[i]
        cosines, sines = cos_ref[rows, :], sin_ref[rows, :]

        def fill(j, c):
            bias[j] = block_bias(seg_col_ref, seg_row_ref, i, j, size)
            return c

        lax.fori_loop(begin, i + 1, fill, 0)

        for hp in range(pairs):
            columns = slice(hp * 128, (hp + 1) * 128)
            stacked = stack_pair(q_ref[rows, columns], low_lanes)
            grad_pair = grad_ref[rows, columns]
            grad_stacked = stack_pair(grad_pair, low_lanes)
            product = (grad_pair.astype(jnp.float32) * mix_ref[rows, columns].astype(jnp.float32)).T
            spread = jnp.concatenate([
                jnp.sum(product[:64], axis=0, keepdims=True), jnp.sum(product[64:], axis=0, keepdims=True)], axis=1)
            logsum = lse_ref[i, hp]

            def piece(j, acc):
                at = pl.ds(pl.multiple_of(j * size, size), size)
                b = bias[j]
                s = dot_t(k_ref[at, :], stacked) + jnp.concatenate([b, b], axis=1)
                p = jnp.exp(s - logsum)
                grad_p = dot_t(v_ref[at, :], grad_stacked)
                grad_s = (p * (grad_p - spread)).astype(jnp.bfloat16)
                grad_v[j] += dot_n(p.astype(jnp.bfloat16), grad_stacked)
                grad_k[j] += dot_n(grad_s, stacked)
                return acc + dot_n(k_turned[j], grad_s)

            acc = lax.fori_loop(begin, i + 1, piece, jnp.zeros((128, 2 * size), jnp.float32))
            acc = jnp.where(low_rows, acc[:, :size], acc[:, size:]).T * 0.125
            out_ref[rows, columns] = (acc * cosines - swap_halves(acc, first_half) * sines).astype(jnp.bfloat16)
        return carry

    lax.fori_loop(0, length // size, row_block, 0)

    def finish(i, carry):
        rows = pl.ds(pl.multiple_of(i * size, size), size)
        cosines, sines = cos_ref[rows, :], sin_ref[rows, :]
        dk = grad_k[i] + pltpu.roll(grad_k[i], 64, 1)
        dk = dk * cosines - swap_halves(dk, first_half) * sines
        dv = grad_v[i] + pltpu.roll(grad_v[i], 64, 1)
        out_ref[rows, width:width + 128] = jnp.where(low_lanes, dk, dv).astype(jnp.bfloat16)
        return carry

    lax.fori_loop(0, length // size, finish, 0)


def attention_backward(q, k, v, mix, grad, lse, cosines, sines, seg_col, seg_row, first, size):
    length, width = q.shape
    pairs = width // 128
    blocks = length // size
    vmem = pl.BlockSpec(memory_space=pltpu.VMEM)
    return pl.pallas_call(
        functools.partial(backward_kernel, size, pairs),
        out_shape=jax.ShapeDtypeStruct((length, width + 128), jnp.bfloat16),
        in_specs=[pl.BlockSpec(memory_space=pltpu.SMEM)] + [vmem] * 10,
        out_specs=vmem,
        scratch_shapes=[
            pltpu.VMEM((blocks, size, size), jnp.float32),
            pltpu.VMEM((blocks, 128, size), jnp.bfloat16),
            pltpu.VMEM((blocks, size, 128), jnp.float32),
            pltpu.VMEM((blocks, size, 128), jnp.float32),
        ],
        compiler_params=pltpu.CompilerParams(vmem_limit_bytes=40 << 20),
        cost_estimate=pl.CostEstimate(flops=20 * length * length * width, bytes_accessed=8 * length * width,
                                      transcendentals=length * length * pairs),
    )(first, q, k, v, mix, grad, lse, cosines, sines, seg_col, seg_row)


class Line:
    def __init__(self, n, chunks, rc, lag, part, got, out, sems):
        self.n, self.chunks, self.rc, self.lag = n, chunks, rc, lag
        self.part, self.got, self.out = part, got, out
        self.send_a, self.recv_a, self.send_g, self.recv_g = sems
        self.me = lax.axis_index("tensor")
        self.steps = chunks + 2 * lag * (n - 1)

    def rows(self, stream, c):
        return pl.ds(pl.multiple_of((stream * self.chunks + c) * self.rc, self.rc), self.rc)

    def side(self, stream):
        pos = self.me if stream == 0 else self.n - 1 - self.me
        fwd = self.me + 1 if stream == 0 else self.me - 1
        bwd = self.me - 1 if stream == 0 else self.me + 1
        return pos, fwd, bwd

    def toward(self, stream, c, nxt, src):
        return pltpu.make_async_remote_copy(
            src_ref=src, dst_ref=self.got.at[stream, c],
            send_sem=self.send_a.at[stream, c], recv_sem=self.recv_a.at[stream, c],
            device_id={"tensor": nxt}, device_id_type=MESH)

    def back(self, stream, c, nxt):
        where = self.rows(stream, c)
        return pltpu.make_async_remote_copy(
            src_ref=self.out.at[where], dst_ref=self.out.at[where],
            send_sem=self.send_g.at[stream, c], recv_sem=self.recv_g.at[stream, c],
            device_id={"tensor": nxt}, device_id_type=MESH)

    def step(self, s):
        n, lag = self.n, self.lag
        for stream in (0, 1):
            pos, fwd, bwd = self.side(stream)
            c = s - lag * pos

            @pl.when((c >= 0) & (c < self.chunks))
            def _():
                where = self.rows(stream, c)
                slot = self.got.at[stream, c]

                def summed():
                    self.toward(stream, c, fwd, slot).wait_recv()
                    return (
                        self.part[where, :].astype(jnp.float32) + self.got[stream, c].astype(jnp.float32)
                    ).astype(self.out.dtype)

                @pl.when(pos == 0)
                def _():
                    self.toward(stream, c, fwd, self.part.at[where]).start()

                @pl.when((pos > 0) & (pos < n - 1))
                def _():
                    self.got[stream, c] = summed()
                    self.toward(stream, c, fwd, slot).start()

                @pl.when(pos == n - 1)
                def _():
                    self.out[where, :] = summed()
                    self.back(stream, c, bwd).start()
            d = s - lag * (n - 1) - lag * (n - 1 - pos)

            @pl.when((d >= 0) & (d < self.chunks) & (pos < n - 1))
            def _():
                self.back(stream, d, bwd).wait_recv()

                @pl.when(pos > 0)
                def _():
                    self.back(stream, d, bwd).start()

    def drain(self):
        def one(c, carry):
            for stream in (0, 1):
                pos, fwd, bwd = self.side(stream)

                @pl.when(pos < self.n - 1)
                def _():
                    self.toward(stream, c, fwd, self.got.at[stream, c]).wait_send()

                @pl.when(pos > 0)
                def _():
                    self.back(stream, c, bwd).wait_send()
            return carry

        lax.fori_loop(0, self.chunks, one, 0)


def greet(n):
    me = lax.axis_index("tensor")
    barrier = pltpu.get_barrier_semaphore()

    @pl.when(me > 0)
    def _():
        pl.semaphore_signal(barrier, inc=1, device_id={"tensor": me - 1}, device_id_type=MESH)

    @pl.when(me < n - 1)
    def _():
        pl.semaphore_signal(barrier, inc=1, device_id={"tensor": me + 1}, device_id_type=MESH)

    @pl.when((me > 0) & (me < n - 1))
    def _():
        pl.semaphore_wait(barrier, 2)

    @pl.when((me == 0) | (me == n - 1))
    def _():
        pl.semaphore_wait(barrier, 1)


def line_scratch(chunks, rc, width):
    return [pltpu.VMEM((2, chunks, rc, width), jnp.bfloat16)] + [pltpu.SemaphoreType.DMA((2, chunks))] * 4


def line_kernel(n, chunks, lag, count, *refs):
    parts, outs, scratch = refs[:count], refs[count:2 * count], refs[2 * count:]
    rc = parts[0].shape[0] // (2 * chunks)
    lines = [
        Line(n, chunks, rc, lag, parts[k], scratch[5 * k], outs[k], scratch[5 * k + 1:5 * k + 5])
        for k in range(count)
    ]
    greet(n)

    def step(s, carry):
        for k, line in enumerate(lines):
            line.step(s - k * chunks)
        return carry

    lax.fori_loop(0, lines[0].steps + (count - 1) * chunks, step, 0)
    for line in lines:
        line.drain()


def line_reduce(parts, n, chunks, cid, lag=2):
    rows, width = parts[0].shape
    count = len(parts)
    rc = rows // (2 * chunks)
    scratch = []
    for _ in parts:
        scratch += line_scratch(chunks, rc, width)
    vmem = pl.BlockSpec(memory_space=pltpu.VMEM)
    return pl.pallas_call(
        functools.partial(line_kernel, n, chunks, lag, count),
        out_shape=tuple(jax.ShapeDtypeStruct((rows, width), jnp.bfloat16) for _ in parts),
        in_specs=[vmem] * count,
        out_specs=(vmem,) * count,
        scratch_shapes=scratch,
        compiler_params=pltpu.CompilerParams(collective_id=cid, has_side_effects=True, vmem_limit_bytes=40 << 20),
        cost_estimate=pl.CostEstimate(flops=rows * width * 2 * count, bytes_accessed=rows * width * 120 * count,
                                      transcendentals=0),
    )(*parts)


def ff_kernel(n, chunks, lag, eps, part, gain, x_hbm, cot_hbm, gu_hbm, down_hbm,
              branch, two_sum, hidden_hbm, gg_hbm, feed_hbm, normed_hbm,
              got_one, sa1, ra1, sg1, rg1, got_two, sa2, ra2, sg2, rg2,
              two_part, gu_w, down_w, x_buf, cot_buf, normed, hidden, gg, feed,
              w_sem, x_sem, cot_sem, out_sem):
    rows, width = part.shape
    ff = down_w.shape[0]
    rc = rows // (2 * chunks)
    per = 4
    half = rows // 2
    hb = per * rc
    blocks = chunks // per
    one = Line(n, chunks, rc, lag, part, got_one, branch, (sa1, ra1, sg1, rg1))
    two = Line(n, chunks, rc, lag, two_part, got_two, two_sum, (sa2, ra2, sg2, rg2))
    ready = 2 * lag * (n - 1) + per
    tile = 256
    full, rest = ff // tile, ff % tile

    weights = (
        pltpu.make_async_copy(gu_hbm, gu_w, w_sem.at[0]),
        pltpu.make_async_copy(down_hbm, down_w, w_sem.at[1]),
    )
    for copy in weights:
        copy.start()

    def sides(b):
        for k in (0, 1):
            yield k, pl.ds(pl.multiple_of(k * half + b * hb, hb), hb), pl.ds(k * hb, hb)

    def load(src, buf, sem, b):
        return [pltpu.make_async_copy(src.at[where], buf.at[local], sem.at[k]) for k, where, local in sides(b)]

    def saves(b, which):
        copies = []
        for k, where, local in sides(b):
            if which == "normed":
                copies.append(pltpu.make_async_copy(normed.at[local], normed_hbm.at[where], out_sem.at[0, k]))
            if which == "tiles":
                copies.append(pltpu.make_async_copy(hidden.at[local], hidden_hbm.at[where], out_sem.at[1, k]))
                for t in (0, 1):
                    copies.append(pltpu.make_async_copy(gg.at[t, local], gg_hbm.at[t, where], out_sem.at[2 + t, k]))
            if which == "feed":
                copies.append(pltpu.make_async_copy(feed.at[local], feed_hbm.at[where], out_sem.at[4, k]))
        return copies

    def start(copies):
        for copy in copies:
            copy.start()

    def wait(copies):
        for copy in copies:
            copy.wait()

    start(load(x_hbm, x_buf, x_sem, 0))
    start(load(cot_hbm, cot_buf, cot_sem, 0))
    greet(n)

    def normalize(b):
        sub = 32

        def some(r, carry):
            for k, _, _ in sides(b):
                at = pl.ds(pl.multiple_of(k * hb + r * sub, sub), sub)
                where = pl.ds(pl.multiple_of(k * half + b * hb + r * sub, sub), sub)
                middle = x_buf[at, :].astype(jnp.float32) + branch[where, :].astype(jnp.float32)
                inverse = lax.rsqrt(jnp.mean(middle * middle, axis=-1, keepdims=True) + eps)
                normed[at, :] = (middle * inverse * gain[...]).astype(jnp.bfloat16)
            return carry

        lax.fori_loop(0, hb // sub, some, 0)

    def units(at, count):
        columns = pl.ds(at, count)
        gate = dot_n(normed[...], gu_w[0, :, columns])
        up = dot_n(normed[...], gu_w[1, :, columns])
        grad_hidden = dot_t(cot_buf[...], down_w[columns, :])
        sg = 1.0 / (1.0 + jnp.exp(-gate))
        silu = gate * sg
        hidden[:, columns] = (silu * up).astype(jnp.bfloat16)
        gg[0, :, columns] = (grad_hidden * up * sg * (1.0 + gate * (1.0 - sg))).astype(jnp.bfloat16)
        gg[1, :, columns] = (grad_hidden * silu).astype(jnp.bfloat16)

    def unit_tile(t, carry):
        units(pl.multiple_of(t * tile, tile), tile)
        return carry

    def step(s, carry):
        one.step(s)
        two.step(s - ready - per)
        u = s - ready
        b = u // per
        phase = u - b * per
        live = (u >= 0) & (u < chunks)

        @pl.when(live & (phase == 0))
        def _():
            wait(load(x_hbm, x_buf, x_sem, b))

            @pl.when(b == 0)
            def _():
                wait(weights)

            @pl.when(b > 0)
            def _():
                wait(saves(b - 1, "normed"))
            normalize(b)
            start(saves(b, "normed"))
            wait(load(cot_hbm, cot_buf, cot_sem, b))

            @pl.when(b > 0)
            def _():
                wait(saves(b - 1, "tiles"))

        @pl.when(live & (phase < 2))
        def _():
            lax.fori_loop(phase * 2, jnp.where(phase == 0, 2, full), unit_tile, 0)

        @pl.when(live & (phase == 1) & (b + 1 < blocks))
        def _():
            start(load(x_hbm, x_buf, x_sem, b + 1))

        @pl.when(live & (phase == 2))
        def _():
            if rest:
                units(full * tile, rest)
            start(saves(b, "tiles"))

            @pl.when(b + 1 < blocks)
            def _():
                start(load(cot_hbm, cot_buf, cot_sem, b + 1))

            @pl.when(b > 0)
            def _():
                wait(saves(b - 1, "feed"))

            def feed_tile(t, c):
                columns = pl.ds(pl.multiple_of(t * tile, tile), tile)
                feed[:, columns] = dot_n(hidden[...], down_w[:, columns]).astype(jnp.bfloat16)
                return c

            lax.fori_loop(0, width // tile, feed_tile, 0)
            start(saves(b, "feed"))

        @pl.when(live & (phase == 3))
        def _():
            def two_tile(t, c):
                at = pl.ds(pl.multiple_of(t * tile, tile), tile)
                value = (dot_t(gg[0], gu_w[0, at, :]) + dot_t(gg[1], gu_w[1, at, :])).astype(jnp.bfloat16)
                for k, where, _ in sides(b):
                    two_part[where, at] = value[k * hb:(k + 1) * hb]
                return c

            lax.fori_loop(0, width // tile, two_tile, 0)
        return carry

    lax.fori_loop(0, ready + per + two.steps, step, 0)
    one.drain()
    two.drain()
    for which in ("normed", "tiles", "feed"):
        wait(saves(blocks - 1, which))


def feed_forward(part, gain, x, cot, gateup_w, down_w, n, cid, chunks=16, lag=2):
    rows, width = part.shape
    ff = down_w.shape[0]
    rc = rows // (2 * chunks)
    block = 8 * rc
    low = jnp.bfloat16
    vmem = pl.BlockSpec(memory_space=pltpu.VMEM)
    hbm = pl.BlockSpec(memory_space=pl.ANY)
    dma = pltpu.SemaphoreType.DMA
    full = jax.ShapeDtypeStruct((rows, width), low)
    return pl.pallas_call(
        functools.partial(ff_kernel, n, chunks, lag, norm_eps),
        out_shape=(full, full, jax.ShapeDtypeStruct((rows, ff), low), jax.ShapeDtypeStruct((2, rows, ff), low), full, full),
        in_specs=[vmem, vmem, hbm, hbm, hbm, hbm],
        out_specs=(vmem, vmem, hbm, hbm, hbm, hbm),
        scratch_shapes=line_scratch(chunks, rc, width) + line_scratch(chunks, rc, width) + [
            pltpu.VMEM((rows, width), low),
            pltpu.VMEM((2, width, ff), low),
            pltpu.VMEM((ff, width), low),
            pltpu.VMEM((block, width), low),
            pltpu.VMEM((block, width), low),
            pltpu.VMEM((block, width), low),
            pltpu.VMEM((block, ff), low),
            pltpu.VMEM((2, block, ff), low),
            pltpu.VMEM((block, width), low),
            dma((2,)), dma((2,)), dma((2,)), dma((5, 2)),
        ],
        compiler_params=pltpu.CompilerParams(collective_id=cid, has_side_effects=True, vmem_limit_bytes=62 << 20),
        cost_estimate=pl.CostEstimate(flops=12 * rows * width * ff, bytes_accessed=rows * width * 250,
                                      transcendentals=rows * ff),
    )(part, gain, x, cot, gateup_w, down_w)


def total_kernel(n, m, gains_ref, square_ref, total_ref, gain_ref, line, got_gains, got_line, got_plane,
                 send_gains, recv_gains, send_line, recv_line, send_plane, recv_plane):
    z = lax.axis_index("tensor")
    d = lax.axis_index("dp")
    barrier = pltpu.get_barrier_semaphore()
    for k in range(1, n):
        pl.semaphore_signal(barrier, inc=1, device_id={"tensor": lax.rem(z + k, n)}, device_id_type=MESH)
    for k in range(1, m):
        pl.semaphore_signal(barrier, inc=1, device_id={"dp": lax.rem(d + k, m)}, device_id_type=MESH)
    pl.semaphore_wait(barrier, n - 1 + m - 1)

    def gains_to(k, sender):
        peer = lax.rem(d + k, m)
        return pltpu.make_async_remote_copy(
            src_ref=gains_ref.at[peer], dst_ref=got_gains.at[sender], send_sem=send_gains.at[k],
            recv_sem=recv_gains.at[sender], device_id={"dp": peer}, device_id_type=MESH)

    def along_line(k, sender):
        return pltpu.make_async_remote_copy(
            src_ref=line.at[0], dst_ref=got_line.at[sender], send_sem=send_line.at[k], recv_sem=recv_line.at[sender],
            device_id={"tensor": lax.rem(z + k, n)}, device_id_type=MESH)

    def over_plane(k, sender):
        return pltpu.make_async_remote_copy(
            src_ref=line.at[1], dst_ref=got_plane.at[sender], send_sem=send_plane.at[k], recv_sem=recv_plane.at[sender],
            device_id={"dp": lax.rem(d + k, m)}, device_id_type=MESH)

    def summed(ref, count):
        whole = ref[0]
        for k in range(1, count):
            whole = whole + ref[k]
        return whole

    for k in range(1, m):
        gains_to(k, d).start()
    got_gains[d] = gains_ref[d]
    for k in range(1, m):
        gains_to(k, d).wait_send()
        gains_to(k, lax.rem(d + m - k, m)).wait_recv()
    gains = summed(got_gains, m)
    gain_ref[...] = gains
    own = jnp.sum(jnp.sum(gains * gains, axis=1, keepdims=True), axis=0, keepdims=True)
    own = jnp.where(z == 0, own, jnp.zeros_like(own))
    line[0] = square_ref[...] + jnp.broadcast_to(own, square_ref.shape)
    for k in range(1, n):
        along_line(k, z).start()
    got_line[z] = line[0]
    for k in range(1, n):
        along_line(k, z).wait_send()
        along_line(k, lax.rem(z + n - k, n)).wait_recv()
    line[1] = summed(got_line, n)
    for k in range(1, m):
        over_plane(k, d).start()
    got_plane[d] = line[1]
    for k in range(1, m):
        over_plane(k, d).wait_send()
        over_plane(k, lax.rem(d + m - k, m)).wait_recv()
    total_ref[...] = summed(got_plane, m)


def reduce_tail(gains, square, n, m, cid):
    share = gains.shape[1] // m
    parts = gains.reshape(2, m, share).transpose(1, 0, 2)
    tile = jnp.broadcast_to(square.reshape(1, 1), (8, 128))
    vmem = pl.BlockSpec(memory_space=pltpu.VMEM)
    dma = pltpu.SemaphoreType.DMA
    total, gain = pl.pallas_call(
        functools.partial(total_kernel, n, m),
        out_shape=(jax.ShapeDtypeStruct((8, 128), jnp.float32), jax.ShapeDtypeStruct((2, share), jnp.float32)),
        in_specs=[vmem, vmem],
        out_specs=(vmem, vmem),
        scratch_shapes=[
            pltpu.VMEM((2, 8, 128), jnp.float32),
            pltpu.VMEM((m, 2, share), jnp.float32),
            pltpu.VMEM((n, 8, 128), jnp.float32),
            pltpu.VMEM((m, 8, 128), jnp.float32),
            dma((m,)), dma((m,)), dma((n,)), dma((n,)), dma((m,)), dma((m,)),
        ],
        compiler_params=pltpu.CompilerParams(collective_id=cid, has_side_effects=True),
    )(parts, tile)
    return total[0, 0], gain


norm_eps = 1e-05
beta_first = 0.9
beta_second = 0.95
adam_eps = 1e-08
weight_decay = 0.1
weight_rate = 0.02
out_rate = 0.1
gain_rate = 0.2
clip_limit = 1.0


def positions(segment):
    length = segment.shape[0]
    indices = jnp.arange(length, dtype=jnp.int32)
    earlier = jnp.concatenate([segment[:1] - 1, segment[:-1]])
    begins = jnp.where(segment != earlier, indices, jnp.zeros_like(indices))
    return indices - lax.cummax(begins, axis=0)


def paired_tables(places):
    frequency = jnp.power(10000.0, -jnp.arange(HD // 2, dtype=jnp.float32) * (2.0 / HD))
    angles = places.astype(jnp.float32)[:, None] * frequency[None, :]
    cosines, sines = jnp.cos(angles), jnp.sin(angles)
    return (
        jnp.concatenate([cosines] * 4, axis=-1),
        jnp.concatenate([-sines, sines, -sines, sines], axis=-1),
    )


def over_rows(left, right):
    return lax.dot_general(
        left, right, (((0,), (0,)), ((), ())), preferred_element_type=jnp.float32
    )


def against(left, right):
    return lax.dot_general(
        left, right, (((1,), (1,)), ((), ())), preferred_element_type=jnp.float32
    )


def norm_back(grad_output, unit_rows, inverse, gain):
    scaled = grad_output * gain
    gain_grad = jnp.sum(grad_output * unit_rows, axis=0)
    inner_mean = jnp.mean(scaled * unit_rows, axis=-1, keepdims=True)
    return (inverse * (scaled - unit_rows * inner_mean), gain_grad)


def adam_step(weight, first, second, gradient, clip_factor, step_float, step_rate, decay_rate):
    gradient = gradient * clip_factor
    first = beta_first * first + (1.0 - beta_first) * gradient
    second = beta_second * second + (1.0 - beta_second) * gradient * gradient
    correct_one = 1.0 - jnp.power(beta_first, step_float)
    correct_two = 1.0 - jnp.power(beta_second, step_float)
    update = first / correct_one / (jnp.sqrt(second / correct_two) + adam_eps)
    return (first, second, weight - step_rate * (update + decay_rate * weight))


def on_device(
    n,
    m,
    tokens,
    cotangent,
    segment_ids,
    step_count,
    norm_gains,
    gains_first,
    gains_second,
    w_query,
    query_first,
    query_second,
    w_keyval,
    keyval_first,
    keyval_second,
    w_out,
    out_first,
    out_second,
    w_gateup,
    gateup_first,
    gateup_second,
    w_down,
    down_first,
    down_second,
):
    low = jnp.bfloat16
    width = w_query.shape[1]
    kv_width = w_keyval.shape[2]
    gain_rows = lax.all_gather(norm_gains.astype(low), "dp", axis=1, tiled=True)
    qkv_shard = jnp.concatenate([w_query, w_keyval[0], w_keyval[1]], axis=1).astype(low)
    qkv_weight = lax.all_gather(qkv_shard, "dp", axis=0, tiled=True)
    out_weight = lax.all_gather(w_out.astype(low), "dp", axis=1, tiled=True)
    gateup_weight = lax.all_gather(w_gateup.astype(low), "dp", axis=1, tiled=True)
    down_weight = lax.all_gather(w_down.astype(low), "dp", axis=1, tiled=True)
    gain_values = gain_rows.astype(jnp.float32)
    length = tokens.shape[0]
    size = min(256, length)
    segment = segment_ids[0]
    places = positions(segment)
    cosines, sines = paired_tables(places)
    first = (jnp.arange(length, dtype=jnp.int32) - places)[::size] // size
    seg_col, seg_row = segment[:, None], segment[None, :]

    values_in = tokens.astype(jnp.float32)
    inverse_one = lax.rsqrt(jnp.mean(values_in * values_in, axis=-1, keepdims=True) + norm_eps)
    unit_one = values_in * inverse_one
    normed_one = (unit_one * gain_values[0]).astype(low)
    raw = jnp.dot(normed_one, qkv_weight, preferred_element_type=jnp.float32)
    mixture, q, k, v, lse = attention_forward(raw, cosines, sines, seg_col, seg_row, first, size)
    branch_part = jnp.dot(mixture, out_weight, preferred_element_type=jnp.float32).astype(low)
    branch, grad_normed_two, hidden, grad_gateup, feed_part, normed_two = feed_forward(
        branch_part, gain_values[1:], tokens, cotangent, gateup_weight, down_weight, n, 1
    )
    middle = values_in + branch.astype(jnp.float32)
    inverse_two = lax.rsqrt(jnp.mean(middle * middle, axis=-1, keepdims=True) + norm_eps)
    unit_two = middle * inverse_two
    grad_gate_weight = over_rows(normed_two, grad_gateup[0]).astype(low)
    grad_up_weight = over_rows(normed_two, grad_gateup[1]).astype(low)
    grad_down_weight = over_rows(hidden, cotangent).astype(low)
    grad_normed_two, grad_gate_weight, grad_up_weight, grad_down_weight = lax.optimization_barrier(
        (grad_normed_two, grad_gate_weight, grad_up_weight, grad_down_weight)
    )
    gate_reduced = lax.psum_scatter(grad_gate_weight, "dp", scatter_dimension=0, tiled=True)
    up_reduced = lax.psum_scatter(grad_up_weight, "dp", scatter_dimension=0, tiled=True)
    down_reduced = lax.psum_scatter(grad_down_weight, "dp", scatter_dimension=1, tiled=True)
    grad_from_two, gain_grad_two = norm_back(
        grad_normed_two.astype(jnp.float32), unit_two, inverse_two, gain_values[1]
    )
    grad_middle = cotangent.astype(jnp.float32) + grad_from_two
    grad_branch = grad_middle.astype(low)
    grad_mixture = against(grad_branch, out_weight).astype(low)
    grad_qkv = attention_backward(
        q, k, v, mixture, grad_mixture, lse, cosines, sines, seg_col, seg_row, first, size
    )
    partial_one = against(grad_qkv, qkv_weight).astype(low)
    grad_out_weight = over_rows(mixture, grad_branch).astype(low)
    grad_qkv_weight = over_rows(normed_one, grad_qkv).astype(low)
    partial_one, grad_out_weight, grad_qkv_weight, gate_reduced = lax.optimization_barrier(
        (partial_one, grad_out_weight, grad_qkv_weight, gate_reduced)
    )
    out_reduced = lax.psum_scatter(grad_out_weight, "dp", scatter_dimension=1, tiled=True)
    qkv_reduced = lax.psum_scatter(grad_qkv_weight, "dp", scatter_dimension=0, tiled=True)
    feed_out, grad_normed_one = line_reduce((feed_part, partial_one), n, 16, 3)
    grad_normed_one = grad_normed_one.astype(jnp.float32)
    layer_out = (middle + feed_out.astype(jnp.float32)).astype(low)
    grad_from_one, gain_grad_one = norm_back(grad_normed_one, unit_one, inverse_one, gain_values[0])
    input_grad = grad_middle + grad_from_one
    gain_grads = jnp.stack([gain_grad_one, gain_grad_two])
    qkv_reduced = qkv_reduced.astype(jnp.float32)
    reduced = (
        qkv_reduced[:, :width],
        jnp.stack([qkv_reduced[:, width : width + kv_width], qkv_reduced[:, width + kv_width :]]),
        out_reduced.astype(jnp.float32),
        jnp.stack([gate_reduced, up_reduced]).astype(jnp.float32),
        down_reduced.astype(jnp.float32),
    )
    local_square = sum((jnp.sum(g * g) for g in reduced))
    square_total, gains_reduced = reduce_tail(gain_grads, local_square, n, m, 4)
    reduced = (gains_reduced, *reduced)
    grad_norm = jnp.sqrt(square_total)
    clip_factor = jnp.minimum(1.0, clip_limit / (grad_norm + 1e-06))
    step_float = step_count[0].astype(jnp.float32)
    params = (norm_gains, w_query, w_keyval, w_out, w_gateup, w_down)
    states = (
        (gains_first, gains_second),
        (query_first, query_second),
        (keyval_first, keyval_second),
        (out_first, out_second),
        (gateup_first, gateup_second),
        (down_first, down_second),
    )
    step_rates = (gain_rate, weight_rate, weight_rate, out_rate, weight_rate, weight_rate)
    decay_rates = (0.0, weight_decay, weight_decay, weight_decay, weight_decay, weight_decay)
    results = []
    for position_index in range(6):
        one, two = states[position_index]
        results.extend(
            adam_step(
                params[position_index],
                one,
                two,
                reduced[position_index],
                clip_factor,
                step_float,
                step_rates[position_index],
                decay_rates[position_index],
            )
        )
    return (layer_out, input_grad, grad_norm.reshape(1), *results)


def solution(mesh):
    rows = P("dp", None)
    gains = P(None, "dp")
    query = P("dp", "tensor")
    stacked = P(None, "dp", "tensor")
    turned = P("tensor", "dp")
    states = (gains,) * 3 + (query,) * 3 + (stacked,) * 3 + (turned,) * 3 + (stacked,) * 3 + (turned,) * 3
    return jax.shard_map(
        functools.partial(on_device, mesh.shape["tensor"], mesh.shape["dp"]),
        mesh=mesh,
        in_specs=(rows, rows, rows, P()) + states,
        out_specs=(rows, rows, P()) + states,
        check_vma=False,
    )
```

```python
import functools

import jax
import jax.numpy as jnp
from jax import lax
from jax.experimental import pallas as pl
from jax.experimental.pallas import tpu as pltpu
from jax.sharding import PartitionSpec as P

HD = 64
MESH = pl.DeviceIdType.MESH


masked_value = -1e9


def dot_t(left, right):
    return lax.dot_general(left, right, (((1,), (1,)), ((), ())), preferred_element_type=jnp.float32)


def dot_n(left, right):
    return lax.dot_general(left, right, (((1,), (0,)), ((), ())), preferred_element_type=jnp.float32)


def swap_halves(values, first_half):
    return jnp.where(first_half, pltpu.roll(values, 96, 1), pltpu.roll(values, 32, 1))


def lane_tests(rows):
    lane = lax.broadcasted_iota(jnp.int32, (rows, 128), 1)
    return lane < 64, (lane % 64) < 32


def block_bias(seg_col_ref, seg_row_ref, i, j, size):
    keys = seg_col_ref[pl.ds(pl.multiple_of(j * size, size), size), :]
    rows = seg_row_ref[:, pl.ds(pl.multiple_of(i * size, size), size)]
    key_at = j * size + lax.broadcasted_iota(jnp.int32, (size, size), 0)
    row_at = i * size + lax.broadcasted_iota(jnp.int32, (size, size), 1)
    return jnp.where((keys == rows) & (key_at <= row_at), 0.0, masked_value)


def stack_pair(pair, low_lanes):
    zero = jnp.zeros_like(pair)
    return jnp.concatenate([jnp.where(low_lanes, pair, zero), jnp.where(low_lanes, zero, pair)], axis=0)


def forward_kernel(size, pairs, first_ref, raw_ref, cos_ref, sin_ref, seg_col_ref, seg_row_ref,
                   mix_ref, q_ref, k_ref, v_ref, lse_ref, bias, scores, v_turned):
    length = raw_ref.shape[0]
    low_lanes, first_half = lane_tests(size)
    low_rows = lax.broadcasted_iota(jnp.int32, (128, size), 0) < 64
    width = pairs * 128

    def prepare(i, carry):
        rows = pl.ds(pl.multiple_of(i * size, size), size)
        cosines, sines = cos_ref[rows, :], sin_ref[rows, :]
        for hp in range(pairs):
            values = raw_ref[rows, hp * 128:(hp + 1) * 128]
            turned = values * cosines + swap_halves(values, first_half) * sines
            q_ref[rows, hp * 128:(hp + 1) * 128] = (turned.astype(jnp.bfloat16).astype(jnp.float32) * 0.125).astype(jnp.bfloat16)
        both = raw_ref[rows, width:width + 128]
        other = pltpu.roll(both, 64, 1)
        keys = jnp.where(low_lanes, both, other)
        k_ref[rows, :] = (keys * cosines + swap_halves(keys, first_half) * sines).astype(jnp.bfloat16)
        values = jnp.where(low_lanes, other, both)
        v_ref[rows, :] = values.astype(jnp.bfloat16)
        v_turned[i] = values.T.astype(jnp.bfloat16)
        return carry

    lax.fori_loop(0, length // size, prepare, 0)

    def row_block(i, carry):
        rows = pl.ds(pl.multiple_of(i * size, size), size)
        begin = first_ref[i]

        def fill(j, c):
            bias[j] = block_bias(seg_col_ref, seg_row_ref, i, j, size)
            return c

        lax.fori_loop(begin, i + 1, fill, 0)

        for hp in range(pairs):
            stacked = stack_pair(q_ref[rows, hp * 128:(hp + 1) * 128], low_lanes)

            def score(j, top):
                keys = k_ref[pl.ds(pl.multiple_of(j * size, size), size), :]
                b = bias[j]
                s = dot_t(keys, stacked) + jnp.concatenate([b, b], axis=1)
                scores[j] = s
                return jnp.maximum(top, jnp.max(s, axis=0, keepdims=True))

            top = lax.fori_loop(begin, i + 1, score, jnp.full((1, 2 * size), -jnp.inf, jnp.float32))

            def mix(j, c):
                total, acc = c
                p = jnp.exp(scores[j] - top)
                total = total + jnp.sum(p, axis=0, keepdims=True)
                return total, acc + dot_n(v_turned[j], p.astype(jnp.bfloat16))

            total, acc = lax.fori_loop(begin, i + 1, mix, (
                jnp.zeros((1, 2 * size), jnp.float32), jnp.zeros((128, 2 * size), jnp.float32)))
            lse_ref[i, hp] = top + jnp.log(total)
            acc = acc / total
            acc = jnp.where(low_rows, acc[:, :size], acc[:, size:])
            mix_ref[rows, hp * 128:(hp + 1) * 128] = acc.T.astype(jnp.bfloat16)
        return carry

    lax.fori_loop(0, length // size, row_block, 0)


def attention_forward(raw, cosines, sines, seg_col, seg_row, first, size):
    length, wide = raw.shape
    width = wide - 128
    pairs = width // 128
    blocks = length // size
    vmem = pl.BlockSpec(memory_space=pltpu.VMEM)
    return pl.pallas_call(
        functools.partial(forward_kernel, size, pairs),
        out_shape=(
            jax.ShapeDtypeStruct((length, width), jnp.bfloat16),
            jax.ShapeDtypeStruct((length, width), jnp.bfloat16),
            jax.ShapeDtypeStruct((length, 128), jnp.bfloat16),
            jax.ShapeDtypeStruct((length, 128), jnp.bfloat16),
            jax.ShapeDtypeStruct((blocks, pairs, 1, 2 * size), jnp.float32),
        ),
        in_specs=[pl.BlockSpec(memory_space=pltpu.SMEM)] + [vmem] * 5,
        out_specs=(vmem,) * 5,
        scratch_shapes=[
            pltpu.VMEM((blocks, size, size), jnp.float32),
            pltpu.VMEM((blocks, size, 2 * size), jnp.float32),
            pltpu.VMEM((blocks, 128, size), jnp.bfloat16),
        ],
        compiler_params=pltpu.CompilerParams(vmem_limit_bytes=40 << 20),
        cost_estimate=pl.CostEstimate(flops=10 * length * length * width, bytes_accessed=8 * length * width,
                                      transcendentals=length * length * pairs),
    )(first, raw, cosines, sines, seg_col, seg_row)


def backward_kernel(size, pairs, first_ref, q_ref, k_ref, v_ref, mix_ref, grad_ref, lse_ref, cos_ref, sin_ref,
                    seg_col_ref, seg_row_ref, out_ref, bias, k_turned, grad_k, grad_v):
    length = q_ref.shape[0]
    width = pairs * 128
    low_lanes, first_half = lane_tests(size)
    low_rows = lax.broadcasted_iota(jnp.int32, (128, size), 0) < 64

    def prepare(i, carry):
        rows = pl.ds(pl.multiple_of(i * size, size), size)
        k_turned[i] = k_ref[rows, :].astype(jnp.float32).T.astype(jnp.bfloat16)
        grad_k[i] = jnp.zeros((size, 128), jnp.float32)
        grad_v[i] = jnp.zeros((size, 128), jnp.float32)
        return carry

    lax.fori_loop(0, length // size, prepare, 0)

    def row_block(i, carry):
        rows = pl.ds(pl.multiple_of(i * size, size), size)
        begin = first_ref[i]
        cosines, sines = cos_ref[rows, :], sin_ref[rows, :]

        def fill(j, c):
            bias[j] = block_bias(seg_col_ref, seg_row_ref, i, j, size)
            return c

        lax.fori_loop(begin, i + 1, fill, 0)

        for hp in range(pairs):
            columns = slice(hp * 128, (hp + 1) * 128)
            stacked = stack_pair(q_ref[rows, columns], low_lanes)
            grad_pair = grad_ref[rows, columns]
            grad_stacked = stack_pair(grad_pair, low_lanes)
            product = (grad_pair.astype(jnp.float32) * mix_ref[rows, columns].astype(jnp.float32)).T
            spread = jnp.concatenate([
                jnp.sum(product[:64], axis=0, keepdims=True), jnp.sum(product[64:], axis=0, keepdims=True)], axis=1)
            logsum = lse_ref[i, hp]

            def piece(j, acc):
                at = pl.ds(pl.multiple_of(j * size, size), size)
                b = bias[j]
                s = dot_t(k_ref[at, :], stacked) + jnp.concatenate([b, b], axis=1)
                p = jnp.exp(s - logsum)
                grad_p = dot_t(v_ref[at, :], grad_stacked)
                grad_s = (p * (grad_p - spread)).astype(jnp.bfloat16)
                grad_v[j] += dot_n(p.astype(jnp.bfloat16), grad_stacked)
                grad_k[j] += dot_n(grad_s, stacked)
                return acc + dot_n(k_turned[j], grad_s)

            acc = lax.fori_loop(begin, i + 1, piece, jnp.zeros((128, 2 * size), jnp.float32))
            acc = jnp.where(low_rows, acc[:, :size], acc[:, size:]).T * 0.125
            out_ref[rows, columns] = (acc * cosines - swap_halves(acc, first_half) * sines).astype(jnp.bfloat16)
        return carry

    lax.fori_loop(0, length // size, row_block, 0)

    def finish(i, carry):
        rows = pl.ds(pl.multiple_of(i * size, size), size)
        cosines, sines = cos_ref[rows, :], sin_ref[rows, :]
        dk = grad_k[i] + pltpu.roll(grad_k[i], 64, 1)
        dk = dk * cosines - swap_halves(dk, first_half) * sines
        dv = grad_v[i] + pltpu.roll(grad_v[i], 64, 1)
        out_ref[rows, width:width + 128] = jnp.where(low_lanes, dk, dv).astype(jnp.bfloat16)
        return carry

    lax.fori_loop(0, length // size, finish, 0)


def attention_backward(q, k, v, mix, grad, lse, cosines, sines, seg_col, seg_row, first, size):
    length, width = q.shape
    pairs = width // 128
    blocks = length // size
    vmem = pl.BlockSpec(memory_space=pltpu.VMEM)
    return pl.pallas_call(
        functools.partial(backward_kernel, size, pairs),
        out_shape=jax.ShapeDtypeStruct((length, width + 128), jnp.bfloat16),
        in_specs=[pl.BlockSpec(memory_space=pltpu.SMEM)] + [vmem] * 10,
        out_specs=vmem,
        scratch_shapes=[
            pltpu.VMEM((blocks, size, size), jnp.float32),
            pltpu.VMEM((blocks, 128, size), jnp.bfloat16),
            pltpu.VMEM((blocks, size, 128), jnp.float32),
            pltpu.VMEM((blocks, size, 128), jnp.float32),
        ],
        compiler_params=pltpu.CompilerParams(vmem_limit_bytes=40 << 20),
        cost_estimate=pl.CostEstimate(flops=20 * length * length * width, bytes_accessed=8 * length * width,
                                      transcendentals=length * length * pairs),
    )(first, q, k, v, mix, grad, lse, cosines, sines, seg_col, seg_row)


class Line:
    def __init__(self, n, chunks, rc, lag, part, got, out, sems):
        self.n, self.chunks, self.rc, self.lag = n, chunks, rc, lag
        self.part, self.got, self.out = part, got, out
        self.send_a, self.recv_a, self.send_g, self.recv_g = sems
        self.me = lax.axis_index("tensor")
        self.steps = chunks + 2 * lag * (n - 1)

    def rows(self, stream, c):
        return pl.ds(pl.multiple_of((stream * self.chunks + c) * self.rc, self.rc), self.rc)

    def side(self, stream):
        pos = self.me if stream == 0 else self.n - 1 - self.me
        fwd = self.me + 1 if stream == 0 else self.me - 1
        bwd = self.me - 1 if stream == 0 else self.me + 1
        return pos, fwd, bwd

    def toward(self, stream, c, nxt, src):
        return pltpu.make_async_remote_copy(
            src_ref=src, dst_ref=self.got.at[stream, c],
            send_sem=self.send_a.at[stream, c], recv_sem=self.recv_a.at[stream, c],
            device_id={"tensor": nxt}, device_id_type=MESH)

    def back(self, stream, c, nxt):
        where = self.rows(stream, c)
        return pltpu.make_async_remote_copy(
            src_ref=self.out.at[where], dst_ref=self.out.at[where],
            send_sem=self.send_g.at[stream, c], recv_sem=self.recv_g.at[stream, c],
            device_id={"tensor": nxt}, device_id_type=MESH)

    def step(self, s):
        n, lag = self.n, self.lag
        for stream in (0, 1):
            pos, fwd, bwd = self.side(stream)
            c = s - lag * pos

            @pl.when((c >= 0) & (c < self.chunks))
            def _():
                where = self.rows(stream, c)
                slot = self.got.at[stream, c]

                def summed():
                    self.toward(stream, c, fwd, slot).wait_recv()
                    return (
                        self.part[where, :].astype(jnp.float32) + self.got[stream, c].astype(jnp.float32)
                    ).astype(self.out.dtype)

                @pl.when(pos == 0)
                def _():
                    self.toward(stream, c, fwd, self.part.at[where]).start()

                @pl.when((pos > 0) & (pos < n - 1))
                def _():
                    self.got[stream, c] = summed()
                    self.toward(stream, c, fwd, slot).start()

                @pl.when(pos == n - 1)
                def _():
                    self.out[where, :] = summed()
                    self.back(stream, c, bwd).start()
            d = s - lag * (n - 1) - lag * (n - 1 - pos)

            @pl.when((d >= 0) & (d < self.chunks) & (pos < n - 1))
            def _():
                self.back(stream, d, bwd).wait_recv()

                @pl.when(pos > 0)
                def _():
                    self.back(stream, d, bwd).start()

    def drain(self):
        def one(c, carry):
            for stream in (0, 1):
                pos, fwd, bwd = self.side(stream)

                @pl.when(pos < self.n - 1)
                def _():
                    self.toward(stream, c, fwd, self.got.at[stream, c]).wait_send()

                @pl.when(pos > 0)
                def _():
                    self.back(stream, c, bwd).wait_send()
            return carry

        lax.fori_loop(0, self.chunks, one, 0)


def greet(n):
    me = lax.axis_index("tensor")
    barrier = pltpu.get_barrier_semaphore()

    @pl.when(me > 0)
    def _():
        pl.semaphore_signal(barrier, inc=1, device_id={"tensor": me - 1}, device_id_type=MESH)

    @pl.when(me < n - 1)
    def _():
        pl.semaphore_signal(barrier, inc=1, device_id={"tensor": me + 1}, device_id_type=MESH)

    @pl.when((me > 0) & (me < n - 1))
    def _():
        pl.semaphore_wait(barrier, 2)

    @pl.when((me == 0) | (me == n - 1))
    def _():
        pl.semaphore_wait(barrier, 1)


def line_scratch(chunks, rc, width):
    return [pltpu.VMEM((2, chunks, rc, width), jnp.bfloat16)] + [pltpu.SemaphoreType.DMA((2, chunks))] * 4


def line_kernel(n, chunks, lag, count, *refs):
    parts, outs, scratch = refs[:count], refs[count:2 * count], refs[2 * count:]
    rc = parts[0].shape[0] // (2 * chunks)
    lines = [
        Line(n, chunks, rc, lag, parts[k], scratch[5 * k], outs[k], scratch[5 * k + 1:5 * k + 5])
        for k in range(count)
    ]
    greet(n)

    def step(s, carry):
        for k, line in enumerate(lines):
            line.step(s - k * chunks)
        return carry

    lax.fori_loop(0, lines[0].steps + (count - 1) * chunks, step, 0)
    for line in lines:
        line.drain()


def line_reduce(parts, n, chunks, cid, lag=2):
    rows, width = parts[0].shape
    count = len(parts)
    rc = rows // (2 * chunks)
    scratch = []
    for _ in parts:
        scratch += line_scratch(chunks, rc, width)
    vmem = pl.BlockSpec(memory_space=pltpu.VMEM)
    return pl.pallas_call(
        functools.partial(line_kernel, n, chunks, lag, count),
        out_shape=tuple(jax.ShapeDtypeStruct((rows, width), jnp.bfloat16) for _ in parts),
        in_specs=[vmem] * count,
        out_specs=(vmem,) * count,
        scratch_shapes=scratch,
        compiler_params=pltpu.CompilerParams(collective_id=cid, has_side_effects=True, vmem_limit_bytes=40 << 20),
        cost_estimate=pl.CostEstimate(flops=rows * width * 2 * count, bytes_accessed=rows * width * 120 * count,
                                      transcendentals=0),
    )(*parts)


def dot_rows(left, right):
    return lax.dot_general(left, right, (((0,), (0,)), ((), ())), preferred_element_type=jnp.float32)


def ff_kernel(n, chunks, lag, eps, branch, gain, x, cot_hbm, gu_hbm, down_hbm,
              feed_hbm, middle_hbm, low_hbm, gain_out, gate_grad_hbm, up_grad_hbm, down_grad_hbm,
              got, sa, ra, sg, rg, two_sum, two_part, gu_w, down_w, cot, normed, hidden, gg, feed,
              middle_stage, low_stage, unit_stage, down_stage, w_sem, cot_sem, feed_sem, stage_sem, grad_sem):
    rows, width = branch.shape
    ff = down_w.shape[0]
    rc = rows // (2 * chunks)
    per = 4
    half = rows // 2
    hb = per * rc
    block = 2 * hb
    blocks = chunks // per
    line = Line(n, chunks, rc, lag, two_part, got, two_sum, (sa, ra, sg, rg))
    landed = 2 * lag * (n - 1) + per
    tile = 256
    full, rest = ff // tile, ff % tile
    wide = width // tile

    weights = (
        pltpu.make_async_copy(gu_hbm, gu_w, w_sem.at[0]),
        pltpu.make_async_copy(down_hbm, down_w, w_sem.at[1]),
    )
    for copy in weights:
        copy.start()

    def natural(k, b):
        return pl.ds(pl.multiple_of(k * half + b * hb, hb), hb)

    def blocked(k, b):
        return pl.ds(pl.multiple_of(b * block + k * hb, hb), hb)

    def load_cot(b):
        return [pltpu.make_async_copy(cot_hbm.at[natural(k, b)], cot.at[blocked(k, b)], cot_sem.at[b, k])
                for k in (0, 1)]

    def save_feed(b):
        return [pltpu.make_async_copy(feed.at[pl.ds(k * hb, hb)], feed_hbm.at[natural(k, b)], feed_sem.at[k])
                for k in (0, 1)]

    def save_rows(d):
        copies = []
        for k in (0, 1):
            where = line.rows(k, d)
            copies.append(pltpu.make_async_copy(middle_stage.at[k], middle_hbm.at[where], stage_sem.at[0, k]))
            copies.append(pltpu.make_async_copy(low_stage.at[k], low_hbm.at[where], stage_sem.at[1, k]))
        return copies

    def save_units(w):
        at = pl.ds(pl.multiple_of(w * tile, tile), tile)
        return [
            pltpu.make_async_copy(unit_stage.at[0], gate_grad_hbm.at[at], grad_sem.at[0]),
            pltpu.make_async_copy(unit_stage.at[1], up_grad_hbm.at[at], grad_sem.at[1]),
        ]

    def save_down(at, count):
        return [pltpu.make_async_copy(down_stage.at[pl.ds(0, count)], down_grad_hbm.at[pl.ds(at, count)], grad_sem.at[2])]

    def start(copies):
        for copy in copies:
            copy.start()

    def wait(copies):
        for copy in copies:
            copy.wait()

    for b in range(blocks):
        start(load_cot(b))
    gain_out[...] = jnp.zeros_like(gain_out)
    greet(n)

    def unit_rows(where):
        middle = x[where, :].astype(jnp.float32) + branch[where, :].astype(jnp.float32)
        inverse = lax.rsqrt(jnp.mean(middle * middle, axis=-1, keepdims=True) + eps)
        return middle * inverse, inverse

    def normalize(b):
        def some(r, carry):
            for k in (0, 1):
                where = pl.ds(pl.multiple_of(k * half + b * hb + r * rc, rc), rc)
                at = pl.ds(pl.multiple_of(b * block + k * hb + r * rc, rc), rc)
                normed[at, :] = (unit_rows(where)[0] * gain[...]).astype(jnp.bfloat16)
            return carry

        lax.fori_loop(0, per, some, 0)

    def step(s, carry):
        line.step(s - per)
        b = s // per
        phase = s - b * per
        live = s < chunks
        mine = pl.ds(pl.multiple_of(b * block, block), block)

        def units(at, count):
            columns = pl.ds(at, count)
            gate = dot_n(normed[mine, :], gu_w[0, :, columns])
            up = dot_n(normed[mine, :], gu_w[1, :, columns])
            grad_hidden = dot_t(cot[mine, :], down_w[columns, :])
            sg_gate = 1.0 / (1.0 + jnp.exp(-gate))
            silu = gate * sg_gate
            hidden[mine, columns] = (silu * up).astype(jnp.bfloat16)
            gg[0, mine, columns] = (grad_hidden * up * sg_gate * (1.0 + gate * (1.0 - sg_gate))).astype(jnp.bfloat16)
            gg[1, mine, columns] = (grad_hidden * silu).astype(jnp.bfloat16)

        def unit_tile(t, c):
            units(pl.multiple_of(t * tile, tile), tile)
            return c

        @pl.when(live & (phase == 0))
        def _():
            normalize(b)

            @pl.when(b == 0)
            def _():
                wait(weights)
            wait(load_cot(b))

        @pl.when(live & (phase < 2))
        def _():
            lax.fori_loop(phase * 2, jnp.where(phase == 0, 2, full), unit_tile, 0)

        @pl.when(live & (phase == 2))
        def _():
            if rest:
                units(full * tile, rest)

            @pl.when(b > 0)
            def _():
                wait(save_feed(b - 1))

            def feed_tile(t, c):
                columns = pl.ds(pl.multiple_of(t * tile, tile), tile)
                feed[:, columns] = dot_n(hidden[mine, :], down_w[:, columns]).astype(jnp.bfloat16)
                return c

            lax.fori_loop(0, wide, feed_tile, 0)
            start(save_feed(b))

        @pl.when(live & (phase == 3))
        def _():
            def two_tile(t, c):
                at = pl.ds(pl.multiple_of(t * tile, tile), tile)
                value = (dot_t(gg[0, mine, :], gu_w[0, at, :]) + dot_t(gg[1, mine, :], gu_w[1, at, :])).astype(jnp.bfloat16)
                for k in (0, 1):
                    two_part[natural(k, b), at] = value[k * hb:(k + 1) * hb]
                return c

            lax.fori_loop(0, wide, two_tile, 0)

        d = s - landed

        @pl.when(d >= 0)
        def _():
            @pl.when(d > 0)
            def _():
                wait(save_rows(d - 1))
            for k in (0, 1):
                where = line.rows(k, d)
                at = pl.ds(pl.multiple_of((d // per) * block + k * hb + (d - (d // per) * per) * rc, rc), rc)
                unit, inverse = unit_rows(where)
                grad = two_sum[where, :].astype(jnp.float32)
                scaled = grad * gain[...]
                inner = jnp.mean(scaled * unit, axis=-1, keepdims=True)
                value = cot[at, :].astype(jnp.float32) + inverse * (scaled - unit * inner)
                middle_stage[k] = value
                low_stage[k] = value.astype(jnp.bfloat16)
                gain_out[...] += jnp.sum(grad * unit, axis=0, keepdims=True)
            start(save_rows(d))

        w = s - chunks

        @pl.when((w >= 0) & (w < wide))
        def _():
            @pl.when(w > 0)
            def _():
                wait(save_units(w - 1))
            columns = pl.ds(pl.multiple_of(w * tile, tile), tile)
            left = normed[:, columns]
            for t in (0, 1):
                unit_stage[t] = dot_rows(left, gg[t]).astype(jnp.bfloat16)
            start(save_units(w))

        v = w - wide

        @pl.when((v >= 0) & (v < full))
        def _():
            @pl.when(v > 0)
            def _():
                wait(save_down((v - 1) * tile, tile))
            at = pl.multiple_of(v * tile, tile)
            down_stage[...] = dot_rows(hidden[:, pl.ds(at, tile)], cot[...]).astype(jnp.bfloat16)
            start(save_down(at, tile))

        if rest:
            @pl.when(v == full)
            def _():
                wait(save_down((full - 1) * tile, tile))
                down_stage[pl.ds(0, rest), :] = dot_rows(hidden[:, full * tile:], cot[...]).astype(jnp.bfloat16)
                start(save_down(full * tile, rest))
        return carry

    lax.fori_loop(0, per + line.steps, step, 0)
    line.drain()
    wait(save_feed(blocks - 1))
    wait(save_rows(chunks - 1))
    wait(save_units(wide - 1))
    wait(save_down(full * tile, rest) if rest else save_down((full - 1) * tile, tile))


def feed_forward(branch, gain, x, cot, gateup_w, down_w, n, cid, chunks=16, lag=2):
    rows, width = branch.shape
    ff = down_w.shape[0]
    rc = rows // (2 * chunks)
    block = 8 * rc
    blocks = chunks // 4
    low = jnp.bfloat16
    vmem = pl.BlockSpec(memory_space=pltpu.VMEM)
    hbm = pl.BlockSpec(memory_space=pl.ANY)
    dma = pltpu.SemaphoreType.DMA
    shape = jax.ShapeDtypeStruct
    return pl.pallas_call(
        functools.partial(ff_kernel, n, chunks, lag, norm_eps),
        out_shape=(
            shape((rows, width), low), shape((rows, width), jnp.float32), shape((rows, width), low),
            shape((1, width), jnp.float32), shape((width, ff), low), shape((width, ff), low), shape((ff, width), low),
        ),
        in_specs=[vmem, vmem, vmem, hbm, hbm, hbm],
        out_specs=(hbm, hbm, hbm, vmem, hbm, hbm, hbm),
        scratch_shapes=line_scratch(chunks, rc, width) + [
            pltpu.VMEM((rows, width), low),
            pltpu.VMEM((rows, width), low),
            pltpu.VMEM((2, width, ff), low),
            pltpu.VMEM((ff, width), low),
            pltpu.VMEM((rows, width), low),
            pltpu.VMEM((rows, width), low),
            pltpu.VMEM((rows, ff), low),
            pltpu.VMEM((2, rows, ff), low),
            pltpu.VMEM((block, width), low),
            pltpu.VMEM((2, rc, width), jnp.float32),
            pltpu.VMEM((2, rc, width), low),
            pltpu.VMEM((2, 256, ff), low),
            pltpu.VMEM((256, width), low),
            dma((2,)), dma((blocks, 2)), dma((2,)), dma((2, 2)), dma((3,)),
        ],
        compiler_params=pltpu.CompilerParams(collective_id=cid, has_side_effects=True, vmem_limit_bytes=63 << 20),
        cost_estimate=pl.CostEstimate(flops=18 * rows * width * ff, bytes_accessed=rows * width * 150,
                                      transcendentals=rows * ff),
    )(branch, gain, x, cot, gateup_w, down_w)


def total_kernel(n, m, gains_ref, square_ref, total_ref, gain_ref, line, got_gains, got_line, got_plane,
                 send_gains, recv_gains, send_line, recv_line, send_plane, recv_plane):
    z = lax.axis_index("tensor")
    d = lax.axis_index("dp")
    barrier = pltpu.get_barrier_semaphore()
    for k in range(1, n):
        pl.semaphore_signal(barrier, inc=1, device_id={"tensor": lax.rem(z + k, n)}, device_id_type=MESH)
    for k in range(1, m):
        pl.semaphore_signal(barrier, inc=1, device_id={"dp": lax.rem(d + k, m)}, device_id_type=MESH)
    pl.semaphore_wait(barrier, n - 1 + m - 1)

    def gains_to(k, sender):
        peer = lax.rem(d + k, m)
        return pltpu.make_async_remote_copy(
            src_ref=gains_ref.at[peer], dst_ref=got_gains.at[sender], send_sem=send_gains.at[k],
            recv_sem=recv_gains.at[sender], device_id={"dp": peer}, device_id_type=MESH)

    def along_line(k, sender):
        return pltpu.make_async_remote_copy(
            src_ref=line.at[0], dst_ref=got_line.at[sender], send_sem=send_line.at[k], recv_sem=recv_line.at[sender],
            device_id={"tensor": lax.rem(z + k, n)}, device_id_type=MESH)

    def over_plane(k, sender):
        return pltpu.make_async_remote_copy(
            src_ref=line.at[1], dst_ref=got_plane.at[sender], send_sem=send_plane.at[k], recv_sem=recv_plane.at[sender],
            device_id={"dp": lax.rem(d + k, m)}, device_id_type=MESH)

    def summed(ref, count):
        whole = ref[0]
        for k in range(1, count):
            whole = whole + ref[k]
        return whole

    for k in range(1, m):
        gains_to(k, d).start()
    got_gains[d] = gains_ref[d]
    for k in range(1, m):
        gains_to(k, d).wait_send()
        gains_to(k, lax.rem(d + m - k, m)).wait_recv()
    gains = summed(got_gains, m)
    gain_ref[...] = gains
    own = jnp.sum(jnp.sum(gains * gains, axis=1, keepdims=True), axis=0, keepdims=True)
    own = jnp.where(z == 0, own, jnp.zeros_like(own))
    line[0] = square_ref[...] + jnp.broadcast_to(own, square_ref.shape)
    for k in range(1, n):
        along_line(k, z).start()
    got_line[z] = line[0]
    for k in range(1, n):
        along_line(k, z).wait_send()
        along_line(k, lax.rem(z + n - k, n)).wait_recv()
    line[1] = summed(got_line, n)
    for k in range(1, m):
        over_plane(k, d).start()
    got_plane[d] = line[1]
    for k in range(1, m):
        over_plane(k, d).wait_send()
        over_plane(k, lax.rem(d + m - k, m)).wait_recv()
    total_ref[...] = summed(got_plane, m)


def reduce_tail(gains, square, n, m, cid):
    share = gains.shape[1] // m
    parts = gains.reshape(2, m, share).transpose(1, 0, 2)
    tile = jnp.broadcast_to(square.reshape(1, 1), (8, 128))
    vmem = pl.BlockSpec(memory_space=pltpu.VMEM)
    dma = pltpu.SemaphoreType.DMA
    total, gain = pl.pallas_call(
        functools.partial(total_kernel, n, m),
        out_shape=(jax.ShapeDtypeStruct((8, 128), jnp.float32), jax.ShapeDtypeStruct((2, share), jnp.float32)),
        in_specs=[vmem, vmem],
        out_specs=(vmem, vmem),
        scratch_shapes=[
            pltpu.VMEM((2, 8, 128), jnp.float32),
            pltpu.VMEM((m, 2, share), jnp.float32),
            pltpu.VMEM((n, 8, 128), jnp.float32),
            pltpu.VMEM((m, 8, 128), jnp.float32),
            dma((m,)), dma((m,)), dma((n,)), dma((n,)), dma((m,)), dma((m,)),
        ],
        compiler_params=pltpu.CompilerParams(collective_id=cid, has_side_effects=True),
    )(parts, tile)
    return total[0, 0], gain


norm_eps = 1e-05
beta_first = 0.9
beta_second = 0.95
adam_eps = 1e-08
weight_decay = 0.1
weight_rate = 0.02
out_rate = 0.1
gain_rate = 0.2
clip_limit = 1.0


def positions(segment):
    length = segment.shape[0]
    indices = jnp.arange(length, dtype=jnp.int32)
    earlier = jnp.concatenate([segment[:1] - 1, segment[:-1]])
    begins = jnp.where(segment != earlier, indices, jnp.zeros_like(indices))
    return indices - lax.cummax(begins, axis=0)


def paired_tables(places):
    frequency = jnp.power(10000.0, -jnp.arange(HD // 2, dtype=jnp.float32) * (2.0 / HD))
    angles = places.astype(jnp.float32)[:, None] * frequency[None, :]
    cosines, sines = jnp.cos(angles), jnp.sin(angles)
    return (
        jnp.concatenate([cosines] * 4, axis=-1),
        jnp.concatenate([-sines, sines, -sines, sines], axis=-1),
    )


def over_rows(left, right):
    return lax.dot_general(
        left, right, (((0,), (0,)), ((), ())), preferred_element_type=jnp.float32
    )


def against(left, right):
    return lax.dot_general(
        left, right, (((1,), (1,)), ((), ())), preferred_element_type=jnp.float32
    )


def norm_back(grad_output, unit_rows, inverse, gain):
    scaled = grad_output * gain
    gain_grad = jnp.sum(grad_output * unit_rows, axis=0)
    inner_mean = jnp.mean(scaled * unit_rows, axis=-1, keepdims=True)
    return (inverse * (scaled - unit_rows * inner_mean), gain_grad)


def adam_step(weight, first, second, gradient, clip_factor, step_float, step_rate, decay_rate):
    gradient = gradient * clip_factor
    first = beta_first * first + (1.0 - beta_first) * gradient
    second = beta_second * second + (1.0 - beta_second) * gradient * gradient
    correct_one = 1.0 - jnp.power(beta_first, step_float)
    correct_two = 1.0 - jnp.power(beta_second, step_float)
    update = first / correct_one / (jnp.sqrt(second / correct_two) + adam_eps)
    return (first, second, weight - step_rate * (update + decay_rate * weight))


def on_device(
    n,
    m,
    tokens,
    cotangent,
    segment_ids,
    step_count,
    norm_gains,
    gains_first,
    gains_second,
    w_query,
    query_first,
    query_second,
    w_keyval,
    keyval_first,
    keyval_second,
    w_out,
    out_first,
    out_second,
    w_gateup,
    gateup_first,
    gateup_second,
    w_down,
    down_first,
    down_second,
):
    low = jnp.bfloat16
    width = w_query.shape[1]
    kv_width = w_keyval.shape[2]
    gain_rows = lax.all_gather(norm_gains.astype(low), "dp", axis=1, tiled=True)
    qkv_shard = jnp.concatenate([w_query, w_keyval[0], w_keyval[1]], axis=1).astype(low)
    qkv_weight = lax.all_gather(qkv_shard, "dp", axis=0, tiled=True)
    out_weight = lax.all_gather(w_out.astype(low), "dp", axis=1, tiled=True)
    gateup_weight = lax.all_gather(w_gateup.astype(low), "dp", axis=1, tiled=True)
    down_weight = lax.all_gather(w_down.astype(low), "dp", axis=1, tiled=True)
    gain_values = gain_rows.astype(jnp.float32)
    length = tokens.shape[0]
    size = min(256, length)
    segment = segment_ids[0]
    places = positions(segment)
    cosines, sines = paired_tables(places)
    first = (jnp.arange(length, dtype=jnp.int32) - places)[::size] // size
    seg_col, seg_row = segment[:, None], segment[None, :]

    values_in = tokens.astype(jnp.float32)
    inverse_one = lax.rsqrt(jnp.mean(values_in * values_in, axis=-1, keepdims=True) + norm_eps)
    unit_one = values_in * inverse_one
    normed_one = (unit_one * gain_values[0]).astype(low)
    raw = jnp.dot(normed_one, qkv_weight, preferred_element_type=jnp.float32)
    mixture, q, k, v, lse = attention_forward(raw, cosines, sines, seg_col, seg_row, first, size)
    branch_part = jnp.dot(mixture, out_weight, preferred_element_type=jnp.float32).astype(low)
    (branch,) = line_reduce((branch_part,), n, 16, 1)
    feed_part, grad_middle, grad_branch, gain_grad_two, grad_gate_weight, grad_up_weight, grad_down_weight = feed_forward(
        branch, gain_values[1:], tokens, cotangent, gateup_weight, down_weight, n, 2
    )
    gate_reduced = lax.psum_scatter(grad_gate_weight, "dp", scatter_dimension=0, tiled=True)
    up_reduced = lax.psum_scatter(grad_up_weight, "dp", scatter_dimension=0, tiled=True)
    down_reduced = lax.psum_scatter(grad_down_weight, "dp", scatter_dimension=1, tiled=True)
    grad_mixture = against(grad_branch, out_weight).astype(low)
    grad_qkv = attention_backward(
        q, k, v, mixture, grad_mixture, lse, cosines, sines, seg_col, seg_row, first, size
    )
    partial_one = against(grad_qkv, qkv_weight).astype(low)
    grad_out_weight = over_rows(mixture, grad_branch).astype(low)
    grad_qkv_weight = over_rows(normed_one, grad_qkv).astype(low)
    partial_one, grad_out_weight, grad_qkv_weight, gate_reduced = lax.optimization_barrier(
        (partial_one, grad_out_weight, grad_qkv_weight, gate_reduced)
    )
    out_reduced = lax.psum_scatter(grad_out_weight, "dp", scatter_dimension=1, tiled=True)
    qkv_reduced = lax.psum_scatter(grad_qkv_weight, "dp", scatter_dimension=0, tiled=True)
    feed_out, grad_normed_one = line_reduce((feed_part, partial_one), n, 16, 3)
    grad_normed_one = grad_normed_one.astype(jnp.float32)
    middle = values_in + branch.astype(jnp.float32)
    layer_out = (middle + feed_out.astype(jnp.float32)).astype(low)
    grad_from_one, gain_grad_one = norm_back(grad_normed_one, unit_one, inverse_one, gain_values[0])
    input_grad = grad_middle + grad_from_one
    gain_grads = jnp.concatenate([gain_grad_one[None], gain_grad_two])
    qkv_reduced = qkv_reduced.astype(jnp.float32)
    reduced = (
        qkv_reduced[:, :width],
        jnp.stack([qkv_reduced[:, width : width + kv_width], qkv_reduced[:, width + kv_width :]]),
        out_reduced.astype(jnp.float32),
        jnp.stack([gate_reduced, up_reduced]).astype(jnp.float32),
        down_reduced.astype(jnp.float32),
    )
    local_square = sum((jnp.sum(g * g) for g in reduced))
    square_total, gains_reduced = reduce_tail(gain_grads, local_square, n, m, 4)
    reduced = (gains_reduced, *reduced)
    grad_norm = jnp.sqrt(square_total)
    clip_factor = jnp.minimum(1.0, clip_limit / (grad_norm + 1e-06))
    step_float = step_count[0].astype(jnp.float32)
    params = (norm_gains, w_query, w_keyval, w_out, w_gateup, w_down)
    states = (
        (gains_first, gains_second),
        (query_first, query_second),
        (keyval_first, keyval_second),
        (out_first, out_second),
        (gateup_first, gateup_second),
        (down_first, down_second),
    )
    step_rates = (gain_rate, weight_rate, weight_rate, out_rate, weight_rate, weight_rate)
    decay_rates = (0.0, weight_decay, weight_decay, weight_decay, weight_decay, weight_decay)
    results = []
    for position_index in range(6):
        one, two = states[position_index]
        results.extend(
            adam_step(
                params[position_index],
                one,
                two,
                reduced[position_index],
                clip_factor,
                step_float,
                step_rates[position_index],
                decay_rates[position_index],
            )
        )
    return (layer_out, input_grad, grad_norm.reshape(1), *results)


def solution(mesh):
    rows = P("dp", None)
    gains = P(None, "dp")
    query = P("dp", "tensor")
    stacked = P(None, "dp", "tensor")
    turned = P("tensor", "dp")
    states = (gains,) * 3 + (query,) * 3 + (stacked,) * 3 + (turned,) * 3 + (stacked,) * 3 + (turned,) * 3
    return jax.shard_map(
        functools.partial(on_device, mesh.shape["tensor"], mesh.shape["dp"]),
        mesh=mesh,
        in_specs=(rows, rows, rows, P()) + states,
        out_specs=(rows, rows, P()) + states,
        check_vma=False,
    )
```

```python
import functools

import jax
import jax.numpy as jnp
from jax import lax
from jax.experimental import pallas as pl
from jax.experimental.pallas import tpu as pltpu
from jax.sharding import PartitionSpec as P

HD = 64
MESH = pl.DeviceIdType.MESH


masked_value = -1e9


def dot_t(left, right):
    return lax.dot_general(left, right, (((1,), (1,)), ((), ())), preferred_element_type=jnp.float32)


def dot_n(left, right):
    return lax.dot_general(left, right, (((1,), (0,)), ((), ())), preferred_element_type=jnp.float32)


def swap_halves(values, first_half):
    return jnp.where(first_half, pltpu.roll(values, 96, 1), pltpu.roll(values, 32, 1))


def lane_tests(rows):
    lane = lax.broadcasted_iota(jnp.int32, (rows, 128), 1)
    return lane < 64, (lane % 64) < 32


def block_bias(seg_col_ref, seg_row_ref, i, j, size):
    keys = seg_col_ref[pl.ds(pl.multiple_of(j * size, size), size), :]
    rows = seg_row_ref[:, pl.ds(pl.multiple_of(i * size, size), size)]
    key_at = j * size + lax.broadcasted_iota(jnp.int32, (size, size), 0)
    row_at = i * size + lax.broadcasted_iota(jnp.int32, (size, size), 1)
    return jnp.where((keys == rows) & (key_at <= row_at), 0.0, masked_value)


def stack_pair(pair, low_lanes):
    zero = jnp.zeros_like(pair)
    return jnp.concatenate([jnp.where(low_lanes, pair, zero), jnp.where(low_lanes, zero, pair)], axis=0)


def forward_kernel(size, pairs, first_ref, raw_ref, cos_ref, sin_ref, seg_col_ref, seg_row_ref,
                   mix_ref, q_ref, k_ref, v_ref, lse_ref, bias, scores, v_turned):
    length = raw_ref.shape[0]
    low_lanes, first_half = lane_tests(size)
    low_rows = lax.broadcasted_iota(jnp.int32, (128, size), 0) < 64
    width = pairs * 128

    def prepare(i, carry):
        rows = pl.ds(pl.multiple_of(i * size, size), size)
        cosines, sines = cos_ref[rows, :], sin_ref[rows, :]
        for hp in range(pairs):
            values = raw_ref[rows, hp * 128:(hp + 1) * 128]
            turned = values * cosines + swap_halves(values, first_half) * sines
            q_ref[rows, hp * 128:(hp + 1) * 128] = (turned.astype(jnp.bfloat16).astype(jnp.float32) * 0.125).astype(jnp.bfloat16)
        both = raw_ref[rows, width:width + 128]
        other = pltpu.roll(both, 64, 1)
        keys = jnp.where(low_lanes, both, other)
        k_ref[rows, :] = (keys * cosines + swap_halves(keys, first_half) * sines).astype(jnp.bfloat16)
        values = jnp.where(low_lanes, other, both)
        v_ref[rows, :] = values.astype(jnp.bfloat16)
        v_turned[i] = values.T.astype(jnp.bfloat16)
        return carry

    lax.fori_loop(0, length // size, prepare, 0)

    def row_block(i, carry):
        rows = pl.ds(pl.multiple_of(i * size, size), size)
        begin = first_ref[i]

        def fill(j, c):
            bias[j] = block_bias(seg_col_ref, seg_row_ref, i, j, size)
            return c

        lax.fori_loop(begin, i + 1, fill, 0)

        for hp in range(pairs):
            stacked = stack_pair(q_ref[rows, hp * 128:(hp + 1) * 128], low_lanes)

            def score(j, top):
                keys = k_ref[pl.ds(pl.multiple_of(j * size, size), size), :]
                b = bias[j]
                s = dot_t(keys, stacked) + jnp.concatenate([b, b], axis=1)
                scores[j] = s
                return jnp.maximum(top, jnp.max(s, axis=0, keepdims=True))

            top = lax.fori_loop(begin, i + 1, score, jnp.full((1, 2 * size), -jnp.inf, jnp.float32))

            def mix(j, c):
                total, acc = c
                p = jnp.exp(scores[j] - top)
                total = total + jnp.sum(p, axis=0, keepdims=True)
                return total, acc + dot_n(v_turned[j], p.astype(jnp.bfloat16))

            total, acc = lax.fori_loop(begin, i + 1, mix, (
                jnp.zeros((1, 2 * size), jnp.float32), jnp.zeros((128, 2 * size), jnp.float32)))
            lse_ref[i, hp] = top + jnp.log(total)
            acc = acc / total
            acc = jnp.where(low_rows, acc[:, :size], acc[:, size:])
            mix_ref[rows, hp * 128:(hp + 1) * 128] = acc.T.astype(jnp.bfloat16)
        return carry

    lax.fori_loop(0, length // size, row_block, 0)


def attention_forward(raw, cosines, sines, seg_col, seg_row, first, size):
    length, wide = raw.shape
    width = wide - 128
    pairs = width // 128
    blocks = length // size
    vmem = pl.BlockSpec(memory_space=pltpu.VMEM)
    return pl.pallas_call(
        functools.partial(forward_kernel, size, pairs),
        out_shape=(
            jax.ShapeDtypeStruct((length, width), jnp.bfloat16),
            jax.ShapeDtypeStruct((length, width), jnp.bfloat16),
            jax.ShapeDtypeStruct((length, 128), jnp.bfloat16),
            jax.ShapeDtypeStruct((length, 128), jnp.bfloat16),
            jax.ShapeDtypeStruct((blocks, pairs, 1, 2 * size), jnp.float32),
        ),
        in_specs=[pl.BlockSpec(memory_space=pltpu.SMEM)] + [vmem] * 5,
        out_specs=(vmem,) * 5,
        scratch_shapes=[
            pltpu.VMEM((blocks, size, size), jnp.float32),
            pltpu.VMEM((blocks, size, 2 * size), jnp.float32),
            pltpu.VMEM((blocks, 128, size), jnp.bfloat16),
        ],
        compiler_params=pltpu.CompilerParams(vmem_limit_bytes=40 << 20),
        cost_estimate=pl.CostEstimate(flops=10 * length * length * width, bytes_accessed=8 * length * width,
                                      transcendentals=length * length * pairs),
    )(first, raw, cosines, sines, seg_col, seg_row)


class Line:
    def __init__(self, n, chunks, rc, lag, part, got, out, sems, order=None):
        self.order = order
        self.n, self.chunks, self.rc, self.lag = n, chunks, rc, lag
        self.part, self.got, self.out = part, got, out
        self.send_a, self.recv_a, self.send_g, self.recv_g = sems
        self.me = lax.axis_index("tensor")
        self.steps = chunks + 2 * lag * (n - 1)

    def rows(self, stream, c):
        begin = (stream * self.chunks + c) * self.rc if self.order is None else self.order(stream, c)
        return pl.ds(pl.multiple_of(begin, self.rc), self.rc)

    def side(self, stream):
        pos = self.me if stream == 0 else self.n - 1 - self.me
        fwd = self.me + 1 if stream == 0 else self.me - 1
        bwd = self.me - 1 if stream == 0 else self.me + 1
        return pos, fwd, bwd

    def toward(self, stream, c, nxt, src):
        return pltpu.make_async_remote_copy(
            src_ref=src, dst_ref=self.got.at[stream, c],
            send_sem=self.send_a.at[stream, c], recv_sem=self.recv_a.at[stream, c],
            device_id={"tensor": nxt}, device_id_type=MESH)

    def back(self, stream, c, nxt):
        where = self.rows(stream, c)
        return pltpu.make_async_remote_copy(
            src_ref=self.out.at[where], dst_ref=self.out.at[where],
            send_sem=self.send_g.at[stream, c], recv_sem=self.recv_g.at[stream, c],
            device_id={"tensor": nxt}, device_id_type=MESH)

    def step(self, s):
        n, lag = self.n, self.lag
        for stream in (0, 1):
            pos, fwd, bwd = self.side(stream)
            c = s - lag * pos

            @pl.when((c >= 0) & (c < self.chunks))
            def _():
                where = self.rows(stream, c)
                slot = self.got.at[stream, c]

                def summed():
                    self.toward(stream, c, fwd, slot).wait_recv()
                    return (
                        self.part[where, :].astype(jnp.float32) + self.got[stream, c].astype(jnp.float32)
                    ).astype(self.out.dtype)

                @pl.when(pos == 0)
                def _():
                    self.toward(stream, c, fwd, self.part.at[where]).start()

                @pl.when((pos > 0) & (pos < n - 1))
                def _():
                    self.got[stream, c] = summed()
                    self.toward(stream, c, fwd, slot).start()

                @pl.when(pos == n - 1)
                def _():
                    self.out[where, :] = summed()
                    self.back(stream, c, bwd).start()
            d = s - lag * (n - 1) - lag * (n - 1 - pos)

            @pl.when((d >= 0) & (d < self.chunks) & (pos < n - 1))
            def _():
                self.back(stream, d, bwd).wait_recv()

                @pl.when(pos > 0)
                def _():
                    self.back(stream, d, bwd).start()

    def drain(self):
        def one(c, carry):
            for stream in (0, 1):
                pos, fwd, bwd = self.side(stream)

                @pl.when(pos < self.n - 1)
                def _():
                    self.toward(stream, c, fwd, self.got.at[stream, c]).wait_send()

                @pl.when(pos > 0)
                def _():
                    self.back(stream, c, bwd).wait_send()
            return carry

        lax.fori_loop(0, self.chunks, one, 0)


def greet(n):
    me = lax.axis_index("tensor")
    barrier = pltpu.get_barrier_semaphore()

    @pl.when(me > 0)
    def _():
        pl.semaphore_signal(barrier, inc=1, device_id={"tensor": me - 1}, device_id_type=MESH)

    @pl.when(me < n - 1)
    def _():
        pl.semaphore_signal(barrier, inc=1, device_id={"tensor": me + 1}, device_id_type=MESH)

    @pl.when((me > 0) & (me < n - 1))
    def _():
        pl.semaphore_wait(barrier, 2)

    @pl.when((me == 0) | (me == n - 1))
    def _():
        pl.semaphore_wait(barrier, 1)


def line_scratch(chunks, rc, width):
    return [pltpu.VMEM((2, chunks, rc, width), jnp.bfloat16)] + [pltpu.SemaphoreType.DMA((2, chunks))] * 4


def line_kernel(n, chunks, lag, count, *refs):
    parts, outs, scratch = refs[:count], refs[count:2 * count], refs[2 * count:]
    rc = parts[0].shape[0] // (2 * chunks)
    lines = [
        Line(n, chunks, rc, lag, parts[k], scratch[5 * k], outs[k], scratch[5 * k + 1:5 * k + 5])
        for k in range(count)
    ]
    greet(n)

    def step(s, carry):
        for k, line in enumerate(lines):
            line.step(s - k * chunks)
        return carry

    lax.fori_loop(0, lines[0].steps + (count - 1) * chunks, step, 0)
    for line in lines:
        line.drain()


def line_reduce(parts, n, chunks, cid, lag=2):
    rows, width = parts[0].shape
    count = len(parts)
    rc = rows // (2 * chunks)
    scratch = []
    for _ in parts:
        scratch += line_scratch(chunks, rc, width)
    vmem = pl.BlockSpec(memory_space=pltpu.VMEM)
    return pl.pallas_call(
        functools.partial(line_kernel, n, chunks, lag, count),
        out_shape=tuple(jax.ShapeDtypeStruct((rows, width), jnp.bfloat16) for _ in parts),
        in_specs=[vmem] * count,
        out_specs=(vmem,) * count,
        scratch_shapes=scratch,
        compiler_params=pltpu.CompilerParams(collective_id=cid, has_side_effects=True, vmem_limit_bytes=40 << 20),
        cost_estimate=pl.CostEstimate(flops=rows * width * 2 * count, bytes_accessed=rows * width * 120 * count,
                                      transcendentals=0),
    )(*parts)


def dot_rows(left, right):
    return lax.dot_general(left, right, (((0,), (0,)), ((), ())), preferred_element_type=jnp.float32)


def ff_kernel(n, chunks, lag, eps, branch, gain, x, cot_hbm, gu_hbm, down_hbm,
              feed_hbm, middle_hbm, low_hbm, gain_out, grads_hbm,
              got, sa, ra, sg, rg, two_sum, two_part, gu_w, down_w, cot, normed, hidden, gg, feed,
              middle_stage, low_stage, unit_stage, w_sem, cot_sem, feed_sem, stage_sem, grad_sem):
    rows, width = branch.shape
    ff = down_w.shape[0]
    rc = rows // (2 * chunks)
    per = 4
    half = rows // 2
    hb = per * rc
    block = 2 * hb
    blocks = chunks // per
    line = Line(n, chunks, rc, lag, two_part, got, two_sum, (sa, ra, sg, rg))
    landed = 2 * lag * (n - 1) + per
    tile = 256
    full, rest = ff // tile, ff % tile
    wide = width // tile

    weights = (
        pltpu.make_async_copy(gu_hbm, gu_w, w_sem.at[0]),
        pltpu.make_async_copy(down_hbm, down_w, w_sem.at[1]),
    )
    for copy in weights:
        copy.start()

    def natural(k, b):
        return pl.ds(pl.multiple_of(k * half + b * hb, hb), hb)

    def blocked(k, b):
        return pl.ds(pl.multiple_of(b * block + k * hb, hb), hb)

    def load_cot(b):
        return [pltpu.make_async_copy(cot_hbm.at[natural(k, b)], cot.at[blocked(k, b)], cot_sem.at[b, k])
                for k in (0, 1)]

    def save_feed(b):
        return [pltpu.make_async_copy(feed.at[pl.ds(k * hb, hb)], feed_hbm.at[natural(k, b)], feed_sem.at[k])
                for k in (0, 1)]

    def save_rows(d):
        copies = []
        for k in (0, 1):
            where = line.rows(k, d)
            copies.append(pltpu.make_async_copy(middle_stage.at[k], middle_hbm.at[where], stage_sem.at[0, k]))
            copies.append(pltpu.make_async_copy(low_stage.at[k], low_hbm.at[where], stage_sem.at[1, k]))
        return copies

    def save_units(w):
        return [pltpu.make_async_copy(unit_stage, grads_hbm.at[pl.ds(pl.multiple_of(w * tile, tile), tile)], grad_sem.at[0])]

    def start(copies):
        for copy in copies:
            copy.start()

    def wait(copies):
        for copy in copies:
            copy.wait()

    for b in range(blocks):
        start(load_cot(b))
    gain_out[...] = jnp.zeros_like(gain_out)
    greet(n)

    def unit_rows(where):
        middle = x[where, :].astype(jnp.float32) + branch[where, :].astype(jnp.float32)
        inverse = lax.rsqrt(jnp.mean(middle * middle, axis=-1, keepdims=True) + eps)
        return middle * inverse, inverse

    def normalize(b):
        def some(r, carry):
            for k in (0, 1):
                where = pl.ds(pl.multiple_of(k * half + b * hb + r * rc, rc), rc)
                at = pl.ds(pl.multiple_of(b * block + k * hb + r * rc, rc), rc)
                normed[at, :] = (unit_rows(where)[0] * gain[...]).astype(jnp.bfloat16)
            return carry

        lax.fori_loop(0, per, some, 0)

    def step(s, carry):
        line.step(s - per)
        b = s // per
        phase = s - b * per
        live = s < chunks
        mine = pl.ds(pl.multiple_of(b * block, block), block)

        def units(at, count):
            columns = pl.ds(at, count)
            gate = dot_n(normed[mine, :], gu_w[0, :, columns])
            up = dot_n(normed[mine, :], gu_w[1, :, columns])
            grad_hidden = dot_t(cot[mine, :], down_w[columns, :])
            sg_gate = 1.0 / (1.0 + jnp.exp(-gate))
            silu = gate * sg_gate
            hidden[mine, columns] = (silu * up).astype(jnp.bfloat16)
            gg[0, mine, columns] = (grad_hidden * up * sg_gate * (1.0 + gate * (1.0 - sg_gate))).astype(jnp.bfloat16)
            gg[1, mine, columns] = (grad_hidden * silu).astype(jnp.bfloat16)

        def unit_tile(t, c):
            units(pl.multiple_of(t * tile, tile), tile)
            return c

        @pl.when(live & (phase == 0))
        def _():
            normalize(b)

            @pl.when(b == 0)
            def _():
                wait(weights)
            wait(load_cot(b))

        @pl.when(live & (phase < 2))
        def _():
            lax.fori_loop(phase * 2, jnp.where(phase == 0, 2, full), unit_tile, 0)

        @pl.when(live & (phase == 2))
        def _():
            if rest:
                units(full * tile, rest)

            @pl.when(b > 0)
            def _():
                wait(save_feed(b - 1))

            def feed_tile(t, c):
                columns = pl.ds(pl.multiple_of(t * tile, tile), tile)
                feed[:, columns] = dot_n(hidden[mine, :], down_w[:, columns]).astype(jnp.bfloat16)
                return c

            lax.fori_loop(0, wide, feed_tile, 0)
            start(save_feed(b))

        @pl.when(live & (phase == 3))
        def _():
            def two_tile(t, c):
                at = pl.ds(pl.multiple_of(t * tile, tile), tile)
                value = (dot_t(gg[0, mine, :], gu_w[0, at, :]) + dot_t(gg[1, mine, :], gu_w[1, at, :])).astype(jnp.bfloat16)
                for k in (0, 1):
                    two_part[natural(k, b), at] = value[k * hb:(k + 1) * hb]
                return c

            lax.fori_loop(0, wide, two_tile, 0)

        d = s - landed

        @pl.when(d >= 0)
        def _():
            @pl.when(d > 0)
            def _():
                wait(save_rows(d - 1))
            for k in (0, 1):
                where = line.rows(k, d)
                at = pl.ds(pl.multiple_of((d // per) * block + k * hb + (d - (d // per) * per) * rc, rc), rc)
                unit, inverse = unit_rows(where)
                grad = two_sum[where, :].astype(jnp.float32)
                scaled = grad * gain[...]
                inner = jnp.mean(scaled * unit, axis=-1, keepdims=True)
                value = cot[at, :].astype(jnp.float32) + inverse * (scaled - unit * inner)
                middle_stage[k] = value
                low_stage[k] = value.astype(jnp.bfloat16)
                gain_out[...] += jnp.sum(grad * unit, axis=0, keepdims=True)
            start(save_rows(d))

        w = s - chunks

        @pl.when((w >= 0) & (w < wide))
        def _():
            @pl.when(w > 0)
            def _():
                wait(save_units(w - 1))
            columns = pl.ds(pl.multiple_of(w * tile, tile), tile)
            left = normed[:, columns]
            for t in (0, 1):
                unit_stage[:, t * ff:(t + 1) * ff] = dot_rows(left, gg[t]).astype(jnp.bfloat16)
            unit_stage[:, 2 * ff:] = dot_rows(cot[:, columns], hidden[...]).astype(jnp.bfloat16)
            start(save_units(w))
        return carry

    lax.fori_loop(0, per + line.steps, step, 0)
    line.drain()
    wait(save_feed(blocks - 1))
    wait(save_rows(chunks - 1))
    wait(save_units(wide - 1))


def feed_forward(branch, gain, x, cot, gateup_w, down_w, n, cid, chunks=16, lag=2):
    rows, width = branch.shape
    ff = down_w.shape[0]
    rc = rows // (2 * chunks)
    block = 8 * rc
    blocks = chunks // 4
    low = jnp.bfloat16
    vmem = pl.BlockSpec(memory_space=pltpu.VMEM)
    hbm = pl.BlockSpec(memory_space=pl.ANY)
    dma = pltpu.SemaphoreType.DMA
    shape = jax.ShapeDtypeStruct
    return pl.pallas_call(
        functools.partial(ff_kernel, n, chunks, lag, norm_eps),
        out_shape=(
            shape((rows, width), low), shape((rows, width), jnp.float32), shape((rows, width), low),
            shape((1, width), jnp.float32), shape((width, 3 * ff), low),
        ),
        in_specs=[vmem, vmem, vmem, hbm, hbm, hbm],
        out_specs=(hbm, hbm, hbm, vmem, hbm),
        scratch_shapes=line_scratch(chunks, rc, width) + [
            pltpu.VMEM((rows, width), low),
            pltpu.VMEM((rows, width), low),
            pltpu.VMEM((2, width, ff), low),
            pltpu.VMEM((ff, width), low),
            pltpu.VMEM((rows, width), low),
            pltpu.VMEM((rows, width), low),
            pltpu.VMEM((rows, ff), low),
            pltpu.VMEM((2, rows, ff), low),
            pltpu.VMEM((block, width), low),
            pltpu.VMEM((2, rc, width), jnp.float32),
            pltpu.VMEM((2, rc, width), low),
            pltpu.VMEM((256, 3 * ff), low),
            dma((2,)), dma((blocks, 2)), dma((2,)), dma((2, 2)), dma((1,)),
        ],
        compiler_params=pltpu.CompilerParams(collective_id=cid, has_side_effects=True, vmem_limit_bytes=63 << 20),
        cost_estimate=pl.CostEstimate(flops=18 * rows * width * ff, bytes_accessed=rows * width * 150,
                                      transcendentals=rows * ff),
    )(branch, gain, x, cot, gateup_w, down_w)


def back_kernel(n, m, chunks, lag, eps, size, pairs,
                feed_part, grad_low, gain, q_ref, k_ref, v_ref, mix_ref, lse_ref, cos_ref, sin_ref,
                seg_col_ref, seg_row_ref, out_w, x_hbm, qkv_hbm, branch_hbm, middle_hbm,
                layer_hbm, input_hbm, gain_out, reduced,
                got2, sa2, ra2, sg2, rg2, got4, sa4, ra4, sg4, rg4, feed_sum, part, grad_sum,
                x, qkv_w, normed, grad_mix, bias, k_turned, grad_k, grad_v, grad_qkv, send, recv,
                branch_stage, layer_stage, middle_stage, input_stage,
                w_sem, branch_sem, middle_sem, layer_sem, input_sem, send_sem, recv_sem):
    rows, width = feed_part.shape
    q_width = pairs * 128
    z = lax.axis_index("tensor")
    dp = lax.axis_index("dp")
    rc = rows // (2 * chunks)
    per = size // (2 * rc)
    hb = size // 2
    blocks = rows // size
    tile = 256
    wide = width // tile
    share = width // m
    owners = tile // share
    lead = 2 * lag * (n - 1)
    low_lanes, first_half = lane_tests(size)
    low_rows = lax.broadcasted_iota(jnp.int32, (128, size), 0) < 64

    def descending(stream, c):
        b = c // per
        return (blocks - 1 - b) * size + stream * hb + (c - b * per) * rc

    two = Line(n, chunks, rc, lag, feed_part, got2, feed_sum, (sa2, ra2, sg2, rg2))
    four = Line(n, chunks, rc, lag, part, got4, grad_sum, (sa4, ra4, sg4, rg4), descending)
    loads = (
        pltpu.make_async_copy(x_hbm, x, w_sem.at[0]),
        pltpu.make_async_copy(qkv_hbm, qkv_w, w_sem.at[1]),
    )
    for copy in loads:
        copy.start()

    def start(copies):
        for copy in copies:
            copy.start()

    def wait(copies):
        for copy in copies:
            copy.wait()

    def load_branch(d, slot):
        return [pltpu.make_async_copy(branch_hbm.at[two.rows(k, d)], branch_stage.at[slot, k], branch_sem.at[slot, k])
                for k in (0, 1)]

    def load_middle(d, slot):
        return [pltpu.make_async_copy(middle_hbm.at[four.rows(k, d)], middle_stage.at[slot, k], middle_sem.at[slot, k])
                for k in (0, 1)]

    def save_layer(d):
        return [pltpu.make_async_copy(layer_stage.at[k], layer_hbm.at[two.rows(k, d)], layer_sem.at[k]) for k in (0, 1)]

    def save_input(d):
        return [pltpu.make_async_copy(input_stage.at[k], input_hbm.at[four.rows(k, d)], input_sem.at[k]) for k in (0, 1)]

    def to_owner(w, o):
        owner = w * owners + o
        return pltpu.make_async_remote_copy(
            src_ref=send.at[w, pl.ds(o * share, share)], dst_ref=recv.at[dp], send_sem=send_sem.at[owner],
            recv_sem=recv_sem.at[dp], device_id={"dp": owner}, device_id_type=MESH)

    gain_out[...] = jnp.zeros_like(gain_out)

    def prepare(i, carry):
        at = pl.ds(pl.multiple_of(i * size, size), size)
        k_turned[i] = k_ref[at, :].astype(jnp.float32).T.astype(jnp.bfloat16)
        grad_k[i] = jnp.zeros((size, 128), jnp.float32)
        grad_v[i] = jnp.zeros((size, 128), jnp.float32)
        return carry

    lax.fori_loop(0, blocks, prepare, 0)

    barrier = pltpu.get_barrier_semaphore()

    @pl.when(z > 0)
    def _():
        pl.semaphore_signal(barrier, inc=1, device_id={"tensor": z - 1}, device_id_type=MESH)

    @pl.when(z < n - 1)
    def _():
        pl.semaphore_signal(barrier, inc=1, device_id={"tensor": z + 1}, device_id_type=MESH)

    for k in range(1, m):
        pl.semaphore_signal(barrier, inc=1, device_id={"dp": lax.rem(dp + k, m)}, device_id_type=MESH)

    @pl.when((z > 0) & (z < n - 1))
    def _():
        pl.semaphore_wait(barrier, m + 1)

    @pl.when((z == 0) | (z == n - 1))
    def _():
        pl.semaphore_wait(barrier, m)

    def unit_rows(where):
        values = x[where, :].astype(jnp.float32)
        inverse = lax.rsqrt(jnp.mean(values * values, axis=-1, keepdims=True) + eps)
        return values * inverse, inverse

    def attend(i, hp):
        at_rows = pl.ds(pl.multiple_of(i * size, size), size)
        columns = pl.ds(pl.multiple_of(hp * 128, 128), 128)
        stacked = stack_pair(q_ref[at_rows, columns], low_lanes)
        grad_pair = grad_mix[:, columns]
        grad_stacked = stack_pair(grad_pair, low_lanes)
        product = (grad_pair.astype(jnp.float32) * mix_ref[at_rows, columns].astype(jnp.float32)).T
        spread = jnp.concatenate([
            jnp.sum(product[:64], axis=0, keepdims=True), jnp.sum(product[64:], axis=0, keepdims=True)], axis=1)
        logsum = lse_ref[i, hp]

        def piece(j, acc):
            at = pl.ds(pl.multiple_of(j * size, size), size)
            b = bias[j]
            s = dot_t(k_ref[at, :], stacked) + jnp.concatenate([b, b], axis=1)
            p = jnp.exp(s - logsum)
            grad_p = dot_t(v_ref[at, :], grad_stacked)
            grad_s = (p * (grad_p - spread)).astype(jnp.bfloat16)
            grad_v[j] += dot_n(p.astype(jnp.bfloat16), grad_stacked)
            grad_k[j] += dot_n(grad_s, stacked)
            return acc + dot_n(k_turned[j], grad_s)

        acc = lax.fori_loop(0, i + 1, piece, jnp.zeros((128, 2 * size), jnp.float32))
        acc = jnp.where(low_rows, acc[:, :size], acc[:, size:]).T * 0.125
        turned = acc * cos_ref[at_rows, :] - swap_halves(acc, first_half) * sin_ref[at_rows, :]
        grad_qkv[at_rows, columns] = turned.astype(jnp.bfloat16)

    def step(s, carry):
        two.step(s)
        four.step(s - per)
        b = s // per
        hp = s - b * per
        i = blocks - 1 - b
        live = s < blocks * per
        at_rows = pl.ds(pl.multiple_of(i * size, size), size)

        @pl.when(s == 0)
        def _():
            wait(loads)

        @pl.when(live & (hp == 0))
        def _():
            grad_mix[...] = dot_t(grad_low[at_rows, :], out_w[...]).astype(jnp.bfloat16)

            def fill(j, c):
                bias[j] = block_bias(seg_col_ref, seg_row_ref, i, j, size)
                return c

            lax.fori_loop(0, i + 1, fill, 0)

        @pl.when(live)
        def _():
            def each(h, c):
                attend(i, h)
                return c

            lax.fori_loop(hp * pairs // per, (hp + 1) * pairs // per, each, 0)

            def some(r, c):
                at = pl.ds(pl.multiple_of(s * 2 * rc + r * rc, rc), rc)
                normed[at, :] = (unit_rows(at)[0] * gain[...]).astype(jnp.bfloat16)
                return c

            lax.fori_loop(0, 2, some, 0)

        @pl.when(live & (hp == per - 1))
        def _():
            cosines, sines = cos_ref[at_rows, :], sin_ref[at_rows, :]
            dk = grad_k[i] + pltpu.roll(grad_k[i], 64, 1)
            dk = dk * cosines - swap_halves(dk, first_half) * sines
            dv = grad_v[i] + pltpu.roll(grad_v[i], 64, 1)
            grad_qkv[at_rows, q_width:] = jnp.where(low_lanes, dk, dv).astype(jnp.bfloat16)

            def part_tile(t, c):
                at = pl.ds(pl.multiple_of(t * tile, tile), tile)
                part[at_rows, at] = dot_t(grad_qkv[at_rows, :], qkv_w[at, :]).astype(jnp.bfloat16)
                return c

            lax.fori_loop(0, wide, part_tile, 0)

        w = s - blocks * per

        @pl.when((w >= 0) & (w < wide))
        def _():
            columns = pl.ds(pl.multiple_of(w * tile, tile), tile)
            send[w, :, :q_width + 128] = dot_rows(normed[:, columns], grad_qkv[...]).astype(jnp.bfloat16)
            send[w, :, q_width + 128:] = dot_rows(grad_low[:, columns], mix_ref[...]).astype(jnp.bfloat16)
            for o in range(owners):
                owner = w * owners + o

                @pl.when(owner != dp)
                def _():
                    to_owner(w, o).start()

                @pl.when(owner == dp)
                def _():
                    recv[dp] = send[w, o * share:(o + 1) * share, :]

        e = s - lead + 1

        @pl.when((e >= 0) & (e < chunks))
        def _():
            start(load_branch(e, e % 2))

        d = s - lead

        @pl.when((d >= 0) & (d < chunks))
        def _():
            wait(load_branch(d, d % 2))

            @pl.when(d > 0)
            def _():
                wait(save_layer(d - 1))
            for k in (0, 1):
                where = two.rows(k, d)
                layer_stage[k] = (
                    x[where, :].astype(jnp.float32) + branch_stage[d % 2, k].astype(jnp.float32)
                    + feed_sum[where, :].astype(jnp.float32)
                ).astype(jnp.bfloat16)
            start(save_layer(d))

        e4 = s - lead - per + 1

        @pl.when((e4 >= 0) & (e4 < chunks))
        def _():
            start(load_middle(e4, e4 % 2))

        d4 = s - lead - per

        @pl.when(d4 >= 0)
        def _():
            wait(load_middle(d4, d4 % 2))

            @pl.when(d4 > 0)
            def _():
                wait(save_input(d4 - 1))
            for k in (0, 1):
                where = four.rows(k, d4)
                unit, inverse = unit_rows(where)
                grad = grad_sum[where, :].astype(jnp.float32)
                scaled = grad * gain[...]
                inner = jnp.mean(scaled * unit, axis=-1, keepdims=True)
                input_stage[k] = middle_stage[d4 % 2, k] + inverse * (scaled - unit * inner)
                gain_out[...] += jnp.sum(grad * unit, axis=0, keepdims=True)
            start(save_input(d4))
        return carry

    lax.fori_loop(0, per + four.steps, step, 0)
    two.drain()
    four.drain()
    wait(save_layer(chunks - 1))
    wait(save_input(chunks - 1))

    def finish(k, carry):
        owner = lax.rem(dp + k, m)
        w = owner // owners

        def copy(peer):
            return pltpu.make_async_remote_copy(
                src_ref=send.at[0, pl.ds(0, share)], dst_ref=recv.at[peer], send_sem=send_sem.at[peer],
                recv_sem=recv_sem.at[peer], device_id={"dp": peer}, device_id_type=MESH)

        copy(owner).wait_send()
        copy(owner).wait_recv()
        return carry

    lax.fori_loop(1, m, finish, 0)
    reduced[...] = recv[0].astype(jnp.float32)

    def add(k, carry):
        reduced[...] += recv[k].astype(jnp.float32)
        return carry

    lax.fori_loop(1, m, add, 0)


def attention_back(feed_part, grad_low, gain, q, k, v, mix, lse, cosines, sines, seg_col, seg_row, out_w,
                   x, qkv_w, branch, grad_middle, n, m, cid, size, chunks=16, lag=2):
    rows, width = feed_part.shape
    q_width = q.shape[1]
    pairs = q_width // 128
    rc = rows // (2 * chunks)
    blocks = rows // size
    share = width // m
    cat = 2 * q_width + 128
    low = jnp.bfloat16
    vmem = pl.BlockSpec(memory_space=pltpu.VMEM)
    hbm = pl.BlockSpec(memory_space=pl.ANY)
    dma = pltpu.SemaphoreType.DMA
    shape = jax.ShapeDtypeStruct
    return pl.pallas_call(
        functools.partial(back_kernel, n, m, chunks, lag, norm_eps, size, pairs),
        out_shape=(
            shape((rows, width), low), shape((rows, width), jnp.float32), shape((1, width), jnp.float32),
            shape((share, cat), jnp.float32),
        ),
        in_specs=[vmem] * 13 + [hbm] * 4,
        out_specs=(hbm, hbm, vmem, vmem),
        scratch_shapes=line_scratch(chunks, rc, width) + line_scratch(chunks, rc, width) + [
            pltpu.VMEM((rows, width), low),
            pltpu.VMEM((rows, width), low),
            pltpu.VMEM((rows, width), low),
            pltpu.VMEM((rows, width), low),
            pltpu.VMEM((width, q_width + 128), low),
            pltpu.VMEM((rows, width), low),
            pltpu.VMEM((size, q_width), low),
            pltpu.VMEM((blocks, size, size), jnp.float32),
            pltpu.VMEM((blocks, 128, size), low),
            pltpu.VMEM((blocks, size, 128), jnp.float32),
            pltpu.VMEM((blocks, size, 128), jnp.float32),
            pltpu.VMEM((rows, q_width + 128), low),
            pltpu.VMEM((width // 256, 256, cat), low),
            pltpu.VMEM((m, share, cat), low),
            pltpu.VMEM((2, 2, rc, width), low),
            pltpu.VMEM((2, rc, width), low),
            pltpu.VMEM((2, 2, rc, width), jnp.float32),
            pltpu.VMEM((2, rc, width), jnp.float32),
            dma((2,)), dma((2, 2)), dma((2, 2)), dma((2,)), dma((2,)), dma((m,)), dma((m,)),
        ],
        compiler_params=pltpu.CompilerParams(collective_id=cid, has_side_effects=True, vmem_limit_bytes=63 << 20),
        cost_estimate=pl.CostEstimate(flops=40 * rows * width * q_width, bytes_accessed=rows * width * 260,
                                      transcendentals=rows * rows * pairs),
    )(feed_part, grad_low, gain, q, k, v, mix, lse, cosines, sines, seg_col, seg_row, out_w,
      x, qkv_w, branch, grad_middle)


def total_kernel(n, m, gains_ref, square_ref, total_ref, gain_ref, line, got_gains, got_line, got_plane,
                 send_gains, recv_gains, send_line, recv_line, send_plane, recv_plane):
    z = lax.axis_index("tensor")
    d = lax.axis_index("dp")
    barrier = pltpu.get_barrier_semaphore()
    for k in range(1, n):
        pl.semaphore_signal(barrier, inc=1, device_id={"tensor": lax.rem(z + k, n)}, device_id_type=MESH)
    for k in range(1, m):
        pl.semaphore_signal(barrier, inc=1, device_id={"dp": lax.rem(d + k, m)}, device_id_type=MESH)
    pl.semaphore_wait(barrier, n - 1 + m - 1)

    def gains_to(k, sender):
        peer = lax.rem(d + k, m)
        return pltpu.make_async_remote_copy(
            src_ref=gains_ref.at[peer], dst_ref=got_gains.at[sender], send_sem=send_gains.at[k],
            recv_sem=recv_gains.at[sender], device_id={"dp": peer}, device_id_type=MESH)

    def along_line(k, sender):
        return pltpu.make_async_remote_copy(
            src_ref=line.at[0], dst_ref=got_line.at[sender], send_sem=send_line.at[k], recv_sem=recv_line.at[sender],
            device_id={"tensor": lax.rem(z + k, n)}, device_id_type=MESH)

    def over_plane(k, sender):
        return pltpu.make_async_remote_copy(
            src_ref=line.at[1], dst_ref=got_plane.at[sender], send_sem=send_plane.at[k], recv_sem=recv_plane.at[sender],
            device_id={"dp": lax.rem(d + k, m)}, device_id_type=MESH)

    def summed(ref, count):
        whole = ref[0]
        for k in range(1, count):
            whole = whole + ref[k]
        return whole

    for k in range(1, m):
        gains_to(k, d).start()
    got_gains[d] = gains_ref[d]
    for k in range(1, m):
        gains_to(k, d).wait_send()
        gains_to(k, lax.rem(d + m - k, m)).wait_recv()
    gains = summed(got_gains, m)
    gain_ref[...] = gains
    own = jnp.sum(jnp.sum(gains * gains, axis=1, keepdims=True), axis=0, keepdims=True)
    own = jnp.where(z == 0, own, jnp.zeros_like(own))
    line[0] = square_ref[...] + jnp.broadcast_to(own, square_ref.shape)
    for k in range(1, n):
        along_line(k, z).start()
    got_line[z] = line[0]
    for k in range(1, n):
        along_line(k, z).wait_send()
        along_line(k, lax.rem(z + n - k, n)).wait_recv()
    line[1] = summed(got_line, n)
    for k in range(1, m):
        over_plane(k, d).start()
    got_plane[d] = line[1]
    for k in range(1, m):
        over_plane(k, d).wait_send()
        over_plane(k, lax.rem(d + m - k, m)).wait_recv()
    total_ref[...] = summed(got_plane, m)


def reduce_tail(gains, square, n, m, cid):
    share = gains.shape[1] // m
    parts = gains.reshape(2, m, share).transpose(1, 0, 2)
    tile = jnp.broadcast_to(square.reshape(1, 1), (8, 128))
    vmem = pl.BlockSpec(memory_space=pltpu.VMEM)
    dma = pltpu.SemaphoreType.DMA
    total, gain = pl.pallas_call(
        functools.partial(total_kernel, n, m),
        out_shape=(jax.ShapeDtypeStruct((8, 128), jnp.float32), jax.ShapeDtypeStruct((2, share), jnp.float32)),
        in_specs=[vmem, vmem],
        out_specs=(vmem, vmem),
        scratch_shapes=[
            pltpu.VMEM((2, 8, 128), jnp.float32),
            pltpu.VMEM((m, 2, share), jnp.float32),
            pltpu.VMEM((n, 8, 128), jnp.float32),
            pltpu.VMEM((m, 8, 128), jnp.float32),
            dma((m,)), dma((m,)), dma((n,)), dma((n,)), dma((m,)), dma((m,)),
        ],
        compiler_params=pltpu.CompilerParams(collective_id=cid, has_side_effects=True),
    )(parts, tile)
    return total[0, 0], gain


norm_eps = 1e-05
beta_first = 0.9
beta_second = 0.95
adam_eps = 1e-08
weight_decay = 0.1
weight_rate = 0.02
out_rate = 0.1
gain_rate = 0.2
clip_limit = 1.0


def positions(segment):
    length = segment.shape[0]
    indices = jnp.arange(length, dtype=jnp.int32)
    earlier = jnp.concatenate([segment[:1] - 1, segment[:-1]])
    begins = jnp.where(segment != earlier, indices, jnp.zeros_like(indices))
    return indices - lax.cummax(begins, axis=0)


def paired_tables(places):
    frequency = jnp.power(10000.0, -jnp.arange(HD // 2, dtype=jnp.float32) * (2.0 / HD))
    angles = places.astype(jnp.float32)[:, None] * frequency[None, :]
    cosines, sines = jnp.cos(angles), jnp.sin(angles)
    return (
        jnp.concatenate([cosines] * 4, axis=-1),
        jnp.concatenate([-sines, sines, -sines, sines], axis=-1),
    )


def adam_step(weight, first, second, gradient, clip_factor, step_float, step_rate, decay_rate):
    gradient = gradient * clip_factor
    first = beta_first * first + (1.0 - beta_first) * gradient
    second = beta_second * second + (1.0 - beta_second) * gradient * gradient
    correct_one = 1.0 - jnp.power(beta_first, step_float)
    correct_two = 1.0 - jnp.power(beta_second, step_float)
    update = first / correct_one / (jnp.sqrt(second / correct_two) + adam_eps)
    return (first, second, weight - step_rate * (update + decay_rate * weight))


def on_device(
    n,
    m,
    tokens,
    cotangent,
    segment_ids,
    step_count,
    norm_gains,
    gains_first,
    gains_second,
    w_query,
    query_first,
    query_second,
    w_keyval,
    keyval_first,
    keyval_second,
    w_out,
    out_first,
    out_second,
    w_gateup,
    gateup_first,
    gateup_second,
    w_down,
    down_first,
    down_second,
):
    low = jnp.bfloat16
    width = w_query.shape[1]
    kv_width = w_keyval.shape[2]
    gain_rows = lax.all_gather(norm_gains.astype(low), "dp", axis=1, tiled=True)
    qkv_shard = jnp.concatenate([w_query, w_keyval[0], w_keyval[1]], axis=1).astype(low)
    qkv_weight = lax.all_gather(qkv_shard, "dp", axis=0, tiled=True)
    out_weight = lax.all_gather(w_out.astype(low), "dp", axis=1, tiled=True)
    gateup_weight = lax.all_gather(w_gateup.astype(low), "dp", axis=1, tiled=True)
    down_weight = lax.all_gather(w_down.astype(low), "dp", axis=1, tiled=True)
    gain_values = gain_rows.astype(jnp.float32)
    length = tokens.shape[0]
    size = min(256, length)
    segment = segment_ids[0]
    places = positions(segment)
    cosines, sines = paired_tables(places)
    first = (jnp.arange(length, dtype=jnp.int32) - places)[::size] // size
    seg_col, seg_row = segment[:, None], segment[None, :]

    values_in = tokens.astype(jnp.float32)
    inverse_one = lax.rsqrt(jnp.mean(values_in * values_in, axis=-1, keepdims=True) + norm_eps)
    unit_one = values_in * inverse_one
    normed_one = (unit_one * gain_values[0]).astype(low)
    raw = jnp.dot(normed_one, qkv_weight, preferred_element_type=jnp.float32)
    mixture, q, k, v, lse = attention_forward(raw, cosines, sines, seg_col, seg_row, first, size)
    branch_part = jnp.dot(mixture, out_weight, preferred_element_type=jnp.float32).astype(low)
    (branch,) = line_reduce((branch_part,), n, 16, 1)
    feed_part, grad_middle, grad_branch, gain_grad_two, grad_ff_weight = feed_forward(
        branch, gain_values[1:], tokens, cotangent, gateup_weight, down_weight, n, 2
    )
    ff_reduced = lax.psum_scatter(grad_ff_weight, "dp", scatter_dimension=0, tiled=True)
    layer_out, input_grad, gain_grad_one, head_reduced = attention_back(
        feed_part, grad_branch, gain_values[:1], q, k, v, mixture, lse, cosines, sines, seg_col, seg_row,
        out_weight, tokens, qkv_weight, branch, grad_middle, n, m, 3, size
    )
    gain_grads = jnp.concatenate([gain_grad_one, gain_grad_two])
    ff_reduced = ff_reduced.astype(jnp.float32)
    ff = w_down.shape[0]
    wide = width + 2 * kv_width
    local_square = jnp.sum(head_reduced * head_reduced) + jnp.sum(ff_reduced * ff_reduced)
    square_total, gains_reduced = reduce_tail(gain_grads, local_square, n, m, 4)
    reduced = (
        gains_reduced,
        head_reduced[:, :width],
        jnp.stack([head_reduced[:, width : width + kv_width], head_reduced[:, width + kv_width : wide]]),
        head_reduced[:, wide:].T,
        jnp.stack([ff_reduced[:, :ff], ff_reduced[:, ff : 2 * ff]]),
        ff_reduced[:, 2 * ff :].T,
    )
    grad_norm = jnp.sqrt(square_total)
    clip_factor = jnp.minimum(1.0, clip_limit / (grad_norm + 1e-06))
    step_float = step_count[0].astype(jnp.float32)
    params = (norm_gains, w_query, w_keyval, w_out, w_gateup, w_down)
    states = (
        (gains_first, gains_second),
        (query_first, query_second),
        (keyval_first, keyval_second),
        (out_first, out_second),
        (gateup_first, gateup_second),
        (down_first, down_second),
    )
    step_rates = (gain_rate, weight_rate, weight_rate, out_rate, weight_rate, weight_rate)
    decay_rates = (0.0, weight_decay, weight_decay, weight_decay, weight_decay, weight_decay)
    results = []
    for position_index in range(6):
        one, two = states[position_index]
        results.extend(
            adam_step(
                params[position_index],
                one,
                two,
                reduced[position_index],
                clip_factor,
                step_float,
                step_rates[position_index],
                decay_rates[position_index],
            )
        )
    return (layer_out, input_grad, grad_norm.reshape(1), *results)


def solution(mesh):
    rows = P("dp", None)
    gains = P(None, "dp")
    query = P("dp", "tensor")
    stacked = P(None, "dp", "tensor")
    turned = P("tensor", "dp")
    states = (gains,) * 3 + (query,) * 3 + (stacked,) * 3 + (turned,) * 3 + (stacked,) * 3 + (turned,) * 3
    return jax.shard_map(
        functools.partial(on_device, mesh.shape["tensor"], mesh.shape["dp"]),
        mesh=mesh,
        in_specs=(rows, rows, rows, P()) + states,
        out_specs=(rows, rows, P()) + states,
        check_vma=False,
    )
```

```python
import functools

import jax
import jax.numpy as jnp
from jax import lax
from jax.experimental import pallas as pl
from jax.experimental.pallas import tpu as pltpu
from jax.sharding import PartitionSpec as P

HD = 64
MESH = pl.DeviceIdType.MESH


masked_value = -1e9


def dot_t(left, right):
    return lax.dot_general(left, right, (((1,), (1,)), ((), ())), preferred_element_type=jnp.float32)


def dot_n(left, right):
    return lax.dot_general(left, right, (((1,), (0,)), ((), ())), preferred_element_type=jnp.float32)


def swap_halves(values, first_half):
    return jnp.where(first_half, pltpu.roll(values, 96, 1), pltpu.roll(values, 32, 1))


def lane_tests(rows):
    lane = lax.broadcasted_iota(jnp.int32, (rows, 128), 1)
    return lane < 64, (lane % 64) < 32


def block_bias(seg_col_ref, seg_row_ref, i, j, size):
    keys = seg_col_ref[pl.ds(pl.multiple_of(j * size, size), size), :]
    rows = seg_row_ref[:, pl.ds(pl.multiple_of(i * size, size), size)]
    key_at = j * size + lax.broadcasted_iota(jnp.int32, (size, size), 0)
    row_at = i * size + lax.broadcasted_iota(jnp.int32, (size, size), 1)
    return jnp.where((keys == rows) & (key_at <= row_at), 0.0, masked_value)


def stack_pair(pair, low_lanes):
    zero = jnp.zeros_like(pair)
    return jnp.concatenate([jnp.where(low_lanes, pair, zero), jnp.where(low_lanes, zero, pair)], axis=0)


def forward_kernel(size, pairs, first_ref, raw_ref, cos_ref, sin_ref, seg_col_ref, seg_row_ref,
                   mix_ref, q_ref, k_ref, v_ref, lse_ref, bias, scores, v_turned):
    length = raw_ref.shape[0]
    low_lanes, first_half = lane_tests(size)
    low_rows = lax.broadcasted_iota(jnp.int32, (128, size), 0) < 64
    width = pairs * 128

    def prepare(i, carry):
        rows = pl.ds(pl.multiple_of(i * size, size), size)
        cosines, sines = cos_ref[rows, :], sin_ref[rows, :]
        for hp in range(pairs):
            values = raw_ref[rows, hp * 128:(hp + 1) * 128]
            turned = values * cosines + swap_halves(values, first_half) * sines
            q_ref[rows, hp * 128:(hp + 1) * 128] = (turned.astype(jnp.bfloat16).astype(jnp.float32) * 0.125).astype(jnp.bfloat16)
        both = raw_ref[rows, width:width + 128]
        other = pltpu.roll(both, 64, 1)
        keys = jnp.where(low_lanes, both, other)
        k_ref[rows, :] = (keys * cosines + swap_halves(keys, first_half) * sines).astype(jnp.bfloat16)
        values = jnp.where(low_lanes, other, both)
        v_ref[rows, :] = values.astype(jnp.bfloat16)
        v_turned[i] = values.T.astype(jnp.bfloat16)
        return carry

    lax.fori_loop(0, length // size, prepare, 0)

    def row_block(i, carry):
        rows = pl.ds(pl.multiple_of(i * size, size), size)
        begin = first_ref[i]

        def fill(j, c):
            bias[j] = block_bias(seg_col_ref, seg_row_ref, i, j, size)
            return c

        lax.fori_loop(begin, i + 1, fill, 0)

        for hp in range(pairs):
            stacked = stack_pair(q_ref[rows, hp * 128:(hp + 1) * 128], low_lanes)

            def score(j, top):
                keys = k_ref[pl.ds(pl.multiple_of(j * size, size), size), :]
                b = bias[j]
                s = dot_t(keys, stacked) + jnp.concatenate([b, b], axis=1)
                scores[j] = s
                return jnp.maximum(top, jnp.max(s, axis=0, keepdims=True))

            top = lax.fori_loop(begin, i + 1, score, jnp.full((1, 2 * size), -jnp.inf, jnp.float32))

            def mix(j, c):
                total, acc = c
                p = jnp.exp(scores[j] - top)
                total = total + jnp.sum(p, axis=0, keepdims=True)
                return total, acc + dot_n(v_turned[j], p.astype(jnp.bfloat16))

            total, acc = lax.fori_loop(begin, i + 1, mix, (
                jnp.zeros((1, 2 * size), jnp.float32), jnp.zeros((128, 2 * size), jnp.float32)))
            lse_ref[i, hp] = top + jnp.log(total)
            acc = acc / total
            acc = jnp.where(low_rows, acc[:, :size], acc[:, size:])
            mix_ref[rows, hp * 128:(hp + 1) * 128] = acc.T.astype(jnp.bfloat16)
        return carry

    lax.fori_loop(0, length // size, row_block, 0)


def attention_forward(raw, cosines, sines, seg_col, seg_row, first, size):
    length, wide = raw.shape
    width = wide - 128
    pairs = width // 128
    blocks = length // size
    vmem = pl.BlockSpec(memory_space=pltpu.VMEM)
    return pl.pallas_call(
        functools.partial(forward_kernel, size, pairs),
        out_shape=(
            jax.ShapeDtypeStruct((length, width), jnp.bfloat16),
            jax.ShapeDtypeStruct((length, width), jnp.bfloat16),
            jax.ShapeDtypeStruct((length, 128), jnp.bfloat16),
            jax.ShapeDtypeStruct((length, 128), jnp.bfloat16),
            jax.ShapeDtypeStruct((blocks, pairs, 1, 2 * size), jnp.float32),
        ),
        in_specs=[pl.BlockSpec(memory_space=pltpu.SMEM)] + [vmem] * 5,
        out_specs=(vmem,) * 5,
        scratch_shapes=[
            pltpu.VMEM((blocks, size, size), jnp.float32),
            pltpu.VMEM((blocks, size, 2 * size), jnp.float32),
            pltpu.VMEM((blocks, 128, size), jnp.bfloat16),
        ],
        compiler_params=pltpu.CompilerParams(vmem_limit_bytes=40 << 20),
        cost_estimate=pl.CostEstimate(flops=10 * length * length * width, bytes_accessed=8 * length * width,
                                      transcendentals=length * length * pairs),
    )(first, raw, cosines, sines, seg_col, seg_row)


class Line:
    def __init__(self, n, chunks, rc, lag, part, got, out, sems, order=None):
        self.order = order
        self.n, self.chunks, self.rc, self.lag = n, chunks, rc, lag
        self.part, self.got, self.out = part, got, out
        self.send_a, self.recv_a, self.send_g, self.recv_g = sems
        self.me = lax.axis_index("tensor")
        self.steps = chunks + 2 * lag * (n - 1)

    def rows(self, stream, c):
        begin = (stream * self.chunks + c) * self.rc if self.order is None else self.order(stream, c)
        return pl.ds(pl.multiple_of(begin, self.rc), self.rc)

    def side(self, stream):
        pos = self.me if stream == 0 else self.n - 1 - self.me
        fwd = self.me + 1 if stream == 0 else self.me - 1
        bwd = self.me - 1 if stream == 0 else self.me + 1
        return pos, fwd, bwd

    def toward(self, stream, c, nxt, src):
        return pltpu.make_async_remote_copy(
            src_ref=src, dst_ref=self.got.at[stream, c],
            send_sem=self.send_a.at[stream, c], recv_sem=self.recv_a.at[stream, c],
            device_id={"tensor": nxt}, device_id_type=MESH)

    def back(self, stream, c, nxt):
        where = self.rows(stream, c)
        return pltpu.make_async_remote_copy(
            src_ref=self.out.at[where], dst_ref=self.out.at[where],
            send_sem=self.send_g.at[stream, c], recv_sem=self.recv_g.at[stream, c],
            device_id={"tensor": nxt}, device_id_type=MESH)

    def step(self, s):
        n, lag = self.n, self.lag
        for stream in (0, 1):
            pos, fwd, bwd = self.side(stream)
            c = s - lag * pos

            @pl.when((c >= 0) & (c < self.chunks))
            def _():
                where = self.rows(stream, c)
                slot = self.got.at[stream, c]

                def summed():
                    self.toward(stream, c, fwd, slot).wait_recv()
                    return (
                        self.part[where, :].astype(jnp.float32) + self.got[stream, c].astype(jnp.float32)
                    ).astype(self.out.dtype)

                @pl.when(pos == 0)
                def _():
                    self.toward(stream, c, fwd, self.part.at[where]).start()

                @pl.when((pos > 0) & (pos < n - 1))
                def _():
                    self.got[stream, c] = summed()
                    self.toward(stream, c, fwd, slot).start()

                @pl.when(pos == n - 1)
                def _():
                    self.out[where, :] = summed()
                    self.back(stream, c, bwd).start()
            d = s - lag * (n - 1) - lag * (n - 1 - pos)

            @pl.when((d >= 0) & (d < self.chunks) & (pos < n - 1))
            def _():
                self.back(stream, d, bwd).wait_recv()

                @pl.when(pos > 0)
                def _():
                    self.back(stream, d, bwd).start()

    def drain(self):
        def one(c, carry):
            for stream in (0, 1):
                pos, fwd, bwd = self.side(stream)

                @pl.when(pos < self.n - 1)
                def _():
                    self.toward(stream, c, fwd, self.got.at[stream, c]).wait_send()

                @pl.when(pos > 0)
                def _():
                    self.back(stream, c, bwd).wait_send()
            return carry

        lax.fori_loop(0, self.chunks, one, 0)


def greet(n):
    me = lax.axis_index("tensor")
    barrier = pltpu.get_barrier_semaphore()

    @pl.when(me > 0)
    def _():
        pl.semaphore_signal(barrier, inc=1, device_id={"tensor": me - 1}, device_id_type=MESH)

    @pl.when(me < n - 1)
    def _():
        pl.semaphore_signal(barrier, inc=1, device_id={"tensor": me + 1}, device_id_type=MESH)

    @pl.when((me > 0) & (me < n - 1))
    def _():
        pl.semaphore_wait(barrier, 2)

    @pl.when((me == 0) | (me == n - 1))
    def _():
        pl.semaphore_wait(barrier, 1)


def line_scratch(chunks, rc, width):
    return [pltpu.VMEM((2, chunks, rc, width), jnp.bfloat16)] + [pltpu.SemaphoreType.DMA((2, chunks))] * 4


def line_kernel(n, chunks, lag, count, *refs):
    parts, outs, scratch = refs[:count], refs[count:2 * count], refs[2 * count:]
    rc = parts[0].shape[0] // (2 * chunks)
    lines = [
        Line(n, chunks, rc, lag, parts[k], scratch[5 * k], outs[k], scratch[5 * k + 1:5 * k + 5])
        for k in range(count)
    ]
    greet(n)

    def step(s, carry):
        for k, line in enumerate(lines):
            line.step(s - k * chunks)
        return carry

    lax.fori_loop(0, lines[0].steps + (count - 1) * chunks, step, 0)
    for line in lines:
        line.drain()


def line_reduce(parts, n, chunks, cid, lag=2):
    rows, width = parts[0].shape
    count = len(parts)
    rc = rows // (2 * chunks)
    scratch = []
    for _ in parts:
        scratch += line_scratch(chunks, rc, width)
    vmem = pl.BlockSpec(memory_space=pltpu.VMEM)
    return pl.pallas_call(
        functools.partial(line_kernel, n, chunks, lag, count),
        out_shape=tuple(jax.ShapeDtypeStruct((rows, width), jnp.bfloat16) for _ in parts),
        in_specs=[vmem] * count,
        out_specs=(vmem,) * count,
        scratch_shapes=scratch,
        compiler_params=pltpu.CompilerParams(collective_id=cid, has_side_effects=True, vmem_limit_bytes=40 << 20),
        cost_estimate=pl.CostEstimate(flops=rows * width * 2 * count, bytes_accessed=rows * width * 120 * count,
                                      transcendentals=0),
    )(*parts)


def dot_rows(left, right):
    return lax.dot_general(left, right, (((0,), (0,)), ((), ())), preferred_element_type=jnp.float32)


def ff_kernel(n, chunks, lag, eps, branch, gain, x, cot_hbm, gu_hbm, down_hbm,
              feed_hbm, middle_hbm, low_hbm, gain_out, grads_hbm,
              got, sa, ra, sg, rg, two_sum, two_part, gu_w, down_w, cot, normed, hidden, gg, feed,
              middle_stage, low_stage, unit_stage, w_sem, cot_sem, feed_sem, stage_sem, grad_sem):
    rows, width = branch.shape
    ff = down_w.shape[0]
    rc = rows // (2 * chunks)
    per = 4
    half = rows // 2
    hb = per * rc
    block = 2 * hb
    blocks = chunks // per
    line = Line(n, chunks, rc, lag, two_part, got, two_sum, (sa, ra, sg, rg))
    landed = 2 * lag * (n - 1) + per
    tile = 256
    full, rest = ff // tile, ff % tile
    wide = width // tile

    weights = (
        pltpu.make_async_copy(gu_hbm, gu_w, w_sem.at[0]),
        pltpu.make_async_copy(down_hbm, down_w, w_sem.at[1]),
    )
    for copy in weights:
        copy.start()

    def natural(k, b):
        return pl.ds(pl.multiple_of(k * half + b * hb, hb), hb)

    def blocked(k, b):
        return pl.ds(pl.multiple_of(b * block + k * hb, hb), hb)

    def load_cot(b):
        return [pltpu.make_async_copy(cot_hbm.at[natural(k, b)], cot.at[blocked(k, b)], cot_sem.at[b, k])
                for k in (0, 1)]

    def save_feed(b):
        return [pltpu.make_async_copy(feed.at[pl.ds(k * hb, hb)], feed_hbm.at[natural(k, b)], feed_sem.at[k])
                for k in (0, 1)]

    def save_rows(d):
        copies = []
        for k in (0, 1):
            where = line.rows(k, d)
            copies.append(pltpu.make_async_copy(middle_stage.at[k], middle_hbm.at[where], stage_sem.at[0, k]))
            copies.append(pltpu.make_async_copy(low_stage.at[k], low_hbm.at[where], stage_sem.at[1, k]))
        return copies

    def save_units(w):
        return [pltpu.make_async_copy(unit_stage, grads_hbm.at[pl.ds(pl.multiple_of(w * tile, tile), tile)], grad_sem.at[0])]

    def start(copies):
        for copy in copies:
            copy.start()

    def wait(copies):
        for copy in copies:
            copy.wait()

    for b in range(blocks):
        start(load_cot(b))
    gain_out[...] = jnp.zeros_like(gain_out)
    greet(n)

    def unit_rows(where):
        middle = x[where, :].astype(jnp.float32) + branch[where, :].astype(jnp.float32)
        inverse = lax.rsqrt(jnp.mean(middle * middle, axis=-1, keepdims=True) + eps)
        return middle * inverse, inverse

    def normalize(b):
        def some(r, carry):
            for k in (0, 1):
                where = pl.ds(pl.multiple_of(k * half + b * hb + r * rc, rc), rc)
                at = pl.ds(pl.multiple_of(b * block + k * hb + r * rc, rc), rc)
                normed[at, :] = (unit_rows(where)[0] * gain[...]).astype(jnp.bfloat16)
            return carry

        lax.fori_loop(0, per, some, 0)

    def step(s, carry):
        line.step(s - per)
        b = s // per
        phase = s - b * per
        live = s < chunks
        mine = pl.ds(pl.multiple_of(b * block, block), block)

        def units(at, count):
            columns = pl.ds(at, count)
            gate = dot_n(normed[mine, :], gu_w[0, :, columns])
            up = dot_n(normed[mine, :], gu_w[1, :, columns])
            grad_hidden = dot_t(cot[mine, :], down_w[columns, :])
            sg_gate = 1.0 / (1.0 + jnp.exp(-gate))
            silu = gate * sg_gate
            hidden[mine, columns] = (silu * up).astype(jnp.bfloat16)
            gg[0, mine, columns] = (grad_hidden * up * sg_gate * (1.0 + gate * (1.0 - sg_gate))).astype(jnp.bfloat16)
            gg[1, mine, columns] = (grad_hidden * silu).astype(jnp.bfloat16)

        def unit_tile(t, c):
            units(pl.multiple_of(t * tile, tile), tile)
            return c

        @pl.when(live & (phase == 0))
        def _():
            normalize(b)

            @pl.when(b == 0)
            def _():
                wait(weights)
            wait(load_cot(b))

        @pl.when(live & (phase < 2))
        def _():
            lax.fori_loop(phase * 2, jnp.where(phase == 0, 2, full), unit_tile, 0)

        @pl.when(live & (phase == 2))
        def _():
            if rest:
                units(full * tile, rest)

            @pl.when(b > 0)
            def _():
                wait(save_feed(b - 1))

            def feed_tile(t, c):
                columns = pl.ds(pl.multiple_of(t * tile, tile), tile)
                feed[:, columns] = dot_n(hidden[mine, :], down_w[:, columns]).astype(jnp.bfloat16)
                return c

            lax.fori_loop(0, wide, feed_tile, 0)
            start(save_feed(b))

        @pl.when(live & (phase == 3))
        def _():
            def two_tile(t, c):
                at = pl.ds(pl.multiple_of(t * tile, tile), tile)
                value = (dot_t(gg[0, mine, :], gu_w[0, at, :]) + dot_t(gg[1, mine, :], gu_w[1, at, :])).astype(jnp.bfloat16)
                for k in (0, 1):
                    two_part[natural(k, b), at] = value[k * hb:(k + 1) * hb]
                return c

            lax.fori_loop(0, wide, two_tile, 0)

        d = s - landed

        @pl.when(d >= 0)
        def _():
            @pl.when(d > 0)
            def _():
                wait(save_rows(d - 1))
            for k in (0, 1):
                where = line.rows(k, d)
                at = pl.ds(pl.multiple_of((d // per) * block + k * hb + (d - (d // per) * per) * rc, rc), rc)
                unit, inverse = unit_rows(where)
                grad = two_sum[where, :].astype(jnp.float32)
                scaled = grad * gain[...]
                inner = jnp.mean(scaled * unit, axis=-1, keepdims=True)
                value = cot[at, :].astype(jnp.float32) + inverse * (scaled - unit * inner)
                middle_stage[k] = value
                low_stage[k] = value.astype(jnp.bfloat16)
                gain_out[...] += jnp.sum(grad * unit, axis=0, keepdims=True)
            start(save_rows(d))

        w = s - chunks

        @pl.when((w >= 0) & (w < wide))
        def _():
            @pl.when(w > 0)
            def _():
                wait(save_units(w - 1))
            columns = pl.ds(pl.multiple_of(w * tile, tile), tile)
            left = normed[:, columns]
            for t in (0, 1):
                unit_stage[:, t * ff:(t + 1) * ff] = dot_rows(left, gg[t]).astype(jnp.bfloat16)
            unit_stage[:, 2 * ff:] = dot_rows(cot[:, columns], hidden[...]).astype(jnp.bfloat16)
            start(save_units(w))
        return carry

    lax.fori_loop(0, per + line.steps, step, 0)
    line.drain()
    wait(save_feed(blocks - 1))
    wait(save_rows(chunks - 1))
    wait(save_units(wide - 1))


def feed_forward(branch, gain, x, cot, gateup_w, down_w, n, cid, chunks=16, lag=2):
    rows, width = branch.shape
    ff = down_w.shape[0]
    rc = rows // (2 * chunks)
    block = 8 * rc
    blocks = chunks // 4
    low = jnp.bfloat16
    vmem = pl.BlockSpec(memory_space=pltpu.VMEM)
    hbm = pl.BlockSpec(memory_space=pl.ANY)
    dma = pltpu.SemaphoreType.DMA
    shape = jax.ShapeDtypeStruct
    return pl.pallas_call(
        functools.partial(ff_kernel, n, chunks, lag, norm_eps),
        out_shape=(
            shape((rows, width), low), shape((rows, width), jnp.float32), shape((rows, width), low),
            shape((1, width), jnp.float32), shape((width, 3 * ff), low),
        ),
        in_specs=[vmem, vmem, vmem, hbm, hbm, hbm],
        out_specs=(hbm, hbm, hbm, vmem, hbm),
        scratch_shapes=line_scratch(chunks, rc, width) + [
            pltpu.VMEM((rows, width), low),
            pltpu.VMEM((rows, width), low),
            pltpu.VMEM((2, width, ff), low),
            pltpu.VMEM((ff, width), low),
            pltpu.VMEM((rows, width), low),
            pltpu.VMEM((rows, width), low),
            pltpu.VMEM((rows, ff), low),
            pltpu.VMEM((2, rows, ff), low),
            pltpu.VMEM((block, width), low),
            pltpu.VMEM((2, rc, width), jnp.float32),
            pltpu.VMEM((2, rc, width), low),
            pltpu.VMEM((256, 3 * ff), low),
            dma((2,)), dma((blocks, 2)), dma((2,)), dma((2, 2)), dma((1,)),
        ],
        compiler_params=pltpu.CompilerParams(collective_id=cid, has_side_effects=True, vmem_limit_bytes=63 << 20),
        cost_estimate=pl.CostEstimate(flops=18 * rows * width * ff, bytes_accessed=rows * width * 150,
                                      transcendentals=rows * ff),
    )(branch, gain, x, cot, gateup_w, down_w)


def back_kernel(n, m, chunks, lag, eps, size, pairs,
                feed_part, grad_low, gain, q_ref, k_ref, v_ref, mix_ref, lse_ref, cos_ref, sin_ref,
                seg_col_ref, seg_row_ref, out_w, x_hbm, qkv_hbm, branch_hbm, middle_hbm,
                layer_hbm, input_hbm, gain_out, reduced,
                got2, sa2, ra2, sg2, rg2, got4, sa4, ra4, sg4, rg4, feed_sum, part, grad_sum,
                x, qkv_w, normed, grad_mix, bias, k_turned, grad_k, grad_v, grad_qkv, send, recv,
                branch_stage, layer_stage, middle_stage, input_stage,
                w_sem, branch_sem, middle_sem, layer_sem, input_sem, send_sem, recv_sem):
    rows, width = feed_part.shape
    q_width = pairs * 128
    z = lax.axis_index("tensor")
    dp = lax.axis_index("dp")
    rc = rows // (2 * chunks)
    per = size // (2 * rc)
    hb = size // 2
    blocks = rows // size
    tile = 256
    wide = width // tile
    share = width // m
    owners = tile // share
    lead = 2 * lag * (n - 1)
    low_lanes, first_half = lane_tests(size)
    low_rows = lax.broadcasted_iota(jnp.int32, (128, size), 0) < 64

    def descending(stream, c):
        b = c // per
        return (blocks - 1 - b) * size + stream * hb + (c - b * per) * rc

    two = Line(n, chunks, rc, lag, feed_part, got2, feed_sum, (sa2, ra2, sg2, rg2))
    four = Line(n, chunks, rc, lag, part, got4, grad_sum, (sa4, ra4, sg4, rg4), descending)
    loads = (
        pltpu.make_async_copy(x_hbm, x, w_sem.at[0]),
        pltpu.make_async_copy(qkv_hbm, qkv_w, w_sem.at[1]),
    )
    for copy in loads:
        copy.start()

    def start(copies):
        for copy in copies:
            copy.start()

    def wait(copies):
        for copy in copies:
            copy.wait()

    def load_branch(d, slot):
        return [pltpu.make_async_copy(branch_hbm.at[two.rows(k, d)], branch_stage.at[slot, k], branch_sem.at[slot, k])
                for k in (0, 1)]

    def load_middle(d, slot):
        return [pltpu.make_async_copy(middle_hbm.at[four.rows(k, d)], middle_stage.at[slot, k], middle_sem.at[slot, k])
                for k in (0, 1)]

    def save_layer(d):
        return [pltpu.make_async_copy(layer_stage.at[k], layer_hbm.at[two.rows(k, d)], layer_sem.at[k]) for k in (0, 1)]

    def save_input(d):
        return [pltpu.make_async_copy(input_stage.at[k], input_hbm.at[four.rows(k, d)], input_sem.at[k]) for k in (0, 1)]

    def to_owner(w, o):
        owner = w * owners + o
        return pltpu.make_async_remote_copy(
            src_ref=send.at[w, pl.ds(o * share, share)], dst_ref=recv.at[dp], send_sem=send_sem.at[owner],
            recv_sem=recv_sem.at[dp], device_id={"dp": owner}, device_id_type=MESH)

    gain_out[...] = jnp.zeros_like(gain_out)

    def prepare(i, carry):
        at = pl.ds(pl.multiple_of(i * size, size), size)
        k_turned[i] = k_ref[at, :].astype(jnp.float32).T.astype(jnp.bfloat16)
        grad_k[i] = jnp.zeros((size, 128), jnp.float32)
        grad_v[i] = jnp.zeros((size, 128), jnp.float32)
        return carry

    lax.fori_loop(0, blocks, prepare, 0)

    barrier = pltpu.get_barrier_semaphore()

    @pl.when(z > 0)
    def _():
        pl.semaphore_signal(barrier, inc=1, device_id={"tensor": z - 1}, device_id_type=MESH)

    @pl.when(z < n - 1)
    def _():
        pl.semaphore_signal(barrier, inc=1, device_id={"tensor": z + 1}, device_id_type=MESH)

    for k in range(1, m):
        pl.semaphore_signal(barrier, inc=1, device_id={"dp": lax.rem(dp + k, m)}, device_id_type=MESH)

    @pl.when((z > 0) & (z < n - 1))
    def _():
        pl.semaphore_wait(barrier, m + 1)

    @pl.when((z == 0) | (z == n - 1))
    def _():
        pl.semaphore_wait(barrier, m)

    def unit_rows(where):
        values = x[where, :].astype(jnp.float32)
        inverse = lax.rsqrt(jnp.mean(values * values, axis=-1, keepdims=True) + eps)
        return values * inverse, inverse

    def attend(i, hp):
        at_rows = pl.ds(pl.multiple_of(i * size, size), size)
        columns = pl.ds(pl.multiple_of(hp * 128, 128), 128)
        stacked = stack_pair(q_ref[at_rows, columns], low_lanes)
        grad_pair = grad_mix[:, columns]
        grad_stacked = stack_pair(grad_pair, low_lanes)
        product = (grad_pair.astype(jnp.float32) * mix_ref[at_rows, columns].astype(jnp.float32)).T
        spread = jnp.concatenate([
            jnp.sum(product[:64], axis=0, keepdims=True), jnp.sum(product[64:], axis=0, keepdims=True)], axis=1)
        logsum = lse_ref[i, hp]

        def piece(j, acc):
            at = pl.ds(pl.multiple_of(j * size, size), size)
            b = bias[j]
            s = dot_t(k_ref[at, :], stacked) + jnp.concatenate([b, b], axis=1)
            p = jnp.exp(s - logsum)
            grad_p = dot_t(v_ref[at, :], grad_stacked)
            grad_s = (p * (grad_p - spread)).astype(jnp.bfloat16)
            grad_v[j] += dot_n(p.astype(jnp.bfloat16), grad_stacked)
            grad_k[j] += dot_n(grad_s, stacked)
            return acc + dot_n(k_turned[j], grad_s)

        acc = lax.fori_loop(0, i + 1, piece, jnp.zeros((128, 2 * size), jnp.float32))
        acc = jnp.where(low_rows, acc[:, :size], acc[:, size:]).T * 0.125
        turned = acc * cos_ref[at_rows, :] - swap_halves(acc, first_half) * sin_ref[at_rows, :]
        grad_qkv[at_rows, columns] = turned.astype(jnp.bfloat16)

    def step(s, carry):
        two.step(s)
        four.step(s - per)
        b = s // per
        hp = s - b * per
        i = blocks - 1 - b
        live = s < blocks * per
        at_rows = pl.ds(pl.multiple_of(i * size, size), size)

        @pl.when(s == 0)
        def _():
            wait(loads)

        @pl.when(live & (hp == 0))
        def _():
            grad_mix[...] = dot_t(grad_low[at_rows, :], out_w[...]).astype(jnp.bfloat16)

            def fill(j, c):
                bias[j] = block_bias(seg_col_ref, seg_row_ref, i, j, size)
                return c

            lax.fori_loop(0, i + 1, fill, 0)

        @pl.when(live)
        def _():
            def each(h, c):
                attend(i, h)
                return c

            lax.fori_loop(hp * pairs // per, (hp + 1) * pairs // per, each, 0)

            def some(r, c):
                at = pl.ds(pl.multiple_of(s * 2 * rc + r * rc, rc), rc)
                normed[at, :] = (unit_rows(at)[0] * gain[...]).astype(jnp.bfloat16)
                return c

            lax.fori_loop(0, 2, some, 0)

        @pl.when(live & (hp == per - 1))
        def _():
            cosines, sines = cos_ref[at_rows, :], sin_ref[at_rows, :]
            dk = grad_k[i] + pltpu.roll(grad_k[i], 64, 1)
            dk = dk * cosines - swap_halves(dk, first_half) * sines
            dv = grad_v[i] + pltpu.roll(grad_v[i], 64, 1)
            grad_qkv[at_rows, q_width:] = jnp.where(low_lanes, dk, dv).astype(jnp.bfloat16)

            def part_tile(t, c):
                at = pl.ds(pl.multiple_of(t * tile, tile), tile)
                part[at_rows, at] = dot_t(grad_qkv[at_rows, :], qkv_w[at, :]).astype(jnp.bfloat16)
                return c

            lax.fori_loop(0, wide, part_tile, 0)

        w = s - blocks * per

        @pl.when((w >= 0) & (w < wide))
        def _():
            columns = pl.ds(pl.multiple_of(w * tile, tile), tile)
            send[w, :, :q_width + 128] = dot_rows(normed[:, columns], grad_qkv[...]).astype(jnp.bfloat16)
            send[w, :, q_width + 128:] = dot_rows(grad_low[:, columns], mix_ref[...]).astype(jnp.bfloat16)
            for o in range(owners):
                owner = w * owners + o

                @pl.when(owner != dp)
                def _():
                    to_owner(w, o).start()

                @pl.when(owner == dp)
                def _():
                    recv[dp] = send[w, o * share:(o + 1) * share, :]

        e = s - lead + 1

        @pl.when((e >= 0) & (e < chunks))
        def _():
            start(load_branch(e, e % 2))

        d = s - lead

        @pl.when((d >= 0) & (d < chunks))
        def _():
            wait(load_branch(d, d % 2))

            @pl.when(d > 0)
            def _():
                wait(save_layer(d - 1))
            for k in (0, 1):
                where = two.rows(k, d)
                layer_stage[k] = (
                    x[where, :].astype(jnp.float32) + branch_stage[d % 2, k].astype(jnp.float32)
                    + feed_sum[where, :].astype(jnp.float32)
                ).astype(jnp.bfloat16)
            start(save_layer(d))

        e4 = s - lead - per + 1

        @pl.when((e4 >= 0) & (e4 < chunks))
        def _():
            start(load_middle(e4, e4 % 2))

        d4 = s - lead - per

        @pl.when(d4 >= 0)
        def _():
            wait(load_middle(d4, d4 % 2))

            @pl.when(d4 > 0)
            def _():
                wait(save_input(d4 - 1))
            for k in (0, 1):
                where = four.rows(k, d4)
                unit, inverse = unit_rows(where)
                grad = grad_sum[where, :].astype(jnp.float32)
                scaled = grad * gain[...]
                inner = jnp.mean(scaled * unit, axis=-1, keepdims=True)
                input_stage[k] = middle_stage[d4 % 2, k] + inverse * (scaled - unit * inner)
                gain_out[...] += jnp.sum(grad * unit, axis=0, keepdims=True)
            start(save_input(d4))
        return carry

    lax.fori_loop(0, per + four.steps, step, 0)
    two.drain()
    four.drain()
    wait(save_layer(chunks - 1))
    wait(save_input(chunks - 1))

    def finish(k, carry):
        owner = lax.rem(dp + k, m)
        w = owner // owners

        def copy(peer):
            return pltpu.make_async_remote_copy(
                src_ref=send.at[0, pl.ds(0, share)], dst_ref=recv.at[peer], send_sem=send_sem.at[peer],
                recv_sem=recv_sem.at[peer], device_id={"dp": peer}, device_id_type=MESH)

        copy(owner).wait_send()
        copy(owner).wait_recv()
        return carry

    lax.fori_loop(1, m, finish, 0)
    reduced[...] = recv[0].astype(jnp.float32)

    def add(k, carry):
        reduced[...] += recv[k].astype(jnp.float32)
        return carry

    lax.fori_loop(1, m, add, 0)


def attention_back(feed_part, grad_low, gain, q, k, v, mix, lse, cosines, sines, seg_col, seg_row, out_w,
                   x, qkv_w, branch, grad_middle, n, m, cid, size, chunks=16, lag=2):
    rows, width = feed_part.shape
    q_width = q.shape[1]
    pairs = q_width // 128
    rc = rows // (2 * chunks)
    blocks = rows // size
    share = width // m
    cat = 2 * q_width + 128
    low = jnp.bfloat16
    vmem = pl.BlockSpec(memory_space=pltpu.VMEM)
    hbm = pl.BlockSpec(memory_space=pl.ANY)
    dma = pltpu.SemaphoreType.DMA
    shape = jax.ShapeDtypeStruct
    return pl.pallas_call(
        functools.partial(back_kernel, n, m, chunks, lag, norm_eps, size, pairs),
        out_shape=(
            shape((rows, width), low), shape((rows, width), jnp.float32), shape((1, width), jnp.float32),
            shape((share, cat), jnp.float32),
        ),
        in_specs=[vmem] * 13 + [hbm] * 4,
        out_specs=(hbm, hbm, vmem, vmem),
        scratch_shapes=line_scratch(chunks, rc, width) + line_scratch(chunks, rc, width) + [
            pltpu.VMEM((rows, width), low),
            pltpu.VMEM((rows, width), low),
            pltpu.VMEM((rows, width), low),
            pltpu.VMEM((rows, width), low),
            pltpu.VMEM((width, q_width + 128), low),
            pltpu.VMEM((rows, width), low),
            pltpu.VMEM((size, q_width), low),
            pltpu.VMEM((blocks, size, size), jnp.float32),
            pltpu.VMEM((blocks, 128, size), low),
            pltpu.VMEM((blocks, size, 128), jnp.float32),
            pltpu.VMEM((blocks, size, 128), jnp.float32),
            pltpu.VMEM((rows, q_width + 128), low),
            pltpu.VMEM((width // 256, 256, cat), low),
            pltpu.VMEM((m, share, cat), low),
            pltpu.VMEM((2, 2, rc, width), low),
            pltpu.VMEM((2, rc, width), low),
            pltpu.VMEM((2, 2, rc, width), jnp.float32),
            pltpu.VMEM((2, rc, width), jnp.float32),
            dma((2,)), dma((2, 2)), dma((2, 2)), dma((2,)), dma((2,)), dma((m,)), dma((m,)),
        ],
        compiler_params=pltpu.CompilerParams(collective_id=cid, has_side_effects=True, vmem_limit_bytes=63 << 20),
        cost_estimate=pl.CostEstimate(flops=40 * rows * width * q_width, bytes_accessed=rows * width * 260,
                                      transcendentals=rows * rows * pairs),
    )(feed_part, grad_low, gain, q, k, v, mix, lse, cosines, sines, seg_col, seg_row, out_w,
      x, qkv_w, branch, grad_middle)


def tail_kernel(n, m, rates, kv_width, gains_ref, correct_ref, ff_hbm, head_ref, *refs):
    count = len(rates)
    params = refs[:3 * count]
    norm_ref, outs = refs[3 * count], refs[3 * count + 1:6 * count + 1]
    (line, got_gains, got_line, got_plane, ff_grad, turned), rest = refs[6 * count + 1:6 * count + 7], refs[6 * count + 7:]
    held, rest = rest[:3 * count], rest[3 * count:]
    (send_gains, recv_gains, send_line, recv_line, send_plane, recv_plane, ff_sem, load_sem, save_sem) = rest
    z = lax.axis_index("tensor")
    d = lax.axis_index("dp")
    share = head_ref.shape[0]
    q_width = outs[3].shape[1]
    ff = outs[12].shape[2]

    ff_load = pltpu.make_async_copy(ff_hbm, ff_grad, ff_sem)
    ff_load.start()
    loads = [pltpu.make_async_copy(params[k], held[k], load_sem.at[k]) for k in range(3 * count)]
    saves = [pltpu.make_async_copy(held[k], outs[k], save_sem.at[k]) for k in range(3 * count)]
    for copy in loads:
        copy.start()

    barrier = pltpu.get_barrier_semaphore()
    for k in range(1, n):
        pl.semaphore_signal(barrier, inc=1, device_id={"tensor": lax.rem(z + k, n)}, device_id_type=MESH)
    for k in range(1, m):
        pl.semaphore_signal(barrier, inc=1, device_id={"dp": lax.rem(d + k, m)}, device_id_type=MESH)
    pl.semaphore_wait(barrier, n - 1 + m - 1)

    def gains_to(k, sender):
        peer = lax.rem(d + k, m)
        return pltpu.make_async_remote_copy(
            src_ref=gains_ref.at[peer], dst_ref=got_gains.at[sender], send_sem=send_gains.at[k],
            recv_sem=recv_gains.at[sender], device_id={"dp": peer}, device_id_type=MESH)

    def along_line(k, sender):
        return pltpu.make_async_remote_copy(
            src_ref=line.at[0], dst_ref=got_line.at[sender], send_sem=send_line.at[k], recv_sem=recv_line.at[sender],
            device_id={"tensor": lax.rem(z + k, n)}, device_id_type=MESH)

    def over_plane(k, sender):
        return pltpu.make_async_remote_copy(
            src_ref=line.at[1], dst_ref=got_plane.at[sender], send_sem=send_plane.at[k], recv_sem=recv_plane.at[sender],
            device_id={"dp": lax.rem(d + k, m)}, device_id_type=MESH)

    def summed(ref, number):
        whole = ref[0]
        for k in range(1, number):
            whole = whole + ref[k]
        return whole

    def squares(value):
        return jnp.sum(jnp.sum(value * value, axis=0, keepdims=True), axis=1, keepdims=True)

    for k in range(1, m):
        gains_to(k, d).start()
    got_gains[d] = gains_ref[d]
    sub = 32

    def head_rows(r, acc):
        value = head_ref[pl.ds(pl.multiple_of(r * sub, sub), sub), :]
        return acc + squares(value)

    local = lax.fori_loop(0, share // sub, head_rows, jnp.zeros((1, 1), jnp.float32))
    ff_load.wait()

    def ff_rows(r, acc):
        value = ff_grad[pl.ds(pl.multiple_of(r * sub, sub), sub), :].astype(jnp.float32)
        return acc + squares(value)

    local = lax.fori_loop(0, share // sub, ff_rows, local)
    for k in range(1, m):
        gains_to(k, d).wait_send()
        gains_to(k, lax.rem(d + m - k, m)).wait_recv()
    gains = summed(got_gains, m)
    own = squares(gains)
    local = local + jnp.where(z == 0, own, jnp.zeros_like(own))
    line[0] = jnp.broadcast_to(local, (8, 128))
    for k in range(1, n):
        along_line(k, z).start()
    got_line[z] = line[0]
    for k in range(1, n):
        along_line(k, z).wait_send()
        along_line(k, lax.rem(z + n - k, n)).wait_recv()
    line[1] = summed(got_line, n)
    for k in range(1, m):
        over_plane(k, d).start()
    got_plane[d] = line[1]
    for k in range(1, m):
        over_plane(k, d).wait_send()
        over_plane(k, lax.rem(d + m - k, m)).wait_recv()
    norm = jnp.sqrt(summed(got_plane, m))
    norm_ref[...] = norm
    factor = jnp.minimum(1.0, clip_limit / (norm[:1, :1] + 1e-06))
    one, two = correct_ref[0], correct_ref[1]

    def update(which, where, gradient):
        rate, decay = rates[which]
        p, a, b = (held[3 * which + k] for k in range(3))
        gradient = gradient * factor
        first = beta_first * a[where] + (1.0 - beta_first) * gradient
        second = beta_second * b[where] + (1.0 - beta_second) * gradient * gradient
        a[where] = first
        b[where] = second
        change = first / one / (jnp.sqrt(second / two) + adam_eps)
        old = p[where]
        p[where] = old - rate * (change + decay * old)

    def load(which):
        for k in range(3):
            loads[3 * which + k].wait()

    def save(which):
        for k in range(3):
            saves[3 * which + k].start()

    def by_rows(which, body):
        load(which)
        lax.fori_loop(0, share // sub, lambda r, c: (body(pl.ds(pl.multiple_of(r * sub, sub), sub)), c)[1], 0)
        save(which)

    def gateup_rows(where):
        for t in (0, 1):
            update(4, (t, where, slice(None)), ff_grad[where, t * ff:(t + 1) * ff].astype(jnp.float32))

    by_rows(4, gateup_rows)
    load(5)

    def down_tile(t, carry):
        at = pl.ds(pl.multiple_of(t * 128, 128), 128)
        source = pl.ds(pl.multiple_of(2 * ff + t * 128, 128), 128)
        update(5, (at, slice(None)), ff_grad[:, source].astype(jnp.float32).T)
        return carry

    lax.fori_loop(0, ff // 128, down_tile, 0)
    save(5)
    by_rows(1, lambda where: update(1, (where, slice(None)), head_ref[where, :q_width]))
    load(3)

    def out_tile(t, carry):
        at = pl.ds(pl.multiple_of(t * 128, 128), 128)
        source = pl.ds(pl.multiple_of(q_width + 2 * kv_width + t * 128, 128), 128)
        update(3, (at, slice(None)), head_ref[:, source].T)
        return carry

    lax.fori_loop(0, outs[9].shape[0] // 128, out_tile, 0)
    save(3)

    def keyval_rows(where):
        both = head_ref[where, q_width:q_width + 2 * kv_width]
        for t in (0, 1):
            update(2, (t, where, slice(None)), both[:, t * kv_width:(t + 1) * kv_width])

    by_rows(2, keyval_rows)
    load(0)
    update(0, (slice(None), slice(None)), gains)
    save(0)
    for copy in saves:
        copy.wait()


def finish_step(gains, correct, ff_grad, head_grad, params, rates, kv_width, n, m, cid):
    share = gains.shape[1] // m
    parts = gains.reshape(2, m, share).transpose(1, 0, 2)
    vmem = pl.BlockSpec(memory_space=pltpu.VMEM)
    hbm = pl.BlockSpec(memory_space=pl.ANY)
    dma = pltpu.SemaphoreType.DMA
    shapes = [jax.ShapeDtypeStruct(p.shape, jnp.float32) for p in params]
    size = sum(p.size for p in params)
    norm, *outs = pl.pallas_call(
        functools.partial(tail_kernel, n, m, rates, kv_width),
        out_shape=(jax.ShapeDtypeStruct((8, 128), jnp.float32), *shapes),
        in_specs=[vmem, pl.BlockSpec(memory_space=pltpu.SMEM), hbm, vmem] + [hbm] * len(params),
        out_specs=(vmem,) + (hbm,) * len(params),
        scratch_shapes=[
            pltpu.VMEM((2, 8, 128), jnp.float32),
            pltpu.VMEM((m, 2, share), jnp.float32),
            pltpu.VMEM((n, 8, 128), jnp.float32),
            pltpu.VMEM((m, 8, 128), jnp.float32),
            pltpu.VMEM(ff_grad.shape, ff_grad.dtype),
            pltpu.VMEM((8, 128), jnp.float32),
        ] + [pltpu.VMEM(p.shape, jnp.float32) for p in params] + [
            dma((m,)), dma((m,)), dma((n,)), dma((n,)), dma((m,)), dma((m,)), dma,
            dma((len(params),)), dma((len(params),)),
        ],
        compiler_params=pltpu.CompilerParams(collective_id=cid, has_side_effects=True, vmem_limit_bytes=60 << 20),
        cost_estimate=pl.CostEstimate(flops=20 * size, bytes_accessed=8 * size, transcendentals=size),
    )(parts, correct, ff_grad, head_grad, *params)
    return norm, outs


norm_eps = 1e-05
beta_first = 0.9
beta_second = 0.95
adam_eps = 1e-08
weight_decay = 0.1
weight_rate = 0.02
out_rate = 0.1
gain_rate = 0.2
clip_limit = 1.0


def positions(segment):
    length = segment.shape[0]
    indices = jnp.arange(length, dtype=jnp.int32)
    earlier = jnp.concatenate([segment[:1] - 1, segment[:-1]])
    begins = jnp.where(segment != earlier, indices, jnp.zeros_like(indices))
    return indices - lax.cummax(begins, axis=0)


def paired_tables(places):
    frequency = jnp.power(10000.0, -jnp.arange(HD // 2, dtype=jnp.float32) * (2.0 / HD))
    angles = places.astype(jnp.float32)[:, None] * frequency[None, :]
    cosines, sines = jnp.cos(angles), jnp.sin(angles)
    return (
        jnp.concatenate([cosines] * 4, axis=-1),
        jnp.concatenate([-sines, sines, -sines, sines], axis=-1),
    )


def on_device(
    n,
    m,
    tokens,
    cotangent,
    segment_ids,
    step_count,
    norm_gains,
    gains_first,
    gains_second,
    w_query,
    query_first,
    query_second,
    w_keyval,
    keyval_first,
    keyval_second,
    w_out,
    out_first,
    out_second,
    w_gateup,
    gateup_first,
    gateup_second,
    w_down,
    down_first,
    down_second,
):
    low = jnp.bfloat16
    width = w_query.shape[1]
    kv_width = w_keyval.shape[2]
    gain_rows = lax.all_gather(norm_gains.astype(low), "dp", axis=1, tiled=True)
    qkv_shard = jnp.concatenate([w_query, w_keyval[0], w_keyval[1]], axis=1).astype(low)
    qkv_weight = lax.all_gather(qkv_shard, "dp", axis=0, tiled=True)
    out_weight = lax.all_gather(w_out.astype(low), "dp", axis=1, tiled=True)
    gateup_weight = lax.all_gather(w_gateup.astype(low), "dp", axis=1, tiled=True)
    down_weight = lax.all_gather(w_down.astype(low), "dp", axis=1, tiled=True)
    gain_values = gain_rows.astype(jnp.float32)
    length = tokens.shape[0]
    size = min(256, length)
    segment = segment_ids[0]
    places = positions(segment)
    cosines, sines = paired_tables(places)
    first = (jnp.arange(length, dtype=jnp.int32) - places)[::size] // size
    seg_col, seg_row = segment[:, None], segment[None, :]

    values_in = tokens.astype(jnp.float32)
    inverse_one = lax.rsqrt(jnp.mean(values_in * values_in, axis=-1, keepdims=True) + norm_eps)
    unit_one = values_in * inverse_one
    normed_one = (unit_one * gain_values[0]).astype(low)
    raw = jnp.dot(normed_one, qkv_weight, preferred_element_type=jnp.float32)
    mixture, q, k, v, lse = attention_forward(raw, cosines, sines, seg_col, seg_row, first, size)
    branch_part = jnp.dot(mixture, out_weight, preferred_element_type=jnp.float32).astype(low)
    (branch,) = line_reduce((branch_part,), n, 16, 1)
    feed_part, grad_middle, grad_branch, gain_grad_two, grad_ff_weight = feed_forward(
        branch, gain_values[1:], tokens, cotangent, gateup_weight, down_weight, n, 2
    )
    ff_reduced = lax.psum_scatter(grad_ff_weight, "dp", scatter_dimension=0, tiled=True)
    layer_out, input_grad, gain_grad_one, head_reduced = attention_back(
        feed_part, grad_branch, gain_values[:1], q, k, v, mixture, lse, cosines, sines, seg_col, seg_row,
        out_weight, tokens, qkv_weight, branch, grad_middle, n, m, 3, size
    )
    gain_grads = jnp.concatenate([gain_grad_one, gain_grad_two])
    step_float = step_count[0].astype(jnp.float32)
    correct = jnp.stack([1.0 - jnp.power(beta_first, step_float), 1.0 - jnp.power(beta_second, step_float)])
    params = (
        (norm_gains, gains_first, gains_second),
        (w_query, query_first, query_second),
        (w_keyval, keyval_first, keyval_second),
        (w_out, out_first, out_second),
        (w_gateup, gateup_first, gateup_second),
        (w_down, down_first, down_second),
    )
    rates = (
        (gain_rate, 0.0),
        (weight_rate, weight_decay),
        (weight_rate, weight_decay),
        (out_rate, weight_decay),
        (weight_rate, weight_decay),
        (weight_rate, weight_decay),
    )
    norm, updated = finish_step(
        gain_grads, correct, ff_reduced, head_reduced, [a for group in params for a in group], rates, kv_width, n, m, 4
    )
    results = []
    for k in range(len(params)):
        weight, first_state, second_state = updated[3 * k : 3 * k + 3]
        results += [first_state, second_state, weight]
    return (layer_out, input_grad, norm[0, :1], *results)


def solution(mesh):
    rows = P("dp", None)
    gains = P(None, "dp")
    query = P("dp", "tensor")
    stacked = P(None, "dp", "tensor")
    turned = P("tensor", "dp")
    states = (gains,) * 3 + (query,) * 3 + (stacked,) * 3 + (turned,) * 3 + (stacked,) * 3 + (turned,) * 3
    return jax.shard_map(
        functools.partial(on_device, mesh.shape["tensor"], mesh.shape["dp"]),
        mesh=mesh,
        in_specs=(rows, rows, rows, P()) + states,
        out_specs=(rows, rows, P()) + states,
        check_vma=False,
    )
```

```python
import functools

import jax
import jax.numpy as jnp
from jax import lax
from jax.experimental import pallas as pl
from jax.experimental.pallas import tpu as pltpu
from jax.sharding import PartitionSpec as P

HD = 64
MESH = pl.DeviceIdType.MESH


masked_value = -1e9


def dot_t(left, right):
    return lax.dot_general(left, right, (((1,), (1,)), ((), ())), preferred_element_type=jnp.float32)


def dot_n(left, right):
    return lax.dot_general(left, right, (((1,), (0,)), ((), ())), preferred_element_type=jnp.float32)


def swap_halves(values, first_half):
    return jnp.where(first_half, pltpu.roll(values, 96, 1), pltpu.roll(values, 32, 1))


def lane_tests(rows):
    lane = lax.broadcasted_iota(jnp.int32, (rows, 128), 1)
    return lane < 64, (lane % 64) < 32


def block_bias(seg_col_ref, seg_row_ref, i, j, size):
    keys = seg_col_ref[pl.ds(pl.multiple_of(j * size, size), size), :]
    rows = seg_row_ref[:, pl.ds(pl.multiple_of(i * size, size), size)]
    key_at = j * size + lax.broadcasted_iota(jnp.int32, (size, size), 0)
    row_at = i * size + lax.broadcasted_iota(jnp.int32, (size, size), 1)
    return jnp.where((keys == rows) & (key_at <= row_at), 0.0, masked_value)


def stack_pair(pair, low_lanes):
    zero = jnp.zeros_like(pair)
    return jnp.concatenate([jnp.where(low_lanes, pair, zero), jnp.where(low_lanes, zero, pair)], axis=0)


class Line:
    def __init__(self, n, chunks, rc, lag, part, got, out, sems, order=None):
        self.order = order
        self.n, self.chunks, self.rc, self.lag = n, chunks, rc, lag
        self.part, self.got, self.out = part, got, out
        self.send_a, self.recv_a, self.send_g, self.recv_g = sems
        self.me = lax.axis_index("tensor")
        self.steps = chunks + 2 * lag * (n - 1)

    def rows(self, stream, c):
        begin = (stream * self.chunks + c) * self.rc if self.order is None else self.order(stream, c)
        return pl.ds(pl.multiple_of(begin, self.rc), self.rc)

    def side(self, stream):
        pos = self.me if stream == 0 else self.n - 1 - self.me
        fwd = self.me + 1 if stream == 0 else self.me - 1
        bwd = self.me - 1 if stream == 0 else self.me + 1
        return pos, fwd, bwd

    def toward(self, stream, c, nxt, src):
        return pltpu.make_async_remote_copy(
            src_ref=src, dst_ref=self.got.at[stream, c],
            send_sem=self.send_a.at[stream, c], recv_sem=self.recv_a.at[stream, c],
            device_id={"tensor": nxt}, device_id_type=MESH)

    def back(self, stream, c, nxt):
        where = self.rows(stream, c)
        return pltpu.make_async_remote_copy(
            src_ref=self.out.at[where], dst_ref=self.out.at[where],
            send_sem=self.send_g.at[stream, c], recv_sem=self.recv_g.at[stream, c],
            device_id={"tensor": nxt}, device_id_type=MESH)

    def step(self, s):
        n, lag = self.n, self.lag
        for stream in (0, 1):
            pos, fwd, bwd = self.side(stream)
            c = s - lag * pos

            @pl.when((c >= 0) & (c < self.chunks))
            def _():
                where = self.rows(stream, c)
                slot = self.got.at[stream, c]

                def summed():
                    self.toward(stream, c, fwd, slot).wait_recv()
                    return (
                        self.part[where, :].astype(jnp.float32) + self.got[stream, c].astype(jnp.float32)
                    ).astype(self.out.dtype)

                @pl.when(pos == 0)
                def _():
                    self.toward(stream, c, fwd, self.part.at[where]).start()

                @pl.when((pos > 0) & (pos < n - 1))
                def _():
                    self.got[stream, c] = summed()
                    self.toward(stream, c, fwd, slot).start()

                @pl.when(pos == n - 1)
                def _():
                    self.out[where, :] = summed()
                    self.back(stream, c, bwd).start()
            d = s - lag * (n - 1) - lag * (n - 1 - pos)

            @pl.when((d >= 0) & (d < self.chunks) & (pos < n - 1))
            def _():
                self.back(stream, d, bwd).wait_recv()

                @pl.when(pos > 0)
                def _():
                    self.back(stream, d, bwd).start()

    def drain(self):
        def one(c, carry):
            for stream in (0, 1):
                pos, fwd, bwd = self.side(stream)

                @pl.when(pos < self.n - 1)
                def _():
                    self.toward(stream, c, fwd, self.got.at[stream, c]).wait_send()

                @pl.when(pos > 0)
                def _():
                    self.back(stream, c, bwd).wait_send()
            return carry

        lax.fori_loop(0, self.chunks, one, 0)


def greet(n):
    me = lax.axis_index("tensor")
    barrier = pltpu.get_barrier_semaphore()

    @pl.when(me > 0)
    def _():
        pl.semaphore_signal(barrier, inc=1, device_id={"tensor": me - 1}, device_id_type=MESH)

    @pl.when(me < n - 1)
    def _():
        pl.semaphore_signal(barrier, inc=1, device_id={"tensor": me + 1}, device_id_type=MESH)

    @pl.when((me > 0) & (me < n - 1))
    def _():
        pl.semaphore_wait(barrier, 2)

    @pl.when((me == 0) | (me == n - 1))
    def _():
        pl.semaphore_wait(barrier, 1)


def line_scratch(chunks, rc, width):
    return [pltpu.VMEM((2, chunks, rc, width), jnp.bfloat16)] + [pltpu.SemaphoreType.DMA((2, chunks))] * 4


def line_kernel(n, chunks, lag, count, *refs):
    parts, outs, scratch = refs[:count], refs[count:2 * count], refs[2 * count:]
    rc = parts[0].shape[0] // (2 * chunks)
    lines = [
        Line(n, chunks, rc, lag, parts[k], scratch[5 * k], outs[k], scratch[5 * k + 1:5 * k + 5])
        for k in range(count)
    ]
    greet(n)

    def step(s, carry):
        for k, line in enumerate(lines):
            line.step(s - k * chunks)
        return carry

    lax.fori_loop(0, lines[0].steps + (count - 1) * chunks, step, 0)
    for line in lines:
        line.drain()


def line_reduce(parts, n, chunks, cid, lag=2):
    rows, width = parts[0].shape
    count = len(parts)
    rc = rows // (2 * chunks)
    scratch = []
    for _ in parts:
        scratch += line_scratch(chunks, rc, width)
    vmem = pl.BlockSpec(memory_space=pltpu.VMEM)
    return pl.pallas_call(
        functools.partial(line_kernel, n, chunks, lag, count),
        out_shape=tuple(jax.ShapeDtypeStruct((rows, width), jnp.bfloat16) for _ in parts),
        in_specs=[vmem] * count,
        out_specs=(vmem,) * count,
        scratch_shapes=scratch,
        compiler_params=pltpu.CompilerParams(collective_id=cid, has_side_effects=True, vmem_limit_bytes=40 << 20),
        cost_estimate=pl.CostEstimate(flops=rows * width * 2 * count, bytes_accessed=rows * width * 120 * count,
                                      transcendentals=0),
    )(*parts)


def dot_rows(left, right):
    return lax.dot_general(left, right, (((0,), (0,)), ((), ())), preferred_element_type=jnp.float32)


def ff_kernel(n, chunks, lag, eps, branch, gain, x, cot_hbm, gu_hbm, down_hbm,
              feed_hbm, middle_hbm, low_hbm, gain_out, grads_hbm,
              got, sa, ra, sg, rg, two_sum, two_part, gu_w, down_w, cot, normed, hidden, gg, feed,
              middle_stage, low_stage, unit_stage, w_sem, cot_sem, feed_sem, stage_sem, grad_sem):
    rows, width = branch.shape
    ff = down_w.shape[0]
    rc = rows // (2 * chunks)
    per = 4
    half = rows // 2
    hb = per * rc
    block = 2 * hb
    blocks = chunks // per
    line = Line(n, chunks, rc, lag, two_part, got, two_sum, (sa, ra, sg, rg))
    landed = 2 * lag * (n - 1) + per
    tile = 256
    full, rest = ff // tile, ff % tile
    wide = width // tile

    weights = (
        pltpu.make_async_copy(gu_hbm, gu_w, w_sem.at[0]),
        pltpu.make_async_copy(down_hbm, down_w, w_sem.at[1]),
    )
    for copy in weights:
        copy.start()

    def natural(k, b):
        return pl.ds(pl.multiple_of(k * half + b * hb, hb), hb)

    def blocked(k, b):
        return pl.ds(pl.multiple_of(b * block + k * hb, hb), hb)

    def load_cot(b):
        return [pltpu.make_async_copy(cot_hbm.at[natural(k, b)], cot.at[blocked(k, b)], cot_sem.at[b, k])
                for k in (0, 1)]

    def save_feed(b):
        return [pltpu.make_async_copy(feed.at[pl.ds(k * hb, hb)], feed_hbm.at[natural(k, b)], feed_sem.at[k])
                for k in (0, 1)]

    def save_rows(d):
        copies = []
        for k in (0, 1):
            where = line.rows(k, d)
            copies.append(pltpu.make_async_copy(middle_stage.at[k], middle_hbm.at[where], stage_sem.at[0, k]))
            copies.append(pltpu.make_async_copy(low_stage.at[k], low_hbm.at[where], stage_sem.at[1, k]))
        return copies

    def save_units(w):
        return [pltpu.make_async_copy(unit_stage, grads_hbm.at[pl.ds(pl.multiple_of(w * tile, tile), tile)], grad_sem.at[0])]

    def start(copies):
        for copy in copies:
            copy.start()

    def wait(copies):
        for copy in copies:
            copy.wait()

    for b in range(blocks):
        start(load_cot(b))
    gain_out[...] = jnp.zeros_like(gain_out)
    greet(n)

    def unit_rows(where):
        middle = x[where, :].astype(jnp.float32) + branch[where, :].astype(jnp.float32)
        inverse = lax.rsqrt(jnp.mean(middle * middle, axis=-1, keepdims=True) + eps)
        return middle * inverse, inverse

    def normalize(b):
        def some(r, carry):
            for k in (0, 1):
                where = pl.ds(pl.multiple_of(k * half + b * hb + r * rc, rc), rc)
                at = pl.ds(pl.multiple_of(b * block + k * hb + r * rc, rc), rc)
                normed[at, :] = (unit_rows(where)[0] * gain[...]).astype(jnp.bfloat16)
            return carry

        lax.fori_loop(0, per, some, 0)

    def step(s, carry):
        line.step(s - per)
        b = s // per
        phase = s - b * per
        live = s < chunks
        mine = pl.ds(pl.multiple_of(b * block, block), block)

        def units(at, count):
            columns = pl.ds(at, count)
            gate = dot_n(normed[mine, :], gu_w[0, :, columns])
            up = dot_n(normed[mine, :], gu_w[1, :, columns])
            grad_hidden = dot_t(cot[mine, :], down_w[columns, :])
            sg_gate = 1.0 / (1.0 + jnp.exp(-gate))
            silu = gate * sg_gate
            hidden[mine, columns] = (silu * up).astype(jnp.bfloat16)
            gg[0, mine, columns] = (grad_hidden * up * sg_gate * (1.0 + gate * (1.0 - sg_gate))).astype(jnp.bfloat16)
            gg[1, mine, columns] = (grad_hidden * silu).astype(jnp.bfloat16)

        def unit_tile(t, c):
            units(pl.multiple_of(t * tile, tile), tile)
            return c

        @pl.when(live & (phase == 0))
        def _():
            normalize(b)

            @pl.when(b == 0)
            def _():
                wait(weights)
            wait(load_cot(b))

        @pl.when(live & (phase < 2))
        def _():
            lax.fori_loop(phase * 2, jnp.where(phase == 0, 2, full), unit_tile, 0)

        @pl.when(live & (phase == 2))
        def _():
            if rest:
                units(full * tile, rest)

            @pl.when(b > 0)
            def _():
                wait(save_feed(b - 1))

            def feed_tile(t, c):
                columns = pl.ds(pl.multiple_of(t * tile, tile), tile)
                feed[:, columns] = dot_n(hidden[mine, :], down_w[:, columns]).astype(jnp.bfloat16)
                return c

            lax.fori_loop(0, wide, feed_tile, 0)
            start(save_feed(b))

        @pl.when(live & (phase == 3))
        def _():
            def two_tile(t, c):
                at = pl.ds(pl.multiple_of(t * tile, tile), tile)
                value = (dot_t(gg[0, mine, :], gu_w[0, at, :]) + dot_t(gg[1, mine, :], gu_w[1, at, :])).astype(jnp.bfloat16)
                for k in (0, 1):
                    two_part[natural(k, b), at] = value[k * hb:(k + 1) * hb]
                return c

            lax.fori_loop(0, wide, two_tile, 0)

        d = s - landed

        @pl.when(d >= 0)
        def _():
            @pl.when(d > 0)
            def _():
                wait(save_rows(d - 1))
            for k in (0, 1):
                where = line.rows(k, d)
                at = pl.ds(pl.multiple_of((d // per) * block + k * hb + (d - (d // per) * per) * rc, rc), rc)
                unit, inverse = unit_rows(where)
                grad = two_sum[where, :].astype(jnp.float32)
                scaled = grad * gain[...]
                inner = jnp.mean(scaled * unit, axis=-1, keepdims=True)
                value = cot[at, :].astype(jnp.float32) + inverse * (scaled - unit * inner)
                middle_stage[k] = value
                low_stage[k] = value.astype(jnp.bfloat16)
                gain_out[...] += jnp.sum(grad * unit, axis=0, keepdims=True)
            start(save_rows(d))

        w = s - chunks

        @pl.when((w >= 0) & (w < wide))
        def _():
            @pl.when(w > 0)
            def _():
                wait(save_units(w - 1))
            columns = pl.ds(pl.multiple_of(w * tile, tile), tile)
            left = normed[:, columns]
            for t in (0, 1):
                unit_stage[:, t * ff:(t + 1) * ff] = dot_rows(left, gg[t]).astype(jnp.bfloat16)
            unit_stage[:, 2 * ff:] = dot_rows(cot[:, columns], hidden[...]).astype(jnp.bfloat16)
            start(save_units(w))
        return carry

    lax.fori_loop(0, per + line.steps, step, 0)
    line.drain()
    wait(save_feed(blocks - 1))
    wait(save_rows(chunks - 1))
    wait(save_units(wide - 1))


def feed_forward(branch, gain, x, cot, gateup_w, down_w, n, cid, chunks=16, lag=2):
    rows, width = branch.shape
    ff = down_w.shape[0]
    rc = rows // (2 * chunks)
    block = 8 * rc
    blocks = chunks // 4
    low = jnp.bfloat16
    vmem = pl.BlockSpec(memory_space=pltpu.VMEM)
    hbm = pl.BlockSpec(memory_space=pl.ANY)
    dma = pltpu.SemaphoreType.DMA
    shape = jax.ShapeDtypeStruct
    return pl.pallas_call(
        functools.partial(ff_kernel, n, chunks, lag, norm_eps),
        out_shape=(
            shape((rows, width), low), shape((rows, width), jnp.float32), shape((rows, width), low),
            shape((1, width), jnp.float32), shape((width, 3 * ff), low),
        ),
        in_specs=[vmem, vmem, vmem, hbm, hbm, hbm],
        out_specs=(hbm, hbm, hbm, vmem, hbm),
        scratch_shapes=line_scratch(chunks, rc, width) + [
            pltpu.VMEM((rows, width), low),
            pltpu.VMEM((rows, width), low),
            pltpu.VMEM((2, width, ff), low),
            pltpu.VMEM((ff, width), low),
            pltpu.VMEM((rows, width), low),
            pltpu.VMEM((rows, width), low),
            pltpu.VMEM((rows, ff), low),
            pltpu.VMEM((2, rows, ff), low),
            pltpu.VMEM((block, width), low),
            pltpu.VMEM((2, rc, width), jnp.float32),
            pltpu.VMEM((2, rc, width), low),
            pltpu.VMEM((256, 3 * ff), low),
            dma((2,)), dma((blocks, 2)), dma((2,)), dma((2, 2)), dma((1,)),
        ],
        compiler_params=pltpu.CompilerParams(collective_id=cid, has_side_effects=True, vmem_limit_bytes=63 << 20),
        cost_estimate=pl.CostEstimate(flops=18 * rows * width * ff, bytes_accessed=rows * width * 150,
                                      transcendentals=rows * ff),
    )(branch, gain, x, cot, gateup_w, down_w)


def head_kernel(n, m, chunks, lag, eps, size, pairs,
                x, gain_part, qkv_shard, out_shard, cos_ref, sin_ref, seg_col_ref, seg_row_ref,
                branch, mix_ref, q_ref, k_ref, v_ref, lse_ref, qkv_w, out_w, gain,
                got, sa, ra, sg, rg, part, normed, raw, bias, scores, v_turned, got_gain,
                send_gain, recv_gain, send_direct, send_forward, recv_w):
    rows, width = x.shape
    q_width = pairs * 128
    z = lax.axis_index("tensor")
    dp = lax.axis_index("dp")
    share = width // m
    chips = m // 2
    chip, core = dp // 2, dp % 2
    rc = rows // (2 * chunks)
    per = size // (2 * rc)
    hb = size // 2
    blocks = rows // size
    tile = 256
    wide = width // tile
    low_lanes, first_half = lane_tests(size)
    low_rows = lax.broadcasted_iota(jnp.int32, (128, size), 0) < 64
    shards, wholes = (qkv_shard, out_shard), (qkv_w, out_w)

    def ascending(stream, c):
        b = c // per
        return b * size + stream * hb + (c - b * per) * rc

    line = Line(n, chunks, rc, lag, part, got, branch, (sa, ra, sg, rg), ascending)

    def shard_rows(s):
        return pl.ds(pl.multiple_of(s * share, share), share)

    def direct(kind, k):
        peer = 2 * lax.rem(chip + k, chips) + core
        return pltpu.make_async_remote_copy(
            src_ref=shards[kind], dst_ref=wholes[kind].at[shard_rows(dp)], send_sem=send_direct.at[kind, k],
            recv_sem=recv_w.at[kind, dp], device_id={"dp": peer}, device_id_type=MESH)

    def forward(kind, c, side):
        shard = 2 * c + side
        where = shard_rows(shard)
        return pltpu.make_async_remote_copy(
            src_ref=wholes[kind].at[where], dst_ref=wholes[kind].at[where], send_sem=send_forward.at[kind, c],
            recv_sem=recv_w.at[kind, shard], device_id={"dp": 2 * chip + 1 - core}, device_id_type=MESH)

    def send_gains(k, sender):
        return pltpu.make_async_remote_copy(
            src_ref=gain_part, dst_ref=got_gain.at[sender], send_sem=send_gain.at[k], recv_sem=recv_gain.at[sender],
            device_id={"dp": lax.rem(dp + k, m)}, device_id_type=MESH)

    barrier = pltpu.get_barrier_semaphore()

    @pl.when(z > 0)
    def _():
        pl.semaphore_signal(barrier, inc=1, device_id={"tensor": z - 1}, device_id_type=MESH)

    @pl.when(z < n - 1)
    def _():
        pl.semaphore_signal(barrier, inc=1, device_id={"tensor": z + 1}, device_id_type=MESH)

    for k in range(1, m):
        pl.semaphore_signal(barrier, inc=1, device_id={"dp": lax.rem(dp + k, m)}, device_id_type=MESH)

    for kind in (0, 1):
        wholes[kind][shard_rows(dp), :] = shards[kind][...]
    got_gain[dp] = gain_part[...]

    @pl.when((z > 0) & (z < n - 1))
    def _():
        pl.semaphore_wait(barrier, m + 1)

    @pl.when((z == 0) | (z == n - 1))
    def _():
        pl.semaphore_wait(barrier, m)

    for k in range(1, m):
        send_gains(k, dp).start()
    for kind in (0, 1):
        for k in range(1, chips):
            direct(kind, k).start()
        forward(kind, chip, core).start()
    for k in range(1, m):
        send_gains(k, lax.rem(dp + m - k, m)).wait_recv()
    whole = got_gain[0]
    for k in range(1, m):
        whole = whole + got_gain[k]
    gain[...] = whole.astype(jnp.bfloat16).astype(jnp.float32)

    def norm_rows(r, carry):
        where = pl.ds(pl.multiple_of(r * rc, rc), rc)
        values = x[where, :].astype(jnp.float32)
        inverse = lax.rsqrt(jnp.mean(values * values, axis=-1, keepdims=True) + eps)
        normed[where, :] = (values * inverse * gain[0:1, :]).astype(jnp.bfloat16)
        return carry

    lax.fori_loop(0, rows // rc, norm_rows, 0)

    def gather(kind):
        for k in range(1, chips):
            c = lax.rem(chip + chips - k, chips)
            forward(kind, c, core).wait_recv()
            forward(kind, c, core).start()
        for c in range(chips):
            forward(kind, c, 1 - core).wait_recv()

    gather(0)

    def prepare(i, carry):
        where = pl.ds(pl.multiple_of(i * size, size), size)
        raw[...] = dot_n(normed[where, :], qkv_w[...])
        cosines, sines = cos_ref[where, :], sin_ref[where, :]
        for hp in range(pairs):
            values = raw[:, hp * 128:(hp + 1) * 128]
            turned = values * cosines + swap_halves(values, first_half) * sines
            q_ref[where, hp * 128:(hp + 1) * 128] = (
                turned.astype(jnp.bfloat16).astype(jnp.float32) * 0.125).astype(jnp.bfloat16)
        both = raw[:, q_width:q_width + 128]
        other = pltpu.roll(both, 64, 1)
        keys = jnp.where(low_lanes, both, other)
        k_ref[where, :] = (keys * cosines + swap_halves(keys, first_half) * sines).astype(jnp.bfloat16)
        values = jnp.where(low_lanes, other, both)
        v_ref[where, :] = values.astype(jnp.bfloat16)
        v_turned[i] = values.T.astype(jnp.bfloat16)
        return carry

    lax.fori_loop(0, blocks, prepare, 0)
    gather(1)

    def attend(i, hp):
        where = pl.ds(pl.multiple_of(i * size, size), size)
        columns = pl.ds(pl.multiple_of(hp * 128, 128), 128)
        stacked = stack_pair(q_ref[where, columns], low_lanes)

        def score(j, top):
            keys = k_ref[pl.ds(pl.multiple_of(j * size, size), size), :]
            b = bias[j]
            s = dot_t(keys, stacked) + jnp.concatenate([b, b], axis=1)
            scores[j] = s
            return jnp.maximum(top, jnp.max(s, axis=0, keepdims=True))

        top = lax.fori_loop(0, i + 1, score, jnp.full((1, 2 * size), -jnp.inf, jnp.float32))

        def mix(j, c):
            total, acc = c
            p = jnp.exp(scores[j] - top)
            total = total + jnp.sum(p, axis=0, keepdims=True)
            return total, acc + dot_n(v_turned[j], p.astype(jnp.bfloat16))

        total, acc = lax.fori_loop(0, i + 1, mix, (
            jnp.zeros((1, 2 * size), jnp.float32), jnp.zeros((128, 2 * size), jnp.float32)))
        lse_ref[i, hp] = top + jnp.log(total)
        acc = acc / total
        acc = jnp.where(low_rows, acc[:, :size], acc[:, size:])
        mix_ref[where, columns] = acc.T.astype(jnp.bfloat16)

    def step(s, carry):
        line.step(s - per)
        i = s // per
        hp = s - i * per
        live = s < blocks * per

        @pl.when(live & (hp == 0))
        def _():
            def fill(j, c):
                bias[j] = block_bias(seg_col_ref, seg_row_ref, i, j, size)
                return c

            lax.fori_loop(0, i + 1, fill, 0)

        @pl.when(live)
        def _():
            def each(h, c):
                attend(i, h)
                return c

            lax.fori_loop(hp * pairs // per, (hp + 1) * pairs // per, each, 0)

        @pl.when(live & (hp == per - 1))
        def _():
            where = pl.ds(pl.multiple_of(i * size, size), size)

            def part_tile(t, c):
                at = pl.ds(pl.multiple_of(t * tile, tile), tile)
                part[where, at] = dot_t(mix_ref[where, :], out_w[at, :]).astype(jnp.bfloat16)
                return c

            lax.fori_loop(0, wide, part_tile, 0)
        return carry

    lax.fori_loop(0, per + line.steps, step, 0)
    line.drain()
    for k in range(1, m):
        send_gains(k, dp).wait_send()
    for kind in (0, 1):
        for k in range(1, chips):
            direct(kind, k).wait_send()
        for c in range(chips):
            forward(kind, c, core).wait_send()


def attention_head(x, gain_part, qkv_shard, out_shard, cosines, sines, seg_col, seg_row, n, m, cid, size,
                   chunks=16, lag=2):
    rows, width = x.shape
    q_width = out_shard.shape[1]
    pairs = q_width // 128
    rc = rows // (2 * chunks)
    blocks = rows // size
    chips = m // 2
    low = jnp.bfloat16
    vmem = pl.BlockSpec(memory_space=pltpu.VMEM)
    dma = pltpu.SemaphoreType.DMA
    shape = jax.ShapeDtypeStruct
    return pl.pallas_call(
        functools.partial(head_kernel, n, m, chunks, lag, norm_eps, size, pairs),
        out_shape=(
            shape((rows, width), low), shape((rows, q_width), low), shape((rows, q_width), low),
            shape((rows, 128), low), shape((rows, 128), low), shape((blocks, pairs, 1, 2 * size), jnp.float32),
            shape((width, q_width + 128), low), shape((width, q_width), low), shape((2, width), jnp.float32),
        ),
        in_specs=[vmem] * 8,
        out_specs=(vmem,) * 9,
        scratch_shapes=line_scratch(chunks, rc, width) + [
            pltpu.VMEM((rows, width), low),
            pltpu.VMEM((rows, width), low),
            pltpu.VMEM((size, q_width + 128), jnp.float32),
            pltpu.VMEM((blocks, size, size), jnp.float32),
            pltpu.VMEM((blocks, size, 2 * size), jnp.float32),
            pltpu.VMEM((blocks, 128, size), low),
            pltpu.VMEM((m, 2, width), jnp.float32),
            dma((m,)), dma((m,)), dma((2, chips)), dma((2, chips)), dma((2, m)),
        ],
        compiler_params=pltpu.CompilerParams(collective_id=cid, has_side_effects=True, vmem_limit_bytes=56 << 20),
        cost_estimate=pl.CostEstimate(flops=20 * rows * width * q_width, bytes_accessed=rows * width * 170,
                                      transcendentals=rows * rows * pairs),
    )(x, gain_part, qkv_shard, out_shard, cosines, sines, seg_col, seg_row)


def back_kernel(n, m, chunks, lag, eps, size, pairs,
                feed_part, grad_low, gain, q_ref, k_ref, v_ref, mix_ref, lse_ref, cos_ref, sin_ref,
                seg_col_ref, seg_row_ref, out_w, x_hbm, qkv_hbm, branch_hbm, middle_hbm,
                layer_hbm, input_hbm, gain_out, reduced,
                got2, sa2, ra2, sg2, rg2, got4, sa4, ra4, sg4, rg4, feed_sum, part, grad_sum,
                x, qkv_w, normed, grad_mix, bias, k_turned, grad_k, grad_v, grad_qkv, send, recv,
                branch_stage, layer_stage, middle_stage, input_stage,
                w_sem, branch_sem, middle_sem, layer_sem, input_sem, send_sem, recv_sem):
    rows, width = feed_part.shape
    q_width = pairs * 128
    z = lax.axis_index("tensor")
    dp = lax.axis_index("dp")
    rc = rows // (2 * chunks)
    per = size // (2 * rc)
    hb = size // 2
    blocks = rows // size
    tile = 256
    wide = width // tile
    share = width // m
    owners = tile // share
    lead = 2 * lag * (n - 1)
    low_lanes, first_half = lane_tests(size)
    low_rows = lax.broadcasted_iota(jnp.int32, (128, size), 0) < 64

    def descending(stream, c):
        b = c // per
        return (blocks - 1 - b) * size + stream * hb + (c - b * per) * rc

    two = Line(n, chunks, rc, lag, feed_part, got2, feed_sum, (sa2, ra2, sg2, rg2))
    four = Line(n, chunks, rc, lag, part, got4, grad_sum, (sa4, ra4, sg4, rg4), descending)
    loads = (
        pltpu.make_async_copy(x_hbm, x, w_sem.at[0]),
        pltpu.make_async_copy(qkv_hbm, qkv_w, w_sem.at[1]),
    )
    for copy in loads:
        copy.start()

    def start(copies):
        for copy in copies:
            copy.start()

    def wait(copies):
        for copy in copies:
            copy.wait()

    def load_branch(d, slot):
        return [pltpu.make_async_copy(branch_hbm.at[two.rows(k, d)], branch_stage.at[slot, k], branch_sem.at[slot, k])
                for k in (0, 1)]

    def load_middle(d, slot):
        return [pltpu.make_async_copy(middle_hbm.at[four.rows(k, d)], middle_stage.at[slot, k], middle_sem.at[slot, k])
                for k in (0, 1)]

    def save_layer(d):
        return [pltpu.make_async_copy(layer_stage.at[k], layer_hbm.at[two.rows(k, d)], layer_sem.at[k]) for k in (0, 1)]

    def save_input(d):
        return [pltpu.make_async_copy(input_stage.at[k], input_hbm.at[four.rows(k, d)], input_sem.at[k]) for k in (0, 1)]

    def to_owner(w, o):
        owner = w * owners + o
        return pltpu.make_async_remote_copy(
            src_ref=send.at[w, pl.ds(o * share, share)], dst_ref=recv.at[dp], send_sem=send_sem.at[owner],
            recv_sem=recv_sem.at[dp], device_id={"dp": owner}, device_id_type=MESH)

    gain_out[...] = jnp.zeros_like(gain_out)

    def prepare(i, carry):
        at = pl.ds(pl.multiple_of(i * size, size), size)
        k_turned[i] = k_ref[at, :].astype(jnp.float32).T.astype(jnp.bfloat16)
        grad_k[i] = jnp.zeros((size, 128), jnp.float32)
        grad_v[i] = jnp.zeros((size, 128), jnp.float32)
        return carry

    lax.fori_loop(0, blocks, prepare, 0)

    barrier = pltpu.get_barrier_semaphore()

    @pl.when(z > 0)
    def _():
        pl.semaphore_signal(barrier, inc=1, device_id={"tensor": z - 1}, device_id_type=MESH)

    @pl.when(z < n - 1)
    def _():
        pl.semaphore_signal(barrier, inc=1, device_id={"tensor": z + 1}, device_id_type=MESH)

    for k in range(1, m):
        pl.semaphore_signal(barrier, inc=1, device_id={"dp": lax.rem(dp + k, m)}, device_id_type=MESH)

    @pl.when((z > 0) & (z < n - 1))
    def _():
        pl.semaphore_wait(barrier, m + 1)

    @pl.when((z == 0) | (z == n - 1))
    def _():
        pl.semaphore_wait(barrier, m)

    def unit_rows(where):
        values = x[where, :].astype(jnp.float32)
        inverse = lax.rsqrt(jnp.mean(values * values, axis=-1, keepdims=True) + eps)
        return values * inverse, inverse

    def attend(i, hp):
        at_rows = pl.ds(pl.multiple_of(i * size, size), size)
        columns = pl.ds(pl.multiple_of(hp * 128, 128), 128)
        stacked = stack_pair(q_ref[at_rows, columns], low_lanes)
        grad_pair = grad_mix[:, columns]
        grad_stacked = stack_pair(grad_pair, low_lanes)
        product = (grad_pair.astype(jnp.float32) * mix_ref[at_rows, columns].astype(jnp.float32)).T
        spread = jnp.concatenate([
            jnp.sum(product[:64], axis=0, keepdims=True), jnp.sum(product[64:], axis=0, keepdims=True)], axis=1)
        logsum = lse_ref[i, hp]

        def piece(j, acc):
            at = pl.ds(pl.multiple_of(j * size, size), size)
            b = bias[j]
            s = dot_t(k_ref[at, :], stacked) + jnp.concatenate([b, b], axis=1)
            p = jnp.exp(s - logsum)
            grad_p = dot_t(v_ref[at, :], grad_stacked)
            grad_s = (p * (grad_p - spread)).astype(jnp.bfloat16)
            grad_v[j] += dot_n(p.astype(jnp.bfloat16), grad_stacked)
            grad_k[j] += dot_n(grad_s, stacked)
            return acc + dot_n(k_turned[j], grad_s)

        acc = lax.fori_loop(0, i + 1, piece, jnp.zeros((128, 2 * size), jnp.float32))
        acc = jnp.where(low_rows, acc[:, :size], acc[:, size:]).T * 0.125
        turned = acc * cos_ref[at_rows, :] - swap_halves(acc, first_half) * sin_ref[at_rows, :]
        grad_qkv[at_rows, columns] = turned.astype(jnp.bfloat16)

    def step(s, carry):
        two.step(s)
        four.step(s - per)
        b = s // per
        hp = s - b * per
        i = blocks - 1 - b
        live = s < blocks * per
        at_rows = pl.ds(pl.multiple_of(i * size, size), size)

        @pl.when(s == 0)
        def _():
            wait(loads)

        @pl.when(live & (hp == 0))
        def _():
            grad_mix[...] = dot_n(grad_low[at_rows, :], out_w[...]).astype(jnp.bfloat16)

            def fill(j, c):
                bias[j] = block_bias(seg_col_ref, seg_row_ref, i, j, size)
                return c

            lax.fori_loop(0, i + 1, fill, 0)

        @pl.when(live)
        def _():
            def each(h, c):
                attend(i, h)
                return c

            lax.fori_loop(hp * pairs // per, (hp + 1) * pairs // per, each, 0)

            def some(r, c):
                at = pl.ds(pl.multiple_of(s * 2 * rc + r * rc, rc), rc)
                normed[at, :] = (unit_rows(at)[0] * gain[...]).astype(jnp.bfloat16)
                return c

            lax.fori_loop(0, 2, some, 0)

        @pl.when(live & (hp == per - 1))
        def _():
            cosines, sines = cos_ref[at_rows, :], sin_ref[at_rows, :]
            dk = grad_k[i] + pltpu.roll(grad_k[i], 64, 1)
            dk = dk * cosines - swap_halves(dk, first_half) * sines
            dv = grad_v[i] + pltpu.roll(grad_v[i], 64, 1)
            grad_qkv[at_rows, q_width:] = jnp.where(low_lanes, dk, dv).astype(jnp.bfloat16)

            def part_tile(t, c):
                at = pl.ds(pl.multiple_of(t * tile, tile), tile)
                part[at_rows, at] = dot_t(grad_qkv[at_rows, :], qkv_w[at, :]).astype(jnp.bfloat16)
                return c

            lax.fori_loop(0, wide, part_tile, 0)

        w = s - blocks * per

        @pl.when((w >= 0) & (w < wide))
        def _():
            columns = pl.ds(pl.multiple_of(w * tile, tile), tile)
            send[w, :, :q_width + 128] = dot_rows(normed[:, columns], grad_qkv[...]).astype(jnp.bfloat16)
            send[w, :, q_width + 128:] = dot_rows(grad_low[:, columns], mix_ref[...]).astype(jnp.bfloat16)
            for o in range(owners):
                owner = w * owners + o

                @pl.when(owner != dp)
                def _():
                    to_owner(w, o).start()

                @pl.when(owner == dp)
                def _():
                    recv[dp] = send[w, o * share:(o + 1) * share, :]

        e = s - lead + 1

        @pl.when((e >= 0) & (e < chunks))
        def _():
            start(load_branch(e, e % 2))

        d = s - lead

        @pl.when((d >= 0) & (d < chunks))
        def _():
            wait(load_branch(d, d % 2))

            @pl.when(d > 0)
            def _():
                wait(save_layer(d - 1))
            for k in (0, 1):
                where = two.rows(k, d)
                layer_stage[k] = (
                    x[where, :].astype(jnp.float32) + branch_stage[d % 2, k].astype(jnp.float32)
                    + feed_sum[where, :].astype(jnp.float32)
                ).astype(jnp.bfloat16)
            start(save_layer(d))

        e4 = s - lead - per + 1

        @pl.when((e4 >= 0) & (e4 < chunks))
        def _():
            start(load_middle(e4, e4 % 2))

        d4 = s - lead - per

        @pl.when(d4 >= 0)
        def _():
            wait(load_middle(d4, d4 % 2))

            @pl.when(d4 > 0)
            def _():
                wait(save_input(d4 - 1))
            for k in (0, 1):
                where = four.rows(k, d4)
                unit, inverse = unit_rows(where)
                grad = grad_sum[where, :].astype(jnp.float32)
                scaled = grad * gain[...]
                inner = jnp.mean(scaled * unit, axis=-1, keepdims=True)
                input_stage[k] = middle_stage[d4 % 2, k] + inverse * (scaled - unit * inner)
                gain_out[...] += jnp.sum(grad * unit, axis=0, keepdims=True)
            start(save_input(d4))
        return carry

    lax.fori_loop(0, per + four.steps, step, 0)
    two.drain()
    four.drain()
    wait(save_layer(chunks - 1))
    wait(save_input(chunks - 1))

    def finish(k, carry):
        owner = lax.rem(dp + k, m)
        w = owner // owners

        def copy(peer):
            return pltpu.make_async_remote_copy(
                src_ref=send.at[0, pl.ds(0, share)], dst_ref=recv.at[peer], send_sem=send_sem.at[peer],
                recv_sem=recv_sem.at[peer], device_id={"dp": peer}, device_id_type=MESH)

        copy(owner).wait_send()
        copy(owner).wait_recv()
        return carry

    lax.fori_loop(1, m, finish, 0)
    reduced[...] = recv[0].astype(jnp.float32)

    def add(k, carry):
        reduced[...] += recv[k].astype(jnp.float32)
        return carry

    lax.fori_loop(1, m, add, 0)


def attention_back(feed_part, grad_low, gain, q, k, v, mix, lse, cosines, sines, seg_col, seg_row, out_w,
                   x, qkv_w, branch, grad_middle, n, m, cid, size, chunks=16, lag=2):
    rows, width = feed_part.shape
    q_width = q.shape[1]
    pairs = q_width // 128
    rc = rows // (2 * chunks)
    blocks = rows // size
    share = width // m
    cat = 2 * q_width + 128
    low = jnp.bfloat16
    vmem = pl.BlockSpec(memory_space=pltpu.VMEM)
    hbm = pl.BlockSpec(memory_space=pl.ANY)
    dma = pltpu.SemaphoreType.DMA
    shape = jax.ShapeDtypeStruct
    return pl.pallas_call(
        functools.partial(back_kernel, n, m, chunks, lag, norm_eps, size, pairs),
        out_shape=(
            shape((rows, width), low), shape((rows, width), jnp.float32), shape((1, width), jnp.float32),
            shape((share, cat), jnp.float32),
        ),
        in_specs=[vmem] * 13 + [hbm] * 4,
        out_specs=(hbm, hbm, vmem, vmem),
        scratch_shapes=line_scratch(chunks, rc, width) + line_scratch(chunks, rc, width) + [
            pltpu.VMEM((rows, width), low),
            pltpu.VMEM((rows, width), low),
            pltpu.VMEM((rows, width), low),
            pltpu.VMEM((rows, width), low),
            pltpu.VMEM((width, q_width + 128), low),
            pltpu.VMEM((rows, width), low),
            pltpu.VMEM((size, q_width), low),
            pltpu.VMEM((blocks, size, size), jnp.float32),
            pltpu.VMEM((blocks, 128, size), low),
            pltpu.VMEM((blocks, size, 128), jnp.float32),
            pltpu.VMEM((blocks, size, 128), jnp.float32),
            pltpu.VMEM((rows, q_width + 128), low),
            pltpu.VMEM((width // 256, 256, cat), low),
            pltpu.VMEM((m, share, cat), low),
            pltpu.VMEM((2, 2, rc, width), low),
            pltpu.VMEM((2, rc, width), low),
            pltpu.VMEM((2, 2, rc, width), jnp.float32),
            pltpu.VMEM((2, rc, width), jnp.float32),
            dma((2,)), dma((2, 2)), dma((2, 2)), dma((2,)), dma((2,)), dma((m,)), dma((m,)),
        ],
        compiler_params=pltpu.CompilerParams(collective_id=cid, has_side_effects=True, vmem_limit_bytes=63 << 20),
        cost_estimate=pl.CostEstimate(flops=40 * rows * width * q_width, bytes_accessed=rows * width * 260,
                                      transcendentals=rows * rows * pairs),
    )(feed_part, grad_low, gain, q, k, v, mix, lse, cosines, sines, seg_col, seg_row, out_w,
      x, qkv_w, branch, grad_middle)


def norm_kernel(n, m, gains_ref, ff_ref, head_ref, norm_ref, gain_ref, line, got_gains, got_line, got_plane,
                send_gains, recv_gains, send_line, recv_line, send_plane, recv_plane):
    z = lax.axis_index("tensor")
    d = lax.axis_index("dp")
    share = head_ref.shape[0]

    barrier = pltpu.get_barrier_semaphore()
    for k in range(1, n):
        pl.semaphore_signal(barrier, inc=1, device_id={"tensor": lax.rem(z + k, n)}, device_id_type=MESH)
    for k in range(1, m):
        pl.semaphore_signal(barrier, inc=1, device_id={"dp": lax.rem(d + k, m)}, device_id_type=MESH)
    pl.semaphore_wait(barrier, n - 1 + m - 1)

    def gains_to(k, sender):
        peer = lax.rem(d + k, m)
        return pltpu.make_async_remote_copy(
            src_ref=gains_ref.at[peer], dst_ref=got_gains.at[sender], send_sem=send_gains.at[k],
            recv_sem=recv_gains.at[sender], device_id={"dp": peer}, device_id_type=MESH)

    def along_line(k, sender):
        return pltpu.make_async_remote_copy(
            src_ref=line.at[0], dst_ref=got_line.at[sender], send_sem=send_line.at[k], recv_sem=recv_line.at[sender],
            device_id={"tensor": lax.rem(z + k, n)}, device_id_type=MESH)

    def over_plane(k, sender):
        return pltpu.make_async_remote_copy(
            src_ref=line.at[1], dst_ref=got_plane.at[sender], send_sem=send_plane.at[k], recv_sem=recv_plane.at[sender],
            device_id={"dp": lax.rem(d + k, m)}, device_id_type=MESH)

    def summed(ref, number):
        whole = ref[0]
        for k in range(1, number):
            whole = whole + ref[k]
        return whole

    def squares(value):
        return jnp.sum(jnp.sum(value * value, axis=0, keepdims=True), axis=1, keepdims=True)

    for k in range(1, m):
        gains_to(k, d).start()
    got_gains[d] = gains_ref[d]
    sub = 32

    def head_rows(r, acc):
        value = head_ref[pl.ds(pl.multiple_of(r * sub, sub), sub), :]
        return acc + squares(value)

    local = lax.fori_loop(0, share // sub, head_rows, jnp.zeros((1, 1), jnp.float32))

    def ff_rows(r, acc):
        value = ff_ref[pl.ds(pl.multiple_of(r * sub, sub), sub), :].astype(jnp.float32)
        return acc + squares(value)

    local = lax.fori_loop(0, share // sub, ff_rows, local)
    for k in range(1, m):
        gains_to(k, d).wait_send()
        gains_to(k, lax.rem(d + m - k, m)).wait_recv()
    gains = summed(got_gains, m)
    gain_ref[...] = gains
    own = squares(gains)
    local = local + jnp.where(z == 0, own, jnp.zeros_like(own))
    line[0] = jnp.broadcast_to(local, (8, 128))
    for k in range(1, n):
        along_line(k, z).start()
    got_line[z] = line[0]
    for k in range(1, n):
        along_line(k, z).wait_send()
        along_line(k, lax.rem(z + n - k, n)).wait_recv()
    line[1] = summed(got_line, n)
    for k in range(1, m):
        over_plane(k, d).start()
    got_plane[d] = line[1]
    for k in range(1, m):
        over_plane(k, d).wait_send()
        over_plane(k, lax.rem(d + m - k, m)).wait_recv()
    norm = jnp.sqrt(summed(got_plane, m))
    norm_ref[...] = norm


def adam_kernel(rates, kv_width, correct_ref, norm_ref, gain_ref, ff_hbm, head_hbm, layer_hbm, input_hbm, *refs):
    count = len(rates)
    params, refs = refs[:3 * count], refs[3 * count:]
    norm_out, layer_out, input_out, outs, refs = refs[0], refs[1], refs[2], refs[3:3 * count + 3], refs[3 * count + 3:]
    (ff_grad, head_ref), held, (grad_sem, load_sem, save_sem, whole_sem) = refs[:2], refs[2:3 * count + 2], refs[3 * count + 2:]
    share = gain_ref.shape[1]
    q_width = outs[3].shape[1]
    ff = outs[12].shape[2]
    sub = 32

    grads = (
        pltpu.make_async_copy(ff_hbm, ff_grad, grad_sem.at[0]),
        pltpu.make_async_copy(head_hbm, head_ref, grad_sem.at[1]),
    )
    loads = [pltpu.make_async_copy(params[k], held[k], load_sem.at[k]) for k in range(3 * count)]
    saves = [pltpu.make_async_copy(held[k], outs[k], save_sem.at[k]) for k in range(3 * count)]
    quarter = layer_hbm.shape[0] // 4
    moves = []
    for k in range(4):
        at = pl.ds(k * quarter, quarter)
        moves.append(pltpu.make_async_copy(layer_hbm.at[at], layer_out.at[at], whole_sem.at[0, k]))
        moves.append(pltpu.make_async_copy(input_hbm.at[at], input_out.at[at], whole_sem.at[1, k]))
    for copy in grads:
        copy.start()
    for which in (1, 2, 3, 5, 4, 0):
        for k in range(3):
            loads[3 * which + k].start()
    for copy in moves:
        copy.start()
    norm_out[...] = norm_ref[...]
    factor = jnp.minimum(1.0, clip_limit / (norm_ref[:1, :1] + 1e-06))
    one, two = correct_ref[0], correct_ref[1]

    def update(which, where, gradient):
        rate, decay = rates[which]
        p, a, b = (held[3 * which + k] for k in range(3))
        gradient = gradient * factor
        first = beta_first * a[where] + (1.0 - beta_first) * gradient
        second = beta_second * b[where] + (1.0 - beta_second) * gradient * gradient
        a[where] = first
        b[where] = second
        change = first / one / (jnp.sqrt(second / two) + adam_eps)
        old = p[where]
        p[where] = old - rate * (change + decay * old)

    def load(which):
        for k in range(3):
            loads[3 * which + k].wait()

    def save(which):
        for k in range(3):
            saves[3 * which + k].start()

    def by_rows(which, body):
        load(which)
        lax.fori_loop(0, share // sub, lambda r, c: (body(pl.ds(pl.multiple_of(r * sub, sub), sub)), c)[1], 0)
        save(which)

    for copy in grads:
        copy.wait()
    by_rows(1, lambda where: update(1, (where, slice(None)), head_ref[where, :q_width]))
    load(3)

    def out_tile(t, carry):
        at = pl.ds(pl.multiple_of(t * 128, 128), 128)
        source = pl.ds(pl.multiple_of(q_width + 2 * kv_width + t * 128, 128), 128)
        update(3, (at, slice(None)), head_ref[:, source].T)
        return carry

    lax.fori_loop(0, outs[9].shape[0] // 128, out_tile, 0)
    save(3)

    load(2)
    both = head_ref[:, q_width:q_width + 2 * kv_width].T
    for t in (0, 1):
        update(2, (t, slice(None), slice(None)), both[t * kv_width:(t + 1) * kv_width])
    save(2)

    def gateup_rows(where):
        for t in (0, 1):
            update(4, (t, where, slice(None)), ff_grad[where, t * ff:(t + 1) * ff].astype(jnp.float32))

    load(5)

    def down_tile(t, carry):
        at = pl.ds(pl.multiple_of(t * 128, 128), 128)
        source = pl.ds(pl.multiple_of(2 * ff + t * 128, 128), 128)
        update(5, (at, slice(None)), ff_grad[:, source].astype(jnp.float32).T)
        return carry

    lax.fori_loop(0, ff // 128, down_tile, 0)
    save(5)
    by_rows(4, gateup_rows)
    load(0)
    update(0, (slice(None), slice(None)), gain_ref[...])
    save(0)
    for copy in saves + moves:
        copy.wait()


def finish_step(gains, correct, ff_grad, head_grad, layer, grad_in, params, rates, kv_width, n, m, cid):
    share = gains.shape[1] // m
    parts = gains.reshape(2, m, share).transpose(1, 0, 2)
    vmem = pl.BlockSpec(memory_space=pltpu.VMEM)
    hbm = pl.BlockSpec(memory_space=pl.ANY)
    dma = pltpu.SemaphoreType.DMA
    shape = jax.ShapeDtypeStruct
    norm, gain = pl.pallas_call(
        functools.partial(norm_kernel, n, m),
        out_shape=(shape((8, 128), jnp.float32), shape((2, share), jnp.float32)),
        in_specs=[vmem, vmem, vmem],
        out_specs=(vmem, vmem),
        scratch_shapes=[
            pltpu.VMEM((2, 8, 128), jnp.float32),
            pltpu.VMEM((m, 2, share), jnp.float32),
            pltpu.VMEM((n, 8, 128), jnp.float32),
            pltpu.VMEM((m, 8, 128), jnp.float32),
            dma((m,)), dma((m,)), dma((n,)), dma((n,)), dma((m,)), dma((m,)),
        ],
        compiler_params=pltpu.CompilerParams(collective_id=cid, has_side_effects=True),
    )(parts, ff_grad, head_grad)
    size = sum(p.size for p in params)
    norm, layer, grad_in, *outs = pl.pallas_call(
        functools.partial(adam_kernel, rates, kv_width),
        out_shape=(shape((8, 128), jnp.float32), shape(layer.shape, layer.dtype), shape(grad_in.shape, grad_in.dtype))
        + tuple(shape(p.shape, jnp.float32) for p in params),
        in_specs=[pl.BlockSpec(memory_space=pltpu.SMEM), vmem, vmem] + [hbm] * (4 + len(params)),
        out_specs=(vmem,) + (hbm,) * (2 + len(params)),
        scratch_shapes=[pltpu.VMEM(ff_grad.shape, ff_grad.dtype), pltpu.VMEM(head_grad.shape, jnp.float32)]
        + [pltpu.VMEM(p.shape, jnp.float32) for p in params]
        + [dma((2,)), dma((len(params),)), dma((len(params),)), dma((2, 4))],
        compiler_params=pltpu.CompilerParams(vmem_limit_bytes=40 << 20),
        cost_estimate=pl.CostEstimate(flops=20 * size, bytes_accessed=24 * size, transcendentals=size),
    )(correct, norm, gain, ff_grad, head_grad, layer, grad_in, *params)
    return norm, layer, grad_in, outs


norm_eps = 1e-05
beta_first = 0.9
beta_second = 0.95
adam_eps = 1e-08
weight_decay = 0.1
weight_rate = 0.02
out_rate = 0.1
gain_rate = 0.2
clip_limit = 1.0


def positions(segment):
    length = segment.shape[0]
    indices = jnp.arange(length, dtype=jnp.int32)
    earlier = jnp.concatenate([segment[:1] - 1, segment[:-1]])
    begins = jnp.where(segment != earlier, indices, jnp.zeros_like(indices))
    return indices - lax.cummax(begins, axis=0)


def paired_tables(places):
    frequency = jnp.power(10000.0, -jnp.arange(HD // 2, dtype=jnp.float32) * (2.0 / HD))
    angles = places.astype(jnp.float32)[:, None] * frequency[None, :]
    cosines, sines = jnp.cos(angles), jnp.sin(angles)
    return (
        jnp.concatenate([cosines] * 4, axis=-1),
        jnp.concatenate([-sines, sines, -sines, sines], axis=-1),
    )


def on_device(
    n,
    m,
    tokens,
    cotangent,
    segment_ids,
    step_count,
    norm_gains,
    gains_first,
    gains_second,
    w_query,
    query_first,
    query_second,
    w_keyval,
    keyval_first,
    keyval_second,
    w_out,
    out_first,
    out_second,
    w_gateup,
    gateup_first,
    gateup_second,
    w_down,
    down_first,
    down_second,
):
    low = jnp.bfloat16
    width = w_query.shape[1]
    kv_width = w_keyval.shape[2]
    gateup_weight = lax.all_gather(w_gateup.astype(low), "dp", axis=1, tiled=True)
    down_weight = lax.all_gather(w_down.astype(low), "dp", axis=1, tiled=True)
    qkv_shard = jnp.concatenate([w_query, w_keyval[0], w_keyval[1]], axis=1).astype(low)
    out_shard = w_out.T.astype(low)
    share = norm_gains.shape[1]
    gain_part = lax.dynamic_update_slice(
        jnp.zeros((2, tokens.shape[1]), jnp.float32), norm_gains, (0, lax.axis_index("dp") * share)
    )
    length = tokens.shape[0]
    size = min(256, length)
    segment = segment_ids[0]
    places = positions(segment)
    cosines, sines = paired_tables(places)
    seg_col, seg_row = segment[:, None], segment[None, :]

    branch, mixture, q, k, v, lse, qkv_weight, out_weight, gain_values = attention_head(
        tokens, gain_part, qkv_shard, out_shard, cosines, sines, seg_col, seg_row, n, m, 1, size
    )
    feed_part, grad_middle, grad_branch, gain_grad_two, grad_ff_weight = feed_forward(
        branch, gain_values[1:], tokens, cotangent, gateup_weight, down_weight, n, 2
    )
    ff_reduced = lax.psum_scatter(grad_ff_weight, "dp", scatter_dimension=0, tiled=True)
    layer_out, input_grad, gain_grad_one, head_reduced = attention_back(
        feed_part, grad_branch, gain_values[:1], q, k, v, mixture, lse, cosines, sines, seg_col, seg_row,
        out_weight, tokens, qkv_weight, branch, grad_middle, n, m, 3, size
    )
    gain_grads = jnp.concatenate([gain_grad_one, gain_grad_two])
    step_float = step_count[0].astype(jnp.float32)
    correct = jnp.stack([1.0 - jnp.power(beta_first, step_float), 1.0 - jnp.power(beta_second, step_float)])
    params = (
        (norm_gains, gains_first, gains_second),
        (w_query, query_first, query_second),
        tuple(a.swapaxes(1, 2) for a in (w_keyval, keyval_first, keyval_second)),
        (w_out, out_first, out_second),
        (w_gateup, gateup_first, gateup_second),
        (w_down, down_first, down_second),
    )
    rates = (
        (gain_rate, 0.0),
        (weight_rate, weight_decay),
        (weight_rate, weight_decay),
        (out_rate, weight_decay),
        (weight_rate, weight_decay),
        (weight_rate, weight_decay),
    )
    norm, layer_out, input_grad, updated = finish_step(
        gain_grads, correct, ff_reduced, head_reduced, layer_out, input_grad,
        [a for group in params for a in group], rates, kv_width, n, m, 4
    )
    results = []
    for k in range(len(params)):
        weight, first_state, second_state = updated[3 * k : 3 * k + 3]
        group = [first_state, second_state, weight]
        results += [a.swapaxes(1, 2) for a in group] if k == 2 else group
    return (layer_out, input_grad, norm[0, :1], *results)


def solution(mesh):
    rows = P("dp", None)
    gains = P(None, "dp")
    query = P("dp", "tensor")
    stacked = P(None, "dp", "tensor")
    turned = P("tensor", "dp")
    states = (gains,) * 3 + (query,) * 3 + (stacked,) * 3 + (turned,) * 3 + (stacked,) * 3 + (turned,) * 3
    return jax.shard_map(
        functools.partial(on_device, mesh.shape["tensor"], mesh.shape["dp"]),
        mesh=mesh,
        in_specs=(rows, rows, rows, P()) + states,
        out_specs=(rows, rows, P()) + states,
        check_vma=False,
    )
```

```python
import functools

import jax
import jax.numpy as jnp
from jax import lax
from jax.experimental import pallas as pl
from jax.experimental.pallas import tpu as pltpu
from jax.sharding import PartitionSpec as P

HD = 64
MESH = pl.DeviceIdType.MESH


masked_value = -1e9


def dot_t(left, right):
    return lax.dot_general(left, right, (((1,), (1,)), ((), ())), preferred_element_type=jnp.float32)


def dot_n(left, right):
    return lax.dot_general(left, right, (((1,), (0,)), ((), ())), preferred_element_type=jnp.float32)


def swap_halves(values, first_half):
    return jnp.where(first_half, pltpu.roll(values, 96, 1), pltpu.roll(values, 32, 1))


def lane_tests(rows):
    lane = lax.broadcasted_iota(jnp.int32, (rows, 128), 1)
    return lane < 64, (lane % 64) < 32


def block_bias(seg_col_ref, seg_row_ref, i, j, size):
    keys = seg_col_ref[pl.ds(pl.multiple_of(j * size, size), size), :]
    rows = seg_row_ref[:, pl.ds(pl.multiple_of(i * size, size), size)]
    key_at = j * size + lax.broadcasted_iota(jnp.int32, (size, size), 0)
    row_at = i * size + lax.broadcasted_iota(jnp.int32, (size, size), 1)
    return jnp.where((keys == rows) & (key_at <= row_at), 0.0, masked_value)


def stack_pair(pair, low_lanes):
    zero = jnp.zeros_like(pair)
    return jnp.concatenate([jnp.where(low_lanes, pair, zero), jnp.where(low_lanes, zero, pair)], axis=0)


class Line:
    def __init__(self, n, chunks, rc, lag, part, got, out, sems, order=None):
        self.order = order
        self.n, self.chunks, self.rc, self.lag = n, chunks, rc, lag
        self.part, self.got, self.out = part, got, out
        self.send_a, self.recv_a, self.send_g, self.recv_g = sems
        self.me = lax.axis_index("tensor")
        self.steps = chunks + 2 * lag * (n - 1)

    def rows(self, stream, c):
        begin = (stream * self.chunks + c) * self.rc if self.order is None else self.order(stream, c)
        return pl.ds(pl.multiple_of(begin, self.rc), self.rc)

    def side(self, stream):
        pos = self.me if stream == 0 else self.n - 1 - self.me
        fwd = self.me + 1 if stream == 0 else self.me - 1
        bwd = self.me - 1 if stream == 0 else self.me + 1
        return pos, fwd, bwd

    def toward(self, stream, c, nxt, src):
        return pltpu.make_async_remote_copy(
            src_ref=src, dst_ref=self.got.at[stream, c],
            send_sem=self.send_a.at[stream, c], recv_sem=self.recv_a.at[stream, c],
            device_id={"tensor": nxt}, device_id_type=MESH)

    def back(self, stream, c, nxt):
        where = self.rows(stream, c)
        return pltpu.make_async_remote_copy(
            src_ref=self.out.at[where], dst_ref=self.out.at[where],
            send_sem=self.send_g.at[stream, c], recv_sem=self.recv_g.at[stream, c],
            device_id={"tensor": nxt}, device_id_type=MESH)

    def step(self, s):
        n, lag = self.n, self.lag
        for stream in (0, 1):
            pos, fwd, bwd = self.side(stream)
            c = s - lag * pos

            @pl.when((c >= 0) & (c < self.chunks))
            def _():
                where = self.rows(stream, c)
                slot = self.got.at[stream, c]

                def summed():
                    self.toward(stream, c, fwd, slot).wait_recv()
                    return (
                        self.part[where, :].astype(jnp.float32) + self.got[stream, c].astype(jnp.float32)
                    ).astype(self.out.dtype)

                @pl.when(pos == 0)
                def _():
                    self.toward(stream, c, fwd, self.part.at[where]).start()

                @pl.when((pos > 0) & (pos < n - 1))
                def _():
                    self.got[stream, c] = summed()
                    self.toward(stream, c, fwd, slot).start()

                @pl.when(pos == n - 1)
                def _():
                    self.out[where, :] = summed()
                    self.back(stream, c, bwd).start()
            d = s - lag * (n - 1) - lag * (n - 1 - pos)

            @pl.when((d >= 0) & (d < self.chunks) & (pos < n - 1))
            def _():
                self.back(stream, d, bwd).wait_recv()

                @pl.when(pos > 0)
                def _():
                    self.back(stream, d, bwd).start()

    def drain(self):
        def one(c, carry):
            for stream in (0, 1):
                pos, fwd, bwd = self.side(stream)

                @pl.when(pos < self.n - 1)
                def _():
                    self.toward(stream, c, fwd, self.got.at[stream, c]).wait_send()

                @pl.when(pos > 0)
                def _():
                    self.back(stream, c, bwd).wait_send()
            return carry

        lax.fori_loop(0, self.chunks, one, 0)


def greet(n):
    me = lax.axis_index("tensor")
    barrier = pltpu.get_barrier_semaphore()

    @pl.when(me > 0)
    def _():
        pl.semaphore_signal(barrier, inc=1, device_id={"tensor": me - 1}, device_id_type=MESH)

    @pl.when(me < n - 1)
    def _():
        pl.semaphore_signal(barrier, inc=1, device_id={"tensor": me + 1}, device_id_type=MESH)

    @pl.when((me > 0) & (me < n - 1))
    def _():
        pl.semaphore_wait(barrier, 2)

    @pl.when((me == 0) | (me == n - 1))
    def _():
        pl.semaphore_wait(barrier, 1)


def line_scratch(chunks, rc, width):
    return [pltpu.VMEM((2, chunks, rc, width), jnp.bfloat16)] + [pltpu.SemaphoreType.DMA((2, chunks))] * 4


def line_kernel(n, chunks, lag, count, *refs):
    parts, outs, scratch = refs[:count], refs[count:2 * count], refs[2 * count:]
    rc = parts[0].shape[0] // (2 * chunks)
    lines = [
        Line(n, chunks, rc, lag, parts[k], scratch[5 * k], outs[k], scratch[5 * k + 1:5 * k + 5])
        for k in range(count)
    ]
    greet(n)

    def step(s, carry):
        for k, line in enumerate(lines):
            line.step(s - k * chunks)
        return carry

    lax.fori_loop(0, lines[0].steps + (count - 1) * chunks, step, 0)
    for line in lines:
        line.drain()


def line_reduce(parts, n, chunks, cid, lag=2):
    rows, width = parts[0].shape
    count = len(parts)
    rc = rows // (2 * chunks)
    scratch = []
    for _ in parts:
        scratch += line_scratch(chunks, rc, width)
    vmem = pl.BlockSpec(memory_space=pltpu.VMEM)
    return pl.pallas_call(
        functools.partial(line_kernel, n, chunks, lag, count),
        out_shape=tuple(jax.ShapeDtypeStruct((rows, width), jnp.bfloat16) for _ in parts),
        in_specs=[vmem] * count,
        out_specs=(vmem,) * count,
        scratch_shapes=scratch,
        compiler_params=pltpu.CompilerParams(collective_id=cid, has_side_effects=True, vmem_limit_bytes=40 << 20),
        cost_estimate=pl.CostEstimate(flops=rows * width * 2 * count, bytes_accessed=rows * width * 120 * count,
                                      transcendentals=0),
    )(*parts)


def dot_rows(left, right):
    return lax.dot_general(left, right, (((0,), (0,)), ((), ())), preferred_element_type=jnp.float32)


def ff_kernel(n, chunks, lag, eps, branch, gain, x, cot_hbm, gu_hbm, down_hbm,
              feed_hbm, middle_hbm, low_hbm, gain_out, grads_hbm,
              got, sa, ra, sg, rg, two_sum, two_part, gu_w, down_w, cot, normed, hidden, gg, feed,
              middle_stage, low_stage, unit_stage, w_sem, cot_sem, feed_sem, stage_sem, grad_sem):
    rows, width = branch.shape
    ff = down_w.shape[0]
    rc = rows // (2 * chunks)
    per = 8
    offset = per - 1
    half = rows // 2
    hb = per * rc
    block = 2 * hb
    blocks = chunks // per
    line = Line(n, chunks, rc, lag, two_part, got, two_sum, (sa, ra, sg, rg))
    landed = 2 * lag * (n - 1) + offset
    tile = 256
    full, rest = ff // tile, ff % tile
    wide = width // tile

    weights = (
        pltpu.make_async_copy(gu_hbm, gu_w, w_sem.at[0]),
        pltpu.make_async_copy(down_hbm, down_w, w_sem.at[1]),
    )
    for copy in weights:
        copy.start()

    def natural(k, b):
        return pl.ds(pl.multiple_of(k * half + b * hb, hb), hb)

    def blocked(k, b):
        return pl.ds(pl.multiple_of(b * block + k * hb, hb), hb)

    def load_cot(b):
        return [pltpu.make_async_copy(cot_hbm.at[natural(k, b)], cot.at[blocked(k, b)], cot_sem.at[b, k])
                for k in (0, 1)]

    def save_feed(b):
        return [pltpu.make_async_copy(feed.at[pl.ds(k * hb, hb)], feed_hbm.at[natural(k, b)], feed_sem.at[k])
                for k in (0, 1)]

    def save_rows(d):
        copies = []
        for k in (0, 1):
            where = line.rows(k, d)
            copies.append(pltpu.make_async_copy(middle_stage.at[k], middle_hbm.at[where], stage_sem.at[0, k]))
            copies.append(pltpu.make_async_copy(low_stage.at[k], low_hbm.at[where], stage_sem.at[1, k]))
        return copies

    def save_units(w):
        return [pltpu.make_async_copy(unit_stage, grads_hbm.at[pl.ds(pl.multiple_of(w * tile, tile), tile)], grad_sem.at[0])]

    def start(copies):
        for copy in copies:
            copy.start()

    def wait(copies):
        for copy in copies:
            copy.wait()

    for b in range(blocks):
        start(load_cot(b))
    gain_out[...] = jnp.zeros_like(gain_out)
    greet(n)

    def unit_rows(where):
        middle = x[where, :].astype(jnp.float32) + branch[where, :].astype(jnp.float32)
        inverse = lax.rsqrt(jnp.mean(middle * middle, axis=-1, keepdims=True) + eps)
        return middle * inverse, inverse

    def normalize(b):
        def some(r, carry):
            for k in (0, 1):
                where = pl.ds(pl.multiple_of(k * half + b * hb + r * rc, rc), rc)
                at = pl.ds(pl.multiple_of(b * block + k * hb + r * rc, rc), rc)
                normed[at, :] = (unit_rows(where)[0] * gain[...]).astype(jnp.bfloat16)
            return carry

        lax.fori_loop(0, per, some, 0)

    def step(s, carry):
        line.step(s - offset)
        b = s // per
        phase = s - b * per
        live = s < chunks
        mine = pl.ds(pl.multiple_of(b * block, block), block)

        def units(at, count):
            columns = pl.ds(at, count)
            gate = dot_n(normed[mine, :], gu_w[0, :, columns])
            up = dot_n(normed[mine, :], gu_w[1, :, columns])
            grad_hidden = dot_t(cot[mine, :], down_w[columns, :])
            sg_gate = 1.0 / (1.0 + jnp.exp(-gate))
            silu = gate * sg_gate
            hidden[mine, columns] = (silu * up).astype(jnp.bfloat16)
            gg[0, mine, columns] = (grad_hidden * up * sg_gate * (1.0 + gate * (1.0 - sg_gate))).astype(jnp.bfloat16)
            gg[1, mine, columns] = (grad_hidden * silu).astype(jnp.bfloat16)

        def unit_tile(t, c):
            units(pl.multiple_of(t * tile, tile), tile)
            return c

        @pl.when(live & (phase == 0))
        def _():
            normalize(b)

            @pl.when(b == 0)
            def _():
                wait(weights)
            wait(load_cot(b))

        @pl.when(live & (phase < 3))
        def _():
            lax.fori_loop(jnp.maximum(2 * phase - 1, 0), jnp.minimum(2 * phase + 1, full), unit_tile, 0)

        @pl.when(live & (phase == 3))
        def _():
            if rest:
                units(full * tile, rest)

            @pl.when(b > 0)
            def _():
                wait(save_feed(b - 1))

        @pl.when(live & ((phase == 3) | (phase == 4)))
        def _():
            def feed_tile(t, c):
                columns = pl.ds(pl.multiple_of(t * 2 * tile, 2 * tile), 2 * tile)
                feed[:, columns] = dot_n(hidden[mine, :], down_w[:, columns]).astype(jnp.bfloat16)
                return c

            lax.fori_loop((phase - 3) * (wide // 4), (phase - 2) * (wide // 4), feed_tile, 0)

            @pl.when(phase == 4)
            def _():
                start(save_feed(b))

        @pl.when(live & ((phase == 5) | (phase == 6)))
        def _():
            def two_tile(t, c):
                at = pl.ds(pl.multiple_of(t * 2 * tile, 2 * tile), 2 * tile)
                value = (dot_t(gg[0, mine, :], gu_w[0, at, :]) + dot_t(gg[1, mine, :], gu_w[1, at, :])).astype(jnp.bfloat16)
                for k in (0, 1):
                    two_part[natural(k, b), at] = value[k * hb:(k + 1) * hb]
                return c

            lax.fori_loop((phase - 5) * (wide // 4), (phase - 4) * (wide // 4), two_tile, 0)

        d = s - landed

        @pl.when(d >= 0)
        def _():
            @pl.when(d > 0)
            def _():
                wait(save_rows(d - 1))
            for k in (0, 1):
                where = line.rows(k, d)
                at = pl.ds(pl.multiple_of((d // per) * block + k * hb + (d - (d // per) * per) * rc, rc), rc)
                pieces = [pl.ds(c * tile, tile) for c in range(wide)]

                def middle_at(c):
                    return x[where, c].astype(jnp.float32) + branch[where, c].astype(jnp.float32)

                def folded(value):
                    return value[:, :128] + value[:, 128:]

                total = jnp.zeros((rc, 128), jnp.float32)
                for c in pieces:
                    middle = middle_at(c)
                    total = total + folded(middle * middle)
                inverse = lax.rsqrt(jnp.sum(total, axis=-1, keepdims=True) * (1.0 / width) + eps)
                total = jnp.zeros((rc, 128), jnp.float32)
                for c in pieces:
                    product = two_sum[where, c].astype(jnp.float32) * (middle_at(c) * inverse)
                    gain_out[:, c] += jnp.sum(product, axis=0, keepdims=True)
                    total = total + folded(product * gain[:, c])
                inner = jnp.sum(total, axis=-1, keepdims=True) * (1.0 / width)
                for c in pieces:
                    scaled = two_sum[where, c].astype(jnp.float32) * gain[:, c]
                    value = cot[at, c].astype(jnp.float32) + inverse * (scaled - middle_at(c) * inverse * inner)
                    middle_stage[k, :, c] = value
                    low_stage[k, :, c] = value.astype(jnp.bfloat16)
            start(save_rows(d))

        late = s - chunks
        w = late // 2

        @pl.when((late >= 0) & (late == 2 * w) & (w < wide))
        def _():
            @pl.when(w > 0)
            def _():
                wait(save_units(w - 1))
            columns = pl.ds(pl.multiple_of(w * tile, tile), tile)
            left = normed[:, columns]
            for t in (0, 1):
                unit_stage[:, t * ff:(t + 1) * ff] = dot_rows(left, gg[t]).astype(jnp.bfloat16)
            unit_stage[:, 2 * ff:] = dot_rows(cot[:, columns], hidden[...]).astype(jnp.bfloat16)
            start(save_units(w))
        return carry

    lax.fori_loop(0, offset + line.steps, step, 0)
    line.drain()
    wait(save_feed(blocks - 1))
    wait(save_rows(chunks - 1))
    wait(save_units(wide - 1))


def feed_forward(branch, gain, x, cot, gateup_w, down_w, n, cid, chunks=32, lag=2):
    rows, width = branch.shape
    ff = down_w.shape[0]
    rc = rows // (2 * chunks)
    block = 16 * rc
    blocks = chunks // 8
    low = jnp.bfloat16
    vmem = pl.BlockSpec(memory_space=pltpu.VMEM)
    hbm = pl.BlockSpec(memory_space=pl.ANY)
    dma = pltpu.SemaphoreType.DMA
    shape = jax.ShapeDtypeStruct
    return pl.pallas_call(
        functools.partial(ff_kernel, n, chunks, lag, norm_eps),
        out_shape=(
            shape((rows, width), low), shape((rows, width), jnp.float32), shape((rows, width), low),
            shape((1, width), jnp.float32), shape((width, 3 * ff), low),
        ),
        in_specs=[vmem, vmem, vmem, hbm, hbm, hbm],
        out_specs=(hbm, hbm, hbm, vmem, hbm),
        scratch_shapes=line_scratch(chunks, rc, width) + [
            pltpu.VMEM((rows, width), low),
            pltpu.VMEM((rows, width), low),
            pltpu.VMEM((2, width, ff), low),
            pltpu.VMEM((ff, width), low),
            pltpu.VMEM((rows, width), low),
            pltpu.VMEM((rows, width), low),
            pltpu.VMEM((rows, ff), low),
            pltpu.VMEM((2, rows, ff), low),
            pltpu.VMEM((block, width), low),
            pltpu.VMEM((2, rc, width), jnp.float32),
            pltpu.VMEM((2, rc, width), low),
            pltpu.VMEM((256, 3 * ff), low),
            dma((2,)), dma((blocks, 2)), dma((2,)), dma((2, 2)), dma((1,)),
        ],
        compiler_params=pltpu.CompilerParams(collective_id=cid, has_side_effects=True, vmem_limit_bytes=63 << 20),
        cost_estimate=pl.CostEstimate(flops=18 * rows * width * ff, bytes_accessed=rows * width * 150,
                                      transcendentals=rows * ff),
    )(branch, gain, x, cot, gateup_w, down_w)


def head_kernel(n, m, chunks, lag, eps, size, pairs,
                x, gain_part, qkv_shard, out_shard, cos_ref, sin_ref, seg_col_ref, seg_row_ref,
                branch, mix_ref, q_ref, k_ref, v_ref, lse_ref, qkv_w, out_w, gain,
                got, sa, ra, sg, rg, part, normed, raw, bias, scores, v_turned, got_gain,
                send_gain, recv_gain, send_direct, send_forward, recv_w):
    rows, width = x.shape
    q_width = pairs * 128
    z = lax.axis_index("tensor")
    dp = lax.axis_index("dp")
    share = width // m
    chips = m // 2
    chip, core = dp // 2, dp % 2
    rc = rows // (2 * chunks)
    per = size // (2 * rc)
    hb = size // 2
    blocks = rows // size
    tile = 256
    wide = width // tile
    low_lanes, first_half = lane_tests(size)
    low_rows = lax.broadcasted_iota(jnp.int32, (128, size), 0) < 64
    shards, wholes = (qkv_shard, out_shard), (qkv_w, out_w)

    def ascending(stream, c):
        b = c // per
        return b * size + stream * hb + (c - b * per) * rc

    line = Line(n, chunks, rc, lag, part, got, branch, (sa, ra, sg, rg), ascending)

    def shard_rows(s):
        return pl.ds(pl.multiple_of(s * share, share), share)

    def direct(kind, k):
        peer = 2 * lax.rem(chip + k, chips) + core
        return pltpu.make_async_remote_copy(
            src_ref=shards[kind], dst_ref=wholes[kind].at[shard_rows(dp)], send_sem=send_direct.at[kind, k],
            recv_sem=recv_w.at[kind, dp], device_id={"dp": peer}, device_id_type=MESH)

    def forward(kind, c, side):
        shard = 2 * c + side
        where = shard_rows(shard)
        return pltpu.make_async_remote_copy(
            src_ref=wholes[kind].at[where], dst_ref=wholes[kind].at[where], send_sem=send_forward.at[kind, c],
            recv_sem=recv_w.at[kind, shard], device_id={"dp": 2 * chip + 1 - core}, device_id_type=MESH)

    def send_gains(k, sender):
        return pltpu.make_async_remote_copy(
            src_ref=gain_part, dst_ref=got_gain.at[sender], send_sem=send_gain.at[k], recv_sem=recv_gain.at[sender],
            device_id={"dp": lax.rem(dp + k, m)}, device_id_type=MESH)

    barrier = pltpu.get_barrier_semaphore()

    @pl.when(z > 0)
    def _():
        pl.semaphore_signal(barrier, inc=1, device_id={"tensor": z - 1}, device_id_type=MESH)

    @pl.when(z < n - 1)
    def _():
        pl.semaphore_signal(barrier, inc=1, device_id={"tensor": z + 1}, device_id_type=MESH)

    for k in range(1, m):
        pl.semaphore_signal(barrier, inc=1, device_id={"dp": lax.rem(dp + k, m)}, device_id_type=MESH)

    for kind in (0, 1):
        wholes[kind][shard_rows(dp), :] = shards[kind][...]
    got_gain[dp] = gain_part[...]

    @pl.when((z > 0) & (z < n - 1))
    def _():
        pl.semaphore_wait(barrier, m + 1)

    @pl.when((z == 0) | (z == n - 1))
    def _():
        pl.semaphore_wait(barrier, m)

    for k in range(1, m):
        send_gains(k, dp).start()
    for kind in (0, 1):
        for k in range(1, chips):
            direct(kind, k).start()
        forward(kind, chip, core).start()
    for k in range(1, m):
        send_gains(k, lax.rem(dp + m - k, m)).wait_recv()
    whole = got_gain[0]
    for k in range(1, m):
        whole = whole + got_gain[k]
    gain[...] = whole.astype(jnp.bfloat16).astype(jnp.float32)

    def norm_rows(r, carry):
        where = pl.ds(pl.multiple_of(r * rc, rc), rc)
        values = x[where, :].astype(jnp.float32)
        inverse = lax.rsqrt(jnp.mean(values * values, axis=-1, keepdims=True) + eps)
        normed[where, :] = (values * inverse * gain[0:1, :]).astype(jnp.bfloat16)
        return carry

    lax.fori_loop(0, rows // rc, norm_rows, 0)

    def gather(kind):
        for k in range(1, chips):
            c = lax.rem(chip + chips - k, chips)
            forward(kind, c, core).wait_recv()
            forward(kind, c, core).start()
        for c in range(chips):
            forward(kind, c, 1 - core).wait_recv()

    gather(0)

    def prepare(i, carry):
        where = pl.ds(pl.multiple_of(i * size, size), size)
        raw[...] = dot_n(normed[where, :], qkv_w[...])
        cosines, sines = cos_ref[where, :], sin_ref[where, :]
        for hp in range(pairs):
            values = raw[:, hp * 128:(hp + 1) * 128]
            turned = values * cosines + swap_halves(values, first_half) * sines
            q_ref[where, hp * 128:(hp + 1) * 128] = (
                turned.astype(jnp.bfloat16).astype(jnp.float32) * 0.125).astype(jnp.bfloat16)
        both = raw[:, q_width:q_width + 128]
        other = pltpu.roll(both, 64, 1)
        keys = jnp.where(low_lanes, both, other)
        k_ref[where, :] = (keys * cosines + swap_halves(keys, first_half) * sines).astype(jnp.bfloat16)
        values = jnp.where(low_lanes, other, both)
        v_ref[where, :] = values.astype(jnp.bfloat16)
        v_turned[i] = values.T.astype(jnp.bfloat16)
        return carry

    lax.fori_loop(0, blocks, prepare, 0)
    gather(1)

    def attend(i, hp):
        where = pl.ds(pl.multiple_of(i * size, size), size)
        columns = pl.ds(pl.multiple_of(hp * 128, 128), 128)
        stacked = stack_pair(q_ref[where, columns], low_lanes)

        def score(j, top):
            keys = k_ref[pl.ds(pl.multiple_of(j * size, size), size), :]
            b = bias[j]
            s = dot_t(keys, stacked) + jnp.concatenate([b, b], axis=1)
            scores[j] = s
            return jnp.maximum(top, jnp.max(s, axis=0, keepdims=True))

        top = lax.fori_loop(0, i + 1, score, jnp.full((1, 2 * size), -jnp.inf, jnp.float32))

        def mix(j, c):
            total, acc = c
            p = jnp.exp(scores[j] - top)
            total = total + jnp.sum(p, axis=0, keepdims=True)
            return total, acc + dot_n(v_turned[j], p.astype(jnp.bfloat16))

        total, acc = lax.fori_loop(0, i + 1, mix, (
            jnp.zeros((1, 2 * size), jnp.float32), jnp.zeros((128, 2 * size), jnp.float32)))
        lse_ref[i, hp] = top + jnp.log(total)
        acc = acc / total
        acc = jnp.where(low_rows, acc[:, :size], acc[:, size:])
        mix_ref[where, columns] = acc.T.astype(jnp.bfloat16)

    def step(s, carry):
        line.step(s - per)
        i = s // per
        hp = s - i * per
        live = s < blocks * per

        @pl.when(live & (hp == 0))
        def _():
            def fill(j, c):
                bias[j] = block_bias(seg_col_ref, seg_row_ref, i, j, size)
                return c

            lax.fori_loop(0, i + 1, fill, 0)

        @pl.when(live)
        def _():
            def each(h, c):
                attend(i, h)
                return c

            lax.fori_loop(hp * pairs // per, (hp + 1) * pairs // per, each, 0)

        @pl.when(live & (hp == per - 1))
        def _():
            where = pl.ds(pl.multiple_of(i * size, size), size)

            def part_tile(t, c):
                at = pl.ds(pl.multiple_of(t * tile, tile), tile)
                part[where, at] = dot_t(mix_ref[where, :], out_w[at, :]).astype(jnp.bfloat16)
                return c

            lax.fori_loop(0, wide, part_tile, 0)
        return carry

    lax.fori_loop(0, per + line.steps, step, 0)
    line.drain()
    for k in range(1, m):
        send_gains(k, dp).wait_send()
    for kind in (0, 1):
        for k in range(1, chips):
            direct(kind, k).wait_send()
        for c in range(chips):
            forward(kind, c, core).wait_send()


def attention_head(x, gain_part, qkv_shard, out_shard, cosines, sines, seg_col, seg_row, n, m, cid, size,
                   chunks=32, lag=2):
    rows, width = x.shape
    q_width = out_shard.shape[1]
    pairs = q_width // 128
    rc = rows // (2 * chunks)
    blocks = rows // size
    chips = m // 2
    low = jnp.bfloat16
    vmem = pl.BlockSpec(memory_space=pltpu.VMEM)
    dma = pltpu.SemaphoreType.DMA
    shape = jax.ShapeDtypeStruct
    return pl.pallas_call(
        functools.partial(head_kernel, n, m, chunks, lag, norm_eps, size, pairs),
        out_shape=(
            shape((rows, width), low), shape((rows, q_width), low), shape((rows, q_width), low),
            shape((rows, 128), low), shape((rows, 128), low), shape((blocks, pairs, 1, 2 * size), jnp.float32),
            shape((width, q_width + 128), low), shape((width, q_width), low), shape((2, width), jnp.float32),
        ),
        in_specs=[vmem] * 8,
        out_specs=(vmem,) * 9,
        scratch_shapes=line_scratch(chunks, rc, width) + [
            pltpu.VMEM((rows, width), low),
            pltpu.VMEM((rows, width), low),
            pltpu.VMEM((size, q_width + 128), jnp.float32),
            pltpu.VMEM((blocks, size, size), jnp.float32),
            pltpu.VMEM((blocks, size, 2 * size), jnp.float32),
            pltpu.VMEM((blocks, 128, size), low),
            pltpu.VMEM((m, 2, width), jnp.float32),
            dma((m,)), dma((m,)), dma((2, chips)), dma((2, chips)), dma((2, m)),
        ],
        compiler_params=pltpu.CompilerParams(collective_id=cid, has_side_effects=True, vmem_limit_bytes=56 << 20),
        cost_estimate=pl.CostEstimate(flops=20 * rows * width * q_width, bytes_accessed=rows * width * 170,
                                      transcendentals=rows * rows * pairs),
    )(x, gain_part, qkv_shard, out_shard, cosines, sines, seg_col, seg_row)


def back_kernel(n, m, chunks, lag, eps, size, pairs,
                feed_part, grad_low, gain, q_ref, k_ref, v_ref, mix_ref, lse_ref, cos_ref, sin_ref,
                seg_col_ref, seg_row_ref, out_w, x_hbm, qkv_hbm, branch_hbm, middle_hbm,
                layer_hbm, input_hbm, gain_out, reduced,
                got2, sa2, ra2, sg2, rg2, got4, sa4, ra4, sg4, rg4, feed_sum, part, grad_sum,
                x, qkv_w, normed, grad_mix, bias, k_turned, grad_k, grad_v, grad_qkv, send, recv,
                branch_stage, layer_stage, middle_stage, input_stage,
                w_sem, branch_sem, middle_sem, layer_sem, input_sem, send_sem, recv_sem):
    rows, width = feed_part.shape
    q_width = pairs * 128
    z = lax.axis_index("tensor")
    dp = lax.axis_index("dp")
    rc = rows // (2 * chunks)
    per = size // (2 * rc)
    hb = size // 2
    blocks = rows // size
    tile = 256
    wide = width // tile
    share = width // m
    owners = tile // share
    lead = 2 * lag * (n - 1)
    low_lanes, first_half = lane_tests(size)
    low_rows = lax.broadcasted_iota(jnp.int32, (128, size), 0) < 64

    def descending(stream, c):
        b = c // per
        return (blocks - 1 - b) * size + stream * hb + (c - b * per) * rc

    two = Line(n, chunks, rc, lag, feed_part, got2, feed_sum, (sa2, ra2, sg2, rg2))
    four = Line(n, chunks, rc, lag, part, got4, grad_sum, (sa4, ra4, sg4, rg4), descending)
    loads = (
        pltpu.make_async_copy(x_hbm, x, w_sem.at[0]),
        pltpu.make_async_copy(qkv_hbm, qkv_w, w_sem.at[1]),
    )
    for copy in loads:
        copy.start()

    def start(copies):
        for copy in copies:
            copy.start()

    def wait(copies):
        for copy in copies:
            copy.wait()

    def load_branch(d, slot):
        return [pltpu.make_async_copy(branch_hbm.at[two.rows(k, d)], branch_stage.at[slot, k], branch_sem.at[slot, k])
                for k in (0, 1)]

    def load_middle(d, slot):
        return [pltpu.make_async_copy(middle_hbm.at[four.rows(k, d)], middle_stage.at[slot, k], middle_sem.at[slot, k])
                for k in (0, 1)]

    def save_layer(d):
        return [pltpu.make_async_copy(layer_stage.at[k], layer_hbm.at[two.rows(k, d)], layer_sem.at[k]) for k in (0, 1)]

    def save_input(d):
        return [pltpu.make_async_copy(input_stage.at[k], input_hbm.at[four.rows(k, d)], input_sem.at[k]) for k in (0, 1)]

    def to_owner(w, o):
        owner = w * owners + o
        return pltpu.make_async_remote_copy(
            src_ref=send.at[w, pl.ds(o * share, share)], dst_ref=recv.at[dp], send_sem=send_sem.at[owner],
            recv_sem=recv_sem.at[dp], device_id={"dp": owner}, device_id_type=MESH)

    gain_out[...] = jnp.zeros_like(gain_out)

    def prepare(i, carry):
        at = pl.ds(pl.multiple_of(i * size, size), size)
        k_turned[i] = k_ref[at, :].astype(jnp.float32).T.astype(jnp.bfloat16)
        grad_k[i] = jnp.zeros((size, 128), jnp.float32)
        grad_v[i] = jnp.zeros((size, 128), jnp.float32)
        return carry

    lax.fori_loop(0, blocks, prepare, 0)

    barrier = pltpu.get_barrier_semaphore()

    @pl.when(z > 0)
    def _():
        pl.semaphore_signal(barrier, inc=1, device_id={"tensor": z - 1}, device_id_type=MESH)

    @pl.when(z < n - 1)
    def _():
        pl.semaphore_signal(barrier, inc=1, device_id={"tensor": z + 1}, device_id_type=MESH)

    for k in range(1, m):
        pl.semaphore_signal(barrier, inc=1, device_id={"dp": lax.rem(dp + k, m)}, device_id_type=MESH)

    @pl.when((z > 0) & (z < n - 1))
    def _():
        pl.semaphore_wait(barrier, m + 1)

    @pl.when((z == 0) | (z == n - 1))
    def _():
        pl.semaphore_wait(barrier, m)

    def unit_rows(where):
        values = x[where, :].astype(jnp.float32)
        inverse = lax.rsqrt(jnp.mean(values * values, axis=-1, keepdims=True) + eps)
        return values * inverse, inverse

    def attend(i, hp):
        at_rows = pl.ds(pl.multiple_of(i * size, size), size)
        columns = pl.ds(pl.multiple_of(hp * 128, 128), 128)
        stacked = stack_pair(q_ref[at_rows, columns], low_lanes)
        grad_pair = grad_mix[:, columns]
        grad_stacked = stack_pair(grad_pair, low_lanes)
        product = (grad_pair.astype(jnp.float32) * mix_ref[at_rows, columns].astype(jnp.float32)).T
        spread = jnp.concatenate([
            jnp.sum(product[:64], axis=0, keepdims=True), jnp.sum(product[64:], axis=0, keepdims=True)], axis=1)
        logsum = lse_ref[i, hp]

        def piece(j, acc):
            at = pl.ds(pl.multiple_of(j * size, size), size)
            b = bias[j]
            s = dot_t(k_ref[at, :], stacked) + jnp.concatenate([b, b], axis=1)
            p = jnp.exp(s - logsum)
            grad_p = dot_t(v_ref[at, :], grad_stacked)
            grad_s = (p * (grad_p - spread)).astype(jnp.bfloat16)
            grad_v[j] += dot_n(p.astype(jnp.bfloat16), grad_stacked)
            grad_k[j] += dot_n(grad_s, stacked)
            return acc + dot_n(k_turned[j], grad_s)

        acc = lax.fori_loop(0, i + 1, piece, jnp.zeros((128, 2 * size), jnp.float32))
        acc = jnp.where(low_rows, acc[:, :size], acc[:, size:]).T * 0.125
        turned = acc * cos_ref[at_rows, :] - swap_halves(acc, first_half) * sin_ref[at_rows, :]
        grad_qkv[at_rows, columns] = turned.astype(jnp.bfloat16)

    def step(s, carry):
        two.step(s)
        four.step(s - per)
        b = s // per
        hp = s - b * per
        i = blocks - 1 - b
        live = s < blocks * per
        at_rows = pl.ds(pl.multiple_of(i * size, size), size)

        @pl.when(s == 0)
        def _():
            wait(loads)

        @pl.when(live & (hp == 0))
        def _():
            grad_mix[...] = dot_n(grad_low[at_rows, :], out_w[...]).astype(jnp.bfloat16)

            def fill(j, c):
                bias[j] = block_bias(seg_col_ref, seg_row_ref, i, j, size)
                return c

            lax.fori_loop(0, i + 1, fill, 0)

        @pl.when(live)
        def _():
            def each(h, c):
                attend(i, h)
                return c

            lax.fori_loop(hp * pairs // per, (hp + 1) * pairs // per, each, 0)

            def some(r, c):
                at = pl.ds(pl.multiple_of(s * 2 * rc + r * rc, rc), rc)
                normed[at, :] = (unit_rows(at)[0] * gain[...]).astype(jnp.bfloat16)
                return c

            lax.fori_loop(0, 2, some, 0)

        @pl.when(live & (hp == per - 1))
        def _():
            cosines, sines = cos_ref[at_rows, :], sin_ref[at_rows, :]
            dk = grad_k[i] + pltpu.roll(grad_k[i], 64, 1)
            dk = dk * cosines - swap_halves(dk, first_half) * sines
            dv = grad_v[i] + pltpu.roll(grad_v[i], 64, 1)
            grad_qkv[at_rows, q_width:] = jnp.where(low_lanes, dk, dv).astype(jnp.bfloat16)

            def part_tile(t, c):
                at = pl.ds(pl.multiple_of(t * tile, tile), tile)
                part[at_rows, at] = dot_t(grad_qkv[at_rows, :], qkv_w[at, :]).astype(jnp.bfloat16)
                return c

            lax.fori_loop(0, wide, part_tile, 0)

        w = s - blocks * per

        @pl.when((w >= 0) & (w < wide))
        def _():
            columns = pl.ds(pl.multiple_of(w * tile, tile), tile)
            send[w, :, :q_width + 128] = dot_rows(normed[:, columns], grad_qkv[...]).astype(jnp.bfloat16)
            send[w, :, q_width + 128:] = dot_rows(grad_low[:, columns], mix_ref[...]).astype(jnp.bfloat16)
            for o in range(owners):
                owner = w * owners + o

                @pl.when(owner != dp)
                def _():
                    to_owner(w, o).start()

                @pl.when(owner == dp)
                def _():
                    recv[dp] = send[w, o * share:(o + 1) * share, :]

        e = s - lead + 1

        @pl.when((e >= 0) & (e < chunks))
        def _():
            start(load_branch(e, e % 2))

        d = s - lead

        @pl.when((d >= 0) & (d < chunks))
        def _():
            wait(load_branch(d, d % 2))

            @pl.when(d > 0)
            def _():
                wait(save_layer(d - 1))
            for k in (0, 1):
                where = two.rows(k, d)
                layer_stage[k] = (
                    x[where, :].astype(jnp.float32) + branch_stage[d % 2, k].astype(jnp.float32)
                    + feed_sum[where, :].astype(jnp.float32)
                ).astype(jnp.bfloat16)
            start(save_layer(d))

        e4 = s - lead - per + 1

        @pl.when((e4 >= 0) & (e4 < chunks))
        def _():
            start(load_middle(e4, e4 % 2))

        d4 = s - lead - per

        @pl.when(d4 >= 0)
        def _():
            wait(load_middle(d4, d4 % 2))

            @pl.when(d4 > 0)
            def _():
                wait(save_input(d4 - 1))
            for k in (0, 1):
                where = four.rows(k, d4)
                unit, inverse = unit_rows(where)
                grad = grad_sum[where, :].astype(jnp.float32)
                scaled = grad * gain[...]
                inner = jnp.mean(scaled * unit, axis=-1, keepdims=True)
                input_stage[k] = middle_stage[d4 % 2, k] + inverse * (scaled - unit * inner)
                gain_out[...] += jnp.sum(grad * unit, axis=0, keepdims=True)
            start(save_input(d4))
        return carry

    lax.fori_loop(0, per + four.steps, step, 0)
    two.drain()
    four.drain()
    wait(save_layer(chunks - 1))
    wait(save_input(chunks - 1))

    def finish(k, carry):
        owner = lax.rem(dp + k, m)
        w = owner // owners

        def copy(peer):
            return pltpu.make_async_remote_copy(
                src_ref=send.at[0, pl.ds(0, share)], dst_ref=recv.at[peer], send_sem=send_sem.at[peer],
                recv_sem=recv_sem.at[peer], device_id={"dp": peer}, device_id_type=MESH)

        copy(owner).wait_send()
        copy(owner).wait_recv()
        return carry

    lax.fori_loop(1, m, finish, 0)
    reduced[...] = recv[0].astype(jnp.float32)

    def add(k, carry):
        reduced[...] += recv[k].astype(jnp.float32)
        return carry

    lax.fori_loop(1, m, add, 0)


def attention_back(feed_part, grad_low, gain, q, k, v, mix, lse, cosines, sines, seg_col, seg_row, out_w,
                   x, qkv_w, branch, grad_middle, n, m, cid, size, chunks=16, lag=2):
    rows, width = feed_part.shape
    q_width = q.shape[1]
    pairs = q_width // 128
    rc = rows // (2 * chunks)
    blocks = rows // size
    share = width // m
    cat = 2 * q_width + 128
    low = jnp.bfloat16
    vmem = pl.BlockSpec(memory_space=pltpu.VMEM)
    hbm = pl.BlockSpec(memory_space=pl.ANY)
    dma = pltpu.SemaphoreType.DMA
    shape = jax.ShapeDtypeStruct
    return pl.pallas_call(
        functools.partial(back_kernel, n, m, chunks, lag, norm_eps, size, pairs),
        out_shape=(
            shape((rows, width), low), shape((rows, width), jnp.float32), shape((1, width), jnp.float32),
            shape((share, cat), jnp.float32),
        ),
        in_specs=[vmem] * 13 + [hbm] * 4,
        out_specs=(hbm, hbm, vmem, vmem),
        scratch_shapes=line_scratch(chunks, rc, width) + line_scratch(chunks, rc, width) + [
            pltpu.VMEM((rows, width), low),
            pltpu.VMEM((rows, width), low),
            pltpu.VMEM((rows, width), low),
            pltpu.VMEM((rows, width), low),
            pltpu.VMEM((width, q_width + 128), low),
            pltpu.VMEM((rows, width), low),
            pltpu.VMEM((size, q_width), low),
            pltpu.VMEM((blocks, size, size), jnp.float32),
            pltpu.VMEM((blocks, 128, size), low),
            pltpu.VMEM((blocks, size, 128), jnp.float32),
            pltpu.VMEM((blocks, size, 128), jnp.float32),
            pltpu.VMEM((rows, q_width + 128), low),
            pltpu.VMEM((width // 256, 256, cat), low),
            pltpu.VMEM((m, share, cat), low),
            pltpu.VMEM((2, 2, rc, width), low),
            pltpu.VMEM((2, rc, width), low),
            pltpu.VMEM((2, 2, rc, width), jnp.float32),
            pltpu.VMEM((2, rc, width), jnp.float32),
            dma((2,)), dma((2, 2)), dma((2, 2)), dma((2,)), dma((2,)), dma((m,)), dma((m,)),
        ],
        compiler_params=pltpu.CompilerParams(collective_id=cid, has_side_effects=True, vmem_limit_bytes=63 << 20),
        cost_estimate=pl.CostEstimate(flops=40 * rows * width * q_width, bytes_accessed=rows * width * 260,
                                      transcendentals=rows * rows * pairs),
    )(feed_part, grad_low, gain, q, k, v, mix, lse, cosines, sines, seg_col, seg_row, out_w,
      x, qkv_w, branch, grad_middle)


def norm_kernel(n, m, gains_ref, ff_ref, head_ref, norm_ref, gain_ref, line, got_gains, got_line, got_plane, got_squares,
                send_squares, recv_squares, send_gains, recv_gains, send_line, recv_line, send_plane, recv_plane):
    z = lax.axis_index("tensor")
    d = lax.axis_index("dp")
    share = head_ref.shape[0]

    barrier = pltpu.get_barrier_semaphore()
    for k in range(1, n):
        pl.semaphore_signal(barrier, inc=1, device_id={"tensor": lax.rem(z + k, n)}, device_id_type=MESH)
    for k in range(1, m):
        pl.semaphore_signal(barrier, inc=1, device_id={"dp": lax.rem(d + k, m)}, device_id_type=MESH)
    pl.semaphore_wait(barrier, n - 1 + m - 1)

    def gains_to(k, sender):
        peer = lax.rem(d + k, m)
        return pltpu.make_async_remote_copy(
            src_ref=gains_ref.at[peer], dst_ref=got_gains.at[sender], send_sem=send_gains.at[k],
            recv_sem=recv_gains.at[sender], device_id={"dp": peer}, device_id_type=MESH)

    def squares_to(k, sender):
        return pltpu.make_async_remote_copy(
            src_ref=line.at[2], dst_ref=got_squares.at[sender], send_sem=send_squares.at[k],
            recv_sem=recv_squares.at[sender], device_id={"dp": lax.rem(d + k, m)}, device_id_type=MESH)

    def along_line(k, sender):
        return pltpu.make_async_remote_copy(
            src_ref=line.at[0], dst_ref=got_line.at[sender], send_sem=send_line.at[k], recv_sem=recv_line.at[sender],
            device_id={"tensor": lax.rem(z + k, n)}, device_id_type=MESH)

    def over_plane(k, sender):
        return pltpu.make_async_remote_copy(
            src_ref=line.at[1], dst_ref=got_plane.at[sender], send_sem=send_plane.at[k], recv_sem=recv_plane.at[sender],
            device_id={"dp": lax.rem(d + k, m)}, device_id_type=MESH)

    def summed(ref, number):
        whole = ref[0]
        for k in range(1, number):
            whole = whole + ref[k]
        return whole

    def squares(value):
        return jnp.sum(jnp.sum(value * value, axis=0, keepdims=True), axis=1, keepdims=True)

    for k in range(1, m):
        gains_to(k, d).start()
    got_gains[d] = gains_ref[d]
    sub = 32

    def head_rows(r, acc):
        value = head_ref[pl.ds(pl.multiple_of(r * sub, sub), sub), :]
        return acc + squares(value)

    local = lax.fori_loop(0, share // sub, head_rows, jnp.zeros((1, 1), jnp.float32))

    def ff_rows(r, acc):
        value = ff_ref[pl.ds(pl.multiple_of(r * sub, sub), sub), :].astype(jnp.float32)
        return acc + squares(value)

    local = lax.fori_loop(0, share // sub, ff_rows, local)
    line[2] = jnp.broadcast_to(local, (8, 128))
    for k in range(1, m):
        squares_to(k, d).start()
    got_squares[d] = line[2]
    for k in range(1, m):
        gains_to(k, d).wait_send()
        gains_to(k, lax.rem(d + m - k, m)).wait_recv()
    for k in range(1, m):
        squares_to(k, d).wait_send()
        squares_to(k, lax.rem(d + m - k, m)).wait_recv()
    line[0] = summed(got_squares, m)
    gains = summed(got_gains, m)
    gain_ref[...] = gains
    line[1] = jnp.broadcast_to(squares(gains), (8, 128))
    for k in range(1, m):
        over_plane(k, d).start()
    got_plane[d] = line[1]
    for k in range(1, n):
        along_line(k, z).start()
    got_line[z] = line[0]
    for k in range(1, n):
        along_line(k, z).wait_send()
        along_line(k, lax.rem(z + n - k, n)).wait_recv()
    for k in range(1, m):
        over_plane(k, d).wait_send()
        over_plane(k, lax.rem(d + m - k, m)).wait_recv()
    norm_ref[...] = jnp.sqrt(summed(got_line, n) + summed(got_plane, m))


def adam_kernel(rates, kv_width, correct_ref, norm_ref, gain_ref, ff_hbm, head_hbm, layer_hbm, input_hbm, *refs):
    count = len(rates)
    params, refs = refs[:3 * count], refs[3 * count:]
    norm_out, layer_out, input_out, outs, refs = refs[0], refs[1], refs[2], refs[3:3 * count + 3], refs[3 * count + 3:]
    (ff_grad, head_ref, layer_held, input_held), held = refs[:4], refs[4:3 * count + 4]
    grad_sem, load_sem, save_sem, in_sem, back_sem = refs[3 * count + 4:]
    share = gain_ref.shape[1]
    q_width = outs[3].shape[1]
    ff = outs[12].shape[2]
    sub = 32

    grads = (
        pltpu.make_async_copy(ff_hbm, ff_grad, grad_sem.at[0]),
        pltpu.make_async_copy(head_hbm, head_ref, grad_sem.at[1]),
    )
    loads = [pltpu.make_async_copy(params[k], held[k], load_sem.at[k]) for k in range(3 * count)]
    saves = [pltpu.make_async_copy(held[k], outs[k], save_sem.at[k]) for k in range(3 * count)]
    quarter = layer_hbm.shape[0] // 4
    arrive, depart = [], []
    for k in range(4):
        at = pl.ds(k * quarter, quarter)
        for t, (source, kept, target) in enumerate(
                ((layer_hbm, layer_held, layer_out), (input_hbm, input_held, input_out))):
            arrive.append(pltpu.make_async_copy(source.at[at], kept.at[at], in_sem.at[t, k]))
            depart.append(pltpu.make_async_copy(kept.at[at], target.at[at], back_sem.at[t, k]))
    for copy in grads:
        copy.start()
    for which in (1, 3, 2, 5, 4, 0):
        for k in range(3):
            loads[3 * which + k].start()
    for copy in arrive:
        copy.start()
    norm_out[...] = norm_ref[...]
    factor = jnp.minimum(1.0, clip_limit / (norm_ref[:1, :1] + 1e-06))
    one, two = correct_ref[0], correct_ref[1]

    def update(which, where, gradient):
        rate, decay = rates[which]
        p, a, b = (held[3 * which + k] for k in range(3))
        gradient = gradient * factor
        first = beta_first * a[where] + (1.0 - beta_first) * gradient
        second = beta_second * b[where] + (1.0 - beta_second) * gradient * gradient
        a[where] = first
        b[where] = second
        change = first / one / (jnp.sqrt(second / two) + adam_eps)
        old = p[where]
        p[where] = old - rate * (change + decay * old)

    def load(which):
        for k in range(3):
            loads[3 * which + k].wait()

    def save(which):
        for k in range(3):
            saves[3 * which + k].start()

    def by_rows(which, body):
        load(which)
        lax.fori_loop(0, share // sub, lambda r, c: (body(pl.ds(pl.multiple_of(r * sub, sub), sub)), c)[1], 0)
        save(which)

    for copy in grads:
        copy.wait()
    by_rows(1, lambda where: update(1, (where, slice(None)), head_ref[where, :q_width]))
    load(3)

    def out_tile(t, carry):
        at = pl.ds(pl.multiple_of(t * 128, 128), 128)
        source = pl.ds(pl.multiple_of(q_width + 2 * kv_width + t * 128, 128), 128)
        update(3, (at, slice(None)), head_ref[:, source].T)
        return carry

    lax.fori_loop(0, outs[9].shape[0] // 128, out_tile, 0)
    save(3)

    load(2)
    both = head_ref[:, q_width:q_width + 2 * kv_width].T
    for t in (0, 1):
        update(2, (t, slice(None), slice(None)), both[t * kv_width:(t + 1) * kv_width])
    save(2)

    def gateup_rows(where):
        for t in (0, 1):
            update(4, (t, where, slice(None)), ff_grad[where, t * ff:(t + 1) * ff].astype(jnp.float32))

    load(5)

    def down_tile(t, carry):
        at = pl.ds(pl.multiple_of(t * 128, 128), 128)
        source = pl.ds(pl.multiple_of(2 * ff + t * 128, 128), 128)
        update(5, (at, slice(None)), ff_grad[:, source].astype(jnp.float32).T)
        return carry

    lax.fori_loop(0, ff // 128, down_tile, 0)
    save(5)
    by_rows(4, gateup_rows)
    for came, left in zip(arrive, depart):
        came.wait()
        left.start()
    load(0)
    update(0, (slice(None), slice(None)), gain_ref[...])
    save(0)
    for copy in saves + depart:
        copy.wait()


def finish_step(gains, correct, ff_grad, head_grad, layer, grad_in, params, rates, kv_width, n, m, cid):
    share = gains.shape[1] // m
    parts = gains.reshape(2, m, share).transpose(1, 0, 2)
    vmem = pl.BlockSpec(memory_space=pltpu.VMEM)
    hbm = pl.BlockSpec(memory_space=pl.ANY)
    dma = pltpu.SemaphoreType.DMA
    shape = jax.ShapeDtypeStruct
    norm, gain = pl.pallas_call(
        functools.partial(norm_kernel, n, m),
        out_shape=(shape((8, 128), jnp.float32), shape((2, share), jnp.float32)),
        in_specs=[vmem, vmem, vmem],
        out_specs=(vmem, vmem),
        scratch_shapes=[
            pltpu.VMEM((3, 8, 128), jnp.float32),
            pltpu.VMEM((m, 2, share), jnp.float32),
            pltpu.VMEM((n, 8, 128), jnp.float32),
            pltpu.VMEM((m, 8, 128), jnp.float32),
            pltpu.VMEM((m, 8, 128), jnp.float32),
            dma((m,)), dma((m,)), dma((m,)), dma((m,)), dma((n,)), dma((n,)), dma((m,)), dma((m,)),
        ],
        compiler_params=pltpu.CompilerParams(collective_id=cid, has_side_effects=True),
    )(parts, ff_grad, head_grad)
    size = sum(p.size for p in params)
    norm, layer, grad_in, *outs = pl.pallas_call(
        functools.partial(adam_kernel, rates, kv_width),
        out_shape=(shape((8, 128), jnp.float32), shape(layer.shape, layer.dtype), shape(grad_in.shape, grad_in.dtype))
        + tuple(shape(p.shape, jnp.float32) for p in params),
        in_specs=[pl.BlockSpec(memory_space=pltpu.SMEM), vmem, vmem] + [hbm] * (4 + len(params)),
        out_specs=(vmem,) + (hbm,) * (2 + len(params)),
        scratch_shapes=[pltpu.VMEM(a.shape, a.dtype) for a in (ff_grad, head_grad, layer, grad_in)]
        + [pltpu.VMEM(p.shape, jnp.float32) for p in params]
        + [dma((2,)), dma((len(params),)), dma((len(params),)), dma((2, 4)), dma((2, 4))],
        compiler_params=pltpu.CompilerParams(vmem_limit_bytes=63 << 20),
        cost_estimate=pl.CostEstimate(flops=20 * size, bytes_accessed=24 * size, transcendentals=size),
    )(correct, norm, gain, ff_grad, head_grad, layer, grad_in, *params)
    return norm, layer, grad_in, outs


norm_eps = 1e-05
beta_first = 0.9
beta_second = 0.95
adam_eps = 1e-08
weight_decay = 0.1
weight_rate = 0.02
out_rate = 0.1
gain_rate = 0.2
clip_limit = 1.0


def positions(segment):
    length = segment.shape[0]
    indices = jnp.arange(length, dtype=jnp.int32)
    earlier = jnp.concatenate([segment[:1] - 1, segment[:-1]])
    begins = jnp.where(segment != earlier, indices, jnp.zeros_like(indices))
    return indices - lax.cummax(begins, axis=0)


def paired_tables(places):
    lane = jnp.arange(128, dtype=jnp.int32) % HD
    frequency = jnp.power(10000.0, -(lane % (HD // 2)).astype(jnp.float32) * (2.0 / HD))
    angles = places.astype(jnp.float32)[:, None] * frequency[None, :]
    sines = jnp.sin(angles)
    return jnp.cos(angles), jnp.where(lane < HD // 2, -sines, sines)


def on_device(
    n,
    m,
    tokens,
    cotangent,
    segment_ids,
    step_count,
    norm_gains,
    gains_first,
    gains_second,
    w_query,
    query_first,
    query_second,
    w_keyval,
    keyval_first,
    keyval_second,
    w_out,
    out_first,
    out_second,
    w_gateup,
    gateup_first,
    gateup_second,
    w_down,
    down_first,
    down_second,
):
    low = jnp.bfloat16
    width = w_query.shape[1]
    kv_width = w_keyval.shape[2]
    qkv_shard = jnp.concatenate([w_query, w_keyval[0], w_keyval[1]], axis=1).astype(low)
    out_shard = w_out.T.astype(low)
    share = norm_gains.shape[1]
    gain_part = lax.dynamic_update_slice(
        jnp.zeros((2, tokens.shape[1]), jnp.float32), norm_gains, (0, lax.axis_index("dp") * share)
    )
    length = tokens.shape[0]
    size = min(256, length)
    segment = segment_ids[0]
    places = positions(segment)
    cosines, sines = paired_tables(places)
    seg_col, seg_row = segment[:, None], segment[None, :]
    qkv_shard, out_shard, gain_part, cosines, sines, seg_col, late_gateup, late_down = lax.optimization_barrier(
        (qkv_shard, out_shard, gain_part, cosines, sines, seg_col, w_gateup, w_down)
    )
    gateup_weight = lax.all_gather(late_gateup.astype(low), "dp", axis=1, tiled=True)
    down_weight = lax.all_gather(late_down.astype(low), "dp", axis=1, tiled=True)

    branch, mixture, q, k, v, lse, qkv_weight, out_weight, gain_values = attention_head(
        tokens, gain_part, qkv_shard, out_shard, cosines, sines, seg_col, seg_row, n, m, 1, size
    )
    feed_part, grad_middle, grad_branch, gain_grad_two, grad_ff_weight = feed_forward(
        branch, gain_values[1:], tokens, cotangent, gateup_weight, down_weight, n, 2
    )
    ff_reduced = lax.psum_scatter(grad_ff_weight, "dp", scatter_dimension=0, tiled=True)
    layer_out, input_grad, gain_grad_one, head_reduced = attention_back(
        feed_part, grad_branch, gain_values[:1], q, k, v, mixture, lse, cosines, sines, seg_col, seg_row,
        out_weight, tokens, qkv_weight, branch, grad_middle, n, m, 3, size
    )
    gain_grads = jnp.concatenate([gain_grad_one, gain_grad_two])
    step_float = step_count[0].astype(jnp.float32)
    correct = jnp.stack([1.0 - jnp.power(beta_first, step_float), 1.0 - jnp.power(beta_second, step_float)])
    params = (
        (norm_gains, gains_first, gains_second),
        (w_query, query_first, query_second),
        tuple(a.swapaxes(1, 2) for a in (w_keyval, keyval_first, keyval_second)),
        (w_out, out_first, out_second),
        (w_gateup, gateup_first, gateup_second),
        (w_down, down_first, down_second),
    )
    rates = (
        (gain_rate, 0.0),
        (weight_rate, weight_decay),
        (weight_rate, weight_decay),
        (out_rate, weight_decay),
        (weight_rate, weight_decay),
        (weight_rate, weight_decay),
    )
    norm, layer_out, input_grad, updated = finish_step(
        gain_grads, correct, ff_reduced, head_reduced, layer_out, input_grad,
        [a for group in params for a in group], rates, kv_width, n, m, 4
    )
    results = []
    for k in range(len(params)):
        weight, first_state, second_state = updated[3 * k : 3 * k + 3]
        group = [first_state, second_state, weight]
        results += [a.swapaxes(1, 2) for a in group] if k == 2 else group
    return (layer_out, input_grad, norm[0, :1], *results)


def solution(mesh):
    rows = P("dp", None)
    gains = P(None, "dp")
    query = P("dp", "tensor")
    stacked = P(None, "dp", "tensor")
    turned = P("tensor", "dp")
    states = (gains,) * 3 + (query,) * 3 + (stacked,) * 3 + (turned,) * 3 + (stacked,) * 3 + (turned,) * 3
    return jax.shard_map(
        functools.partial(on_device, mesh.shape["tensor"], mesh.shape["dp"]),
        mesh=mesh,
        in_specs=(rows, rows, rows, P()) + states,
        out_specs=(rows, rows, P()) + states,
        check_vma=False,
    )
```

```python
import functools

import jax
import jax.numpy as jnp
from jax import lax
from jax.experimental import pallas as pl
from jax.experimental.pallas import tpu as pltpu
from jax.sharding import PartitionSpec as P

HD = 64
MESH = pl.DeviceIdType.MESH


masked_value = -1e9


def dot_t(left, right):
    return lax.dot_general(left, right, (((1,), (1,)), ((), ())), preferred_element_type=jnp.float32)


def dot_n(left, right):
    return lax.dot_general(left, right, (((1,), (0,)), ((), ())), preferred_element_type=jnp.float32)


def swap_halves(values, first_half):
    return jnp.where(first_half, pltpu.roll(values, 96, 1), pltpu.roll(values, 32, 1))


def lane_tests(rows):
    lane = lax.broadcasted_iota(jnp.int32, (rows, 128), 1)
    return lane < 64, (lane % 64) < 32


def block_bias(seg_col_ref, seg_row_ref, i, j, size):
    keys = seg_col_ref[pl.ds(pl.multiple_of(j * size, size), size), :]
    rows = seg_row_ref[:, pl.ds(pl.multiple_of(i * size, size), size)]
    key_at = j * size + lax.broadcasted_iota(jnp.int32, (size, size), 0)
    row_at = i * size + lax.broadcasted_iota(jnp.int32, (size, size), 1)
    return jnp.where((keys == rows) & (key_at <= row_at), 0.0, masked_value)


def stack_pair(pair, low_lanes):
    zero = jnp.zeros_like(pair)
    return jnp.concatenate([jnp.where(low_lanes, pair, zero), jnp.where(low_lanes, zero, pair)], axis=0)


class Line:
    def __init__(self, n, chunks, rc, lag, part, got, out, sems, order=None):
        self.order = order
        self.n, self.chunks, self.rc, self.lag = n, chunks, rc, lag
        self.part, self.got, self.out = part, got, out
        self.send_a, self.recv_a, self.send_g, self.recv_g = sems
        self.me = lax.axis_index("tensor")
        self.steps = chunks + 2 * lag * (n - 1)

    def rows(self, stream, c):
        begin = (stream * self.chunks + c) * self.rc if self.order is None else self.order(stream, c)
        return pl.ds(pl.multiple_of(begin, self.rc), self.rc)

    def side(self, stream):
        pos = self.me if stream == 0 else self.n - 1 - self.me
        fwd = self.me + 1 if stream == 0 else self.me - 1
        bwd = self.me - 1 if stream == 0 else self.me + 1
        return pos, fwd, bwd

    def toward(self, stream, c, nxt, src):
        return pltpu.make_async_remote_copy(
            src_ref=src, dst_ref=self.got.at[stream, c],
            send_sem=self.send_a.at[stream, c], recv_sem=self.recv_a.at[stream, c],
            device_id={"tensor": nxt}, device_id_type=MESH)

    def back(self, stream, c, nxt):
        where = self.rows(stream, c)
        return pltpu.make_async_remote_copy(
            src_ref=self.out.at[where], dst_ref=self.out.at[where],
            send_sem=self.send_g.at[stream, c], recv_sem=self.recv_g.at[stream, c],
            device_id={"tensor": nxt}, device_id_type=MESH)

    def step(self, s):
        n, lag = self.n, self.lag
        for stream in (0, 1):
            pos, fwd, bwd = self.side(stream)
            c = s - lag * pos

            @pl.when((c >= 0) & (c < self.chunks))
            def _():
                where = self.rows(stream, c)
                slot = self.got.at[stream, c]

                def summed():
                    self.toward(stream, c, fwd, slot).wait_recv()
                    return (
                        self.part[where, :].astype(jnp.float32) + self.got[stream, c].astype(jnp.float32)
                    ).astype(self.out.dtype)

                @pl.when(pos == 0)
                def _():
                    self.toward(stream, c, fwd, self.part.at[where]).start()

                @pl.when((pos > 0) & (pos < n - 1))
                def _():
                    self.got[stream, c] = summed()
                    self.toward(stream, c, fwd, slot).start()

                @pl.when(pos == n - 1)
                def _():
                    self.out[where, :] = summed()
                    self.back(stream, c, bwd).start()
            d = s - lag * (n - 1) - lag * (n - 1 - pos)

            @pl.when((d >= 0) & (d < self.chunks) & (pos < n - 1))
            def _():
                self.back(stream, d, bwd).wait_recv()

                @pl.when(pos > 0)
                def _():
                    self.back(stream, d, bwd).start()

    def drain(self):
        def one(c, carry):
            for stream in (0, 1):
                pos, fwd, bwd = self.side(stream)

                @pl.when(pos < self.n - 1)
                def _():
                    self.toward(stream, c, fwd, self.got.at[stream, c]).wait_send()

                @pl.when(pos > 0)
                def _():
                    self.back(stream, c, bwd).wait_send()
            return carry

        lax.fori_loop(0, self.chunks, one, 0)


def greet(n):
    me = lax.axis_index("tensor")
    barrier = pltpu.get_barrier_semaphore()

    @pl.when(me > 0)
    def _():
        pl.semaphore_signal(barrier, inc=1, device_id={"tensor": me - 1}, device_id_type=MESH)

    @pl.when(me < n - 1)
    def _():
        pl.semaphore_signal(barrier, inc=1, device_id={"tensor": me + 1}, device_id_type=MESH)

    @pl.when((me > 0) & (me < n - 1))
    def _():
        pl.semaphore_wait(barrier, 2)

    @pl.when((me == 0) | (me == n - 1))
    def _():
        pl.semaphore_wait(barrier, 1)


def line_scratch(chunks, rc, width):
    return [pltpu.VMEM((2, chunks, rc, width), jnp.bfloat16)] + [pltpu.SemaphoreType.DMA((2, chunks))] * 4


def line_kernel(n, chunks, lag, count, *refs):
    parts, outs, scratch = refs[:count], refs[count:2 * count], refs[2 * count:]
    rc = parts[0].shape[0] // (2 * chunks)
    lines = [
        Line(n, chunks, rc, lag, parts[k], scratch[5 * k], outs[k], scratch[5 * k + 1:5 * k + 5])
        for k in range(count)
    ]
    greet(n)

    def step(s, carry):
        for k, line in enumerate(lines):
            line.step(s - k * chunks)
        return carry

    lax.fori_loop(0, lines[0].steps + (count - 1) * chunks, step, 0)
    for line in lines:
        line.drain()


def line_reduce(parts, n, chunks, cid, lag=2):
    rows, width = parts[0].shape
    count = len(parts)
    rc = rows // (2 * chunks)
    scratch = []
    for _ in parts:
        scratch += line_scratch(chunks, rc, width)
    vmem = pl.BlockSpec(memory_space=pltpu.VMEM)
    return pl.pallas_call(
        functools.partial(line_kernel, n, chunks, lag, count),
        out_shape=tuple(jax.ShapeDtypeStruct((rows, width), jnp.bfloat16) for _ in parts),
        in_specs=[vmem] * count,
        out_specs=(vmem,) * count,
        scratch_shapes=scratch,
        compiler_params=pltpu.CompilerParams(collective_id=cid, has_side_effects=True, vmem_limit_bytes=40 << 20),
        cost_estimate=pl.CostEstimate(flops=rows * width * 2 * count, bytes_accessed=rows * width * 120 * count,
                                      transcendentals=0),
    )(*parts)


def dot_rows(left, right):
    return lax.dot_general(left, right, (((0,), (0,)), ((), ())), preferred_element_type=jnp.float32)


def ff_kernel(n, chunks, lag, eps, branch, gain, x, cot_hbm, w_hbm,
              feed_hbm, middle_hbm, low_hbm, gain_out, grads_hbm,
              got, sa, ra, sg, rg, two_sum, two_part, weight, cot, normed, hidden, gg, feed,
              middle_stage, low_stage, unit_stage, w_sem, cot_sem, feed_sem, stage_sem, grad_sem):
    rows, width = branch.shape
    ff = hidden.shape[1]
    rc = rows // (2 * chunks)
    per = 8
    offset = per - 1
    half = rows // 2
    hb = per * rc
    block = 2 * hb
    blocks = chunks // per
    line = Line(n, chunks, rc, lag, two_part, got, two_sum, (sa, ra, sg, rg))
    landed = 2 * lag * (n - 1) + offset
    tile = 256
    full, rest = ff // tile, ff % tile
    wide = width // tile

    groups = []
    for g, (begin, end) in enumerate(((0, tile), (tile, 2 * tile), (2 * tile, ff))):
        groups.append([
            pltpu.make_async_copy(w_hbm.at[:, pl.ds(t * ff + begin, end - begin)],
                                  weight.at[:, pl.ds(t * ff + begin, end - begin)], w_sem.at[g, t])
            for t in range(3)
        ])
    for copy in sum(groups, []):
        copy.start()

    def natural(k, b):
        return pl.ds(pl.multiple_of(k * half + b * hb, hb), hb)

    def blocked(k, b):
        return pl.ds(pl.multiple_of(b * block + k * hb, hb), hb)

    def load_cot(b):
        return [pltpu.make_async_copy(cot_hbm.at[natural(k, b)], cot.at[blocked(k, b)], cot_sem.at[b, k])
                for k in (0, 1)]

    def save_feed(b):
        return [pltpu.make_async_copy(feed.at[pl.ds(k * hb, hb)], feed_hbm.at[natural(k, b)], feed_sem.at[k])
                for k in (0, 1)]

    def save_rows(d):
        copies = []
        for k in (0, 1):
            where = line.rows(k, d)
            copies.append(pltpu.make_async_copy(middle_stage.at[k], middle_hbm.at[where], stage_sem.at[0, k]))
            copies.append(pltpu.make_async_copy(low_stage.at[k], low_hbm.at[where], stage_sem.at[1, k]))
        return copies

    def save_units(w):
        return [pltpu.make_async_copy(unit_stage, grads_hbm.at[pl.ds(pl.multiple_of(w * tile, tile), tile)], grad_sem.at[0])]

    def start(copies):
        for copy in copies:
            copy.start()

    def wait(copies):
        for copy in copies:
            copy.wait()

    for b in range(blocks):
        start(load_cot(b))
    gain_out[...] = jnp.zeros_like(gain_out)
    greet(n)

    def unit_rows(where):
        middle = x[where, :].astype(jnp.float32) + branch[where, :].astype(jnp.float32)
        inverse = lax.rsqrt(jnp.mean(middle * middle, axis=-1, keepdims=True) + eps)
        return middle * inverse, inverse

    def normalize(b):
        def some(r, carry):
            for k in (0, 1):
                where = pl.ds(pl.multiple_of(k * half + b * hb + r * rc, rc), rc)
                at = pl.ds(pl.multiple_of(b * block + k * hb + r * rc, rc), rc)
                normed[at, :] = (unit_rows(where)[0] * gain[...]).astype(jnp.bfloat16)
            return carry

        lax.fori_loop(0, per, some, 0)

    def step(s, carry):
        line.step(s - offset)
        b = s // per
        phase = s - b * per
        live = s < chunks
        mine = pl.ds(pl.multiple_of(b * block, block), block)

        def units(at, count):
            columns = pl.ds(at, count)
            second = pl.ds(pl.multiple_of(ff + at, 128), count)
            third = pl.ds(pl.multiple_of(2 * ff + at, 128), count)
            gate = dot_n(normed[mine, :], weight[:, columns])
            up = dot_n(normed[mine, :], weight[:, second])
            grad_hidden = dot_n(cot[mine, :], weight[:, third])
            sg_gate = 1.0 / (1.0 + jnp.exp(-gate))
            silu = gate * sg_gate
            hidden[mine, columns] = (silu * up).astype(jnp.bfloat16)
            gg[mine, columns] = (grad_hidden * up * sg_gate * (1.0 + gate * (1.0 - sg_gate))).astype(jnp.bfloat16)
            gg[mine, second] = (grad_hidden * silu).astype(jnp.bfloat16)

        def unit_tile(t, c):
            for g in range(3):
                @pl.when((b == 0) & (t == g))
                def _():
                    wait(groups[g])
            units(pl.multiple_of(t * tile, tile), tile)
            return c

        @pl.when(live & (phase == 0))
        def _():
            normalize(b)
            wait(load_cot(b))

        @pl.when(live & (phase < 3))
        def _():
            lax.fori_loop(jnp.maximum(2 * phase - 1, 0), jnp.minimum(2 * phase + 1, full), unit_tile, 0)

        @pl.when(live & (phase == 3))
        def _():
            if rest:
                units(full * tile, rest)

            @pl.when(b > 0)
            def _():
                wait(save_feed(b - 1))

        @pl.when(live & ((phase == 3) | (phase == 4)))
        def _():
            def feed_tile(t, c):
                columns = pl.ds(pl.multiple_of(t * 2 * tile, 2 * tile), 2 * tile)
                feed[:, columns] = dot_t(hidden[mine, :], weight[columns, 2 * ff:]).astype(jnp.bfloat16)
                return c

            lax.fori_loop((phase - 3) * (wide // 4), (phase - 2) * (wide // 4), feed_tile, 0)

            @pl.when(phase == 4)
            def _():
                start(save_feed(b))

        @pl.when(live & ((phase == 5) | (phase == 6)))
        def _():
            def two_tile(t, c):
                at = pl.ds(pl.multiple_of(t * 2 * tile, 2 * tile), 2 * tile)
                value = dot_t(gg[mine, :], weight[at, :2 * ff]).astype(jnp.bfloat16)
                for k in (0, 1):
                    two_part[natural(k, b), at] = value[k * hb:(k + 1) * hb]
                return c

            lax.fori_loop((phase - 5) * (wide // 4), (phase - 4) * (wide // 4), two_tile, 0)

        d = s - landed

        @pl.when(d >= 0)
        def _():
            @pl.when(d > 0)
            def _():
                wait(save_rows(d - 1))
            for k in (0, 1):
                where = line.rows(k, d)
                at = pl.ds(pl.multiple_of((d // per) * block + k * hb + (d - (d // per) * per) * rc, rc), rc)
                pieces = [pl.ds(c * tile, tile) for c in range(wide)]

                def middle_at(c):
                    return x[where, c].astype(jnp.float32) + branch[where, c].astype(jnp.float32)

                def folded(value):
                    return value[:, :128] + value[:, 128:]

                total = jnp.zeros((rc, 128), jnp.float32)
                for c in pieces:
                    middle = middle_at(c)
                    total = total + folded(middle * middle)
                inverse = lax.rsqrt(jnp.sum(total, axis=-1, keepdims=True) * (1.0 / width) + eps)
                total = jnp.zeros((rc, 128), jnp.float32)
                for c in pieces:
                    product = two_sum[where, c].astype(jnp.float32) * (middle_at(c) * inverse)
                    gain_out[:, c] += jnp.sum(product, axis=0, keepdims=True)
                    total = total + folded(product * gain[:, c])
                inner = jnp.sum(total, axis=-1, keepdims=True) * (1.0 / width)
                for c in pieces:
                    scaled = two_sum[where, c].astype(jnp.float32) * gain[:, c]
                    value = cot[at, c].astype(jnp.float32) + inverse * (scaled - middle_at(c) * inverse * inner)
                    middle_stage[k, :, c] = value
                    low_stage[k, :, c] = value.astype(jnp.bfloat16)
            start(save_rows(d))

        late = s - chunks
        w = late // 2

        @pl.when((late >= 0) & (late == 2 * w) & (w < wide))
        def _():
            @pl.when(w > 0)
            def _():
                wait(save_units(w - 1))
            columns = pl.ds(pl.multiple_of(w * tile, tile), tile)
            left = normed[:, columns]
            for t in (0, 1):
                unit_stage[:, t * ff:(t + 1) * ff] = dot_rows(left, gg[:, t * ff:(t + 1) * ff]).astype(jnp.bfloat16)
            unit_stage[:, 2 * ff:] = dot_rows(cot[:, columns], hidden[...]).astype(jnp.bfloat16)
            start(save_units(w))
        return carry

    lax.fori_loop(0, offset + line.steps, step, 0)
    line.drain()
    wait(save_feed(blocks - 1))
    wait(save_rows(chunks - 1))
    wait(save_units(wide - 1))


def feed_forward(branch, gain, x, cot, weight, n, cid, chunks=32, lag=2):
    rows, width = branch.shape
    ff = weight.shape[1] // 3
    rc = rows // (2 * chunks)
    block = 16 * rc
    blocks = chunks // 8
    low = jnp.bfloat16
    vmem = pl.BlockSpec(memory_space=pltpu.VMEM)
    hbm = pl.BlockSpec(memory_space=pl.ANY)
    dma = pltpu.SemaphoreType.DMA
    shape = jax.ShapeDtypeStruct
    return pl.pallas_call(
        functools.partial(ff_kernel, n, chunks, lag, norm_eps),
        out_shape=(
            shape((rows, width), low), shape((rows, width), jnp.float32), shape((rows, width), low),
            shape((1, width), jnp.float32), shape((width, 3 * ff), low),
        ),
        in_specs=[vmem, vmem, vmem, hbm, hbm],
        out_specs=(hbm, hbm, hbm, vmem, hbm),
        scratch_shapes=line_scratch(chunks, rc, width) + [
            pltpu.VMEM((rows, width), low),
            pltpu.VMEM((rows, width), low),
            pltpu.VMEM((width, 3 * ff), low),
            pltpu.VMEM((rows, width), low),
            pltpu.VMEM((rows, width), low),
            pltpu.VMEM((rows, ff), low),
            pltpu.VMEM((rows, 2 * ff), low),
            pltpu.VMEM((block, width), low),
            pltpu.VMEM((2, rc, width), jnp.float32),
            pltpu.VMEM((2, rc, width), low),
            pltpu.VMEM((256, 3 * ff), low),
            dma((3, 3)), dma((blocks, 2)), dma((2,)), dma((2, 2)), dma((1,)),
        ],
        compiler_params=pltpu.CompilerParams(collective_id=cid, has_side_effects=True, vmem_limit_bytes=63 << 20),
        cost_estimate=pl.CostEstimate(flops=18 * rows * width * ff, bytes_accessed=rows * width * 150,
                                      transcendentals=rows * ff),
    )(branch, gain, x, cot, weight)


def head_kernel(n, m, chunks, lag, eps, size, pairs,
                x, gain_part, query_own, keyval_own, out_own, cos_ref, sin_ref, seg_col_ref, seg_row_ref,
                gateup_hbm, down_hbm,
                branch, mix_ref, q_ref, k_ref, v_ref, lse_ref, qkv_w, out_w, gain, ff_hbm,
                got, sa, ra, sg, rg, part, normed, raw, bias, scores, v_turned, got_gain,
                gateup_own, down_own, ff_own,
                send_gain, recv_gain, send_direct, send_forward, recv_w, own_sem, save_sem,
                send_ff, pass_ff, recv_ff):
    rows, width = x.shape
    q_width = pairs * 128
    z = lax.axis_index("tensor")
    dp = lax.axis_index("dp")
    share = width // m
    chips = m // 2
    chip, core = dp // 2, dp % 2
    rc = rows // (2 * chunks)
    per = size // (2 * rc)
    hb = size // 2
    blocks = rows // size
    tile = 256
    wide = width // tile
    low_lanes, first_half = lane_tests(size)
    low_rows = lax.broadcasted_iota(jnp.int32, (128, size), 0) < 64
    wholes = (qkv_w, out_w)
    ff = down_own.shape[0]
    piece = 32
    pieces = share // piece
    spacing = 40 // pieces
    owned = (
        pltpu.make_async_copy(gateup_hbm, gateup_own, own_sem.at[0]),
        pltpu.make_async_copy(down_hbm, down_own, own_sem.at[1]),
    )
    for copy in owned:
        copy.start()

    def ascending(stream, c):
        b = c // per
        return b * size + stream * hb + (c - b * per) * rc

    line = Line(n, chunks, rc, lag, part, got, branch, (sa, ra, sg, rg), ascending)

    def shard_rows(s):
        return pl.ds(pl.multiple_of(s * share, share), share)

    def direct(kind, k):
        peer = 2 * lax.rem(chip + k, chips) + core
        return pltpu.make_async_remote_copy(
            src_ref=wholes[kind].at[shard_rows(dp)], dst_ref=wholes[kind].at[shard_rows(dp)], send_sem=send_direct.at[kind, k],
            recv_sem=recv_w.at[kind, dp], device_id={"dp": peer}, device_id_type=MESH)

    def forward(kind, c, side):
        shard = 2 * c + side
        where = shard_rows(shard)
        return pltpu.make_async_remote_copy(
            src_ref=wholes[kind].at[where], dst_ref=wholes[kind].at[where], send_sem=send_forward.at[kind, c],
            recv_sem=recv_w.at[kind, shard], device_id={"dp": 2 * chip + 1 - core}, device_id_type=MESH)

    def piece_rows(shard, p):
        return pl.ds(pl.multiple_of(shard * share + p * piece, piece), piece)

    def own_piece(p):
        return ff_own.at[pl.ds(pl.multiple_of(p * piece, piece), piece)]

    def send_piece(k, p):
        peer = 2 * lax.rem(chip + k, chips) + core
        return pltpu.make_async_remote_copy(
            src_ref=own_piece(p), dst_ref=ff_hbm.at[piece_rows(dp, p)], send_sem=send_ff.at[k, p],
            recv_sem=recv_ff.at[dp, p], device_id={"dp": peer}, device_id_type=MESH)

    def pass_piece(c, side, p, src=None):
        shard = 2 * c + side
        where = ff_hbm.at[piece_rows(shard, p)]
        return pltpu.make_async_remote_copy(
            src_ref=where if src is None else src, dst_ref=where, send_sem=pass_ff.at[c, p],
            recv_sem=recv_ff.at[shard, p], device_id={"dp": 2 * chip + 1 - core}, device_id_type=MESH)

    def save_own():
        return pltpu.make_async_copy(ff_own, ff_hbm.at[shard_rows(dp)], save_sem)

    def send_gains(k, sender):
        return pltpu.make_async_remote_copy(
            src_ref=gain_part, dst_ref=got_gain.at[sender], send_sem=send_gain.at[k], recv_sem=recv_gain.at[sender],
            device_id={"dp": lax.rem(dp + k, m)}, device_id_type=MESH)

    barrier = pltpu.get_barrier_semaphore()

    @pl.when(z > 0)
    def _():
        pl.semaphore_signal(barrier, inc=1, device_id={"tensor": z - 1}, device_id_type=MESH)

    @pl.when(z < n - 1)
    def _():
        pl.semaphore_signal(barrier, inc=1, device_id={"tensor": z + 1}, device_id_type=MESH)

    for k in range(1, m):
        pl.semaphore_signal(barrier, inc=1, device_id={"dp": lax.rem(dp + k, m)}, device_id_type=MESH)

    qkv_w[shard_rows(dp), :q_width] = query_own[...].astype(jnp.bfloat16)
    both_own = jnp.concatenate([keyval_own[0], keyval_own[1]], axis=0)
    qkv_w[shard_rows(dp), q_width:] = both_own.T.astype(jnp.bfloat16)
    for t in range(q_width // 128):
        out_w[shard_rows(dp), t * 128:(t + 1) * 128] = out_own[t * 128:(t + 1) * 128, :].T.astype(jnp.bfloat16)
    got_gain[dp] = gain_part[...]

    @pl.when((z > 0) & (z < n - 1))
    def _():
        pl.semaphore_wait(barrier, m + 1)

    @pl.when((z == 0) | (z == n - 1))
    def _():
        pl.semaphore_wait(barrier, m)

    for k in range(1, m):
        send_gains(k, dp).start()
    for kind in (0, 1):
        for k in range(1, chips):
            direct(kind, k).start()
        forward(kind, chip, core).start()
    for k in range(1, m):
        send_gains(k, lax.rem(dp + m - k, m)).wait_recv()
    whole = got_gain[0]
    for k in range(1, m):
        whole = whole + got_gain[k]
    gain[...] = whole.astype(jnp.bfloat16).astype(jnp.float32)

    def norm_rows(r, carry):
        where = pl.ds(pl.multiple_of(r * rc, rc), rc)
        values = x[where, :].astype(jnp.float32)
        inverse = lax.rsqrt(jnp.mean(values * values, axis=-1, keepdims=True) + eps)
        normed[where, :] = (values * inverse * gain[0:1, :]).astype(jnp.bfloat16)
        return carry

    lax.fori_loop(0, rows // rc, norm_rows, 0)
    for copy in owned:
        copy.wait()

    def own_rows(r, carry):
        where = pl.ds(pl.multiple_of(r * piece, piece), piece)
        for t in (0, 1):
            ff_own[where, t * ff:(t + 1) * ff] = gateup_own[t, where, :].astype(jnp.bfloat16)
        return carry

    lax.fori_loop(0, pieces, own_rows, 0)

    def own_columns(t, carry):
        at = pl.ds(pl.multiple_of(2 * ff + t * 128, 128), 128)
        ff_own[:, at] = down_own[pl.ds(pl.multiple_of(t * 128, 128), 128), :].T.astype(jnp.bfloat16)
        return carry

    lax.fori_loop(0, ff // 128, own_columns, 0)
    save_own().start()

    def gather(kind):
        for k in range(1, chips):
            c = lax.rem(chip + chips - k, chips)
            forward(kind, c, core).wait_recv()
            forward(kind, c, core).start()
        for c in range(chips):
            forward(kind, c, 1 - core).wait_recv()

    gather(0)
    for p in range(min(2, pieces)):
        for k in range(1, chips):
            send_piece(k, p).start()

    def prepare(i, carry):
        where = pl.ds(pl.multiple_of(i * size, size), size)
        raw[...] = dot_n(normed[where, :], qkv_w[...])
        cosines, sines = cos_ref[where, :], sin_ref[where, :]
        for hp in range(pairs):
            values = raw[:, hp * 128:(hp + 1) * 128]
            turned = values * cosines + swap_halves(values, first_half) * sines
            q_ref[where, hp * 128:(hp + 1) * 128] = (
                turned.astype(jnp.bfloat16).astype(jnp.float32) * 0.125).astype(jnp.bfloat16)
        both = raw[:, q_width:q_width + 128]
        other = pltpu.roll(both, 64, 1)
        keys = jnp.where(low_lanes, both, other)
        k_ref[where, :] = (keys * cosines + swap_halves(keys, first_half) * sines).astype(jnp.bfloat16)
        values = jnp.where(low_lanes, other, both)
        v_ref[where, :] = values.astype(jnp.bfloat16)
        v_turned[i] = values.T.astype(jnp.bfloat16)
        return carry

    lax.fori_loop(0, blocks, prepare, 0)
    gather(1)

    def attend(i, hp):
        where = pl.ds(pl.multiple_of(i * size, size), size)
        columns = pl.ds(pl.multiple_of(hp * 128, 128), 128)
        stacked = stack_pair(q_ref[where, columns], low_lanes)

        def score(j, top):
            keys = k_ref[pl.ds(pl.multiple_of(j * size, size), size), :]
            b = bias[j]
            s = dot_t(keys, stacked) + jnp.concatenate([b, b], axis=1)
            scores[j] = s
            return jnp.maximum(top, jnp.max(s, axis=0, keepdims=True))

        top = lax.fori_loop(0, i + 1, score, jnp.full((1, 2 * size), -jnp.inf, jnp.float32))

        def mix(j, c):
            total, acc = c
            p = jnp.exp(scores[j] - top)
            total = total + jnp.sum(p, axis=0, keepdims=True)
            return total, acc + dot_n(v_turned[j], p.astype(jnp.bfloat16))

        total, acc = lax.fori_loop(0, i + 1, mix, (
            jnp.zeros((1, 2 * size), jnp.float32), jnp.zeros((128, 2 * size), jnp.float32)))
        lse_ref[i, hp] = top + jnp.log(total)
        acc = acc / total
        acc = jnp.where(low_rows, acc[:, :size], acc[:, size:])
        mix_ref[where, columns] = acc.T.astype(jnp.bfloat16)

    def step(s, carry):
        line.step(s - per)
        p_send = (s - 1) // spacing + 2
        p_pass = (s - 4) // spacing

        @pl.when((s >= 1) & ((p_send - 2) * spacing == s - 1) & (p_send < pieces))
        def _():
            for k in range(1, chips):
                send_piece(k, p_send).start()

        @pl.when((s >= 4) & (p_pass * spacing == s - 4) & (p_pass < pieces))
        def _():
            pass_piece(chip, core, p_pass, own_piece(p_pass)).start()
            for k in range(1, chips):
                c = lax.rem(chip + chips - k, chips)
                pass_piece(c, core, p_pass).wait_recv()
                pass_piece(c, core, p_pass).start()

        i = s // per
        hp = s - i * per
        live = s < blocks * per

        @pl.when(live & (hp == 0))
        def _():
            def fill(j, c):
                bias[j] = block_bias(seg_col_ref, seg_row_ref, i, j, size)
                return c

            lax.fori_loop(0, i + 1, fill, 0)

        @pl.when(live)
        def _():
            def each(h, c):
                attend(i, h)
                return c

            lax.fori_loop(hp * pairs // per, (hp + 1) * pairs // per, each, 0)

        @pl.when(live & (hp == per - 1))
        def _():
            where = pl.ds(pl.multiple_of(i * size, size), size)

            def part_tile(t, c):
                at = pl.ds(pl.multiple_of(t * tile, tile), tile)
                part[where, at] = dot_t(mix_ref[where, :], out_w[at, :]).astype(jnp.bfloat16)
                return c

            lax.fori_loop(0, wide, part_tile, 0)
        return carry

    lax.fori_loop(0, per + line.steps, step, 0)
    line.drain()
    save_own().wait()

    def settle(p, carry):
        for k in range(1, chips):
            send_piece(k, p).wait_send()
        for c in range(chips):
            pass_piece(c, core, p).wait_send()
            pass_piece(c, 1 - core, p).wait_recv()
        return carry

    lax.fori_loop(0, pieces, settle, 0)
    for k in range(1, m):
        send_gains(k, dp).wait_send()
    for kind in (0, 1):
        for k in range(1, chips):
            direct(kind, k).wait_send()
        for c in range(chips):
            forward(kind, c, core).wait_send()


def attention_head(x, gain_part, query, keyval, out, cosines, sines, seg_col, seg_row, gateup, down, n, m, cid, size,
                   chunks=32, lag=2):
    rows, width = x.shape
    q_width = query.shape[1]
    share, ff = width // m, down.shape[0]
    pairs = q_width // 128
    rc = rows // (2 * chunks)
    blocks = rows // size
    chips = m // 2
    low = jnp.bfloat16
    vmem = pl.BlockSpec(memory_space=pltpu.VMEM)
    hbm = pl.BlockSpec(memory_space=pl.ANY)
    dma = pltpu.SemaphoreType.DMA
    shape = jax.ShapeDtypeStruct
    return pl.pallas_call(
        functools.partial(head_kernel, n, m, chunks, lag, norm_eps, size, pairs),
        out_shape=(
            shape((rows, width), low), shape((rows, q_width), low), shape((rows, q_width), low),
            shape((rows, 128), low), shape((rows, 128), low), shape((blocks, pairs, 1, 2 * size), jnp.float32),
            shape((width, q_width + 128), low), shape((width, q_width), low), shape((2, width), jnp.float32),
            shape((width, 3 * ff), low),
        ),
        in_specs=[vmem] * 9 + [hbm] * 2,
        out_specs=(vmem,) * 9 + (hbm,),
        scratch_shapes=line_scratch(chunks, rc, width) + [
            pltpu.VMEM((rows, width), low),
            pltpu.VMEM((rows, width), low),
            pltpu.VMEM((size, q_width + 128), jnp.float32),
            pltpu.VMEM((blocks, size, size), jnp.float32),
            pltpu.VMEM((blocks, size, 2 * size), jnp.float32),
            pltpu.VMEM((blocks, 128, size), low),
            pltpu.VMEM((m, 2, width), jnp.float32),
            pltpu.VMEM(gateup.shape, jnp.float32),
            pltpu.VMEM(down.shape, jnp.float32),
            pltpu.VMEM((share, 3 * ff), low),
            dma((m,)), dma((m,)), dma((2, chips)), dma((2, chips)), dma((2, m)), dma((2,)), dma,
            dma((chips, share // 32)), dma((chips, share // 32)), dma((m, share // 32)),
        ],
        compiler_params=pltpu.CompilerParams(collective_id=cid, has_side_effects=True, vmem_limit_bytes=56 << 20),
        cost_estimate=pl.CostEstimate(flops=20 * rows * width * q_width, bytes_accessed=rows * width * 170,
                                      transcendentals=rows * rows * pairs),
    )(x, gain_part, query, keyval, out, cosines, sines, seg_col, seg_row, gateup, down)


def back_kernel(n, m, chunks, lag, eps, size, pairs,
                feed_part, grad_low, gain, q_ref, k_ref, v_ref, mix_ref, lse_ref, cos_ref, sin_ref,
                seg_col_ref, seg_row_ref, out_w, x_hbm, qkv_hbm, branch_hbm, middle_hbm,
                layer_hbm, input_hbm, gain_out, reduced,
                got2, sa2, ra2, sg2, rg2, got4, sa4, ra4, sg4, rg4, feed_sum, part, grad_sum,
                x, qkv_w, normed, grad_mix, bias, k_turned, grad_k, grad_v, grad_qkv, send, recv,
                branch_stage, layer_stage, middle_stage, input_stage,
                w_sem, branch_sem, middle_sem, layer_sem, input_sem, send_sem, recv_sem):
    rows, width = feed_part.shape
    q_width = pairs * 128
    z = lax.axis_index("tensor")
    dp = lax.axis_index("dp")
    rc = rows // (2 * chunks)
    per = size // (2 * rc)
    hb = size // 2
    blocks = rows // size
    tile = 256
    wide = width // tile
    share = width // m
    owners = tile // share
    lead = 2 * lag * (n - 1)
    low_lanes, first_half = lane_tests(size)
    low_rows = lax.broadcasted_iota(jnp.int32, (128, size), 0) < 64

    def descending(stream, c):
        b = c // per
        return (blocks - 1 - b) * size + stream * hb + (c - b * per) * rc

    two = Line(n, chunks, rc, lag, feed_part, got2, feed_sum, (sa2, ra2, sg2, rg2))
    four = Line(n, chunks, rc, lag, part, got4, grad_sum, (sa4, ra4, sg4, rg4), descending)
    loads = (
        pltpu.make_async_copy(x_hbm, x, w_sem.at[0]),
        pltpu.make_async_copy(qkv_hbm, qkv_w, w_sem.at[1]),
    )
    for copy in loads:
        copy.start()

    def start(copies):
        for copy in copies:
            copy.start()

    def wait(copies):
        for copy in copies:
            copy.wait()

    def load_branch(d, slot):
        return [pltpu.make_async_copy(branch_hbm.at[two.rows(k, d)], branch_stage.at[slot, k], branch_sem.at[slot, k])
                for k in (0, 1)]

    def load_middle(d, slot):
        return [pltpu.make_async_copy(middle_hbm.at[four.rows(k, d)], middle_stage.at[slot, k], middle_sem.at[slot, k])
                for k in (0, 1)]

    def save_layer(d):
        return [pltpu.make_async_copy(layer_stage.at[k], layer_hbm.at[two.rows(k, d)], layer_sem.at[k]) for k in (0, 1)]

    def save_input(d):
        return [pltpu.make_async_copy(input_stage.at[k], input_hbm.at[four.rows(k, d)], input_sem.at[k]) for k in (0, 1)]

    def to_owner(w, o):
        owner = w * owners + o
        return pltpu.make_async_remote_copy(
            src_ref=send.at[w, pl.ds(o * share, share)], dst_ref=recv.at[dp], send_sem=send_sem.at[owner],
            recv_sem=recv_sem.at[dp], device_id={"dp": owner}, device_id_type=MESH)

    gain_out[...] = jnp.zeros_like(gain_out)

    def prepare(i, carry):
        at = pl.ds(pl.multiple_of(i * size, size), size)
        k_turned[i] = k_ref[at, :].astype(jnp.float32).T.astype(jnp.bfloat16)
        grad_k[i] = jnp.zeros((size, 128), jnp.float32)
        grad_v[i] = jnp.zeros((size, 128), jnp.float32)
        return carry

    lax.fori_loop(0, blocks, prepare, 0)

    barrier = pltpu.get_barrier_semaphore()

    @pl.when(z > 0)
    def _():
        pl.semaphore_signal(barrier, inc=1, device_id={"tensor": z - 1}, device_id_type=MESH)

    @pl.when(z < n - 1)
    def _():
        pl.semaphore_signal(barrier, inc=1, device_id={"tensor": z + 1}, device_id_type=MESH)

    for k in range(1, m):
        pl.semaphore_signal(barrier, inc=1, device_id={"dp": lax.rem(dp + k, m)}, device_id_type=MESH)

    @pl.when((z > 0) & (z < n - 1))
    def _():
        pl.semaphore_wait(barrier, m + 1)

    @pl.when((z == 0) | (z == n - 1))
    def _():
        pl.semaphore_wait(barrier, m)

    def unit_rows(where):
        values = x[where, :].astype(jnp.float32)
        inverse = lax.rsqrt(jnp.mean(values * values, axis=-1, keepdims=True) + eps)
        return values * inverse, inverse

    def attend(i, hp):
        at_rows = pl.ds(pl.multiple_of(i * size, size), size)
        columns = pl.ds(pl.multiple_of(hp * 128, 128), 128)
        stacked = stack_pair(q_ref[at_rows, columns], low_lanes)
        grad_pair = grad_mix[:, columns]
        grad_stacked = stack_pair(grad_pair, low_lanes)
        product = (grad_pair.astype(jnp.float32) * mix_ref[at_rows, columns].astype(jnp.float32)).T
        spread = jnp.concatenate([
            jnp.sum(product[:64], axis=0, keepdims=True), jnp.sum(product[64:], axis=0, keepdims=True)], axis=1)
        logsum = lse_ref[i, hp]

        def piece(j, acc):
            at = pl.ds(pl.multiple_of(j * size, size), size)
            b = bias[j]
            s = dot_t(k_ref[at, :], stacked) + jnp.concatenate([b, b], axis=1)
            p = jnp.exp(s - logsum)
            grad_p = dot_t(v_ref[at, :], grad_stacked)
            grad_s = (p * (grad_p - spread)).astype(jnp.bfloat16)
            grad_v[j] += dot_n(p.astype(jnp.bfloat16), grad_stacked)
            grad_k[j] += dot_n(grad_s, stacked)
            return acc + dot_n(k_turned[j], grad_s)

        acc = lax.fori_loop(0, i + 1, piece, jnp.zeros((128, 2 * size), jnp.float32))
        acc = jnp.where(low_rows, acc[:, :size], acc[:, size:]).T * 0.125
        turned = acc * cos_ref[at_rows, :] - swap_halves(acc, first_half) * sin_ref[at_rows, :]
        grad_qkv[at_rows, columns] = turned.astype(jnp.bfloat16)

    def step(s, carry):
        two.step(s)
        four.step(s - per)
        b = s // per
        hp = s - b * per
        i = blocks - 1 - b
        live = s < blocks * per
        at_rows = pl.ds(pl.multiple_of(i * size, size), size)

        @pl.when(s == 0)
        def _():
            wait(loads)

        @pl.when(live & (hp == 0))
        def _():
            grad_mix[...] = dot_n(grad_low[at_rows, :], out_w[...]).astype(jnp.bfloat16)

            def fill(j, c):
                bias[j] = block_bias(seg_col_ref, seg_row_ref, i, j, size)
                return c

            lax.fori_loop(0, i + 1, fill, 0)

        @pl.when(live)
        def _():
            def each(h, c):
                attend(i, h)
                return c

            lax.fori_loop(hp * pairs // per, (hp + 1) * pairs // per, each, 0)

            def some(r, c):
                at = pl.ds(pl.multiple_of(s * 2 * rc + r * rc, rc), rc)
                normed[at, :] = (unit_rows(at)[0] * gain[...]).astype(jnp.bfloat16)
                return c

            lax.fori_loop(0, 2, some, 0)

        @pl.when(live & (hp == per - 1))
        def _():
            cosines, sines = cos_ref[at_rows, :], sin_ref[at_rows, :]
            dk = grad_k[i] + pltpu.roll(grad_k[i], 64, 1)
            dk = dk * cosines - swap_halves(dk, first_half) * sines
            dv = grad_v[i] + pltpu.roll(grad_v[i], 64, 1)
            grad_qkv[at_rows, q_width:] = jnp.where(low_lanes, dk, dv).astype(jnp.bfloat16)

            def part_tile(t, c):
                at = pl.ds(pl.multiple_of(t * tile, tile), tile)
                part[at_rows, at] = dot_t(grad_qkv[at_rows, :], qkv_w[at, :]).astype(jnp.bfloat16)
                return c

            lax.fori_loop(0, wide, part_tile, 0)

        w = s - blocks * per

        @pl.when((w >= 0) & (w < wide))
        def _():
            columns = pl.ds(pl.multiple_of(w * tile, tile), tile)
            send[w, :, :q_width + 128] = dot_rows(normed[:, columns], grad_qkv[...]).astype(jnp.bfloat16)
            send[w, :, q_width + 128:] = dot_rows(grad_low[:, columns], mix_ref[...]).astype(jnp.bfloat16)
            for o in range(owners):
                owner = w * owners + o

                @pl.when(owner != dp)
                def _():
                    to_owner(w, o).start()

                @pl.when(owner == dp)
                def _():
                    recv[dp] = send[w, o * share:(o + 1) * share, :]

        e = s - lead + 1

        @pl.when((e >= 0) & (e < chunks))
        def _():
            start(load_branch(e, e % 2))

        d = s - lead

        @pl.when((d >= 0) & (d < chunks))
        def _():
            wait(load_branch(d, d % 2))

            @pl.when(d > 0)
            def _():
                wait(save_layer(d - 1))
            for k in (0, 1):
                where = two.rows(k, d)
                layer_stage[k] = (
                    x[where, :].astype(jnp.float32) + branch_stage[d % 2, k].astype(jnp.float32)
                    + feed_sum[where, :].astype(jnp.float32)
                ).astype(jnp.bfloat16)
            start(save_layer(d))

        e4 = s - lead - per + 1

        @pl.when((e4 >= 0) & (e4 < chunks))
        def _():
            start(load_middle(e4, e4 % 2))

        d4 = s - lead - per

        @pl.when(d4 >= 0)
        def _():
            wait(load_middle(d4, d4 % 2))

            @pl.when(d4 > 0)
            def _():
                wait(save_input(d4 - 1))
            for k in (0, 1):
                where = four.rows(k, d4)
                unit, inverse = unit_rows(where)
                grad = grad_sum[where, :].astype(jnp.float32)
                scaled = grad * gain[...]
                inner = jnp.mean(scaled * unit, axis=-1, keepdims=True)
                input_stage[k] = middle_stage[d4 % 2, k] + inverse * (scaled - unit * inner)
                gain_out[...] += jnp.sum(grad * unit, axis=0, keepdims=True)
            start(save_input(d4))
        return carry

    lax.fori_loop(0, per + four.steps, step, 0)
    two.drain()
    four.drain()
    wait(save_layer(chunks - 1))
    wait(save_input(chunks - 1))

    def finish(k, carry):
        owner = lax.rem(dp + k, m)
        w = owner // owners

        def copy(peer):
            return pltpu.make_async_remote_copy(
                src_ref=send.at[0, pl.ds(0, share)], dst_ref=recv.at[peer], send_sem=send_sem.at[peer],
                recv_sem=recv_sem.at[peer], device_id={"dp": peer}, device_id_type=MESH)

        copy(owner).wait_send()
        copy(owner).wait_recv()
        return carry

    lax.fori_loop(1, m, finish, 0)
    reduced[...] = recv[0].astype(jnp.float32)

    def add(k, carry):
        reduced[...] += recv[k].astype(jnp.float32)
        return carry

    lax.fori_loop(1, m, add, 0)


def attention_back(feed_part, grad_low, gain, q, k, v, mix, lse, cosines, sines, seg_col, seg_row, out_w,
                   x, qkv_w, branch, grad_middle, n, m, cid, size, chunks=16, lag=2):
    rows, width = feed_part.shape
    q_width = q.shape[1]
    pairs = q_width // 128
    rc = rows // (2 * chunks)
    blocks = rows // size
    share = width // m
    cat = 2 * q_width + 128
    low = jnp.bfloat16
    vmem = pl.BlockSpec(memory_space=pltpu.VMEM)
    hbm = pl.BlockSpec(memory_space=pl.ANY)
    dma = pltpu.SemaphoreType.DMA
    shape = jax.ShapeDtypeStruct
    return pl.pallas_call(
        functools.partial(back_kernel, n, m, chunks, lag, norm_eps, size, pairs),
        out_shape=(
            shape((rows, width), low), shape((rows, width), jnp.float32), shape((1, width), jnp.float32),
            shape((share, cat), jnp.float32),
        ),
        in_specs=[vmem] * 13 + [hbm] * 4,
        out_specs=(hbm, hbm, vmem, vmem),
        scratch_shapes=line_scratch(chunks, rc, width) + line_scratch(chunks, rc, width) + [
            pltpu.VMEM((rows, width), low),
            pltpu.VMEM((rows, width), low),
            pltpu.VMEM((rows, width), low),
            pltpu.VMEM((rows, width), low),
            pltpu.VMEM((width, q_width + 128), low),
            pltpu.VMEM((rows, width), low),
            pltpu.VMEM((size, q_width), low),
            pltpu.VMEM((blocks, size, size), jnp.float32),
            pltpu.VMEM((blocks, 128, size), low),
            pltpu.VMEM((blocks, size, 128), jnp.float32),
            pltpu.VMEM((blocks, size, 128), jnp.float32),
            pltpu.VMEM((rows, q_width + 128), low),
            pltpu.VMEM((width // 256, 256, cat), low),
            pltpu.VMEM((m, share, cat), low),
            pltpu.VMEM((2, 2, rc, width), low),
            pltpu.VMEM((2, rc, width), low),
            pltpu.VMEM((2, 2, rc, width), jnp.float32),
            pltpu.VMEM((2, rc, width), jnp.float32),
            dma((2,)), dma((2, 2)), dma((2, 2)), dma((2,)), dma((2,)), dma((m,)), dma((m,)),
        ],
        compiler_params=pltpu.CompilerParams(collective_id=cid, has_side_effects=True, vmem_limit_bytes=63 << 20),
        cost_estimate=pl.CostEstimate(flops=40 * rows * width * q_width, bytes_accessed=rows * width * 260,
                                      transcendentals=rows * rows * pairs),
    )(feed_part, grad_low, gain, q, k, v, mix, lse, cosines, sines, seg_col, seg_row, out_w,
      x, qkv_w, branch, grad_middle)


def norm_kernel(n, m, gains_ref, ff_ref, head_ref, norm_ref, gain_ref, line, got_gains, got_line, got_plane, got_squares,
                send_squares, recv_squares, send_gains, recv_gains, send_line, recv_line, send_plane, recv_plane):
    z = lax.axis_index("tensor")
    d = lax.axis_index("dp")
    share = head_ref.shape[0]

    barrier = pltpu.get_barrier_semaphore()
    for k in range(1, n):
        pl.semaphore_signal(barrier, inc=1, device_id={"tensor": lax.rem(z + k, n)}, device_id_type=MESH)
    for k in range(1, m):
        pl.semaphore_signal(barrier, inc=1, device_id={"dp": lax.rem(d + k, m)}, device_id_type=MESH)
    pl.semaphore_wait(barrier, n - 1 + m - 1)

    def gains_to(k, sender):
        peer = lax.rem(d + k, m)
        return pltpu.make_async_remote_copy(
            src_ref=gains_ref.at[peer], dst_ref=got_gains.at[sender], send_sem=send_gains.at[k],
            recv_sem=recv_gains.at[sender], device_id={"dp": peer}, device_id_type=MESH)

    def squares_to(k, sender):
        return pltpu.make_async_remote_copy(
            src_ref=line.at[2], dst_ref=got_squares.at[sender], send_sem=send_squares.at[k],
            recv_sem=recv_squares.at[sender], device_id={"dp": lax.rem(d + k, m)}, device_id_type=MESH)

    def along_line(k, sender):
        return pltpu.make_async_remote_copy(
            src_ref=line.at[0], dst_ref=got_line.at[sender], send_sem=send_line.at[k], recv_sem=recv_line.at[sender],
            device_id={"tensor": lax.rem(z + k, n)}, device_id_type=MESH)

    def over_plane(k, sender):
        return pltpu.make_async_remote_copy(
            src_ref=line.at[1], dst_ref=got_plane.at[sender], send_sem=send_plane.at[k], recv_sem=recv_plane.at[sender],
            device_id={"dp": lax.rem(d + k, m)}, device_id_type=MESH)

    def summed(ref, number):
        whole = ref[0]
        for k in range(1, number):
            whole = whole + ref[k]
        return whole

    def squares(value):
        return jnp.sum(jnp.sum(value * value, axis=0, keepdims=True), axis=1, keepdims=True)

    for k in range(1, m):
        gains_to(k, d).start()
    got_gains[d] = gains_ref[d]
    sub = 32

    def head_rows(r, acc):
        value = head_ref[pl.ds(pl.multiple_of(r * sub, sub), sub), :]
        return acc + squares(value)

    local = lax.fori_loop(0, share // sub, head_rows, jnp.zeros((1, 1), jnp.float32))

    def ff_rows(r, acc):
        value = ff_ref[pl.ds(pl.multiple_of(r * sub, sub), sub), :].astype(jnp.float32)
        return acc + squares(value)

    local = lax.fori_loop(0, share // sub, ff_rows, local)
    line[2] = jnp.broadcast_to(local, (8, 128))
    for k in range(1, m):
        squares_to(k, d).start()
    got_squares[d] = line[2]
    for k in range(1, m):
        gains_to(k, d).wait_send()
        gains_to(k, lax.rem(d + m - k, m)).wait_recv()
    for k in range(1, m):
        squares_to(k, d).wait_send()
        squares_to(k, lax.rem(d + m - k, m)).wait_recv()
    line[0] = summed(got_squares, m)
    gains = summed(got_gains, m)
    gain_ref[...] = gains
    line[1] = jnp.broadcast_to(squares(gains), (8, 128))
    for k in range(1, m):
        over_plane(k, d).start()
    got_plane[d] = line[1]
    for k in range(1, n):
        along_line(k, z).start()
    got_line[z] = line[0]
    for k in range(1, n):
        along_line(k, z).wait_send()
        along_line(k, lax.rem(z + n - k, n)).wait_recv()
    for k in range(1, m):
        over_plane(k, d).wait_send()
        over_plane(k, lax.rem(d + m - k, m)).wait_recv()
    norm_ref[...] = jnp.sqrt(summed(got_line, n) + summed(got_plane, m))


def adam_kernel(rates, kv_width, correct_ref, norm_ref, gain_ref, ff_hbm, head_hbm, layer_hbm, input_hbm, *refs):
    count = len(rates)
    params, refs = refs[:3 * count], refs[3 * count:]
    norm_out, layer_out, input_out, outs, refs = refs[0], refs[1], refs[2], refs[3:3 * count + 3], refs[3 * count + 3:]
    (ff_grad, head_ref, layer_held, input_held), held = refs[:4], refs[4:3 * count + 4]
    grad_sem, load_sem, save_sem, in_sem, back_sem = refs[3 * count + 4:]
    share = gain_ref.shape[1]
    q_width = outs[3].shape[1]
    ff = outs[12].shape[2]
    sub = 32

    grads = (
        pltpu.make_async_copy(ff_hbm, ff_grad, grad_sem.at[0]),
        pltpu.make_async_copy(head_hbm, head_ref, grad_sem.at[1]),
    )
    loads = [pltpu.make_async_copy(params[k], held[k], load_sem.at[k]) for k in range(3 * count)]
    saves = [pltpu.make_async_copy(held[k], outs[k], save_sem.at[k]) for k in range(3 * count)]
    quarter = layer_hbm.shape[0] // 4
    arrive, depart = [], []
    for k in range(4):
        at = pl.ds(k * quarter, quarter)
        for t, (source, kept, target) in enumerate(
                ((layer_hbm, layer_held, layer_out), (input_hbm, input_held, input_out))):
            arrive.append(pltpu.make_async_copy(source.at[at], kept.at[at], in_sem.at[t, k]))
            depart.append(pltpu.make_async_copy(kept.at[at], target.at[at], back_sem.at[t, k]))
    for copy in grads:
        copy.start()
    for which in (1, 3, 2, 5, 4, 0):
        for k in range(3):
            loads[3 * which + k].start()
    for copy in arrive:
        copy.start()
    norm_out[...] = norm_ref[...]
    factor = jnp.minimum(1.0, clip_limit / (norm_ref[:1, :1] + 1e-06))
    one, two = correct_ref[0], correct_ref[1]

    def update(which, where, gradient):
        rate, decay = rates[which]
        p, a, b = (held[3 * which + k] for k in range(3))
        gradient = gradient * factor
        first = beta_first * a[where] + (1.0 - beta_first) * gradient
        second = beta_second * b[where] + (1.0 - beta_second) * gradient * gradient
        a[where] = first
        b[where] = second
        change = first / one / (jnp.sqrt(second / two) + adam_eps)
        old = p[where]
        p[where] = old - rate * (change + decay * old)

    def load(which):
        for k in range(3):
            loads[3 * which + k].wait()

    def save(which):
        for k in range(3):
            saves[3 * which + k].start()

    def by_rows(which, body):
        load(which)
        lax.fori_loop(0, share // sub, lambda r, c: (body(pl.ds(pl.multiple_of(r * sub, sub), sub)), c)[1], 0)
        save(which)

    for copy in grads:
        copy.wait()
    by_rows(1, lambda where: update(1, (where, slice(None)), head_ref[where, :q_width]))
    load(3)

    def out_tile(t, carry):
        at = pl.ds(pl.multiple_of(t * 128, 128), 128)
        source = pl.ds(pl.multiple_of(q_width + 2 * kv_width + t * 128, 128), 128)
        update(3, (at, slice(None)), head_ref[:, source].T)
        return carry

    lax.fori_loop(0, outs[9].shape[0] // 128, out_tile, 0)
    save(3)

    load(2)
    both = head_ref[:, q_width:q_width + 2 * kv_width].T
    for t in (0, 1):
        update(2, (t, slice(None), slice(None)), both[t * kv_width:(t + 1) * kv_width])
    save(2)

    def gateup_rows(where):
        for t in (0, 1):
            update(4, (t, where, slice(None)), ff_grad[where, t * ff:(t + 1) * ff].astype(jnp.float32))

    load(5)

    def down_tile(t, carry):
        at = pl.ds(pl.multiple_of(t * 128, 128), 128)
        source = pl.ds(pl.multiple_of(2 * ff + t * 128, 128), 128)
        update(5, (at, slice(None)), ff_grad[:, source].astype(jnp.float32).T)
        return carry

    lax.fori_loop(0, ff // 128, down_tile, 0)
    save(5)
    by_rows(4, gateup_rows)
    for came, left in zip(arrive, depart):
        came.wait()
        left.start()
    load(0)
    update(0, (slice(None), slice(None)), gain_ref[...])
    save(0)
    for copy in saves + depart:
        copy.wait()


def finish_step(gains, correct, ff_grad, head_grad, layer, grad_in, params, rates, kv_width, n, m, cid):
    share = gains.shape[1] // m
    parts = gains.reshape(2, m, share).transpose(1, 0, 2)
    vmem = pl.BlockSpec(memory_space=pltpu.VMEM)
    hbm = pl.BlockSpec(memory_space=pl.ANY)
    dma = pltpu.SemaphoreType.DMA
    shape = jax.ShapeDtypeStruct
    norm, gain = pl.pallas_call(
        functools.partial(norm_kernel, n, m),
        out_shape=(shape((8, 128), jnp.float32), shape((2, share), jnp.float32)),
        in_specs=[vmem, vmem, vmem],
        out_specs=(vmem, vmem),
        scratch_shapes=[
            pltpu.VMEM((3, 8, 128), jnp.float32),
            pltpu.VMEM((m, 2, share), jnp.float32),
            pltpu.VMEM((n, 8, 128), jnp.float32),
            pltpu.VMEM((m, 8, 128), jnp.float32),
            pltpu.VMEM((m, 8, 128), jnp.float32),
            dma((m,)), dma((m,)), dma((m,)), dma((m,)), dma((n,)), dma((n,)), dma((m,)), dma((m,)),
        ],
        compiler_params=pltpu.CompilerParams(collective_id=cid, has_side_effects=True),
    )(parts, ff_grad, head_grad)
    size = sum(p.size for p in params)
    norm, layer, grad_in, *outs = pl.pallas_call(
        functools.partial(adam_kernel, rates, kv_width),
        out_shape=(shape((8, 128), jnp.float32), shape(layer.shape, layer.dtype), shape(grad_in.shape, grad_in.dtype))
        + tuple(shape(p.shape, jnp.float32) for p in params),
        in_specs=[pl.BlockSpec(memory_space=pltpu.SMEM), vmem, vmem] + [hbm] * (4 + len(params)),
        out_specs=(vmem,) + (hbm,) * (2 + len(params)),
        scratch_shapes=[pltpu.VMEM(a.shape, a.dtype) for a in (ff_grad, head_grad, layer, grad_in)]
        + [pltpu.VMEM(p.shape, jnp.float32) for p in params]
        + [dma((2,)), dma((len(params),)), dma((len(params),)), dma((2, 4)), dma((2, 4))],
        compiler_params=pltpu.CompilerParams(vmem_limit_bytes=63 << 20),
        cost_estimate=pl.CostEstimate(flops=20 * size, bytes_accessed=24 * size, transcendentals=size),
    )(correct, norm, gain, ff_grad, head_grad, layer, grad_in, *params)
    return norm, layer, grad_in, outs


norm_eps = 1e-05
beta_first = 0.9
beta_second = 0.95
adam_eps = 1e-08
weight_decay = 0.1
weight_rate = 0.02
out_rate = 0.1
gain_rate = 0.2
clip_limit = 1.0


def positions(segment):
    length = segment.shape[0]
    indices = jnp.arange(length, dtype=jnp.int32)
    earlier = jnp.concatenate([segment[:1] - 1, segment[:-1]])
    begins = jnp.where(segment != earlier, indices, jnp.zeros_like(indices))
    return indices - lax.cummax(begins, axis=0)


def paired_tables(places):
    lane = jnp.arange(128, dtype=jnp.int32) % HD
    frequency = jnp.power(10000.0, -(lane % (HD // 2)).astype(jnp.float32) * (2.0 / HD))
    angles = places.astype(jnp.float32)[:, None] * frequency[None, :]
    sines = jnp.sin(angles)
    return jnp.cos(angles), jnp.where(lane < HD // 2, -sines, sines)


def on_device(
    n,
    m,
    tokens,
    cotangent,
    segment_ids,
    step_count,
    norm_gains,
    gains_first,
    gains_second,
    w_query,
    query_first,
    query_second,
    w_keyval,
    keyval_first,
    keyval_second,
    w_out,
    out_first,
    out_second,
    w_gateup,
    gateup_first,
    gateup_second,
    w_down,
    down_first,
    down_second,
):
    low = jnp.bfloat16
    width = w_query.shape[1]
    kv_width = w_keyval.shape[2]
    share = norm_gains.shape[1]
    gain_part = lax.dynamic_update_slice(
        jnp.zeros((2, tokens.shape[1]), jnp.float32), norm_gains, (0, lax.axis_index("dp") * share)
    )
    length = tokens.shape[0]
    size = min(256, length)
    segment = segment_ids[0]
    places = positions(segment)
    cosines, sines = paired_tables(places)
    seg_col, seg_row = segment[:, None], segment[None, :]
    branch, mixture, q, k, v, lse, qkv_weight, out_weight, gain_values, ff_weight = attention_head(
        tokens, gain_part, w_query, w_keyval.swapaxes(1, 2), w_out, cosines, sines, seg_col, seg_row,
        w_gateup, w_down, n, m, 1, size
    )
    feed_part, grad_middle, grad_branch, gain_grad_two, grad_ff_weight = feed_forward(
        branch, gain_values[1:], tokens, cotangent, ff_weight, n, 2
    )
    ff_reduced = lax.psum_scatter(grad_ff_weight, "dp", scatter_dimension=0, tiled=True)
    layer_out, input_grad, gain_grad_one, head_reduced = attention_back(
        feed_part, grad_branch, gain_values[:1], q, k, v, mixture, lse, cosines, sines, seg_col, seg_row,
        out_weight, tokens, qkv_weight, branch, grad_middle, n, m, 3, size
    )
    gain_grads = jnp.concatenate([gain_grad_one, gain_grad_two])
    step_float = step_count[0].astype(jnp.float32)
    correct = jnp.stack([1.0 - jnp.power(beta_first, step_float), 1.0 - jnp.power(beta_second, step_float)])
    params = (
        (norm_gains, gains_first, gains_second),
        (w_query, query_first, query_second),
        tuple(a.swapaxes(1, 2) for a in (w_keyval, keyval_first, keyval_second)),
        (w_out, out_first, out_second),
        (w_gateup, gateup_first, gateup_second),
        (w_down, down_first, down_second),
    )
    rates = (
        (gain_rate, 0.0),
        (weight_rate, weight_decay),
        (weight_rate, weight_decay),
        (out_rate, weight_decay),
        (weight_rate, weight_decay),
        (weight_rate, weight_decay),
    )
    norm, layer_out, input_grad, updated = finish_step(
        gain_grads, correct, ff_reduced, head_reduced, layer_out, input_grad,
        [a for group in params for a in group], rates, kv_width, n, m, 4
    )
    results = []
    for k in range(len(params)):
        weight, first_state, second_state = updated[3 * k : 3 * k + 3]
        group = [first_state, second_state, weight]
        results += [a.swapaxes(1, 2) for a in group] if k == 2 else group
    return (layer_out, input_grad, norm[0, :1], *results)


def solution(mesh):
    rows = P("dp", None)
    gains = P(None, "dp")
    query = P("dp", "tensor")
    stacked = P(None, "dp", "tensor")
    turned = P("tensor", "dp")
    states = (gains,) * 3 + (query,) * 3 + (stacked,) * 3 + (turned,) * 3 + (stacked,) * 3 + (turned,) * 3
    return jax.shard_map(
        functools.partial(on_device, mesh.shape["tensor"], mesh.shape["dp"]),
        mesh=mesh,
        in_specs=(rows, rows, rows, P()) + states,
        out_specs=(rows, rows, P()) + states,
        check_vma=False,
    )
```

```python
import functools

import jax
import jax.numpy as jnp
from jax import lax
from jax.experimental import pallas as pl
from jax.experimental.pallas import tpu as pltpu
from jax.sharding import PartitionSpec as P

HD = 64
MESH = pl.DeviceIdType.MESH


masked_value = -1e9


def dot_t(left, right):
    return lax.dot_general(left, right, (((1,), (1,)), ((), ())), preferred_element_type=jnp.float32)


def dot_n(left, right):
    return lax.dot_general(left, right, (((1,), (0,)), ((), ())), preferred_element_type=jnp.float32)


def swap_halves(values, first_half):
    return jnp.where(first_half, pltpu.roll(values, 96, 1), pltpu.roll(values, 32, 1))


def lane_tests(rows):
    lane = lax.broadcasted_iota(jnp.int32, (rows, 128), 1)
    return lane < 64, (lane % 64) < 32


def block_bias(seg_col_ref, seg_row_ref, i, j, size):
    keys = seg_col_ref[pl.ds(pl.multiple_of(j * size, size), size), :]
    rows = seg_row_ref[:, pl.ds(pl.multiple_of(i * size, size), size)]
    key_at = j * size + lax.broadcasted_iota(jnp.int32, (size, size), 0)
    row_at = i * size + lax.broadcasted_iota(jnp.int32, (size, size), 1)
    return jnp.where((keys == rows) & (key_at <= row_at), 0.0, masked_value)


def stack_pair(pair, low_lanes):
    zero = jnp.zeros_like(pair)
    return jnp.concatenate([jnp.where(low_lanes, pair, zero), jnp.where(low_lanes, zero, pair)], axis=0)


class Line:
    def __init__(self, n, chunks, rc, lag, part, got, out, sems, order=None):
        self.order = order
        self.n, self.chunks, self.rc, self.lag = n, chunks, rc, lag
        self.part, self.got, self.out = part, got, out
        self.send_a, self.recv_a, self.send_g, self.recv_g = sems
        self.me = lax.axis_index("tensor")
        self.steps = chunks + 2 * lag * (n - 1)

    def rows(self, stream, c):
        begin = (stream * self.chunks + c) * self.rc if self.order is None else self.order(stream, c)
        return pl.ds(pl.multiple_of(begin, self.rc), self.rc)

    def side(self, stream):
        pos = self.me if stream == 0 else self.n - 1 - self.me
        fwd = self.me + 1 if stream == 0 else self.me - 1
        bwd = self.me - 1 if stream == 0 else self.me + 1
        return pos, fwd, bwd

    def toward(self, stream, c, nxt, src):
        return pltpu.make_async_remote_copy(
            src_ref=src, dst_ref=self.got.at[stream, c],
            send_sem=self.send_a.at[stream, c], recv_sem=self.recv_a.at[stream, c],
            device_id={"tensor": nxt}, device_id_type=MESH)

    def back(self, stream, c, nxt):
        where = self.rows(stream, c)
        return pltpu.make_async_remote_copy(
            src_ref=self.out.at[where], dst_ref=self.out.at[where],
            send_sem=self.send_g.at[stream, c], recv_sem=self.recv_g.at[stream, c],
            device_id={"tensor": nxt}, device_id_type=MESH)

    def step(self, s):
        n, lag = self.n, self.lag
        for stream in (0, 1):
            pos, fwd, bwd = self.side(stream)
            c = s - lag * pos

            @pl.when((c >= 0) & (c < self.chunks))
            def _():
                where = self.rows(stream, c)
                slot = self.got.at[stream, c]

                def summed():
                    self.toward(stream, c, fwd, slot).wait_recv()
                    return (
                        self.part[where, :].astype(jnp.float32) + self.got[stream, c].astype(jnp.float32)
                    ).astype(self.out.dtype)

                @pl.when(pos == 0)
                def _():
                    self.toward(stream, c, fwd, self.part.at[where]).start()

                @pl.when((pos > 0) & (pos < n - 1))
                def _():
                    self.got[stream, c] = summed()
                    self.toward(stream, c, fwd, slot).start()

                @pl.when(pos == n - 1)
                def _():
                    self.out[where, :] = summed()
                    self.back(stream, c, bwd).start()
            d = s - lag * (n - 1) - lag * (n - 1 - pos)

            @pl.when((d >= 0) & (d < self.chunks) & (pos < n - 1))
            def _():
                self.back(stream, d, bwd).wait_recv()

                @pl.when(pos > 0)
                def _():
                    self.back(stream, d, bwd).start()

    def drain(self):
        def one(c, carry):
            for stream in (0, 1):
                pos, fwd, bwd = self.side(stream)

                @pl.when(pos < self.n - 1)
                def _():
                    self.toward(stream, c, fwd, self.got.at[stream, c]).wait_send()

                @pl.when(pos > 0)
                def _():
                    self.back(stream, c, bwd).wait_send()
            return carry

        lax.fori_loop(0, self.chunks, one, 0)


def greet(n):
    me = lax.axis_index("tensor")
    barrier = pltpu.get_barrier_semaphore()

    @pl.when(me > 0)
    def _():
        pl.semaphore_signal(barrier, inc=1, device_id={"tensor": me - 1}, device_id_type=MESH)

    @pl.when(me < n - 1)
    def _():
        pl.semaphore_signal(barrier, inc=1, device_id={"tensor": me + 1}, device_id_type=MESH)

    @pl.when((me > 0) & (me < n - 1))
    def _():
        pl.semaphore_wait(barrier, 2)

    @pl.when((me == 0) | (me == n - 1))
    def _():
        pl.semaphore_wait(barrier, 1)


def line_scratch(chunks, rc, width):
    return [pltpu.VMEM((2, chunks, rc, width), jnp.bfloat16)] + [pltpu.SemaphoreType.DMA((2, chunks))] * 4


def line_kernel(n, chunks, lag, count, *refs):
    parts, outs, scratch = refs[:count], refs[count:2 * count], refs[2 * count:]
    rc = parts[0].shape[0] // (2 * chunks)
    lines = [
        Line(n, chunks, rc, lag, parts[k], scratch[5 * k], outs[k], scratch[5 * k + 1:5 * k + 5])
        for k in range(count)
    ]
    greet(n)

    def step(s, carry):
        for k, line in enumerate(lines):
            line.step(s - k * chunks)
        return carry

    lax.fori_loop(0, lines[0].steps + (count - 1) * chunks, step, 0)
    for line in lines:
        line.drain()


def line_reduce(parts, n, chunks, cid, lag=2):
    rows, width = parts[0].shape
    count = len(parts)
    rc = rows // (2 * chunks)
    scratch = []
    for _ in parts:
        scratch += line_scratch(chunks, rc, width)
    vmem = pl.BlockSpec(memory_space=pltpu.VMEM)
    return pl.pallas_call(
        functools.partial(line_kernel, n, chunks, lag, count),
        out_shape=tuple(jax.ShapeDtypeStruct((rows, width), jnp.bfloat16) for _ in parts),
        in_specs=[vmem] * count,
        out_specs=(vmem,) * count,
        scratch_shapes=scratch,
        compiler_params=pltpu.CompilerParams(collective_id=cid, has_side_effects=True, vmem_limit_bytes=40 << 20),
        cost_estimate=pl.CostEstimate(flops=rows * width * 2 * count, bytes_accessed=rows * width * 120 * count,
                                      transcendentals=0),
    )(*parts)


def dot_rows(left, right):
    return lax.dot_general(left, right, (((0,), (0,)), ((), ())), preferred_element_type=jnp.float32)


def ff_kernel(n, chunks, lag, eps, branch, gain, x, cot_hbm, w_hbm,
              feed_hbm, middle_hbm, low_hbm, gain_out, grads_hbm,
              got, sa, ra, sg, rg, two_sum, two_part, weight, cot, normed, hidden, gg, feed,
              middle_stage, low_stage, unit_stage, w_sem, cot_sem, feed_sem, stage_sem, grad_sem):
    rows, width = branch.shape
    ff = hidden.shape[1]
    rc = rows // (2 * chunks)
    per = 8
    offset = per - 1
    half = rows // 2
    hb = per * rc
    block = 2 * hb
    blocks = chunks // per
    line = Line(n, chunks, rc, lag, two_part, got, two_sum, (sa, ra, sg, rg))
    landed = 2 * lag * (n - 1) + offset
    tile = 256
    full, rest = ff // tile, ff % tile
    wide = width // tile

    groups = []
    for g, (begin, end) in enumerate(((0, tile), (tile, 2 * tile), (2 * tile, ff))):
        groups.append([
            pltpu.make_async_copy(w_hbm.at[:, pl.ds(t * ff + begin, end - begin)],
                                  weight.at[:, pl.ds(t * ff + begin, end - begin)], w_sem.at[g, t])
            for t in range(3)
        ])
    for copy in sum(groups, []):
        copy.start()

    def natural(k, b):
        return pl.ds(pl.multiple_of(k * half + b * hb, hb), hb)

    def blocked(k, b):
        return pl.ds(pl.multiple_of(b * block + k * hb, hb), hb)

    def load_cot(b):
        return [pltpu.make_async_copy(cot_hbm.at[natural(k, b)], cot.at[blocked(k, b)], cot_sem.at[b, k])
                for k in (0, 1)]

    def save_feed(b):
        return [pltpu.make_async_copy(feed.at[pl.ds(k * hb, hb)], feed_hbm.at[natural(k, b)], feed_sem.at[k])
                for k in (0, 1)]

    def save_rows(d):
        copies = []
        for k in (0, 1):
            where = line.rows(k, d)
            copies.append(pltpu.make_async_copy(middle_stage.at[k], middle_hbm.at[where], stage_sem.at[0, k]))
            copies.append(pltpu.make_async_copy(low_stage.at[k], low_hbm.at[where], stage_sem.at[1, k]))
        return copies

    def save_units(w):
        return [pltpu.make_async_copy(unit_stage, grads_hbm.at[pl.ds(pl.multiple_of(w * tile, tile), tile)], grad_sem.at[0])]

    def start(copies):
        for copy in copies:
            copy.start()

    def wait(copies):
        for copy in copies:
            copy.wait()

    for b in range(blocks):
        start(load_cot(b))
    gain_out[...] = jnp.zeros_like(gain_out)
    greet(n)

    def unit_rows(where):
        middle = x[where, :].astype(jnp.float32) + branch[where, :].astype(jnp.float32)
        inverse = lax.rsqrt(jnp.mean(middle * middle, axis=-1, keepdims=True) + eps)
        return middle * inverse, inverse

    def normalize(b):
        def some(r, carry):
            for k in (0, 1):
                where = pl.ds(pl.multiple_of(k * half + b * hb + r * rc, rc), rc)
                at = pl.ds(pl.multiple_of(b * block + k * hb + r * rc, rc), rc)
                normed[at, :] = (unit_rows(where)[0] * gain[...]).astype(jnp.bfloat16)
            return carry

        lax.fori_loop(0, per, some, 0)

    def step(s, carry):
        line.step(s - offset)
        b = s // per
        phase = s - b * per
        live = s < chunks
        mine = pl.ds(pl.multiple_of(b * block, block), block)

        def units(at, count):
            columns = pl.ds(at, count)
            second = pl.ds(pl.multiple_of(ff + at, 128), count)
            third = pl.ds(pl.multiple_of(2 * ff + at, 128), count)
            gate = dot_n(normed[mine, :], weight[:, columns])
            up = dot_n(normed[mine, :], weight[:, second])
            grad_hidden = dot_n(cot[mine, :], weight[:, third])
            sg_gate = 1.0 / (1.0 + jnp.exp(-gate))
            silu = gate * sg_gate
            hidden[mine, columns] = (silu * up).astype(jnp.bfloat16)
            gg[mine, columns] = (grad_hidden * up * sg_gate * (1.0 + gate * (1.0 - sg_gate))).astype(jnp.bfloat16)
            gg[mine, second] = (grad_hidden * silu).astype(jnp.bfloat16)

        def unit_tile(t, c):
            for g in range(3):
                @pl.when((b == 0) & (t == g))
                def _():
                    wait(groups[g])
            units(pl.multiple_of(t * tile, tile), tile)
            return c

        @pl.when(live & (phase == 0))
        def _():
            normalize(b)
            wait(load_cot(b))

        @pl.when(live & (phase < 3))
        def _():
            lax.fori_loop(jnp.maximum(2 * phase - 1, 0), jnp.minimum(2 * phase + 1, full), unit_tile, 0)

        @pl.when(live & (phase == 3))
        def _():
            if rest:
                units(full * tile, rest)

            @pl.when(b > 0)
            def _():
                wait(save_feed(b - 1))

        @pl.when(live & ((phase == 3) | (phase == 4)))
        def _():
            def feed_tile(t, c):
                columns = pl.ds(pl.multiple_of(t * 2 * tile, 2 * tile), 2 * tile)
                feed[:, columns] = dot_t(hidden[mine, :], weight[columns, 2 * ff:]).astype(jnp.bfloat16)
                return c

            lax.fori_loop((phase - 3) * (wide // 4), (phase - 2) * (wide // 4), feed_tile, 0)

            @pl.when(phase == 4)
            def _():
                start(save_feed(b))

        @pl.when(live & ((phase == 5) | (phase == 6)))
        def _():
            def two_tile(t, c):
                at = pl.ds(pl.multiple_of(t * 2 * tile, 2 * tile), 2 * tile)
                value = dot_t(gg[mine, :], weight[at, :2 * ff]).astype(jnp.bfloat16)
                for k in (0, 1):
                    two_part[natural(k, b), at] = value[k * hb:(k + 1) * hb]
                return c

            lax.fori_loop((phase - 5) * (wide // 4), (phase - 4) * (wide // 4), two_tile, 0)

        d = s - landed

        @pl.when(d >= 0)
        def _():
            @pl.when(d > 0)
            def _():
                wait(save_rows(d - 1))
            for k in (0, 1):
                where = line.rows(k, d)
                at = pl.ds(pl.multiple_of((d // per) * block + k * hb + (d - (d // per) * per) * rc, rc), rc)
                pieces = [pl.ds(c * tile, tile) for c in range(wide)]

                def middle_at(c):
                    return x[where, c].astype(jnp.float32) + branch[where, c].astype(jnp.float32)

                def folded(value):
                    return value[:, :128] + value[:, 128:]

                total = jnp.zeros((rc, 128), jnp.float32)
                for c in pieces:
                    middle = middle_at(c)
                    total = total + folded(middle * middle)
                inverse = lax.rsqrt(jnp.sum(total, axis=-1, keepdims=True) * (1.0 / width) + eps)
                total = jnp.zeros((rc, 128), jnp.float32)
                for c in pieces:
                    product = two_sum[where, c].astype(jnp.float32) * (middle_at(c) * inverse)
                    gain_out[:, c] += jnp.sum(product, axis=0, keepdims=True)
                    total = total + folded(product * gain[:, c])
                inner = jnp.sum(total, axis=-1, keepdims=True) * (1.0 / width)
                for c in pieces:
                    scaled = two_sum[where, c].astype(jnp.float32) * gain[:, c]
                    value = cot[at, c].astype(jnp.float32) + inverse * (scaled - middle_at(c) * inverse * inner)
                    middle_stage[k, :, c] = value
                    low_stage[k, :, c] = value.astype(jnp.bfloat16)
            start(save_rows(d))

        late = s - chunks
        w = late // 2

        @pl.when((late >= 0) & (late == 2 * w) & (w < wide))
        def _():
            @pl.when(w > 0)
            def _():
                wait(save_units(w - 1))
            columns = pl.ds(pl.multiple_of(w * tile, tile), tile)
            left = normed[:, columns]
            for t in (0, 1):
                unit_stage[:, t * ff:(t + 1) * ff] = dot_rows(left, gg[:, t * ff:(t + 1) * ff]).astype(jnp.bfloat16)
            unit_stage[:, 2 * ff:] = dot_rows(cot[:, columns], hidden[...]).astype(jnp.bfloat16)
            start(save_units(w))
        return carry

    lax.fori_loop(0, offset + line.steps, step, 0)
    line.drain()
    wait(save_feed(blocks - 1))
    wait(save_rows(chunks - 1))
    wait(save_units(wide - 1))


def feed_forward(branch, gain, x, cot, weight, n, cid, chunks=32, lag=2):
    rows, width = branch.shape
    ff = weight.shape[1] // 3
    rc = rows // (2 * chunks)
    block = 16 * rc
    blocks = chunks // 8
    low = jnp.bfloat16
    vmem = pl.BlockSpec(memory_space=pltpu.VMEM)
    hbm = pl.BlockSpec(memory_space=pl.ANY)
    dma = pltpu.SemaphoreType.DMA
    shape = jax.ShapeDtypeStruct
    return pl.pallas_call(
        functools.partial(ff_kernel, n, chunks, lag, norm_eps),
        out_shape=(
            shape((rows, width), low), shape((rows, width), jnp.float32), shape((rows, width), low),
            shape((1, width), jnp.float32), shape((width, 3 * ff), low),
        ),
        in_specs=[vmem, vmem, vmem, hbm, hbm],
        out_specs=(hbm, hbm, hbm, vmem, hbm),
        scratch_shapes=line_scratch(chunks, rc, width) + [
            pltpu.VMEM((rows, width), low),
            pltpu.VMEM((rows, width), low),
            pltpu.VMEM((width, 3 * ff), low),
            pltpu.VMEM((rows, width), low),
            pltpu.VMEM((rows, width), low),
            pltpu.VMEM((rows, ff), low),
            pltpu.VMEM((rows, 2 * ff), low),
            pltpu.VMEM((block, width), low),
            pltpu.VMEM((2, rc, width), jnp.float32),
            pltpu.VMEM((2, rc, width), low),
            pltpu.VMEM((256, 3 * ff), low),
            dma((3, 3)), dma((blocks, 2)), dma((2,)), dma((2, 2)), dma((1,)),
        ],
        compiler_params=pltpu.CompilerParams(collective_id=cid, has_side_effects=True, vmem_limit_bytes=63 << 20),
        cost_estimate=pl.CostEstimate(flops=18 * rows * width * ff, bytes_accessed=rows * width * 150,
                                      transcendentals=rows * ff),
    )(branch, gain, x, cot, weight)


def head_kernel(n, m, chunks, lag, eps, size, pairs,
                x, gain_part, query_own, keyval_own, out_own, cos_ref, sin_ref, seg_col_ref, seg_row_ref,
                gateup_hbm, down_hbm,
                branch, mix_ref, q_ref, k_ref, v_ref, lse_ref, qkv_w, out_w, gain, ff_hbm,
                got, sa, ra, sg, rg, part, normed, raw, bias, scores, v_turned, got_gain,
                gateup_own, down_own, ff_own,
                send_gain, recv_gain, send_direct, send_forward, recv_w, own_sem, save_sem,
                send_ff, pass_ff, recv_ff):
    rows, width = x.shape
    q_width = pairs * 128
    z = lax.axis_index("tensor")
    dp = lax.axis_index("dp")
    share = width // m
    chips = m // 2
    chip, core = dp // 2, dp % 2
    rc = rows // (2 * chunks)
    per = size // (2 * rc)
    hb = size // 2
    blocks = rows // size
    tile = 256
    wide = width // tile
    low_lanes, first_half = lane_tests(size)
    low_rows = lax.broadcasted_iota(jnp.int32, (128, size), 0) < 64
    wholes = (qkv_w, out_w)
    ff = down_own.shape[0]
    piece = 32
    pieces = share // piece
    spacing = 40 // pieces
    owned = (
        pltpu.make_async_copy(gateup_hbm, gateup_own, own_sem.at[0]),
        pltpu.make_async_copy(down_hbm, down_own, own_sem.at[1]),
    )
    for copy in owned:
        copy.start()

    def ascending(stream, c):
        b = c // per
        return b * size + stream * hb + (c - b * per) * rc

    line = Line(n, chunks, rc, lag, part, got, branch, (sa, ra, sg, rg), ascending)

    def shard_rows(s):
        return pl.ds(pl.multiple_of(s * share, share), share)

    def direct(kind, k):
        peer = 2 * lax.rem(chip + k, chips) + core
        return pltpu.make_async_remote_copy(
            src_ref=wholes[kind].at[shard_rows(dp)], dst_ref=wholes[kind].at[shard_rows(dp)], send_sem=send_direct.at[kind, k],
            recv_sem=recv_w.at[kind, dp], device_id={"dp": peer}, device_id_type=MESH)

    def forward(kind, c, side):
        shard = 2 * c + side
        where = shard_rows(shard)
        return pltpu.make_async_remote_copy(
            src_ref=wholes[kind].at[where], dst_ref=wholes[kind].at[where], send_sem=send_forward.at[kind, c],
            recv_sem=recv_w.at[kind, shard], device_id={"dp": 2 * chip + 1 - core}, device_id_type=MESH)

    def piece_rows(shard, p):
        return pl.ds(pl.multiple_of(shard * share + p * piece, piece), piece)

    def own_piece(p):
        return ff_own.at[pl.ds(pl.multiple_of(p * piece, piece), piece)]

    def send_piece(k, p):
        peer = 2 * lax.rem(chip + k, chips) + core
        return pltpu.make_async_remote_copy(
            src_ref=own_piece(p), dst_ref=ff_hbm.at[piece_rows(dp, p)], send_sem=send_ff.at[k, p],
            recv_sem=recv_ff.at[dp, p], device_id={"dp": peer}, device_id_type=MESH)

    def pass_piece(c, side, p, src=None):
        shard = 2 * c + side
        where = ff_hbm.at[piece_rows(shard, p)]
        return pltpu.make_async_remote_copy(
            src_ref=where if src is None else src, dst_ref=where, send_sem=pass_ff.at[c, p],
            recv_sem=recv_ff.at[shard, p], device_id={"dp": 2 * chip + 1 - core}, device_id_type=MESH)

    def save_own():
        return pltpu.make_async_copy(ff_own, ff_hbm.at[shard_rows(dp)], save_sem)

    def send_gains(k, sender):
        return pltpu.make_async_remote_copy(
            src_ref=gain_part, dst_ref=got_gain.at[sender], send_sem=send_gain.at[k], recv_sem=recv_gain.at[sender],
            device_id={"dp": lax.rem(dp + k, m)}, device_id_type=MESH)

    barrier = pltpu.get_barrier_semaphore()

    @pl.when(z > 0)
    def _():
        pl.semaphore_signal(barrier, inc=1, device_id={"tensor": z - 1}, device_id_type=MESH)

    @pl.when(z < n - 1)
    def _():
        pl.semaphore_signal(barrier, inc=1, device_id={"tensor": z + 1}, device_id_type=MESH)

    for k in range(1, m):
        pl.semaphore_signal(barrier, inc=1, device_id={"dp": lax.rem(dp + k, m)}, device_id_type=MESH)

    qkv_w[shard_rows(dp), :q_width] = query_own[...].astype(jnp.bfloat16)
    both_own = jnp.concatenate([keyval_own[0], keyval_own[1]], axis=0)
    qkv_w[shard_rows(dp), q_width:] = both_own.T.astype(jnp.bfloat16)
    for t in range(q_width // 128):
        out_w[shard_rows(dp), t * 128:(t + 1) * 128] = out_own[t * 128:(t + 1) * 128, :].T.astype(jnp.bfloat16)
    got_gain[dp] = gain_part[...]

    @pl.when((z > 0) & (z < n - 1))
    def _():
        pl.semaphore_wait(barrier, m + 1)

    @pl.when((z == 0) | (z == n - 1))
    def _():
        pl.semaphore_wait(barrier, m)

    for k in range(1, m):
        send_gains(k, dp).start()
    for kind in (0, 1):
        for k in range(1, chips):
            direct(kind, k).start()
        forward(kind, chip, core).start()
    for k in range(1, m):
        send_gains(k, lax.rem(dp + m - k, m)).wait_recv()
    whole = got_gain[0]
    for k in range(1, m):
        whole = whole + got_gain[k]
    gain[...] = whole.astype(jnp.bfloat16).astype(jnp.float32)

    def norm_rows(r, carry):
        where = pl.ds(pl.multiple_of(r * rc, rc), rc)
        values = x[where, :].astype(jnp.float32)
        inverse = lax.rsqrt(jnp.mean(values * values, axis=-1, keepdims=True) + eps)
        normed[where, :] = (values * inverse * gain[0:1, :]).astype(jnp.bfloat16)
        return carry

    lax.fori_loop(0, rows // rc, norm_rows, 0)
    for copy in owned:
        copy.wait()

    def own_rows(r, carry):
        where = pl.ds(pl.multiple_of(r * piece, piece), piece)
        for t in (0, 1):
            ff_own[where, t * ff:(t + 1) * ff] = gateup_own[t, where, :].astype(jnp.bfloat16)
        return carry

    lax.fori_loop(0, pieces, own_rows, 0)

    def own_columns(t, carry):
        at = pl.ds(pl.multiple_of(2 * ff + t * 128, 128), 128)
        ff_own[:, at] = down_own[pl.ds(pl.multiple_of(t * 128, 128), 128), :].T.astype(jnp.bfloat16)
        return carry

    lax.fori_loop(0, ff // 128, own_columns, 0)
    save_own().start()

    def pass_on(kind):
        for k in range(1, chips):
            c = lax.rem(chip + chips - k, chips)
            forward(kind, c, core).wait_recv()
            forward(kind, c, core).start()

    def receive(kind):
        for c in range(chips):
            forward(kind, c, 1 - core).wait_recv()

    pass_on(0)
    receive(0)
    for p in range(min(2, pieces)):
        for k in range(1, chips):
            send_piece(k, p).start()

    def prepare(i, carry):
        where = pl.ds(pl.multiple_of(i * size, size), size)
        raw[...] = dot_n(normed[where, :], qkv_w[...])
        cosines, sines = cos_ref[where, :], sin_ref[where, :]
        for hp in range(pairs):
            values = raw[:, hp * 128:(hp + 1) * 128]
            turned = values * cosines + swap_halves(values, first_half) * sines
            q_ref[where, hp * 128:(hp + 1) * 128] = (
                turned.astype(jnp.bfloat16).astype(jnp.float32) * 0.125).astype(jnp.bfloat16)
        both = raw[:, q_width:q_width + 128]
        other = pltpu.roll(both, 64, 1)
        keys = jnp.where(low_lanes, both, other)
        k_ref[where, :] = (keys * cosines + swap_halves(keys, first_half) * sines).astype(jnp.bfloat16)
        values = jnp.where(low_lanes, other, both)
        v_ref[where, :] = values.astype(jnp.bfloat16)
        v_turned[i] = values.T.astype(jnp.bfloat16)
        return carry

    lax.fori_loop(0, blocks, prepare, 0)
    pass_on(1)

    def attend(i, hp):
        where = pl.ds(pl.multiple_of(i * size, size), size)
        columns = pl.ds(pl.multiple_of(hp * 128, 128), 128)
        stacked = stack_pair(q_ref[where, columns], low_lanes)

        def score(j, top):
            keys = k_ref[pl.ds(pl.multiple_of(j * size, size), size), :]
            b = bias[j]
            s = dot_t(keys, stacked) + jnp.concatenate([b, b], axis=1)
            scores[j] = s
            return jnp.maximum(top, jnp.max(s, axis=0, keepdims=True))

        top = lax.fori_loop(0, i + 1, score, jnp.full((1, 2 * size), -jnp.inf, jnp.float32))

        def mix(j, c):
            total, acc = c
            p = jnp.exp(scores[j] - top)
            total = total + jnp.sum(p, axis=0, keepdims=True)
            return total, acc + dot_n(v_turned[j], p.astype(jnp.bfloat16))

        total, acc = lax.fori_loop(0, i + 1, mix, (
            jnp.zeros((1, 2 * size), jnp.float32), jnp.zeros((128, 2 * size), jnp.float32)))
        lse_ref[i, hp] = top + jnp.log(total)
        acc = acc / total
        acc = jnp.where(low_rows, acc[:, :size], acc[:, size:])
        mix_ref[where, columns] = acc.T.astype(jnp.bfloat16)

    def step(s, carry):
        line.step(s - per)
        p_send = (s - 1) // spacing + 2
        p_pass = (s - 12) // spacing

        @pl.when((s >= 1) & ((p_send - 2) * spacing == s - 1) & (p_send < pieces))
        def _():
            for k in range(1, chips):
                send_piece(k, p_send).start()

        @pl.when((s >= 12) & (p_pass * spacing == s - 12) & (p_pass < pieces))
        def _():
            pass_piece(chip, core, p_pass, own_piece(p_pass)).start()
            for k in range(1, chips):
                c = lax.rem(chip + chips - k, chips)
                pass_piece(c, core, p_pass).wait_recv()
                pass_piece(c, core, p_pass).start()

        i = s // per
        hp = s - i * per
        live = s < blocks * per

        @pl.when(live & (hp == 0))
        def _():
            def fill(j, c):
                bias[j] = block_bias(seg_col_ref, seg_row_ref, i, j, size)
                return c

            lax.fori_loop(0, i + 1, fill, 0)

        @pl.when(live)
        def _():
            def each(h, c):
                attend(i, h)
                return c

            lax.fori_loop(hp * pairs // per, (hp + 1) * pairs // per, each, 0)

        @pl.when(s == per - 1)
        def _():
            receive(1)

        @pl.when(live & (hp == per - 1))
        def _():
            where = pl.ds(pl.multiple_of(i * size, size), size)

            def part_tile(t, c):
                at = pl.ds(pl.multiple_of(t * tile, tile), tile)
                part[where, at] = dot_t(mix_ref[where, :], out_w[at, :]).astype(jnp.bfloat16)
                return c

            lax.fori_loop(0, wide, part_tile, 0)
        return carry

    lax.fori_loop(0, per + line.steps, step, 0)
    line.drain()
    save_own().wait()

    def settle(p, carry):
        for k in range(1, chips):
            send_piece(k, p).wait_send()
        for c in range(chips):
            pass_piece(c, core, p).wait_send()
            pass_piece(c, 1 - core, p).wait_recv()
        return carry

    lax.fori_loop(0, pieces, settle, 0)
    for k in range(1, m):
        send_gains(k, dp).wait_send()
    for kind in (0, 1):
        for k in range(1, chips):
            direct(kind, k).wait_send()
        for c in range(chips):
            forward(kind, c, core).wait_send()


def attention_head(x, gain_part, query, keyval, out, cosines, sines, seg_col, seg_row, gateup, down, n, m, cid, size,
                   chunks=32, lag=2):
    rows, width = x.shape
    q_width = query.shape[1]
    share, ff = width // m, down.shape[0]
    pairs = q_width // 128
    rc = rows // (2 * chunks)
    blocks = rows // size
    chips = m // 2
    low = jnp.bfloat16
    vmem = pl.BlockSpec(memory_space=pltpu.VMEM)
    hbm = pl.BlockSpec(memory_space=pl.ANY)
    dma = pltpu.SemaphoreType.DMA
    shape = jax.ShapeDtypeStruct
    return pl.pallas_call(
        functools.partial(head_kernel, n, m, chunks, lag, norm_eps, size, pairs),
        out_shape=(
            shape((rows, width), low), shape((rows, q_width), low), shape((rows, q_width), low),
            shape((rows, 128), low), shape((rows, 128), low), shape((blocks, pairs, 1, 2 * size), jnp.float32),
            shape((width, q_width + 128), low), shape((width, q_width), low), shape((2, width), jnp.float32),
            shape((width, 3 * ff), low),
        ),
        in_specs=[vmem] * 9 + [hbm] * 2,
        out_specs=(vmem,) * 9 + (hbm,),
        scratch_shapes=line_scratch(chunks, rc, width) + [
            pltpu.VMEM((rows, width), low),
            pltpu.VMEM((rows, width), low),
            pltpu.VMEM((size, q_width + 128), jnp.float32),
            pltpu.VMEM((blocks, size, size), jnp.float32),
            pltpu.VMEM((blocks, size, 2 * size), jnp.float32),
            pltpu.VMEM((blocks, 128, size), low),
            pltpu.VMEM((m, 2, width), jnp.float32),
            pltpu.VMEM(gateup.shape, jnp.float32),
            pltpu.VMEM(down.shape, jnp.float32),
            pltpu.VMEM((share, 3 * ff), low),
            dma((m,)), dma((m,)), dma((2, chips)), dma((2, chips)), dma((2, m)), dma((2,)), dma,
            dma((chips, share // 32)), dma((chips, share // 32)), dma((m, share // 32)),
        ],
        compiler_params=pltpu.CompilerParams(collective_id=cid, has_side_effects=True, vmem_limit_bytes=56 << 20),
        cost_estimate=pl.CostEstimate(flops=20 * rows * width * q_width, bytes_accessed=rows * width * 170,
                                      transcendentals=rows * rows * pairs),
    )(x, gain_part, query, keyval, out, cosines, sines, seg_col, seg_row, gateup, down)


def back_kernel(n, m, chunks, lag, eps, size, pairs,
                feed_part, grad_low, gain, q_ref, k_ref, v_ref, mix_ref, lse_ref, cos_ref, sin_ref,
                seg_col_ref, seg_row_ref, out_w, x_hbm, qkv_hbm, branch_hbm, middle_hbm,
                layer_hbm, input_hbm, gain_out, reduced,
                got2, sa2, ra2, sg2, rg2, got4, sa4, ra4, sg4, rg4, feed_sum, part, grad_sum,
                x, qkv_w, normed, grad_mix, bias, k_turned, grad_k, grad_v, grad_qkv, send, recv,
                branch_stage, layer_stage, middle_stage, input_stage,
                w_sem, branch_sem, middle_sem, layer_sem, input_sem, send_sem, recv_sem):
    rows, width = feed_part.shape
    q_width = pairs * 128
    z = lax.axis_index("tensor")
    dp = lax.axis_index("dp")
    rc = rows // (2 * chunks)
    per = size // (2 * rc)
    hb = size // 2
    blocks = rows // size
    tile = 256
    wide = width // tile
    share = width // m
    owners = tile // share
    lead = 2 * lag * (n - 1)
    shift = chunks + per
    low_lanes, first_half = lane_tests(size)
    low_rows = lax.broadcasted_iota(jnp.int32, (128, size), 0) < 64

    def descending(stream, c):
        b = c // per
        return (blocks - 1 - b) * size + stream * hb + (c - b * per) * rc

    two = Line(n, chunks, rc, lag, feed_part, got2, feed_sum, (sa2, ra2, sg2, rg2))
    four = Line(n, chunks, rc, lag, part, got4, grad_sum, (sa4, ra4, sg4, rg4), descending)
    loads = (
        pltpu.make_async_copy(x_hbm, x, w_sem.at[0]),
        pltpu.make_async_copy(qkv_hbm, qkv_w, w_sem.at[1]),
    )
    for copy in loads:
        copy.start()

    def start(copies):
        for copy in copies:
            copy.start()

    def wait(copies):
        for copy in copies:
            copy.wait()

    def load_branch(d, slot):
        return [pltpu.make_async_copy(branch_hbm.at[two.rows(k, d)], branch_stage.at[slot, k], branch_sem.at[slot, k])
                for k in (0, 1)]

    def load_middle(d, slot):
        return [pltpu.make_async_copy(middle_hbm.at[four.rows(k, d)], middle_stage.at[slot, k], middle_sem.at[slot, k])
                for k in (0, 1)]

    def save_layer(d):
        return [pltpu.make_async_copy(layer_stage.at[k], layer_hbm.at[two.rows(k, d)], layer_sem.at[k]) for k in (0, 1)]

    def save_input(d):
        return [pltpu.make_async_copy(input_stage.at[k], input_hbm.at[four.rows(k, d)], input_sem.at[k]) for k in (0, 1)]

    def to_owner(w, o):
        owner = w * owners + o
        return pltpu.make_async_remote_copy(
            src_ref=send.at[w, pl.ds(o * share, share)], dst_ref=recv.at[dp], send_sem=send_sem.at[owner],
            recv_sem=recv_sem.at[dp], device_id={"dp": owner}, device_id_type=MESH)

    gain_out[...] = jnp.zeros_like(gain_out)

    def prepare(i, carry):
        at = pl.ds(pl.multiple_of(i * size, size), size)
        k_turned[i] = k_ref[at, :].astype(jnp.float32).T.astype(jnp.bfloat16)
        grad_k[i] = jnp.zeros((size, 128), jnp.float32)
        grad_v[i] = jnp.zeros((size, 128), jnp.float32)
        return carry

    lax.fori_loop(0, blocks, prepare, 0)

    barrier = pltpu.get_barrier_semaphore()

    @pl.when(z > 0)
    def _():
        pl.semaphore_signal(barrier, inc=1, device_id={"tensor": z - 1}, device_id_type=MESH)

    @pl.when(z < n - 1)
    def _():
        pl.semaphore_signal(barrier, inc=1, device_id={"tensor": z + 1}, device_id_type=MESH)

    for k in range(1, m):
        pl.semaphore_signal(barrier, inc=1, device_id={"dp": lax.rem(dp + k, m)}, device_id_type=MESH)

    @pl.when((z > 0) & (z < n - 1))
    def _():
        pl.semaphore_wait(barrier, m + 1)

    @pl.when((z == 0) | (z == n - 1))
    def _():
        pl.semaphore_wait(barrier, m)

    def unit_rows(where):
        values = x[where, :].astype(jnp.float32)
        inverse = lax.rsqrt(jnp.mean(values * values, axis=-1, keepdims=True) + eps)
        return values * inverse, inverse

    def attend(i, hp):
        at_rows = pl.ds(pl.multiple_of(i * size, size), size)
        columns = pl.ds(pl.multiple_of(hp * 128, 128), 128)
        stacked = stack_pair(q_ref[at_rows, columns], low_lanes)
        grad_pair = grad_mix[:, columns]
        grad_stacked = stack_pair(grad_pair, low_lanes)
        product = (grad_pair.astype(jnp.float32) * mix_ref[at_rows, columns].astype(jnp.float32)).T
        spread = jnp.concatenate([
            jnp.sum(product[:64], axis=0, keepdims=True), jnp.sum(product[64:], axis=0, keepdims=True)], axis=1)
        logsum = lse_ref[i, hp]

        def piece(j, acc):
            at = pl.ds(pl.multiple_of(j * size, size), size)
            b = bias[j]
            s = dot_t(k_ref[at, :], stacked) + jnp.concatenate([b, b], axis=1)
            p = jnp.exp(s - logsum)
            grad_p = dot_t(v_ref[at, :], grad_stacked)
            grad_s = (p * (grad_p - spread)).astype(jnp.bfloat16)
            grad_v[j] += dot_n(p.astype(jnp.bfloat16), grad_stacked)
            grad_k[j] += dot_n(grad_s, stacked)
            return acc + dot_n(k_turned[j], grad_s)

        acc = lax.fori_loop(0, i + 1, piece, jnp.zeros((128, 2 * size), jnp.float32))
        acc = jnp.where(low_rows, acc[:, :size], acc[:, size:]).T * 0.125
        turned = acc * cos_ref[at_rows, :] - swap_halves(acc, first_half) * sin_ref[at_rows, :]
        grad_qkv[at_rows, columns] = turned.astype(jnp.bfloat16)

    def step(s, carry):
        two.step(s)
        four.step(s - shift)
        b = s // per
        hp = s - b * per
        i = blocks - 1 - b
        live = s < blocks * per
        at_rows = pl.ds(pl.multiple_of(i * size, size), size)

        @pl.when(s == 0)
        def _():
            wait(loads)

        @pl.when(live & (hp == 0))
        def _():
            grad_mix[...] = dot_n(grad_low[at_rows, :], out_w[...]).astype(jnp.bfloat16)

            def fill(j, c):
                bias[j] = block_bias(seg_col_ref, seg_row_ref, i, j, size)
                return c

            lax.fori_loop(0, i + 1, fill, 0)

        @pl.when(live)
        def _():
            def each(h, c):
                attend(i, h)
                return c

            lax.fori_loop(hp * pairs // per, (hp + 1) * pairs // per, each, 0)

            def some(r, c):
                at = pl.ds(pl.multiple_of(s * 2 * rc + r * rc, rc), rc)
                normed[at, :] = (unit_rows(at)[0] * gain[...]).astype(jnp.bfloat16)
                return c

            lax.fori_loop(0, 2, some, 0)

        @pl.when(live & (hp == per - 1))
        def _():
            cosines, sines = cos_ref[at_rows, :], sin_ref[at_rows, :]
            dk = grad_k[i] + pltpu.roll(grad_k[i], 64, 1)
            dk = dk * cosines - swap_halves(dk, first_half) * sines
            dv = grad_v[i] + pltpu.roll(grad_v[i], 64, 1)
            grad_qkv[at_rows, q_width:] = jnp.where(low_lanes, dk, dv).astype(jnp.bfloat16)

            def part_tile(t, c):
                at = pl.ds(pl.multiple_of(t * tile, tile), tile)
                part[at_rows, at] = dot_t(grad_qkv[at_rows, :], qkv_w[at, :]).astype(jnp.bfloat16)
                return c

            lax.fori_loop(0, wide, part_tile, 0)

        w = s - blocks * per

        @pl.when((w >= 0) & (w < wide))
        def _():
            columns = pl.ds(pl.multiple_of(w * tile, tile), tile)
            send[w, :, :q_width + 128] = dot_rows(normed[:, columns], grad_qkv[...]).astype(jnp.bfloat16)
            send[w, :, q_width + 128:] = dot_rows(grad_low[:, columns], mix_ref[...]).astype(jnp.bfloat16)
            for o in range(owners):
                owner = w * owners + o

                @pl.when(owner != dp)
                def _():
                    to_owner(w, o).start()

                @pl.when(owner == dp)
                def _():
                    recv[dp] = send[w, o * share:(o + 1) * share, :]

        e = s - lead + 1

        @pl.when((e >= 0) & (e < chunks))
        def _():
            start(load_branch(e, e % 2))

        d = s - lead

        @pl.when((d >= 0) & (d < chunks))
        def _():
            wait(load_branch(d, d % 2))

            @pl.when(d > 0)
            def _():
                wait(save_layer(d - 1))
            for k in (0, 1):
                where = two.rows(k, d)
                layer_stage[k] = (
                    x[where, :].astype(jnp.float32) + branch_stage[d % 2, k].astype(jnp.float32)
                    + feed_sum[where, :].astype(jnp.float32)
                ).astype(jnp.bfloat16)
            start(save_layer(d))

        e4 = s - lead - shift + 1

        @pl.when((e4 >= 0) & (e4 < chunks))
        def _():
            start(load_middle(e4, e4 % 2))

        d4 = s - lead - shift

        @pl.when(d4 >= 0)
        def _():
            wait(load_middle(d4, d4 % 2))

            @pl.when(d4 > 0)
            def _():
                wait(save_input(d4 - 1))
            for k in (0, 1):
                where = four.rows(k, d4)
                unit, inverse = unit_rows(where)
                grad = grad_sum[where, :].astype(jnp.float32)
                scaled = grad * gain[...]
                inner = jnp.mean(scaled * unit, axis=-1, keepdims=True)
                input_stage[k] = middle_stage[d4 % 2, k] + inverse * (scaled - unit * inner)
                gain_out[...] += jnp.sum(grad * unit, axis=0, keepdims=True)
            start(save_input(d4))
        return carry

    lax.fori_loop(0, shift + four.steps, step, 0)
    two.drain()
    four.drain()
    wait(save_layer(chunks - 1))
    wait(save_input(chunks - 1))

    def finish(k, carry):
        owner = lax.rem(dp + k, m)
        w = owner // owners

        def copy(peer):
            return pltpu.make_async_remote_copy(
                src_ref=send.at[0, pl.ds(0, share)], dst_ref=recv.at[peer], send_sem=send_sem.at[peer],
                recv_sem=recv_sem.at[peer], device_id={"dp": peer}, device_id_type=MESH)

        copy(owner).wait_send()
        copy(owner).wait_recv()
        return carry

    lax.fori_loop(1, m, finish, 0)
    reduced[...] = recv[0].astype(jnp.float32)

    def add(k, carry):
        reduced[...] += recv[k].astype(jnp.float32)
        return carry

    lax.fori_loop(1, m, add, 0)


def attention_back(feed_part, grad_low, gain, q, k, v, mix, lse, cosines, sines, seg_col, seg_row, out_w,
                   x, qkv_w, branch, grad_middle, n, m, cid, size, chunks=16, lag=2):
    rows, width = feed_part.shape
    q_width = q.shape[1]
    pairs = q_width // 128
    rc = rows // (2 * chunks)
    blocks = rows // size
    share = width // m
    cat = 2 * q_width + 128
    low = jnp.bfloat16
    vmem = pl.BlockSpec(memory_space=pltpu.VMEM)
    hbm = pl.BlockSpec(memory_space=pl.ANY)
    dma = pltpu.SemaphoreType.DMA
    shape = jax.ShapeDtypeStruct
    return pl.pallas_call(
        functools.partial(back_kernel, n, m, chunks, lag, norm_eps, size, pairs),
        out_shape=(
            shape((rows, width), low), shape((rows, width), jnp.float32), shape((1, width), jnp.float32),
            shape((share, cat), jnp.float32),
        ),
        in_specs=[vmem] * 13 + [hbm] * 4,
        out_specs=(hbm, hbm, vmem, vmem),
        scratch_shapes=line_scratch(chunks, rc, width) + line_scratch(chunks, rc, width) + [
            pltpu.VMEM((rows, width), low),
            pltpu.VMEM((rows, width), low),
            pltpu.VMEM((rows, width), low),
            pltpu.VMEM((rows, width), low),
            pltpu.VMEM((width, q_width + 128), low),
            pltpu.VMEM((rows, width), low),
            pltpu.VMEM((size, q_width), low),
            pltpu.VMEM((blocks, size, size), jnp.float32),
            pltpu.VMEM((blocks, 128, size), low),
            pltpu.VMEM((blocks, size, 128), jnp.float32),
            pltpu.VMEM((blocks, size, 128), jnp.float32),
            pltpu.VMEM((rows, q_width + 128), low),
            pltpu.VMEM((width // 256, 256, cat), low),
            pltpu.VMEM((m, share, cat), low),
            pltpu.VMEM((2, 2, rc, width), low),
            pltpu.VMEM((2, rc, width), low),
            pltpu.VMEM((2, 2, rc, width), jnp.float32),
            pltpu.VMEM((2, rc, width), jnp.float32),
            dma((2,)), dma((2, 2)), dma((2, 2)), dma((2,)), dma((2,)), dma((m,)), dma((m,)),
        ],
        compiler_params=pltpu.CompilerParams(collective_id=cid, has_side_effects=True, vmem_limit_bytes=63 << 20),
        cost_estimate=pl.CostEstimate(flops=40 * rows * width * q_width, bytes_accessed=rows * width * 260,
                                      transcendentals=rows * rows * pairs),
    )(feed_part, grad_low, gain, q, k, v, mix, lse, cosines, sines, seg_col, seg_row, out_w,
      x, qkv_w, branch, grad_middle)


def norm_kernel(n, m, gains_ref, ff_ref, head_ref, norm_ref, gain_ref, line, got_gains, got_line, got_plane, got_squares,
                send_squares, recv_squares, send_gains, recv_gains, send_line, recv_line, send_plane, recv_plane):
    z = lax.axis_index("tensor")
    d = lax.axis_index("dp")
    share = head_ref.shape[0]

    barrier = pltpu.get_barrier_semaphore()
    for k in range(1, n):
        pl.semaphore_signal(barrier, inc=1, device_id={"tensor": lax.rem(z + k, n)}, device_id_type=MESH)
    for k in range(1, m):
        pl.semaphore_signal(barrier, inc=1, device_id={"dp": lax.rem(d + k, m)}, device_id_type=MESH)
    pl.semaphore_wait(barrier, n - 1 + m - 1)

    def gains_to(k, sender):
        peer = lax.rem(d + k, m)
        return pltpu.make_async_remote_copy(
            src_ref=gains_ref.at[peer], dst_ref=got_gains.at[sender], send_sem=send_gains.at[k],
            recv_sem=recv_gains.at[sender], device_id={"dp": peer}, device_id_type=MESH)

    def squares_to(k, sender):
        return pltpu.make_async_remote_copy(
            src_ref=line.at[2], dst_ref=got_squares.at[sender], send_sem=send_squares.at[k],
            recv_sem=recv_squares.at[sender], device_id={"dp": lax.rem(d + k, m)}, device_id_type=MESH)

    def along_line(k, sender):
        return pltpu.make_async_remote_copy(
            src_ref=line.at[0], dst_ref=got_line.at[sender], send_sem=send_line.at[k], recv_sem=recv_line.at[sender],
            device_id={"tensor": lax.rem(z + k, n)}, device_id_type=MESH)

    def over_plane(k, sender):
        return pltpu.make_async_remote_copy(
            src_ref=line.at[1], dst_ref=got_plane.at[sender], send_sem=send_plane.at[k], recv_sem=recv_plane.at[sender],
            device_id={"dp": lax.rem(d + k, m)}, device_id_type=MESH)

    def summed(ref, number):
        whole = ref[0]
        for k in range(1, number):
            whole = whole + ref[k]
        return whole

    def squares(value):
        return jnp.sum(jnp.sum(value * value, axis=0, keepdims=True), axis=1, keepdims=True)

    for k in range(1, m):
        gains_to(k, d).start()
    got_gains[d] = gains_ref[d]
    sub = 32

    def head_rows(r, acc):
        value = head_ref[pl.ds(pl.multiple_of(r * sub, sub), sub), :]
        return acc + squares(value)

    local = lax.fori_loop(0, share // sub, head_rows, jnp.zeros((1, 1), jnp.float32))

    def ff_rows(r, acc):
        value = ff_ref[pl.ds(pl.multiple_of(r * sub, sub), sub), :].astype(jnp.float32)
        return acc + squares(value)

    local = lax.fori_loop(0, share // sub, ff_rows, local)
    line[2] = jnp.broadcast_to(local, (8, 128))
    for k in range(1, m):
        squares_to(k, d).start()
    got_squares[d] = line[2]
    for k in range(1, m):
        gains_to(k, d).wait_send()
        gains_to(k, lax.rem(d + m - k, m)).wait_recv()
    for k in range(1, m):
        squares_to(k, d).wait_send()
        squares_to(k, lax.rem(d + m - k, m)).wait_recv()
    line[0] = summed(got_squares, m)
    gains = summed(got_gains, m)
    gain_ref[...] = gains
    line[1] = jnp.broadcast_to(squares(gains), (8, 128))
    for k in range(1, m):
        over_plane(k, d).start()
    got_plane[d] = line[1]
    for k in range(1, n):
        along_line(k, z).start()
    got_line[z] = line[0]
    for k in range(1, n):
        along_line(k, z).wait_send()
        along_line(k, lax.rem(z + n - k, n)).wait_recv()
    for k in range(1, m):
        over_plane(k, d).wait_send()
        over_plane(k, lax.rem(d + m - k, m)).wait_recv()
    norm_ref[...] = jnp.sqrt(summed(got_line, n) + summed(got_plane, m))


def adam_kernel(rates, kv_width, correct_ref, norm_ref, gain_ref, ff_hbm, head_hbm, layer_hbm, input_hbm, *refs):
    count = len(rates)
    params, refs = refs[:3 * count], refs[3 * count:]
    norm_out, layer_out, input_out, outs, refs = refs[0], refs[1], refs[2], refs[3:3 * count + 3], refs[3 * count + 3:]
    (ff_grad, head_ref, layer_held, input_held), held = refs[:4], refs[4:3 * count + 4]
    grad_sem, load_sem, save_sem, in_sem, back_sem = refs[3 * count + 4:]
    share = gain_ref.shape[1]
    q_width = outs[3].shape[1]
    ff = outs[12].shape[2]
    sub = 32

    grads = (
        pltpu.make_async_copy(ff_hbm, ff_grad, grad_sem.at[0]),
        pltpu.make_async_copy(head_hbm, head_ref, grad_sem.at[1]),
    )
    loads = [pltpu.make_async_copy(params[k], held[k], load_sem.at[k]) for k in range(3 * count)]
    saves = [pltpu.make_async_copy(held[k], outs[k], save_sem.at[k]) for k in range(3 * count)]
    quarter = layer_hbm.shape[0] // 4
    arrive, depart = [], []
    for k in range(4):
        at = pl.ds(k * quarter, quarter)
        for t, (source, kept, target) in enumerate(
                ((layer_hbm, layer_held, layer_out), (input_hbm, input_held, input_out))):
            arrive.append(pltpu.make_async_copy(source.at[at], kept.at[at], in_sem.at[t, k]))
            depart.append(pltpu.make_async_copy(kept.at[at], target.at[at], back_sem.at[t, k]))
    for copy in grads:
        copy.start()
    for which in (1, 3, 2):
        for k in range(3):
            loads[3 * which + k].start()
    for copy in arrive:
        copy.start()
    for which in (5, 4, 0):
        for k in range(3):
            loads[3 * which + k].start()
    norm_out[...] = norm_ref[...]
    factor = jnp.minimum(1.0, clip_limit / (norm_ref[:1, :1] + 1e-06))
    one, two = correct_ref[0], correct_ref[1]

    def update(which, where, gradient):
        rate, decay = rates[which]
        p, a, b = (held[3 * which + k] for k in range(3))
        gradient = gradient * factor
        first = beta_first * a[where] + (1.0 - beta_first) * gradient
        second = beta_second * b[where] + (1.0 - beta_second) * gradient * gradient
        a[where] = first
        b[where] = second
        change = first / one / (jnp.sqrt(second / two) + adam_eps)
        old = p[where]
        p[where] = old - rate * (change + decay * old)

    def load(which):
        for k in range(3):
            loads[3 * which + k].wait()

    def save(which):
        for k in range(3):
            saves[3 * which + k].start()

    def by_rows(which, body):
        load(which)
        lax.fori_loop(0, share // sub, lambda r, c: (body(pl.ds(pl.multiple_of(r * sub, sub), sub)), c)[1], 0)
        save(which)

    for copy in grads:
        copy.wait()
    by_rows(1, lambda where: update(1, (where, slice(None)), head_ref[where, :q_width]))
    load(3)

    def out_tile(t, carry):
        at = pl.ds(pl.multiple_of(t * 128, 128), 128)
        source = pl.ds(pl.multiple_of(q_width + 2 * kv_width + t * 128, 128), 128)
        update(3, (at, slice(None)), head_ref[:, source].T)
        return carry

    lax.fori_loop(0, outs[9].shape[0] // 128, out_tile, 0)
    save(3)

    load(2)
    both = head_ref[:, q_width:q_width + 2 * kv_width].T
    for t in (0, 1):
        update(2, (t, slice(None), slice(None)), both[t * kv_width:(t + 1) * kv_width])
    save(2)

    def gateup_rows(where):
        for t in (0, 1):
            update(4, (t, where, slice(None)), ff_grad[where, t * ff:(t + 1) * ff].astype(jnp.float32))

    for came, left in zip(arrive, depart):
        came.wait()
        left.start()
    load(5)

    def down_tile(t, carry):
        at = pl.ds(pl.multiple_of(t * 128, 128), 128)
        source = pl.ds(pl.multiple_of(2 * ff + t * 128, 128), 128)
        update(5, (at, slice(None)), ff_grad[:, source].astype(jnp.float32).T)
        return carry

    lax.fori_loop(0, ff // 128, down_tile, 0)
    save(5)
    by_rows(4, gateup_rows)
    load(0)
    update(0, (slice(None), slice(None)), gain_ref[...])
    save(0)
    for copy in saves + depart:
        copy.wait()


def finish_step(gains, correct, ff_grad, head_grad, layer, grad_in, params, rates, kv_width, n, m, cid):
    share = gains.shape[1] // m
    parts = gains.reshape(2, m, share).transpose(1, 0, 2)
    vmem = pl.BlockSpec(memory_space=pltpu.VMEM)
    hbm = pl.BlockSpec(memory_space=pl.ANY)
    dma = pltpu.SemaphoreType.DMA
    shape = jax.ShapeDtypeStruct
    norm, gain = pl.pallas_call(
        functools.partial(norm_kernel, n, m),
        out_shape=(shape((8, 128), jnp.float32), shape((2, share), jnp.float32)),
        in_specs=[vmem, vmem, vmem],
        out_specs=(vmem, vmem),
        scratch_shapes=[
            pltpu.VMEM((3, 8, 128), jnp.float32),
            pltpu.VMEM((m, 2, share), jnp.float32),
            pltpu.VMEM((n, 8, 128), jnp.float32),
            pltpu.VMEM((m, 8, 128), jnp.float32),
            pltpu.VMEM((m, 8, 128), jnp.float32),
            dma((m,)), dma((m,)), dma((m,)), dma((m,)), dma((n,)), dma((n,)), dma((m,)), dma((m,)),
        ],
        compiler_params=pltpu.CompilerParams(collective_id=cid, has_side_effects=True),
    )(parts, ff_grad, head_grad)
    size = sum(p.size for p in params)
    norm, layer, grad_in, *outs = pl.pallas_call(
        functools.partial(adam_kernel, rates, kv_width),
        out_shape=(shape((8, 128), jnp.float32), shape(layer.shape, layer.dtype), shape(grad_in.shape, grad_in.dtype))
        + tuple(shape(p.shape, jnp.float32) for p in params),
        in_specs=[pl.BlockSpec(memory_space=pltpu.SMEM), vmem, vmem] + [hbm] * (4 + len(params)),
        out_specs=(vmem,) + (hbm,) * (2 + len(params)),
        scratch_shapes=[pltpu.VMEM(a.shape, a.dtype) for a in (ff_grad, head_grad, layer, grad_in)]
        + [pltpu.VMEM(p.shape, jnp.float32) for p in params]
        + [dma((2,)), dma((len(params),)), dma((len(params),)), dma((2, 4)), dma((2, 4))],
        compiler_params=pltpu.CompilerParams(vmem_limit_bytes=63 << 20),
        cost_estimate=pl.CostEstimate(flops=20 * size, bytes_accessed=24 * size, transcendentals=size),
    )(correct, norm, gain, ff_grad, head_grad, layer, grad_in, *params)
    return norm, layer, grad_in, outs


norm_eps = 1e-05
beta_first = 0.9
beta_second = 0.95
adam_eps = 1e-08
weight_decay = 0.1
weight_rate = 0.02
out_rate = 0.1
gain_rate = 0.2
clip_limit = 1.0


def positions(segment):
    length = segment.shape[0]
    indices = jnp.arange(length, dtype=jnp.int32)
    earlier = jnp.concatenate([segment[:1] - 1, segment[:-1]])
    begins = jnp.where(segment != earlier, indices, jnp.zeros_like(indices))
    return indices - lax.cummax(begins, axis=0)


def paired_tables(places):
    lane = jnp.arange(128, dtype=jnp.int32) % HD
    frequency = jnp.power(10000.0, -(lane % (HD // 2)).astype(jnp.float32) * (2.0 / HD))
    angles = places.astype(jnp.float32)[:, None] * frequency[None, :]
    sines = jnp.sin(angles)
    return jnp.cos(angles), jnp.where(lane < HD // 2, -sines, sines)


def on_device(
    n,
    m,
    tokens,
    cotangent,
    segment_ids,
    step_count,
    norm_gains,
    gains_first,
    gains_second,
    w_query,
    query_first,
    query_second,
    w_keyval,
    keyval_first,
    keyval_second,
    w_out,
    out_first,
    out_second,
    w_gateup,
    gateup_first,
    gateup_second,
    w_down,
    down_first,
    down_second,
):
    low = jnp.bfloat16
    width = w_query.shape[1]
    kv_width = w_keyval.shape[2]
    share = norm_gains.shape[1]
    gain_part = lax.dynamic_update_slice(
        jnp.zeros((2, tokens.shape[1]), jnp.float32), norm_gains, (0, lax.axis_index("dp") * share)
    )
    length = tokens.shape[0]
    size = min(256, length)
    segment = segment_ids[0]
    places = positions(segment)
    cosines, sines = paired_tables(places)
    seg_col, seg_row = segment[:, None], segment[None, :]
    branch, mixture, q, k, v, lse, qkv_weight, out_weight, gain_values, ff_weight = attention_head(
        tokens, gain_part, w_query, w_keyval.swapaxes(1, 2), w_out, cosines, sines, seg_col, seg_row,
        w_gateup, w_down, n, m, 1, size
    )
    feed_part, grad_middle, grad_branch, gain_grad_two, grad_ff_weight = feed_forward(
        branch, gain_values[1:], tokens, cotangent, ff_weight, n, 2
    )
    ff_reduced = lax.psum_scatter(grad_ff_weight, "dp", scatter_dimension=0, tiled=True)
    layer_out, input_grad, gain_grad_one, head_reduced = attention_back(
        feed_part, grad_branch, gain_values[:1], q, k, v, mixture, lse, cosines, sines, seg_col, seg_row,
        out_weight, tokens, qkv_weight, branch, grad_middle, n, m, 3, size
    )
    gain_grads = jnp.concatenate([gain_grad_one, gain_grad_two])
    step_float = step_count[0].astype(jnp.float32)
    correct = jnp.stack([1.0 - jnp.power(beta_first, step_float), 1.0 - jnp.power(beta_second, step_float)])
    params = (
        (norm_gains, gains_first, gains_second),
        (w_query, query_first, query_second),
        tuple(a.swapaxes(1, 2) for a in (w_keyval, keyval_first, keyval_second)),
        (w_out, out_first, out_second),
        (w_gateup, gateup_first, gateup_second),
        (w_down, down_first, down_second),
    )
    rates = (
        (gain_rate, 0.0),
        (weight_rate, weight_decay),
        (weight_rate, weight_decay),
        (out_rate, weight_decay),
        (weight_rate, weight_decay),
        (weight_rate, weight_decay),
    )
    norm, layer_out, input_grad, updated = finish_step(
        gain_grads, correct, ff_reduced, head_reduced, layer_out, input_grad,
        [a for group in params for a in group], rates, kv_width, n, m, 4
    )
    results = []
    for k in range(len(params)):
        weight, first_state, second_state = updated[3 * k : 3 * k + 3]
        group = [first_state, second_state, weight]
        results += [a.swapaxes(1, 2) for a in group] if k == 2 else group
    return (layer_out, input_grad, norm[0, :1], *results)


def solution(mesh):
    rows = P("dp", None)
    gains = P(None, "dp")
    query = P("dp", "tensor")
    stacked = P(None, "dp", "tensor")
    turned = P("tensor", "dp")
    states = (gains,) * 3 + (query,) * 3 + (stacked,) * 3 + (turned,) * 3 + (stacked,) * 3 + (turned,) * 3
    return jax.shard_map(
        functools.partial(on_device, mesh.shape["tensor"], mesh.shape["dp"]),
        mesh=mesh,
        in_specs=(rows, rows, rows, P()) + states,
        out_specs=(rows, rows, P()) + states,
        check_vma=False,
    )
```

```python
import functools

import jax
import jax.numpy as jnp
from jax import lax
from jax.experimental import pallas as pl
from jax.experimental.pallas import tpu as pltpu
from jax.sharding import PartitionSpec as P

HD = 64
MESH = pl.DeviceIdType.MESH


masked_value = -1e9


def dot_t(left, right):
    return lax.dot_general(left, right, (((1,), (1,)), ((), ())), preferred_element_type=jnp.float32)


def dot_n(left, right):
    return lax.dot_general(left, right, (((1,), (0,)), ((), ())), preferred_element_type=jnp.float32)


def swap_halves(values, first_half):
    return jnp.where(first_half, pltpu.roll(values, 96, 1), pltpu.roll(values, 32, 1))


def lane_tests(rows):
    lane = lax.broadcasted_iota(jnp.int32, (rows, 128), 1)
    return lane < 64, (lane % 64) < 32


def block_bias(seg_col_ref, seg_row_ref, i, j, size):
    keys = seg_col_ref[pl.ds(pl.multiple_of(j * size, size), size), :]
    rows = seg_row_ref[:, pl.ds(pl.multiple_of(i * size, size), size)]
    key_at = j * size + lax.broadcasted_iota(jnp.int32, (size, size), 0)
    row_at = i * size + lax.broadcasted_iota(jnp.int32, (size, size), 1)
    return jnp.where((keys == rows) & (key_at <= row_at), 0.0, masked_value)


def stack_pair(pair, low_lanes):
    zero = jnp.zeros_like(pair)
    return jnp.concatenate([jnp.where(low_lanes, pair, zero), jnp.where(low_lanes, zero, pair)], axis=0)


class Line:
    def __init__(self, n, chunks, rc, lag, part, got, out, sems, order=None):
        self.order = order
        self.n, self.chunks, self.rc, self.lag = n, chunks, rc, lag
        self.part, self.got, self.out = part, got, out
        self.send_a, self.recv_a, self.send_g, self.recv_g = sems
        self.me = lax.axis_index("tensor")
        self.steps = chunks + 2 * lag * (n - 1)

    def rows(self, stream, c):
        begin = (stream * self.chunks + c) * self.rc if self.order is None else self.order(stream, c)
        return pl.ds(pl.multiple_of(begin, self.rc), self.rc)

    def side(self, stream):
        pos = self.me if stream == 0 else self.n - 1 - self.me
        fwd = self.me + 1 if stream == 0 else self.me - 1
        bwd = self.me - 1 if stream == 0 else self.me + 1
        return pos, fwd, bwd

    def toward(self, stream, c, nxt, src):
        return pltpu.make_async_remote_copy(
            src_ref=src, dst_ref=self.got.at[stream, c],
            send_sem=self.send_a.at[stream, c], recv_sem=self.recv_a.at[stream, c],
            device_id={"tensor": nxt}, device_id_type=MESH)

    def back(self, stream, c, nxt):
        where = self.rows(stream, c)
        return pltpu.make_async_remote_copy(
            src_ref=self.out.at[where], dst_ref=self.out.at[where],
            send_sem=self.send_g.at[stream, c], recv_sem=self.recv_g.at[stream, c],
            device_id={"tensor": nxt}, device_id_type=MESH)

    def step(self, s):
        n, lag = self.n, self.lag
        for stream in (0, 1):
            pos, fwd, bwd = self.side(stream)
            c = s - lag * pos

            @pl.when((c >= 0) & (c < self.chunks))
            def _():
                where = self.rows(stream, c)
                slot = self.got.at[stream, c]

                def summed():
                    self.toward(stream, c, fwd, slot).wait_recv()
                    return (
                        self.part[where, :].astype(jnp.float32) + self.got[stream, c].astype(jnp.float32)
                    ).astype(self.out.dtype)

                @pl.when(pos == 0)
                def _():
                    self.toward(stream, c, fwd, self.part.at[where]).start()

                @pl.when((pos > 0) & (pos < n - 1))
                def _():
                    self.got[stream, c] = summed()
                    self.toward(stream, c, fwd, slot).start()

                @pl.when(pos == n - 1)
                def _():
                    self.out[where, :] = summed()
                    self.back(stream, c, bwd).start()
            d = s - lag * (n - 1) - lag * (n - 1 - pos)

            @pl.when((d >= 0) & (d < self.chunks) & (pos < n - 1))
            def _():
                self.back(stream, d, bwd).wait_recv()

                @pl.when(pos > 0)
                def _():
                    self.back(stream, d, bwd).start()

    def drain(self):
        def one(c, carry):
            for stream in (0, 1):
                pos, fwd, bwd = self.side(stream)

                @pl.when(pos < self.n - 1)
                def _():
                    self.toward(stream, c, fwd, self.got.at[stream, c]).wait_send()

                @pl.when(pos > 0)
                def _():
                    self.back(stream, c, bwd).wait_send()
            return carry

        lax.fori_loop(0, self.chunks, one, 0)


def greet(n):
    me = lax.axis_index("tensor")
    barrier = pltpu.get_barrier_semaphore()

    @pl.when(me > 0)
    def _():
        pl.semaphore_signal(barrier, inc=1, device_id={"tensor": me - 1}, device_id_type=MESH)

    @pl.when(me < n - 1)
    def _():
        pl.semaphore_signal(barrier, inc=1, device_id={"tensor": me + 1}, device_id_type=MESH)

    @pl.when((me > 0) & (me < n - 1))
    def _():
        pl.semaphore_wait(barrier, 2)

    @pl.when((me == 0) | (me == n - 1))
    def _():
        pl.semaphore_wait(barrier, 1)


def line_scratch(chunks, rc, width):
    return [pltpu.VMEM((2, chunks, rc, width), jnp.bfloat16)] + [pltpu.SemaphoreType.DMA((2, chunks))] * 4


def line_kernel(n, chunks, lag, count, *refs):
    parts, outs, scratch = refs[:count], refs[count:2 * count], refs[2 * count:]
    rc = parts[0].shape[0] // (2 * chunks)
    lines = [
        Line(n, chunks, rc, lag, parts[k], scratch[5 * k], outs[k], scratch[5 * k + 1:5 * k + 5])
        for k in range(count)
    ]
    greet(n)

    def step(s, carry):
        for k, line in enumerate(lines):
            line.step(s - k * chunks)
        return carry

    lax.fori_loop(0, lines[0].steps + (count - 1) * chunks, step, 0)
    for line in lines:
        line.drain()


def line_reduce(parts, n, chunks, cid, lag=2):
    rows, width = parts[0].shape
    count = len(parts)
    rc = rows // (2 * chunks)
    scratch = []
    for _ in parts:
        scratch += line_scratch(chunks, rc, width)
    vmem = pl.BlockSpec(memory_space=pltpu.VMEM)
    return pl.pallas_call(
        functools.partial(line_kernel, n, chunks, lag, count),
        out_shape=tuple(jax.ShapeDtypeStruct((rows, width), jnp.bfloat16) for _ in parts),
        in_specs=[vmem] * count,
        out_specs=(vmem,) * count,
        scratch_shapes=scratch,
        compiler_params=pltpu.CompilerParams(collective_id=cid, has_side_effects=True, vmem_limit_bytes=40 << 20),
        cost_estimate=pl.CostEstimate(flops=rows * width * 2 * count, bytes_accessed=rows * width * 120 * count,
                                      transcendentals=0),
    )(*parts)


def dot_rows(left, right):
    return lax.dot_general(left, right, (((0,), (0,)), ((), ())), preferred_element_type=jnp.float32)


def ff_kernel(n, chunks, lag, eps, branch, gain, x, cot_hbm, w_hbm,
              feed_hbm, middle_hbm, low_hbm, gain_out, grads_hbm,
              got, sa, ra, sg, rg, two_sum, two_part, weight, cot, normed, hidden, gg, feed,
              middle_stage, low_stage, unit_stage, w_sem, cot_sem, feed_sem, stage_sem, grad_sem):
    rows, width = branch.shape
    ff = hidden.shape[1]
    rc = rows // (2 * chunks)
    per = 8
    offset = per - 1
    half = rows // 2
    hb = per * rc
    block = 2 * hb
    blocks = chunks // per
    line = Line(n, chunks, rc, lag, two_part, got, two_sum, (sa, ra, sg, rg))
    landed = 2 * lag * (n - 1) + offset
    tile = 256
    full, rest = ff // tile, ff % tile
    wide = width // tile

    groups = []
    for g, (begin, end) in enumerate(((0, tile), (tile, 2 * tile), (2 * tile, ff))):
        groups.append([
            pltpu.make_async_copy(w_hbm.at[:, pl.ds(t * ff + begin, end - begin)],
                                  weight.at[:, pl.ds(t * ff + begin, end - begin)], w_sem.at[g, t])
            for t in range(3)
        ])
    for copy in sum(groups, []):
        copy.start()

    def natural(k, b):
        return pl.ds(pl.multiple_of(k * half + b * hb, hb), hb)

    def blocked(k, b):
        return pl.ds(pl.multiple_of(b * block + k * hb, hb), hb)

    def load_cot(b):
        return [pltpu.make_async_copy(cot_hbm.at[natural(k, b)], cot.at[blocked(k, b)], cot_sem.at[b, k])
                for k in (0, 1)]

    def save_feed(b):
        return [pltpu.make_async_copy(feed.at[pl.ds(k * hb, hb)], feed_hbm.at[natural(k, b)], feed_sem.at[k])
                for k in (0, 1)]

    def save_rows(d):
        copies = []
        for k in (0, 1):
            where = line.rows(k, d)
            copies.append(pltpu.make_async_copy(middle_stage.at[k], middle_hbm.at[where], stage_sem.at[0, k]))
            copies.append(pltpu.make_async_copy(low_stage.at[k], low_hbm.at[where], stage_sem.at[1, k]))
        return copies

    def save_units(w):
        return [pltpu.make_async_copy(unit_stage, grads_hbm.at[pl.ds(pl.multiple_of(w * tile, tile), tile)], grad_sem.at[0])]

    def start(copies):
        for copy in copies:
            copy.start()

    def wait(copies):
        for copy in copies:
            copy.wait()

    for b in range(blocks):
        start(load_cot(b))
    gain_out[...] = jnp.zeros_like(gain_out)
    greet(n)

    def unit_rows(where):
        middle = x[where, :].astype(jnp.float32) + branch[where, :].astype(jnp.float32)
        inverse = lax.rsqrt(jnp.mean(middle * middle, axis=-1, keepdims=True) + eps)
        return middle * inverse, inverse

    def normalize(b):
        def some(r, carry):
            for k in (0, 1):
                where = pl.ds(pl.multiple_of(k * half + b * hb + r * rc, rc), rc)
                at = pl.ds(pl.multiple_of(b * block + k * hb + r * rc, rc), rc)
                normed[at, :] = (unit_rows(where)[0] * gain[1:2, :]).astype(jnp.bfloat16)
            return carry

        lax.fori_loop(0, per, some, 0)

    def step(s, carry):
        line.step(s - offset)
        b = s // per
        phase = s - b * per
        live = s < chunks
        mine = pl.ds(pl.multiple_of(b * block, block), block)

        def units(at, count):
            columns = pl.ds(at, count)
            second = pl.ds(pl.multiple_of(ff + at, 128), count)
            third = pl.ds(pl.multiple_of(2 * ff + at, 128), count)
            gate = dot_n(normed[mine, :], weight[:, columns])
            up = dot_n(normed[mine, :], weight[:, second])
            grad_hidden = dot_n(cot[mine, :], weight[:, third])
            sg_gate = 1.0 / (1.0 + jnp.exp(-gate))
            silu = gate * sg_gate
            hidden[mine, columns] = (silu * up).astype(jnp.bfloat16)
            gg[mine, columns] = (grad_hidden * up * sg_gate * (1.0 + gate * (1.0 - sg_gate))).astype(jnp.bfloat16)
            gg[mine, second] = (grad_hidden * silu).astype(jnp.bfloat16)

        def unit_tile(t, c):
            for g in range(3):
                @pl.when((b == 0) & (t == g))
                def _():
                    wait(groups[g])
            units(pl.multiple_of(t * tile, tile), tile)
            return c

        @pl.when(live & (phase == 0))
        def _():
            normalize(b)
            wait(load_cot(b))

        @pl.when(live & (phase < 3))
        def _():
            lax.fori_loop(jnp.maximum(2 * phase - 1, 0), jnp.minimum(2 * phase + 1, full), unit_tile, 0)

        @pl.when(live & (phase == 3))
        def _():
            if rest:
                units(full * tile, rest)

            @pl.when(b > 0)
            def _():
                wait(save_feed(b - 1))

        @pl.when(live & ((phase == 3) | (phase == 4)))
        def _():
            def feed_tile(t, c):
                columns = pl.ds(pl.multiple_of(t * 2 * tile, 2 * tile), 2 * tile)
                feed[:, columns] = dot_t(hidden[mine, :], weight[columns, 2 * ff:]).astype(jnp.bfloat16)
                return c

            lax.fori_loop((phase - 3) * (wide // 4), (phase - 2) * (wide // 4), feed_tile, 0)

            @pl.when(phase == 4)
            def _():
                start(save_feed(b))

        @pl.when(live & ((phase == 5) | (phase == 6)))
        def _():
            def two_tile(t, c):
                at = pl.ds(pl.multiple_of(t * 2 * tile, 2 * tile), 2 * tile)
                value = dot_t(gg[mine, :], weight[at, :2 * ff]).astype(jnp.bfloat16)
                for k in (0, 1):
                    two_part[natural(k, b), at] = value[k * hb:(k + 1) * hb]
                return c

            lax.fori_loop((phase - 5) * (wide // 4), (phase - 4) * (wide // 4), two_tile, 0)

        d = s - landed

        @pl.when(d >= 0)
        def _():
            @pl.when(d > 0)
            def _():
                wait(save_rows(d - 1))
            for k in (0, 1):
                where = line.rows(k, d)
                at = pl.ds(pl.multiple_of((d // per) * block + k * hb + (d - (d // per) * per) * rc, rc), rc)
                pieces = [pl.ds(c * tile, tile) for c in range(wide)]

                def middle_at(c):
                    return x[where, c].astype(jnp.float32) + branch[where, c].astype(jnp.float32)

                def folded(value):
                    return value[:, :128] + value[:, 128:]

                total = jnp.zeros((rc, 128), jnp.float32)
                for c in pieces:
                    middle = middle_at(c)
                    total = total + folded(middle * middle)
                inverse = lax.rsqrt(jnp.sum(total, axis=-1, keepdims=True) * (1.0 / width) + eps)
                total = jnp.zeros((rc, 128), jnp.float32)
                for c in pieces:
                    product = two_sum[where, c].astype(jnp.float32) * (middle_at(c) * inverse)
                    gain_out[:, c] += jnp.sum(product, axis=0, keepdims=True)
                    total = total + folded(product * gain[1:2, c])
                inner = jnp.sum(total, axis=-1, keepdims=True) * (1.0 / width)
                for c in pieces:
                    scaled = two_sum[where, c].astype(jnp.float32) * gain[1:2, c]
                    value = cot[at, c].astype(jnp.float32) + inverse * (scaled - middle_at(c) * inverse * inner)
                    middle_stage[k, :, c] = value
                    low_stage[k, :, c] = value.astype(jnp.bfloat16)
            start(save_rows(d))

        late = s - chunks
        w = late // 2

        @pl.when((late >= 0) & (late == 2 * w) & (w < wide))
        def _():
            @pl.when(w > 0)
            def _():
                wait(save_units(w - 1))
            columns = pl.ds(pl.multiple_of(w * tile, tile), tile)
            left = normed[:, columns]
            for t in (0, 1):
                unit_stage[:, t * ff:(t + 1) * ff] = dot_rows(left, gg[:, t * ff:(t + 1) * ff]).astype(jnp.bfloat16)
            unit_stage[:, 2 * ff:] = dot_rows(cot[:, columns], hidden[...]).astype(jnp.bfloat16)
            start(save_units(w))
        return carry

    lax.fori_loop(0, offset + line.steps, step, 0)
    line.drain()
    wait(save_feed(blocks - 1))
    wait(save_rows(chunks - 1))
    wait(save_units(wide - 1))


def feed_forward(branch, gain, x, cot, weight, n, cid, chunks=32, lag=2):
    rows, width = branch.shape
    ff = weight.shape[1] // 3
    rc = rows // (2 * chunks)
    block = 16 * rc
    blocks = chunks // 8
    low = jnp.bfloat16
    vmem = pl.BlockSpec(memory_space=pltpu.VMEM)
    hbm = pl.BlockSpec(memory_space=pl.ANY)
    dma = pltpu.SemaphoreType.DMA
    shape = jax.ShapeDtypeStruct
    return pl.pallas_call(
        functools.partial(ff_kernel, n, chunks, lag, norm_eps),
        out_shape=(
            shape((rows, width), low), shape((rows, width), jnp.float32), shape((rows, width), low),
            shape((1, width), jnp.float32), shape((width, 3 * ff), low),
        ),
        in_specs=[vmem, vmem, vmem, hbm, hbm],
        out_specs=(hbm, hbm, hbm, vmem, hbm),
        scratch_shapes=line_scratch(chunks, rc, width) + [
            pltpu.VMEM((rows, width), low),
            pltpu.VMEM((rows, width), low),
            pltpu.VMEM((width, 3 * ff), low),
            pltpu.VMEM((rows, width), low),
            pltpu.VMEM((rows, width), low),
            pltpu.VMEM((rows, ff), low),
            pltpu.VMEM((rows, 2 * ff), low),
            pltpu.VMEM((block, width), low),
            pltpu.VMEM((2, rc, width), jnp.float32),
            pltpu.VMEM((2, rc, width), low),
            pltpu.VMEM((256, 3 * ff), low),
            dma((3, 3)), dma((blocks, 2)), dma((2,)), dma((2, 2)), dma((1,)),
        ],
        compiler_params=pltpu.CompilerParams(collective_id=cid, has_side_effects=True, vmem_limit_bytes=63 << 20),
        cost_estimate=pl.CostEstimate(flops=18 * rows * width * ff, bytes_accessed=rows * width * 150,
                                      transcendentals=rows * ff),
    )(branch, gain, x, cot, weight)


def head_kernel(n, m, chunks, lag, eps, size, pairs,
                gain_part, query_own, keyval_own, out_own, frequency, seg_row_ref,
                x_hbm, gateup_hbm, down_hbm,
                branch, gain, lse_ref, seg_col_ref, cos_hbm, sin_hbm, mix_hbm, q_hbm, k_hbm, v_hbm, qkv_hbm, out_hbm, ff_hbm,
                got, sa, ra, sg, rg, part, normed, raw, bias, scores, v_turned, got_gain,
                x, cos_ref, sin_ref, mix_ref, q_ref, k_ref, v_ref, qkv_w, out_w, gateup_own, down_own, ff_own,
                send_gain, recv_gain, send_direct, send_forward, recv_w, own_sem, save_sem, result_sem, x_sem,
                send_ff, pass_ff, recv_ff):
    rows, width = branch.shape
    q_width = pairs * 128
    x_load = pltpu.make_async_copy(x_hbm, x, x_sem)
    x_load.start()
    results = [
        pltpu.make_async_copy(source, target, result_sem.at[k])
        for k, (source, target) in enumerate((
            (q_ref, q_hbm), (k_ref, k_hbm), (v_ref, v_hbm), (cos_ref, cos_hbm), (sin_ref, sin_hbm),
            (qkv_w, qkv_hbm), (out_w, out_hbm), (mix_ref, mix_hbm)))
    ]
    z = lax.axis_index("tensor")
    dp = lax.axis_index("dp")
    share = width // m
    chips = m // 2
    chip, core = dp // 2, dp % 2
    rc = rows // (2 * chunks)
    per = size // (2 * rc)
    hb = size // 2
    blocks = rows // size
    tile = 256
    wide = width // tile
    low_lanes, first_half = lane_tests(size)
    low_rows = lax.broadcasted_iota(jnp.int32, (128, size), 0) < 64
    wholes = (qkv_w, out_w)
    ff = down_own.shape[0]
    piece = 32
    pieces = share // piece
    spacing = 40 // pieces
    owned = (
        pltpu.make_async_copy(gateup_hbm, gateup_own, own_sem.at[0]),
        pltpu.make_async_copy(down_hbm, down_own, own_sem.at[1]),
    )
    for copy in owned:
        copy.start()

    def ascending(stream, c):
        b = c // per
        return b * size + stream * hb + (c - b * per) * rc

    line = Line(n, chunks, rc, lag, part, got, branch, (sa, ra, sg, rg), ascending)

    def shard_rows(s):
        return pl.ds(pl.multiple_of(s * share, share), share)

    def direct(kind, k):
        peer = 2 * lax.rem(chip + k, chips) + core
        return pltpu.make_async_remote_copy(
            src_ref=wholes[kind].at[shard_rows(dp)], dst_ref=wholes[kind].at[shard_rows(dp)], send_sem=send_direct.at[kind, k],
            recv_sem=recv_w.at[kind, dp], device_id={"dp": peer}, device_id_type=MESH)

    def forward(kind, c, side):
        shard = 2 * c + side
        where = shard_rows(shard)
        return pltpu.make_async_remote_copy(
            src_ref=wholes[kind].at[where], dst_ref=wholes[kind].at[where], send_sem=send_forward.at[kind, c],
            recv_sem=recv_w.at[kind, shard], device_id={"dp": 2 * chip + 1 - core}, device_id_type=MESH)

    def piece_rows(shard, p):
        return pl.ds(pl.multiple_of(shard * share + p * piece, piece), piece)

    def own_piece(p):
        return ff_own.at[pl.ds(pl.multiple_of(p * piece, piece), piece)]

    def send_piece(k, p):
        peer = 2 * lax.rem(chip + k, chips) + core
        return pltpu.make_async_remote_copy(
            src_ref=own_piece(p), dst_ref=ff_hbm.at[piece_rows(dp, p)], send_sem=send_ff.at[k, p],
            recv_sem=recv_ff.at[dp, p], device_id={"dp": peer}, device_id_type=MESH)

    def pass_piece(c, side, p, src=None):
        shard = 2 * c + side
        where = ff_hbm.at[piece_rows(shard, p)]
        return pltpu.make_async_remote_copy(
            src_ref=where if src is None else src, dst_ref=where, send_sem=pass_ff.at[c, p],
            recv_sem=recv_ff.at[shard, p], device_id={"dp": 2 * chip + 1 - core}, device_id_type=MESH)

    def save_own():
        return pltpu.make_async_copy(ff_own, ff_hbm.at[shard_rows(dp)], save_sem)

    def send_gains(k, sender):
        return pltpu.make_async_remote_copy(
            src_ref=gain_part, dst_ref=got_gain.at[sender], send_sem=send_gain.at[k], recv_sem=recv_gain.at[sender],
            device_id={"dp": lax.rem(dp + k, m)}, device_id_type=MESH)

    barrier = pltpu.get_barrier_semaphore()

    @pl.when(z > 0)
    def _():
        pl.semaphore_signal(barrier, inc=1, device_id={"tensor": z - 1}, device_id_type=MESH)

    @pl.when(z < n - 1)
    def _():
        pl.semaphore_signal(barrier, inc=1, device_id={"tensor": z + 1}, device_id_type=MESH)

    for k in range(1, m):
        pl.semaphore_signal(barrier, inc=1, device_id={"dp": lax.rem(dp + k, m)}, device_id_type=MESH)

    qkv_w[shard_rows(dp), :q_width] = query_own[...].astype(jnp.bfloat16)
    both_own = jnp.concatenate([keyval_own[0], keyval_own[1]], axis=0)
    qkv_w[shard_rows(dp), q_width:] = both_own.T.astype(jnp.bfloat16)
    for t in range(q_width // 128):
        out_w[shard_rows(dp), t * 128:(t + 1) * 128] = out_own[t * 128:(t + 1) * 128, :].T.astype(jnp.bfloat16)
    got_gain[dp] = gain_part[...]

    @pl.when((z > 0) & (z < n - 1))
    def _():
        pl.semaphore_wait(barrier, m + 1)

    @pl.when((z == 0) | (z == n - 1))
    def _():
        pl.semaphore_wait(barrier, m)

    for k in range(1, m):
        send_gains(k, dp).start()
    for kind in (0, 1):
        for k in range(1, chips):
            direct(kind, k).start()
        forward(kind, chip, core).start()
    for k in range(1, m):
        send_gains(k, lax.rem(dp + m - k, m)).wait_recv()
    whole = got_gain[0]
    for k in range(1, m):
        whole = whole + got_gain[k]
    gain[...] = whole.astype(jnp.bfloat16).astype(jnp.float32)

    x_load.wait()

    def norm_rows(r, carry):
        where = pl.ds(pl.multiple_of(r * rc, rc), rc)
        values = x[where, :].astype(jnp.float32)
        inverse = lax.rsqrt(jnp.mean(values * values, axis=-1, keepdims=True) + eps)
        normed[where, :] = (values * inverse * gain[0:1, :]).astype(jnp.bfloat16)
        return carry

    lax.fori_loop(0, rows // rc, norm_rows, 0)
    def tables(i, carry):
        where = pl.ds(pl.multiple_of(i * size, size), size)
        ids = jnp.broadcast_to(seg_row_ref[:, where].astype(jnp.float32), (128, size)).T[:, :1]
        seg_col_ref[where, :] = ids.astype(jnp.int32)
        earlier = jnp.where(seg_row_ref[...].astype(jnp.float32) < ids, 1.0, 0.0)
        place = (i * size + lax.broadcasted_iota(jnp.int32, (size, 1), 0)).astype(jnp.float32) - jnp.sum(
            earlier, axis=1, keepdims=True)
        angles = place * frequency[...]
        sines = jnp.sin(angles)
        cos_ref[where, :] = jnp.cos(angles)
        sin_ref[where, :] = jnp.where(first_half, -sines, sines)
        return carry

    lax.fori_loop(0, blocks, tables, 0)
    for copy in owned:
        copy.wait()

    def own_rows(r, carry):
        where = pl.ds(pl.multiple_of(r * piece, piece), piece)
        for t in (0, 1):
            ff_own[where, t * ff:(t + 1) * ff] = gateup_own[t, where, :].astype(jnp.bfloat16)
        return carry

    lax.fori_loop(0, pieces, own_rows, 0)

    def own_columns(t, carry):
        at = pl.ds(pl.multiple_of(2 * ff + t * 128, 128), 128)
        ff_own[:, at] = down_own[pl.ds(pl.multiple_of(t * 128, 128), 128), :].T.astype(jnp.bfloat16)
        return carry

    lax.fori_loop(0, ff // 128, own_columns, 0)
    save_own().start()

    def pass_on(kind):
        for k in range(1, chips):
            c = lax.rem(chip + chips - k, chips)
            forward(kind, c, core).wait_recv()
            forward(kind, c, core).start()

    def receive(kind):
        for c in range(chips):
            forward(kind, c, 1 - core).wait_recv()

    pass_on(0)
    receive(0)
    for p in range(min(2, pieces)):
        for k in range(1, chips):
            send_piece(k, p).start()

    def prepare(i, carry):
        where = pl.ds(pl.multiple_of(i * size, size), size)
        raw[...] = dot_n(normed[where, :], qkv_w[...])
        cosines, sines = cos_ref[where, :], sin_ref[where, :]
        for hp in range(pairs):
            values = raw[:, hp * 128:(hp + 1) * 128]
            turned = values * cosines + swap_halves(values, first_half) * sines
            q_ref[where, hp * 128:(hp + 1) * 128] = (
                turned.astype(jnp.bfloat16).astype(jnp.float32) * 0.125).astype(jnp.bfloat16)
        both = raw[:, q_width:q_width + 128]
        other = pltpu.roll(both, 64, 1)
        keys = jnp.where(low_lanes, both, other)
        k_ref[where, :] = (keys * cosines + swap_halves(keys, first_half) * sines).astype(jnp.bfloat16)
        values = jnp.where(low_lanes, other, both)
        v_ref[where, :] = values.astype(jnp.bfloat16)
        v_turned[i] = values.T.astype(jnp.bfloat16)
        return carry

    lax.fori_loop(0, blocks, prepare, 0)
    for copy in results[:5]:
        copy.start()
    pass_on(1)

    def attend(i, hp):
        where = pl.ds(pl.multiple_of(i * size, size), size)
        columns = pl.ds(pl.multiple_of(hp * 128, 128), 128)
        stacked = stack_pair(q_ref[where, columns], low_lanes)

        def score(j, top):
            keys = k_ref[pl.ds(pl.multiple_of(j * size, size), size), :]
            b = bias[j]
            s = dot_t(keys, stacked) + jnp.concatenate([b, b], axis=1)
            scores[j] = s
            return jnp.maximum(top, jnp.max(s, axis=0, keepdims=True))

        top = lax.fori_loop(0, i + 1, score, jnp.full((1, 2 * size), -jnp.inf, jnp.float32))

        def mix(j, c):
            total, acc = c
            p = jnp.exp(scores[j] - top)
            total = total + jnp.sum(p, axis=0, keepdims=True)
            return total, acc + dot_n(v_turned[j], p.astype(jnp.bfloat16))

        total, acc = lax.fori_loop(0, i + 1, mix, (
            jnp.zeros((1, 2 * size), jnp.float32), jnp.zeros((128, 2 * size), jnp.float32)))
        lse_ref[i, hp] = top + jnp.log(total)
        acc = acc / total
        acc = jnp.where(low_rows, acc[:, :size], acc[:, size:])
        mix_ref[where, columns] = acc.T.astype(jnp.bfloat16)

    def step(s, carry):
        line.step(s - per)
        p_send = (s - 1) // spacing + 2
        p_pass = (s - 12) // spacing

        @pl.when((s >= 1) & ((p_send - 2) * spacing == s - 1) & (p_send < pieces))
        def _():
            for k in range(1, chips):
                send_piece(k, p_send).start()

        @pl.when((s >= 12) & (p_pass * spacing == s - 12) & (p_pass < pieces))
        def _():
            pass_piece(chip, core, p_pass, own_piece(p_pass)).start()
            for k in range(1, chips):
                c = lax.rem(chip + chips - k, chips)
                pass_piece(c, core, p_pass).wait_recv()
                pass_piece(c, core, p_pass).start()

        i = s // per
        hp = s - i * per
        live = s < blocks * per

        @pl.when(live & (hp == 0))
        def _():
            def fill(j, c):
                bias[j] = block_bias(seg_col_ref, seg_row_ref, i, j, size)
                return c

            lax.fori_loop(0, i + 1, fill, 0)

        @pl.when(live)
        def _():
            def each(h, c):
                attend(i, h)
                return c

            lax.fori_loop(hp * pairs // per, (hp + 1) * pairs // per, each, 0)

        @pl.when(s == per - 1)
        def _():
            receive(1)
            for copy in results[5:7]:
                copy.start()

        @pl.when(s == blocks * per)
        def _():
            results[7].start()

        @pl.when(live & (hp == per - 1))
        def _():
            where = pl.ds(pl.multiple_of(i * size, size), size)

            def part_tile(t, c):
                at = pl.ds(pl.multiple_of(t * tile, tile), tile)
                part[where, at] = dot_t(mix_ref[where, :], out_w[at, :]).astype(jnp.bfloat16)
                return c

            lax.fori_loop(0, wide, part_tile, 0)
        return carry

    lax.fori_loop(0, per + line.steps, step, 0)
    line.drain()
    save_own().wait()
    for copy in results:
        copy.wait()

    def settle(p, carry):
        for k in range(1, chips):
            send_piece(k, p).wait_send()
        for c in range(chips):
            pass_piece(c, core, p).wait_send()
            pass_piece(c, 1 - core, p).wait_recv()
        return carry

    lax.fori_loop(0, pieces, settle, 0)
    for k in range(1, m):
        send_gains(k, dp).wait_send()
    for kind in (0, 1):
        for k in range(1, chips):
            direct(kind, k).wait_send()
        for c in range(chips):
            forward(kind, c, core).wait_send()


def attention_head(x, gain_part, query, keyval, out, frequency, seg_row, gateup, down, n, m, cid, size,
                   chunks=32, lag=2):
    rows, width = x.shape
    q_width = query.shape[1]
    share, ff = width // m, down.shape[0]
    pairs = q_width // 128
    rc = rows // (2 * chunks)
    blocks = rows // size
    chips = m // 2
    low = jnp.bfloat16
    vmem = pl.BlockSpec(memory_space=pltpu.VMEM)
    hbm = pl.BlockSpec(memory_space=pl.ANY)
    dma = pltpu.SemaphoreType.DMA
    shape = jax.ShapeDtypeStruct
    return pl.pallas_call(
        functools.partial(head_kernel, n, m, chunks, lag, norm_eps, size, pairs),
        out_shape=(
            shape((rows, width), low), shape((2, width), jnp.float32),
            shape((blocks, pairs, 1, 2 * size), jnp.float32), shape((rows, 1), jnp.int32),
            shape((rows, 128), jnp.float32), shape((rows, 128), jnp.float32), shape((rows, q_width), low),
            shape((rows, q_width), low), shape((rows, 128), low), shape((rows, 128), low),
            shape((width, q_width + 128), low), shape((width, q_width), low), shape((width, 3 * ff), low),
        ),
        in_specs=[vmem] * 6 + [hbm] * 3,
        out_specs=(vmem,) * 4 + (hbm,) * 9,
        scratch_shapes=line_scratch(chunks, rc, width) + [
            pltpu.VMEM((rows, width), low),
            pltpu.VMEM((rows, width), low),
            pltpu.VMEM((size, q_width + 128), jnp.float32),
            pltpu.VMEM((blocks, size, size), jnp.float32),
            pltpu.VMEM((blocks, size, 2 * size), jnp.float32),
            pltpu.VMEM((blocks, 128, size), low),
            pltpu.VMEM((m, 2, width), jnp.float32),
            pltpu.VMEM((rows, width), low),
            pltpu.VMEM((rows, 128), jnp.float32),
            pltpu.VMEM((rows, 128), jnp.float32),
            pltpu.VMEM((rows, q_width), low),
            pltpu.VMEM((rows, q_width), low),
            pltpu.VMEM((rows, 128), low),
            pltpu.VMEM((rows, 128), low),
            pltpu.VMEM((width, q_width + 128), low),
            pltpu.VMEM((width, q_width), low),
            pltpu.VMEM(gateup.shape, jnp.float32),
            pltpu.VMEM(down.shape, jnp.float32),
            pltpu.VMEM((share, 3 * ff), low),
            dma((m,)), dma((m,)), dma((2, chips)), dma((2, chips)), dma((2, m)), dma((2,)), dma, dma((8,)), dma,
            dma((chips, share // 32)), dma((chips, share // 32)), dma((m, share // 32)),
        ],
        compiler_params=pltpu.CompilerParams(collective_id=cid, has_side_effects=True, vmem_limit_bytes=56 << 20),
        cost_estimate=pl.CostEstimate(flops=20 * rows * width * q_width, bytes_accessed=rows * width * 170,
                                      transcendentals=rows * rows * pairs),
    )(gain_part, query, keyval, out, frequency, seg_row, x, gateup, down)


def back_kernel(n, m, chunks, lag, eps, size, pairs,
                feed_part, gain, lse_ref, seg_row_ref,
                low_hbm, q_hbm, k_hbm, v_hbm, mix_hbm, cos_hbm, sin_hbm, seg_hbm, out_hbm, x_hbm, qkv_hbm,
                branch_hbm, middle_hbm,
                layer_hbm, input_hbm, gain_out, reduced,
                got2, sa2, ra2, sg2, rg2, got4, sa4, ra4, sg4, rg4, feed_sum, part, grad_sum,
                grad_low, q_ref, k_ref, v_ref, mix_ref, cos_ref, sin_ref, seg_col_ref, out_w, x, qkv_w,
                normed, grad_mix, bias, k_turned, grad_k, grad_v, grad_qkv, send, recv,
                branch_stage, layer_stage, middle_stage, input_stage,
                w_sem, branch_sem, middle_sem, layer_sem, input_sem, send_sem, recv_sem):
    rows, width = feed_part.shape
    q_width = pairs * 128
    z = lax.axis_index("tensor")
    dp = lax.axis_index("dp")
    rc = rows // (2 * chunks)
    per = size // (2 * rc)
    hb = size // 2
    blocks = rows // size
    tile = 256
    wide = width // tile
    share = width // m
    owners = tile // share
    lead = 2 * lag * (n - 1)
    shift = chunks + per
    low_lanes, first_half = lane_tests(size)
    low_rows = lax.broadcasted_iota(jnp.int32, (128, size), 0) < 64

    def descending(stream, c):
        b = c // per
        return (blocks - 1 - b) * size + stream * hb + (c - b * per) * rc

    two = Line(n, chunks, rc, lag, feed_part, got2, feed_sum, (sa2, ra2, sg2, rg2))
    four = Line(n, chunks, rc, lag, part, got4, grad_sum, (sa4, ra4, sg4, rg4), descending)
    loads = [
        pltpu.make_async_copy(source, target, w_sem.at[k])
        for k, (source, target) in enumerate((
            (k_hbm, k_ref), (q_hbm, q_ref), (low_hbm, grad_low), (out_hbm, out_w), (v_hbm, v_ref), (mix_hbm, mix_ref),
            (cos_hbm, cos_ref), (sin_hbm, sin_ref), (seg_hbm, seg_col_ref), (x_hbm, x), (qkv_hbm, qkv_w)))
    ]
    for copy in loads:
        copy.start()

    def start(copies):
        for copy in copies:
            copy.start()

    def wait(copies):
        for copy in copies:
            copy.wait()

    def load_branch(d, slot):
        return [pltpu.make_async_copy(branch_hbm.at[two.rows(k, d)], branch_stage.at[slot, k], branch_sem.at[slot, k])
                for k in (0, 1)]

    def load_middle(d, slot):
        return [pltpu.make_async_copy(middle_hbm.at[four.rows(k, d)], middle_stage.at[slot, k], middle_sem.at[slot, k])
                for k in (0, 1)]

    def save_layer(d):
        return [pltpu.make_async_copy(layer_stage.at[k], layer_hbm.at[two.rows(k, d)], layer_sem.at[k]) for k in (0, 1)]

    def save_input(d):
        return [pltpu.make_async_copy(input_stage.at[k], input_hbm.at[four.rows(k, d)], input_sem.at[k]) for k in (0, 1)]

    def to_owner(w, o):
        owner = w * owners + o
        return pltpu.make_async_remote_copy(
            src_ref=send.at[w, pl.ds(o * share, share)], dst_ref=recv.at[dp], send_sem=send_sem.at[owner],
            recv_sem=recv_sem.at[dp], device_id={"dp": owner}, device_id_type=MESH)

    gain_out[...] = jnp.zeros_like(gain_out)

    def prepare(i, carry):
        at = pl.ds(pl.multiple_of(i * size, size), size)
        k_turned[i] = k_ref[at, :].astype(jnp.float32).T.astype(jnp.bfloat16)
        grad_k[i] = jnp.zeros((size, 128), jnp.float32)
        grad_v[i] = jnp.zeros((size, 128), jnp.float32)
        return carry

    barrier = pltpu.get_barrier_semaphore()

    @pl.when(z > 0)
    def _():
        pl.semaphore_signal(barrier, inc=1, device_id={"tensor": z - 1}, device_id_type=MESH)

    @pl.when(z < n - 1)
    def _():
        pl.semaphore_signal(barrier, inc=1, device_id={"tensor": z + 1}, device_id_type=MESH)

    for k in range(1, m):
        pl.semaphore_signal(barrier, inc=1, device_id={"dp": lax.rem(dp + k, m)}, device_id_type=MESH)

    @pl.when((z > 0) & (z < n - 1))
    def _():
        pl.semaphore_wait(barrier, m + 1)

    @pl.when((z == 0) | (z == n - 1))
    def _():
        pl.semaphore_wait(barrier, m)

    def unit_rows(where):
        values = x[where, :].astype(jnp.float32)
        inverse = lax.rsqrt(jnp.mean(values * values, axis=-1, keepdims=True) + eps)
        return values * inverse, inverse

    def attend(i, hp):
        at_rows = pl.ds(pl.multiple_of(i * size, size), size)
        columns = pl.ds(pl.multiple_of(hp * 128, 128), 128)
        stacked = stack_pair(q_ref[at_rows, columns], low_lanes)
        grad_pair = grad_mix[:, columns]
        grad_stacked = stack_pair(grad_pair, low_lanes)
        product = (grad_pair.astype(jnp.float32) * mix_ref[at_rows, columns].astype(jnp.float32)).T
        spread = jnp.concatenate([
            jnp.sum(product[:64], axis=0, keepdims=True), jnp.sum(product[64:], axis=0, keepdims=True)], axis=1)
        logsum = lse_ref[i, hp]

        def piece(j, acc):
            at = pl.ds(pl.multiple_of(j * size, size), size)
            b = bias[j]
            s = dot_t(k_ref[at, :], stacked) + jnp.concatenate([b, b], axis=1)
            p = jnp.exp(s - logsum)
            grad_p = dot_t(v_ref[at, :], grad_stacked)
            grad_s = (p * (grad_p - spread)).astype(jnp.bfloat16)
            grad_v[j] += dot_n(p.astype(jnp.bfloat16), grad_stacked)
            grad_k[j] += dot_n(grad_s, stacked)
            return acc + dot_n(k_turned[j], grad_s)

        acc = lax.fori_loop(0, i + 1, piece, jnp.zeros((128, 2 * size), jnp.float32))
        acc = jnp.where(low_rows, acc[:, :size], acc[:, size:]).T * 0.125
        turned = acc * cos_ref[at_rows, :] - swap_halves(acc, first_half) * sin_ref[at_rows, :]
        grad_qkv[at_rows, columns] = turned.astype(jnp.bfloat16)

    def step(s, carry):
        two.step(s)
        four.step(s - shift)
        b = s // per
        hp = s - b * per
        i = blocks - 1 - b
        live = s < blocks * per
        at_rows = pl.ds(pl.multiple_of(i * size, size), size)

        @pl.when(s == 0)
        def _():
            wait(loads)
            lax.fori_loop(0, blocks, prepare, 0)

        @pl.when(live & (hp == 0))
        def _():
            grad_mix[...] = dot_n(grad_low[at_rows, :], out_w[...]).astype(jnp.bfloat16)

            def fill(j, c):
                bias[j] = block_bias(seg_col_ref, seg_row_ref, i, j, size)
                return c

            lax.fori_loop(0, i + 1, fill, 0)

        @pl.when(live)
        def _():
            def each(h, c):
                attend(i, h)
                return c

            lax.fori_loop(hp * pairs // per, (hp + 1) * pairs // per, each, 0)

            def some(r, c):
                at = pl.ds(pl.multiple_of(s * 2 * rc + r * rc, rc), rc)
                normed[at, :] = (unit_rows(at)[0] * gain[0:1, :]).astype(jnp.bfloat16)
                return c

            lax.fori_loop(0, 2, some, 0)

        @pl.when(live & (hp == per - 1))
        def _():
            cosines, sines = cos_ref[at_rows, :], sin_ref[at_rows, :]
            dk = grad_k[i] + pltpu.roll(grad_k[i], 64, 1)
            dk = dk * cosines - swap_halves(dk, first_half) * sines
            dv = grad_v[i] + pltpu.roll(grad_v[i], 64, 1)
            grad_qkv[at_rows, q_width:] = jnp.where(low_lanes, dk, dv).astype(jnp.bfloat16)

            def part_tile(t, c):
                at = pl.ds(pl.multiple_of(t * tile, tile), tile)
                part[at_rows, at] = dot_t(grad_qkv[at_rows, :], qkv_w[at, :]).astype(jnp.bfloat16)
                return c

            lax.fori_loop(0, wide, part_tile, 0)

        w = s - blocks * per

        @pl.when((w >= 0) & (w < wide))
        def _():
            columns = pl.ds(pl.multiple_of(w * tile, tile), tile)
            send[w, :, :q_width + 128] = dot_rows(normed[:, columns], grad_qkv[...]).astype(jnp.bfloat16)
            send[w, :, q_width + 128:] = dot_rows(grad_low[:, columns], mix_ref[...]).astype(jnp.bfloat16)
            for o in range(owners):
                owner = w * owners + o

                @pl.when(owner != dp)
                def _():
                    to_owner(w, o).start()

                @pl.when(owner == dp)
                def _():
                    recv[dp] = send[w, o * share:(o + 1) * share, :]

        e = s - lead + 1

        @pl.when((e >= 0) & (e < chunks))
        def _():
            start(load_branch(e, e % 2))

        d = s - lead

        @pl.when((d >= 0) & (d < chunks))
        def _():
            wait(load_branch(d, d % 2))

            @pl.when(d > 0)
            def _():
                wait(save_layer(d - 1))
            for k in (0, 1):
                where = two.rows(k, d)
                layer_stage[k] = (
                    x[where, :].astype(jnp.float32) + branch_stage[d % 2, k].astype(jnp.float32)
                    + feed_sum[where, :].astype(jnp.float32)
                ).astype(jnp.bfloat16)
            start(save_layer(d))

        e4 = s - lead - shift + 1

        @pl.when((e4 >= 0) & (e4 < chunks))
        def _():
            start(load_middle(e4, e4 % 2))

        d4 = s - lead - shift

        @pl.when(d4 >= 0)
        def _():
            wait(load_middle(d4, d4 % 2))

            @pl.when(d4 > 0)
            def _():
                wait(save_input(d4 - 1))
            for k in (0, 1):
                where = four.rows(k, d4)
                unit, inverse = unit_rows(where)
                grad = grad_sum[where, :].astype(jnp.float32)
                scaled = grad * gain[0:1, :]
                inner = jnp.mean(scaled * unit, axis=-1, keepdims=True)
                input_stage[k] = middle_stage[d4 % 2, k] + inverse * (scaled - unit * inner)
                gain_out[...] += jnp.sum(grad * unit, axis=0, keepdims=True)
            start(save_input(d4))
        return carry

    lax.fori_loop(0, shift + four.steps, step, 0)
    two.drain()
    four.drain()
    wait(save_layer(chunks - 1))
    wait(save_input(chunks - 1))

    def finish(k, carry):
        owner = lax.rem(dp + k, m)
        w = owner // owners

        def copy(peer):
            return pltpu.make_async_remote_copy(
                src_ref=send.at[0, pl.ds(0, share)], dst_ref=recv.at[peer], send_sem=send_sem.at[peer],
                recv_sem=recv_sem.at[peer], device_id={"dp": peer}, device_id_type=MESH)

        copy(owner).wait_send()
        copy(owner).wait_recv()
        return carry

    lax.fori_loop(1, m, finish, 0)
    reduced[...] = recv[0].astype(jnp.float32)

    def add(k, carry):
        reduced[...] += recv[k].astype(jnp.float32)
        return carry

    lax.fori_loop(1, m, add, 0)


def attention_back(feed_part, grad_low, gain, q, k, v, mix, lse, cosines, sines, seg_col, seg_row, out_w,
                   x, qkv_w, branch, grad_middle, n, m, cid, size, chunks=16, lag=2):
    rows, width = feed_part.shape
    q_width = q.shape[1]
    pairs = q_width // 128
    rc = rows // (2 * chunks)
    blocks = rows // size
    share = width // m
    cat = 2 * q_width + 128
    low = jnp.bfloat16
    vmem = pl.BlockSpec(memory_space=pltpu.VMEM)
    hbm = pl.BlockSpec(memory_space=pl.ANY)
    dma = pltpu.SemaphoreType.DMA
    shape = jax.ShapeDtypeStruct
    return pl.pallas_call(
        functools.partial(back_kernel, n, m, chunks, lag, norm_eps, size, pairs),
        out_shape=(
            shape((rows, width), low), shape((rows, width), jnp.float32), shape((1, width), jnp.float32),
            shape((share, cat), jnp.float32),
        ),
        in_specs=[vmem] * 4 + [hbm] * 13,
        out_specs=(hbm, hbm, vmem, vmem),
        scratch_shapes=line_scratch(chunks, rc, width) + line_scratch(chunks, rc, width) + [
            pltpu.VMEM((rows, width), low),
            pltpu.VMEM((rows, width), low),
            pltpu.VMEM((rows, width), low),
            pltpu.VMEM((rows, width), low),
            pltpu.VMEM((rows, q_width), low),
            pltpu.VMEM((rows, 128), low),
            pltpu.VMEM((rows, 128), low),
            pltpu.VMEM((rows, q_width), low),
            pltpu.VMEM((rows, 128), jnp.float32),
            pltpu.VMEM((rows, 128), jnp.float32),
            pltpu.VMEM((rows, 1), jnp.int32),
            pltpu.VMEM((width, q_width), low),
            pltpu.VMEM((rows, width), low),
            pltpu.VMEM((width, q_width + 128), low),
            pltpu.VMEM((rows, width), low),
            pltpu.VMEM((size, q_width), low),
            pltpu.VMEM((blocks, size, size), jnp.float32),
            pltpu.VMEM((blocks, 128, size), low),
            pltpu.VMEM((blocks, size, 128), jnp.float32),
            pltpu.VMEM((blocks, size, 128), jnp.float32),
            pltpu.VMEM((rows, q_width + 128), low),
            pltpu.VMEM((width // 256, 256, cat), low),
            pltpu.VMEM((m, share, cat), low),
            pltpu.VMEM((2, 2, rc, width), low),
            pltpu.VMEM((2, rc, width), low),
            pltpu.VMEM((2, 2, rc, width), jnp.float32),
            pltpu.VMEM((2, rc, width), jnp.float32),
            dma((11,)), dma((2, 2)), dma((2, 2)), dma((2,)), dma((2,)), dma((m,)), dma((m,)),
        ],
        compiler_params=pltpu.CompilerParams(collective_id=cid, has_side_effects=True, vmem_limit_bytes=63 << 20),
        cost_estimate=pl.CostEstimate(flops=40 * rows * width * q_width, bytes_accessed=rows * width * 260,
                                      transcendentals=rows * rows * pairs),
    )(feed_part, gain, lse, seg_row, grad_low, q, k, v, mix, cosines, sines, seg_col, out_w,
      x, qkv_w, branch, grad_middle)


def norm_kernel(n, m, gains_ref, ff_ref, head_ref, norm_ref, gain_ref, line, got_gains, got_line, got_plane, got_squares,
                send_squares, recv_squares, send_gains, recv_gains, send_line, recv_line, send_plane, recv_plane):
    z = lax.axis_index("tensor")
    d = lax.axis_index("dp")
    share = head_ref.shape[0]

    barrier = pltpu.get_barrier_semaphore()
    for k in range(1, n):
        pl.semaphore_signal(barrier, inc=1, device_id={"tensor": lax.rem(z + k, n)}, device_id_type=MESH)
    for k in range(1, m):
        pl.semaphore_signal(barrier, inc=1, device_id={"dp": lax.rem(d + k, m)}, device_id_type=MESH)
    pl.semaphore_wait(barrier, n - 1 + m - 1)

    def gains_to(k, sender):
        peer = lax.rem(d + k, m)
        return pltpu.make_async_remote_copy(
            src_ref=gains_ref.at[peer], dst_ref=got_gains.at[sender], send_sem=send_gains.at[k],
            recv_sem=recv_gains.at[sender], device_id={"dp": peer}, device_id_type=MESH)

    def squares_to(k, sender):
        return pltpu.make_async_remote_copy(
            src_ref=line.at[2], dst_ref=got_squares.at[sender], send_sem=send_squares.at[k],
            recv_sem=recv_squares.at[sender], device_id={"dp": lax.rem(d + k, m)}, device_id_type=MESH)

    def along_line(k, sender):
        return pltpu.make_async_remote_copy(
            src_ref=line.at[0], dst_ref=got_line.at[sender], send_sem=send_line.at[k], recv_sem=recv_line.at[sender],
            device_id={"tensor": lax.rem(z + k, n)}, device_id_type=MESH)

    def over_plane(k, sender):
        return pltpu.make_async_remote_copy(
            src_ref=line.at[1], dst_ref=got_plane.at[sender], send_sem=send_plane.at[k], recv_sem=recv_plane.at[sender],
            device_id={"dp": lax.rem(d + k, m)}, device_id_type=MESH)

    def summed(ref, number):
        whole = ref[0]
        for k in range(1, number):
            whole = whole + ref[k]
        return whole

    def squares(value):
        return jnp.sum(jnp.sum(value * value, axis=0, keepdims=True), axis=1, keepdims=True)

    for k in range(1, m):
        gains_to(k, d).start()
    got_gains[d] = gains_ref[d]
    sub = 32

    def head_rows(r, acc):
        value = head_ref[pl.ds(pl.multiple_of(r * sub, sub), sub), :]
        return acc + squares(value)

    local = lax.fori_loop(0, share // sub, head_rows, jnp.zeros((1, 1), jnp.float32))

    def ff_rows(r, acc):
        value = ff_ref[pl.ds(pl.multiple_of(r * sub, sub), sub), :].astype(jnp.float32)
        return acc + squares(value)

    local = lax.fori_loop(0, share // sub, ff_rows, local)
    line[2] = jnp.broadcast_to(local, (8, 128))
    for k in range(1, m):
        squares_to(k, d).start()
    got_squares[d] = line[2]
    for k in range(1, m):
        gains_to(k, d).wait_send()
        gains_to(k, lax.rem(d + m - k, m)).wait_recv()
    for k in range(1, m):
        squares_to(k, d).wait_send()
        squares_to(k, lax.rem(d + m - k, m)).wait_recv()
    line[0] = summed(got_squares, m)
    gains = summed(got_gains, m)
    gain_ref[...] = gains
    line[1] = jnp.broadcast_to(squares(gains), (8, 128))
    for k in range(1, m):
        over_plane(k, d).start()
    got_plane[d] = line[1]
    for k in range(1, n):
        along_line(k, z).start()
    got_line[z] = line[0]
    for k in range(1, n):
        along_line(k, z).wait_send()
        along_line(k, lax.rem(z + n - k, n)).wait_recv()
    for k in range(1, m):
        over_plane(k, d).wait_send()
        over_plane(k, lax.rem(d + m - k, m)).wait_recv()
    norm_ref[...] = jnp.sqrt(summed(got_line, n) + summed(got_plane, m))


def adam_kernel(rates, kv_width, correct_ref, norm_ref, gain_ref, ff_hbm, head_hbm, layer_hbm, input_hbm, *refs):
    count = len(rates)
    params, refs = refs[:3 * count], refs[3 * count:]
    norm_out, layer_out, input_out, outs, refs = refs[0], refs[1], refs[2], refs[3:3 * count + 3], refs[3 * count + 3:]
    (ff_grad, head_ref, layer_held, input_held), held = refs[:4], refs[4:3 * count + 4]
    grad_sem, load_sem, save_sem, in_sem, back_sem = refs[3 * count + 4:]
    share = gain_ref.shape[1]
    q_width = outs[3].shape[1]
    ff = outs[12].shape[2]
    sub = 32

    grads = (
        pltpu.make_async_copy(ff_hbm, ff_grad, grad_sem.at[0]),
        pltpu.make_async_copy(head_hbm, head_ref, grad_sem.at[1]),
    )
    loads = [pltpu.make_async_copy(params[k], held[k], load_sem.at[k]) for k in range(3 * count)]
    saves = [pltpu.make_async_copy(held[k], outs[k], save_sem.at[k]) for k in range(3 * count)]
    quarter = layer_hbm.shape[0] // 4
    arrive, depart = [], []
    for k in range(4):
        at = pl.ds(k * quarter, quarter)
        for t, (source, kept, target) in enumerate(
                ((layer_hbm, layer_held, layer_out), (input_hbm, input_held, input_out))):
            arrive.append(pltpu.make_async_copy(source.at[at], kept.at[at], in_sem.at[t, k]))
            depart.append(pltpu.make_async_copy(kept.at[at], target.at[at], back_sem.at[t, k]))
    for copy in grads:
        copy.start()
    for which in (1, 3, 2):
        for k in range(3):
            loads[3 * which + k].start()
    for copy in arrive:
        copy.start()
    for which in (5, 4, 0):
        for k in range(3):
            loads[3 * which + k].start()
    norm_out[0] = norm_ref[0, 0]
    factor = jnp.minimum(1.0, clip_limit / (norm_ref[:1, :1] + 1e-06))
    one, two = correct_ref[0], correct_ref[1]

    def update(which, where, gradient):
        rate, decay = rates[which]
        p, a, b = (held[3 * which + k] for k in range(3))
        gradient = gradient * factor
        first = beta_first * a[where] + (1.0 - beta_first) * gradient
        second = beta_second * b[where] + (1.0 - beta_second) * gradient * gradient
        a[where] = first
        b[where] = second
        change = first / one / (jnp.sqrt(second / two) + adam_eps)
        old = p[where]
        p[where] = old - rate * (change + decay * old)

    def load(which):
        for k in range(3):
            loads[3 * which + k].wait()

    def save(which):
        for k in range(3):
            saves[3 * which + k].start()

    def by_rows(which, body):
        load(which)
        lax.fori_loop(0, share // sub, lambda r, c: (body(pl.ds(pl.multiple_of(r * sub, sub), sub)), c)[1], 0)
        save(which)

    for copy in grads:
        copy.wait()
    by_rows(1, lambda where: update(1, (where, slice(None)), head_ref[where, :q_width]))
    load(3)

    def out_tile(t, carry):
        at = pl.ds(pl.multiple_of(t * 128, 128), 128)
        source = pl.ds(pl.multiple_of(q_width + 2 * kv_width + t * 128, 128), 128)
        update(3, (at, slice(None)), head_ref[:, source].T)
        return carry

    lax.fori_loop(0, outs[9].shape[0] // 128, out_tile, 0)
    save(3)

    load(2)
    both = head_ref[:, q_width:q_width + 2 * kv_width].T
    for t in (0, 1):
        update(2, (t, slice(None), slice(None)), both[t * kv_width:(t + 1) * kv_width])
    save(2)

    def gateup_rows(where):
        for t in (0, 1):
            update(4, (t, where, slice(None)), ff_grad[where, t * ff:(t + 1) * ff].astype(jnp.float32))

    for came, left in zip(arrive, depart):
        came.wait()
        left.start()
    load(5)

    def down_tile(t, carry):
        at = pl.ds(pl.multiple_of(t * 128, 128), 128)
        source = pl.ds(pl.multiple_of(2 * ff + t * 128, 128), 128)
        update(5, (at, slice(None)), ff_grad[:, source].astype(jnp.float32).T)
        return carry

    lax.fori_loop(0, ff // 128, down_tile, 0)
    save(5)
    by_rows(4, gateup_rows)
    load(0)
    update(0, (slice(None), slice(None)), gain_ref[...])
    save(0)
    for copy in saves + depart:
        copy.wait()


def finish_step(gains, correct, ff_grad, head_grad, layer, grad_in, params, rates, kv_width, n, m, cid):
    share = gains.shape[1] // m
    parts = gains.reshape(2, m, share).transpose(1, 0, 2)
    vmem = pl.BlockSpec(memory_space=pltpu.VMEM)
    hbm = pl.BlockSpec(memory_space=pl.ANY)
    dma = pltpu.SemaphoreType.DMA
    shape = jax.ShapeDtypeStruct
    norm, gain = pl.pallas_call(
        functools.partial(norm_kernel, n, m),
        out_shape=(shape((8, 128), jnp.float32), shape((2, share), jnp.float32)),
        in_specs=[vmem, vmem, vmem],
        out_specs=(vmem, vmem),
        scratch_shapes=[
            pltpu.VMEM((3, 8, 128), jnp.float32),
            pltpu.VMEM((m, 2, share), jnp.float32),
            pltpu.VMEM((n, 8, 128), jnp.float32),
            pltpu.VMEM((m, 8, 128), jnp.float32),
            pltpu.VMEM((m, 8, 128), jnp.float32),
            dma((m,)), dma((m,)), dma((m,)), dma((m,)), dma((n,)), dma((n,)), dma((m,)), dma((m,)),
        ],
        compiler_params=pltpu.CompilerParams(collective_id=cid, has_side_effects=True),
    )(parts, ff_grad, head_grad)
    size = sum(p.size for p in params)
    norm, layer, grad_in, *outs = pl.pallas_call(
        functools.partial(adam_kernel, rates, kv_width),
        out_shape=(shape((1,), jnp.float32), shape(layer.shape, layer.dtype), shape(grad_in.shape, grad_in.dtype))
        + tuple(shape(p.shape, jnp.float32) for p in params),
        in_specs=[pl.BlockSpec(memory_space=pltpu.SMEM), vmem, vmem] + [hbm] * (4 + len(params)),
        out_specs=(pl.BlockSpec(memory_space=pltpu.SMEM),) + (hbm,) * (2 + len(params)),
        scratch_shapes=[pltpu.VMEM(a.shape, a.dtype) for a in (ff_grad, head_grad, layer, grad_in)]
        + [pltpu.VMEM(p.shape, jnp.float32) for p in params]
        + [dma((2,)), dma((len(params),)), dma((len(params),)), dma((2, 4)), dma((2, 4))],
        compiler_params=pltpu.CompilerParams(vmem_limit_bytes=63 << 20),
        cost_estimate=pl.CostEstimate(flops=20 * size, bytes_accessed=24 * size, transcendentals=size),
    )(correct, norm, gain, ff_grad, head_grad, layer, grad_in, *params)
    return norm, layer, grad_in, outs


norm_eps = 1e-05
beta_first = 0.9
beta_second = 0.95
adam_eps = 1e-08
weight_decay = 0.1
weight_rate = 0.02
out_rate = 0.1
gain_rate = 0.2
clip_limit = 1.0


def on_device(
    n,
    m,
    tokens,
    cotangent,
    segment_ids,
    step_count,
    norm_gains,
    gains_first,
    gains_second,
    w_query,
    query_first,
    query_second,
    w_keyval,
    keyval_first,
    keyval_second,
    w_out,
    out_first,
    out_second,
    w_gateup,
    gateup_first,
    gateup_second,
    w_down,
    down_first,
    down_second,
):
    low = jnp.bfloat16
    width = w_query.shape[1]
    kv_width = w_keyval.shape[2]
    share = norm_gains.shape[1]
    gain_part = lax.dynamic_update_slice(
        jnp.zeros((2, tokens.shape[1]), jnp.float32), norm_gains, (0, lax.axis_index("dp") * share)
    )
    length = tokens.shape[0]
    size = min(256, length)
    segment = segment_ids[0]
    seg_row = segment[None, :]
    lane = jnp.arange(128, dtype=jnp.int32) % (HD // 2)
    frequency = jnp.power(10000.0, -lane.astype(jnp.float32) * (2.0 / HD))[None, :]
    (branch, gain_values, lse, seg_col, cosines, sines, mixture, q, k, v, qkv_weight, out_weight, ff_weight) = attention_head(
        tokens, gain_part, w_query, w_keyval.swapaxes(1, 2), w_out, frequency, seg_row, w_gateup, w_down, n, m, 1, size
    )
    feed_part, grad_middle, grad_branch, gain_grad_two, grad_ff_weight = feed_forward(
        branch, gain_values, tokens, cotangent, ff_weight, n, 2
    )
    ff_reduced = lax.psum_scatter(grad_ff_weight, "dp", scatter_dimension=0, tiled=True)
    layer_out, input_grad, gain_grad_one, head_reduced = attention_back(
        feed_part, grad_branch, gain_values, q, k, v, mixture, lse, cosines, sines, seg_col, seg_row,
        out_weight, tokens, qkv_weight, branch, grad_middle, n, m, 3, size
    )
    gain_grads = jnp.concatenate([gain_grad_one, gain_grad_two])
    step_float = step_count[0].astype(jnp.float32)
    correct = jnp.stack([1.0 - jnp.power(beta_first, step_float), 1.0 - jnp.power(beta_second, step_float)])
    params = (
        (norm_gains, gains_first, gains_second),
        (w_query, query_first, query_second),
        tuple(a.swapaxes(1, 2) for a in (w_keyval, keyval_first, keyval_second)),
        (w_out, out_first, out_second),
        (w_gateup, gateup_first, gateup_second),
        (w_down, down_first, down_second),
    )
    rates = (
        (gain_rate, 0.0),
        (weight_rate, weight_decay),
        (weight_rate, weight_decay),
        (out_rate, weight_decay),
        (weight_rate, weight_decay),
        (weight_rate, weight_decay),
    )
    norm, layer_out, input_grad, updated = finish_step(
        gain_grads, correct, ff_reduced, head_reduced, layer_out, input_grad,
        [a for group in params for a in group], rates, kv_width, n, m, 4
    )
    results = []
    for k in range(len(params)):
        weight, first_state, second_state = updated[3 * k : 3 * k + 3]
        group = [first_state, second_state, weight]
        results += [a.swapaxes(1, 2) for a in group] if k == 2 else group
    return (layer_out, input_grad, norm, *results)


def solution(mesh):
    rows = P("dp", None)
    gains = P(None, "dp")
    query = P("dp", "tensor")
    stacked = P(None, "dp", "tensor")
    turned = P("tensor", "dp")
    states = (gains,) * 3 + (query,) * 3 + (stacked,) * 3 + (turned,) * 3 + (stacked,) * 3 + (turned,) * 3
    return jax.shard_map(
        functools.partial(on_device, mesh.shape["tensor"], mesh.shape["dp"]),
        mesh=mesh,
        in_specs=(rows, rows, rows, P()) + states,
        out_specs=(rows, rows, P()) + states,
        check_vma=False,
    )
```

```python
import functools

import jax
import jax.numpy as jnp
from jax import lax
from jax.experimental import pallas as pl
from jax.experimental.pallas import tpu as pltpu
from jax.sharding import PartitionSpec as P

HD = 64
MESH = pl.DeviceIdType.MESH


masked_value = -1e9


def dot_t(left, right):
    return lax.dot_general(left, right, (((1,), (1,)), ((), ())), preferred_element_type=jnp.float32)


def dot_n(left, right):
    return lax.dot_general(left, right, (((1,), (0,)), ((), ())), preferred_element_type=jnp.float32)


def swap_halves(values, first_half):
    return jnp.where(first_half, pltpu.roll(values, 96, 1), pltpu.roll(values, 32, 1))


def lane_tests(rows):
    lane = lax.broadcasted_iota(jnp.int32, (rows, 128), 1)
    return lane < 64, (lane % 64) < 32


def block_bias(seg_col_ref, seg_row_ref, i, j, size):
    keys = seg_col_ref[pl.ds(pl.multiple_of(j * size, size), size), :]
    rows = seg_row_ref[:, pl.ds(pl.multiple_of(i * size, size), size)]
    key_at = j * size + lax.broadcasted_iota(jnp.int32, (size, size), 0)
    row_at = i * size + lax.broadcasted_iota(jnp.int32, (size, size), 1)
    return jnp.where((keys == rows) & (key_at <= row_at), 0.0, masked_value)


def stack_pair(pair, low_lanes):
    zero = jnp.zeros_like(pair)
    return jnp.concatenate([jnp.where(low_lanes, pair, zero), jnp.where(low_lanes, zero, pair)], axis=0)


class Line:
    def __init__(self, n, chunks, rc, lag, part, got, out, sems, order=None):
        self.order = order
        self.n, self.chunks, self.rc, self.lag = n, chunks, rc, lag
        self.part, self.got, self.out = part, got, out
        self.send_a, self.recv_a, self.send_g, self.recv_g = sems
        self.me = lax.axis_index("tensor")
        self.steps = chunks + 2 * lag * (n - 1)

    def rows(self, stream, c):
        begin = (stream * self.chunks + c) * self.rc if self.order is None else self.order(stream, c)
        return pl.ds(pl.multiple_of(begin, self.rc), self.rc)

    def side(self, stream):
        pos = self.me if stream == 0 else self.n - 1 - self.me
        fwd = self.me + 1 if stream == 0 else self.me - 1
        bwd = self.me - 1 if stream == 0 else self.me + 1
        return pos, fwd, bwd

    def toward(self, stream, c, nxt, src):
        return pltpu.make_async_remote_copy(
            src_ref=src, dst_ref=self.got.at[stream, c],
            send_sem=self.send_a.at[stream, c], recv_sem=self.recv_a.at[stream, c],
            device_id={"tensor": nxt}, device_id_type=MESH)

    def back(self, stream, c, nxt):
        where = self.rows(stream, c)
        return pltpu.make_async_remote_copy(
            src_ref=self.out.at[where], dst_ref=self.out.at[where],
            send_sem=self.send_g.at[stream, c], recv_sem=self.recv_g.at[stream, c],
            device_id={"tensor": nxt}, device_id_type=MESH)

    def step(self, s):
        n, lag = self.n, self.lag
        for stream in (0, 1):
            pos, fwd, bwd = self.side(stream)
            c = s - lag * pos

            @pl.when((c >= 0) & (c < self.chunks))
            def _():
                where = self.rows(stream, c)
                slot = self.got.at[stream, c]

                def summed():
                    self.toward(stream, c, fwd, slot).wait_recv()
                    return (
                        self.part[where, :].astype(jnp.float32) + self.got[stream, c].astype(jnp.float32)
                    ).astype(self.out.dtype)

                @pl.when(pos == 0)
                def _():
                    self.toward(stream, c, fwd, self.part.at[where]).start()

                @pl.when((pos > 0) & (pos < n - 1))
                def _():
                    self.got[stream, c] = summed()
                    self.toward(stream, c, fwd, slot).start()

                @pl.when(pos == n - 1)
                def _():
                    self.out[where, :] = summed()
                    self.back(stream, c, bwd).start()
            d = s - lag * (n - 1) - lag * (n - 1 - pos)

            @pl.when((d >= 0) & (d < self.chunks) & (pos < n - 1))
            def _():
                self.back(stream, d, bwd).wait_recv()

                @pl.when(pos > 0)
                def _():
                    self.back(stream, d, bwd).start()

    def drain(self):
        def one(c, carry):
            for stream in (0, 1):
                pos, fwd, bwd = self.side(stream)

                @pl.when(pos < self.n - 1)
                def _():
                    self.toward(stream, c, fwd, self.got.at[stream, c]).wait_send()

                @pl.when(pos > 0)
                def _():
                    self.back(stream, c, bwd).wait_send()
            return carry

        lax.fori_loop(0, self.chunks, one, 0)


def greet(n):
    me = lax.axis_index("tensor")
    barrier = pltpu.get_barrier_semaphore()

    @pl.when(me > 0)
    def _():
        pl.semaphore_signal(barrier, inc=1, device_id={"tensor": me - 1}, device_id_type=MESH)

    @pl.when(me < n - 1)
    def _():
        pl.semaphore_signal(barrier, inc=1, device_id={"tensor": me + 1}, device_id_type=MESH)

    @pl.when((me > 0) & (me < n - 1))
    def _():
        pl.semaphore_wait(barrier, 2)

    @pl.when((me == 0) | (me == n - 1))
    def _():
        pl.semaphore_wait(barrier, 1)


def line_scratch(chunks, rc, width):
    return [pltpu.VMEM((2, chunks, rc, width), jnp.bfloat16)] + [pltpu.SemaphoreType.DMA((2, chunks))] * 4


def line_kernel(n, chunks, lag, count, *refs):
    parts, outs, scratch = refs[:count], refs[count:2 * count], refs[2 * count:]
    rc = parts[0].shape[0] // (2 * chunks)
    lines = [
        Line(n, chunks, rc, lag, parts[k], scratch[5 * k], outs[k], scratch[5 * k + 1:5 * k + 5])
        for k in range(count)
    ]
    greet(n)

    def step(s, carry):
        for k, line in enumerate(lines):
            line.step(s - k * chunks)
        return carry

    lax.fori_loop(0, lines[0].steps + (count - 1) * chunks, step, 0)
    for line in lines:
        line.drain()


def line_reduce(parts, n, chunks, cid, lag=2):
    rows, width = parts[0].shape
    count = len(parts)
    rc = rows // (2 * chunks)
    scratch = []
    for _ in parts:
        scratch += line_scratch(chunks, rc, width)
    vmem = pl.BlockSpec(memory_space=pltpu.VMEM)
    return pl.pallas_call(
        functools.partial(line_kernel, n, chunks, lag, count),
        out_shape=tuple(jax.ShapeDtypeStruct((rows, width), jnp.bfloat16) for _ in parts),
        in_specs=[vmem] * count,
        out_specs=(vmem,) * count,
        scratch_shapes=scratch,
        compiler_params=pltpu.CompilerParams(collective_id=cid, has_side_effects=True, vmem_limit_bytes=40 << 20),
        cost_estimate=pl.CostEstimate(flops=rows * width * 2 * count, bytes_accessed=rows * width * 120 * count,
                                      transcendentals=0),
    )(*parts)


def dot_rows(left, right):
    return lax.dot_general(left, right, (((0,), (0,)), ((), ())), preferred_element_type=jnp.float32)


def ff_kernel(n, chunks, lag, eps, branch, gain, x, cot_hbm, w_hbm,
              feed_hbm, middle_hbm, low_hbm, gain_out, grads_hbm,
              got, sa, ra, sg, rg, two_sum, two_part, weight, cot, normed, hidden, gg, feed,
              middle_stage, low_stage, unit_stage, w_sem, cot_sem, feed_sem, stage_sem, grad_sem):
    rows, width = branch.shape
    ff = hidden.shape[1]
    rc = rows // (2 * chunks)
    per = 8
    offset = per - 1
    half = rows // 2
    hb = per * rc
    block = 2 * hb
    blocks = chunks // per
    line = Line(n, chunks, rc, lag, two_part, got, two_sum, (sa, ra, sg, rg))
    landed = 2 * lag * (n - 1) + offset
    tile = 256
    full, rest = ff // tile, ff % tile
    wide = width // tile

    groups = []
    for g, (begin, end) in enumerate(((0, tile), (tile, 2 * tile), (2 * tile, ff))):
        groups.append([
            pltpu.make_async_copy(w_hbm.at[:, pl.ds(t * ff + begin, end - begin)],
                                  weight.at[:, pl.ds(t * ff + begin, end - begin)], w_sem.at[g, t])
            for t in range(3)
        ])
    for copy in sum(groups, []):
        copy.start()

    def natural(k, b):
        return pl.ds(pl.multiple_of(k * half + b * hb, hb), hb)

    def blocked(k, b):
        return pl.ds(pl.multiple_of(b * block + k * hb, hb), hb)

    def load_cot(b):
        return [pltpu.make_async_copy(cot_hbm.at[natural(k, b)], cot.at[blocked(k, b)], cot_sem.at[b, k])
                for k in (0, 1)]

    def save_feed(b):
        return [pltpu.make_async_copy(feed.at[pl.ds(k * hb, hb)], feed_hbm.at[natural(k, b)], feed_sem.at[k])
                for k in (0, 1)]

    def save_rows(d):
        copies = []
        for k in (0, 1):
            where = line.rows(k, d)
            copies.append(pltpu.make_async_copy(middle_stage.at[k], middle_hbm.at[where], stage_sem.at[0, k]))
            copies.append(pltpu.make_async_copy(low_stage.at[k], low_hbm.at[where], stage_sem.at[1, k]))
        return copies

    def save_units(w):
        return [pltpu.make_async_copy(unit_stage, grads_hbm.at[pl.ds(pl.multiple_of(w * tile, tile), tile)], grad_sem.at[0])]

    def start(copies):
        for copy in copies:
            copy.start()

    def wait(copies):
        for copy in copies:
            copy.wait()

    for b in range(blocks):
        start(load_cot(b))
    gain_out[...] = jnp.zeros_like(gain_out)
    greet(n)

    def unit_rows(where):
        middle = x[where, :].astype(jnp.float32) + branch[where, :].astype(jnp.float32)
        inverse = lax.rsqrt(jnp.mean(middle * middle, axis=-1, keepdims=True) + eps)
        return middle * inverse, inverse

    def normalize(b):
        def some(r, carry):
            for k in (0, 1):
                where = pl.ds(pl.multiple_of(k * half + b * hb + r * rc, rc), rc)
                at = pl.ds(pl.multiple_of(b * block + k * hb + r * rc, rc), rc)
                normed[at, :] = (unit_rows(where)[0] * gain[1:2, :]).astype(jnp.bfloat16)
            return carry

        lax.fori_loop(0, per, some, 0)

    def step(s, carry):
        line.step(s - offset)
        b = s // per
        phase = s - b * per
        live = s < chunks
        mine = pl.ds(pl.multiple_of(b * block, block), block)

        def units(at, count):
            columns = pl.ds(at, count)
            second = pl.ds(pl.multiple_of(ff + at, 128), count)
            third = pl.ds(pl.multiple_of(2 * ff + at, 128), count)
            gate = dot_n(normed[mine, :], weight[:, columns])
            up = dot_n(normed[mine, :], weight[:, second])
            grad_hidden = dot_n(cot[mine, :], weight[:, third])
            sg_gate = 1.0 / (1.0 + jnp.exp(-gate))
            silu = gate * sg_gate
            hidden[mine, columns] = (silu * up).astype(jnp.bfloat16)
            gg[mine, columns] = (grad_hidden * up * sg_gate * (1.0 + gate * (1.0 - sg_gate))).astype(jnp.bfloat16)
            gg[mine, second] = (grad_hidden * silu).astype(jnp.bfloat16)

        def unit_tile(t, c):
            for g in range(3):
                @pl.when((b == 0) & (t == g))
                def _():
                    wait(groups[g])
            units(pl.multiple_of(t * tile, tile), tile)
            return c

        @pl.when(live & (phase == 0))
        def _():
            normalize(b)
            wait(load_cot(b))

        @pl.when(live & (phase < 3))
        def _():
            lax.fori_loop(jnp.maximum(2 * phase - 1, 0), jnp.minimum(2 * phase + 1, full), unit_tile, 0)

        @pl.when(live & (phase == 3))
        def _():
            if rest:
                units(full * tile, rest)

            @pl.when(b > 0)
            def _():
                wait(save_feed(b - 1))

        @pl.when(live & ((phase == 3) | (phase == 4)))
        def _():
            def feed_tile(t, c):
                columns = pl.ds(pl.multiple_of(t * 2 * tile, 2 * tile), 2 * tile)
                feed[:, columns] = dot_t(hidden[mine, :], weight[columns, 2 * ff:]).astype(jnp.bfloat16)
                return c

            lax.fori_loop((phase - 3) * (wide // 4), (phase - 2) * (wide // 4), feed_tile, 0)

            @pl.when(phase == 4)
            def _():
                start(save_feed(b))

        @pl.when(live & ((phase == 5) | (phase == 6)))
        def _():
            def two_tile(t, c):
                at = pl.ds(pl.multiple_of(t * 2 * tile, 2 * tile), 2 * tile)
                value = dot_t(gg[mine, :], weight[at, :2 * ff]).astype(jnp.bfloat16)
                for k in (0, 1):
                    two_part[natural(k, b), at] = value[k * hb:(k + 1) * hb]
                return c

            lax.fori_loop((phase - 5) * (wide // 4), (phase - 4) * (wide // 4), two_tile, 0)

        d = s - landed

        @pl.when(d >= 0)
        def _():
            @pl.when(d > 0)
            def _():
                wait(save_rows(d - 1))
            for k in (0, 1):
                where = line.rows(k, d)
                at = pl.ds(pl.multiple_of((d // per) * block + k * hb + (d - (d // per) * per) * rc, rc), rc)
                pieces = [pl.ds(c * tile, tile) for c in range(wide)]

                def middle_at(c):
                    return x[where, c].astype(jnp.float32) + branch[where, c].astype(jnp.float32)

                def folded(value):
                    return value[:, :128] + value[:, 128:]

                total = jnp.zeros((rc, 128), jnp.float32)
                for c in pieces:
                    middle = middle_at(c)
                    total = total + folded(middle * middle)
                inverse = lax.rsqrt(jnp.sum(total, axis=-1, keepdims=True) * (1.0 / width) + eps)
                total = jnp.zeros((rc, 128), jnp.float32)
                for c in pieces:
                    product = two_sum[where, c].astype(jnp.float32) * (middle_at(c) * inverse)
                    gain_out[:, c] += jnp.sum(product, axis=0, keepdims=True)
                    total = total + folded(product * gain[1:2, c])
                inner = jnp.sum(total, axis=-1, keepdims=True) * (1.0 / width)
                for c in pieces:
                    scaled = two_sum[where, c].astype(jnp.float32) * gain[1:2, c]
                    value = cot[at, c].astype(jnp.float32) + inverse * (scaled - middle_at(c) * inverse * inner)
                    middle_stage[k, :, c] = value
                    low_stage[k, :, c] = value.astype(jnp.bfloat16)
            start(save_rows(d))

        late = s - chunks
        w = late // 2

        @pl.when((late >= 0) & (late == 2 * w) & (w < wide))
        def _():
            @pl.when(w > 0)
            def _():
                wait(save_units(w - 1))
            columns = pl.ds(pl.multiple_of(w * tile, tile), tile)
            left = normed[:, columns]
            for t in (0, 1):
                unit_stage[:, t * ff:(t + 1) * ff] = dot_rows(left, gg[:, t * ff:(t + 1) * ff]).astype(jnp.bfloat16)
            unit_stage[:, 2 * ff:] = dot_rows(cot[:, columns], hidden[...]).astype(jnp.bfloat16)
            start(save_units(w))
        return carry

    lax.fori_loop(0, offset + line.steps, step, 0)
    line.drain()
    wait(save_feed(blocks - 1))
    wait(save_rows(chunks - 1))
    wait(save_units(wide - 1))


def feed_forward(branch, gain, x, cot, weight, n, cid, chunks=32, lag=2):
    rows, width = branch.shape
    ff = weight.shape[1] // 3
    rc = rows // (2 * chunks)
    block = 16 * rc
    blocks = chunks // 8
    low = jnp.bfloat16
    vmem = pl.BlockSpec(memory_space=pltpu.VMEM)
    hbm = pl.BlockSpec(memory_space=pl.ANY)
    dma = pltpu.SemaphoreType.DMA
    shape = jax.ShapeDtypeStruct
    return pl.pallas_call(
        functools.partial(ff_kernel, n, chunks, lag, norm_eps),
        out_shape=(
            shape((rows, width), low), shape((rows, width), jnp.float32), shape((rows, width), low),
            shape((1, width), jnp.float32), shape((width, 3 * ff), low),
        ),
        in_specs=[vmem, vmem, vmem, hbm, hbm],
        out_specs=(hbm, hbm, hbm, vmem, hbm),
        scratch_shapes=line_scratch(chunks, rc, width) + [
            pltpu.VMEM((rows, width), low),
            pltpu.VMEM((rows, width), low),
            pltpu.VMEM((width, 3 * ff), low),
            pltpu.VMEM((rows, width), low),
            pltpu.VMEM((rows, width), low),
            pltpu.VMEM((rows, ff), low),
            pltpu.VMEM((rows, 2 * ff), low),
            pltpu.VMEM((block, width), low),
            pltpu.VMEM((2, rc, width), jnp.float32),
            pltpu.VMEM((2, rc, width), low),
            pltpu.VMEM((256, 3 * ff), low),
            dma((3, 3)), dma((blocks, 2)), dma((2,)), dma((2, 2)), dma((1,)),
        ],
        compiler_params=pltpu.CompilerParams(collective_id=cid, has_side_effects=True, vmem_limit_bytes=63 << 20),
        cost_estimate=pl.CostEstimate(flops=18 * rows * width * ff, bytes_accessed=rows * width * 150,
                                      transcendentals=rows * ff),
    )(branch, gain, x, cot, weight)


def head_kernel(n, m, chunks, lag, eps, size, pairs,
                gain_part, query_own, keyval_own, out_own, frequency, seg_row_ref,
                x_hbm, gateup_hbm, down_hbm,
                branch, gain, lse_ref, seg_col_ref, cos_hbm, sin_hbm, mix_hbm, q_hbm, k_hbm, v_hbm, qkv_hbm, out_hbm, ff_hbm,
                got, sa, ra, sg, rg, part, normed, raw, bias, scores, v_turned, got_gain,
                x, cos_ref, sin_ref, mix_ref, q_ref, k_ref, v_ref, qkv_w, out_w, gateup_own, down_own, ff_own,
                send_gain, recv_gain, send_direct, send_forward, recv_w, own_sem, save_sem, result_sem, x_sem,
                send_ff, pass_ff, recv_ff):
    rows, width = branch.shape
    q_width = pairs * 128
    x_load = pltpu.make_async_copy(x_hbm, x, x_sem)
    x_load.start()
    results = [
        pltpu.make_async_copy(source, target, result_sem.at[k])
        for k, (source, target) in enumerate((
            (q_ref, q_hbm), (k_ref, k_hbm), (v_ref, v_hbm), (cos_ref, cos_hbm), (sin_ref, sin_hbm),
            (qkv_w, qkv_hbm), (out_w, out_hbm), (mix_ref, mix_hbm)))
    ]
    z = lax.axis_index("tensor")
    dp = lax.axis_index("dp")
    share = width // m
    chips = m // 2
    chip, core = dp // 2, dp % 2
    rc = rows // (2 * chunks)
    per = size // (2 * rc)
    hb = size // 2
    blocks = rows // size
    tile = 256
    wide = width // tile
    low_lanes, first_half = lane_tests(size)
    low_rows = lax.broadcasted_iota(jnp.int32, (128, size), 0) < 64
    wholes = (qkv_w, out_w)
    ff = down_own.shape[0]
    piece = 32
    pieces = share // piece
    spacing = 40 // pieces
    owned = (
        pltpu.make_async_copy(gateup_hbm, gateup_own, own_sem.at[0]),
        pltpu.make_async_copy(down_hbm, down_own, own_sem.at[1]),
    )
    for copy in owned:
        copy.start()

    def ascending(stream, c):
        b = c // per
        return b * size + stream * hb + (c - b * per) * rc

    line = Line(n, chunks, rc, lag, part, got, branch, (sa, ra, sg, rg), ascending)

    def shard_rows(s):
        return pl.ds(pl.multiple_of(s * share, share), share)

    def direct(kind, k):
        peer = 2 * lax.rem(chip + k, chips) + core
        return pltpu.make_async_remote_copy(
            src_ref=wholes[kind].at[shard_rows(dp)], dst_ref=wholes[kind].at[shard_rows(dp)], send_sem=send_direct.at[kind, k],
            recv_sem=recv_w.at[kind, dp], device_id={"dp": peer}, device_id_type=MESH)

    def forward(kind, c, side):
        shard = 2 * c + side
        where = shard_rows(shard)
        return pltpu.make_async_remote_copy(
            src_ref=wholes[kind].at[where], dst_ref=wholes[kind].at[where], send_sem=send_forward.at[kind, c],
            recv_sem=recv_w.at[kind, shard], device_id={"dp": 2 * chip + 1 - core}, device_id_type=MESH)

    def piece_rows(shard, p):
        return pl.ds(pl.multiple_of(shard * share + p * piece, piece), piece)

    def own_piece(p):
        return ff_own.at[pl.ds(pl.multiple_of(p * piece, piece), piece)]

    def send_piece(k, p):
        peer = 2 * lax.rem(chip + k, chips) + core
        return pltpu.make_async_remote_copy(
            src_ref=own_piece(p), dst_ref=ff_hbm.at[piece_rows(dp, p)], send_sem=send_ff.at[k, p],
            recv_sem=recv_ff.at[dp, p], device_id={"dp": peer}, device_id_type=MESH)

    def pass_piece(c, side, p, src=None):
        shard = 2 * c + side
        where = ff_hbm.at[piece_rows(shard, p)]
        return pltpu.make_async_remote_copy(
            src_ref=where if src is None else src, dst_ref=where, send_sem=pass_ff.at[c, p],
            recv_sem=recv_ff.at[shard, p], device_id={"dp": 2 * chip + 1 - core}, device_id_type=MESH)

    def save_own():
        return pltpu.make_async_copy(ff_own, ff_hbm.at[shard_rows(dp)], save_sem)

    def send_gains(k, sender):
        return pltpu.make_async_remote_copy(
            src_ref=gain_part, dst_ref=got_gain.at[sender], send_sem=send_gain.at[k], recv_sem=recv_gain.at[sender],
            device_id={"dp": lax.rem(dp + k, m)}, device_id_type=MESH)

    barrier = pltpu.get_barrier_semaphore()

    @pl.when(z > 0)
    def _():
        pl.semaphore_signal(barrier, inc=1, device_id={"tensor": z - 1}, device_id_type=MESH)

    @pl.when(z < n - 1)
    def _():
        pl.semaphore_signal(barrier, inc=1, device_id={"tensor": z + 1}, device_id_type=MESH)

    for k in range(1, m):
        pl.semaphore_signal(barrier, inc=1, device_id={"dp": lax.rem(dp + k, m)}, device_id_type=MESH)

    qkv_w[shard_rows(dp), :q_width] = query_own[...].astype(jnp.bfloat16)
    both_own = jnp.concatenate([keyval_own[0], keyval_own[1]], axis=0)
    qkv_w[shard_rows(dp), q_width:] = both_own.T.astype(jnp.bfloat16)
    for t in range(q_width // 128):
        out_w[shard_rows(dp), t * 128:(t + 1) * 128] = out_own[t * 128:(t + 1) * 128, :].T.astype(jnp.bfloat16)
    got_gain[dp] = gain_part[...]

    @pl.when((z > 0) & (z < n - 1))
    def _():
        pl.semaphore_wait(barrier, m + 1)

    @pl.when((z == 0) | (z == n - 1))
    def _():
        pl.semaphore_wait(barrier, m)

    for k in range(1, m):
        send_gains(k, dp).start()
    for kind in (0, 1):
        for k in range(1, chips):
            direct(kind, k).start()
        forward(kind, chip, core).start()
    for k in range(1, m):
        send_gains(k, lax.rem(dp + m - k, m)).wait_recv()
    whole = got_gain[0]
    for k in range(1, m):
        whole = whole + got_gain[k]
    gain[...] = whole.astype(jnp.bfloat16).astype(jnp.float32)

    x_load.wait()

    def norm_rows(r, carry):
        where = pl.ds(pl.multiple_of(r * rc, rc), rc)
        values = x[where, :].astype(jnp.float32)
        inverse = lax.rsqrt(jnp.mean(values * values, axis=-1, keepdims=True) + eps)
        normed[where, :] = (values * inverse * gain[0:1, :]).astype(jnp.bfloat16)
        return carry

    lax.fori_loop(0, rows // rc, norm_rows, 0)
    def tables(i, carry):
        where = pl.ds(pl.multiple_of(i * size, size), size)
        ids = jnp.broadcast_to(seg_row_ref[:, where].astype(jnp.float32), (128, size)).T[:, :1]
        seg_col_ref[where, :] = ids.astype(jnp.int32)
        earlier = jnp.where(seg_row_ref[...].astype(jnp.float32) < ids, 1.0, 0.0)
        place = (i * size + lax.broadcasted_iota(jnp.int32, (size, 1), 0)).astype(jnp.float32) - jnp.sum(
            earlier, axis=1, keepdims=True)
        angles = place * frequency[...]
        sines = jnp.sin(angles)
        cos_ref[where, :] = jnp.cos(angles)
        sin_ref[where, :] = jnp.where(first_half, -sines, sines)
        return carry

    lax.fori_loop(0, blocks, tables, 0)
    for copy in owned:
        copy.wait()

    def own_rows(r, carry):
        where = pl.ds(pl.multiple_of(r * piece, piece), piece)
        for t in (0, 1):
            ff_own[where, t * ff:(t + 1) * ff] = gateup_own[t, where, :].astype(jnp.bfloat16)
        return carry

    lax.fori_loop(0, pieces, own_rows, 0)

    def own_columns(t, carry):
        at = pl.ds(pl.multiple_of(2 * ff + t * 128, 128), 128)
        ff_own[:, at] = down_own[pl.ds(pl.multiple_of(t * 128, 128), 128), :].T.astype(jnp.bfloat16)
        return carry

    lax.fori_loop(0, ff // 128, own_columns, 0)
    save_own().start()

    def pass_on(kind):
        for k in range(1, chips):
            c = lax.rem(chip + chips - k, chips)
            forward(kind, c, core).wait_recv()
            forward(kind, c, core).start()

    def receive(kind):
        for c in range(chips):
            forward(kind, c, 1 - core).wait_recv()

    pass_on(0)
    receive(0)
    for p in range(min(2, pieces)):
        for k in range(1, chips):
            send_piece(k, p).start()

    def prepare(i, carry):
        where = pl.ds(pl.multiple_of(i * size, size), size)
        raw[...] = dot_n(normed[where, :], qkv_w[...])
        cosines, sines = cos_ref[where, :], sin_ref[where, :]
        for hp in range(pairs):
            values = raw[:, hp * 128:(hp + 1) * 128]
            turned = values * cosines + swap_halves(values, first_half) * sines
            q_ref[where, hp * 128:(hp + 1) * 128] = (
                turned.astype(jnp.bfloat16).astype(jnp.float32) * 0.125).astype(jnp.bfloat16)
        both = raw[:, q_width:q_width + 128]
        other = pltpu.roll(both, 64, 1)
        keys = jnp.where(low_lanes, both, other)
        k_ref[where, :] = (keys * cosines + swap_halves(keys, first_half) * sines).astype(jnp.bfloat16)
        values = jnp.where(low_lanes, other, both)
        v_ref[where, :] = values.astype(jnp.bfloat16)
        v_turned[i] = values.T.astype(jnp.bfloat16)
        return carry

    lax.fori_loop(0, blocks, prepare, 0)
    for copy in results[:5]:
        copy.start()
    pass_on(1)

    def attend(i, hp):
        where = pl.ds(pl.multiple_of(i * size, size), size)
        columns = pl.ds(pl.multiple_of(hp * 128, 128), 128)
        stacked = stack_pair(q_ref[where, columns], low_lanes)

        def score(j, top):
            keys = k_ref[pl.ds(pl.multiple_of(j * size, size), size), :]
            b = bias[j]
            s = dot_t(keys, stacked) + jnp.concatenate([b, b], axis=1)
            scores[j] = s
            return jnp.maximum(top, jnp.max(s, axis=0, keepdims=True))

        top = lax.fori_loop(0, i + 1, score, jnp.full((1, 2 * size), -jnp.inf, jnp.float32))

        def mix(j, c):
            total, acc = c
            p = jnp.exp(scores[j] - top)
            total = total + jnp.sum(p, axis=0, keepdims=True)
            return total, acc + dot_n(v_turned[j], p.astype(jnp.bfloat16))

        total, acc = lax.fori_loop(0, i + 1, mix, (
            jnp.zeros((1, 2 * size), jnp.float32), jnp.zeros((128, 2 * size), jnp.float32)))
        lse_ref[i, hp] = top + jnp.log(total)
        acc = acc / total
        acc = jnp.where(low_rows, acc[:, :size], acc[:, size:])
        mix_ref[where, columns] = acc.T.astype(jnp.bfloat16)

    def step(s, carry):
        line.step(s - per)
        p_send = (s - 1) // spacing + 2
        p_pass = (s - 12) // spacing

        @pl.when((s >= 1) & ((p_send - 2) * spacing == s - 1) & (p_send < pieces))
        def _():
            for k in range(1, chips):
                send_piece(k, p_send).start()

        @pl.when((s >= 12) & (p_pass * spacing == s - 12) & (p_pass < pieces))
        def _():
            pass_piece(chip, core, p_pass, own_piece(p_pass)).start()
            for k in range(1, chips):
                c = lax.rem(chip + chips - k, chips)
                pass_piece(c, core, p_pass).wait_recv()
                pass_piece(c, core, p_pass).start()

        i = s // per
        hp = s - i * per
        live = s < blocks * per

        @pl.when(live & (hp == 0))
        def _():
            def fill(j, c):
                bias[j] = block_bias(seg_col_ref, seg_row_ref, i, j, size)
                return c

            lax.fori_loop(0, i + 1, fill, 0)

        @pl.when(live)
        def _():
            def each(h, c):
                attend(i, h)
                return c

            lax.fori_loop(hp * pairs // per, (hp + 1) * pairs // per, each, 0)

        @pl.when(s == per - 1)
        def _():
            receive(1)
            for copy in results[5:7]:
                copy.start()

        @pl.when(s == blocks * per)
        def _():
            results[7].start()

        @pl.when(live & (hp == per - 1))
        def _():
            where = pl.ds(pl.multiple_of(i * size, size), size)

            def part_tile(t, c):
                at = pl.ds(pl.multiple_of(t * tile, tile), tile)
                part[where, at] = dot_t(mix_ref[where, :], out_w[at, :]).astype(jnp.bfloat16)
                return c

            lax.fori_loop(0, wide, part_tile, 0)
        return carry

    lax.fori_loop(0, per + line.steps, step, 0)
    line.drain()
    save_own().wait()
    for copy in results:
        copy.wait()

    def settle(p, carry):
        for k in range(1, chips):
            send_piece(k, p).wait_send()
        for c in range(chips):
            pass_piece(c, core, p).wait_send()
            pass_piece(c, 1 - core, p).wait_recv()
        return carry

    lax.fori_loop(0, pieces, settle, 0)
    for k in range(1, m):
        send_gains(k, dp).wait_send()
    for kind in (0, 1):
        for k in range(1, chips):
            direct(kind, k).wait_send()
        for c in range(chips):
            forward(kind, c, core).wait_send()


def attention_head(x, gain_part, query, keyval, out, frequency, seg_row, gateup, down, n, m, cid, size,
                   chunks=32, lag=2):
    rows, width = x.shape
    q_width = query.shape[1]
    share, ff = width // m, down.shape[0]
    pairs = q_width // 128
    rc = rows // (2 * chunks)
    blocks = rows // size
    chips = m // 2
    low = jnp.bfloat16
    vmem = pl.BlockSpec(memory_space=pltpu.VMEM)
    hbm = pl.BlockSpec(memory_space=pl.ANY)
    dma = pltpu.SemaphoreType.DMA
    shape = jax.ShapeDtypeStruct
    return pl.pallas_call(
        functools.partial(head_kernel, n, m, chunks, lag, norm_eps, size, pairs),
        out_shape=(
            shape((rows, width), low), shape((2, width), jnp.float32),
            shape((blocks, pairs, 1, 2 * size), jnp.float32), shape((rows, 1), jnp.int32),
            shape((rows, 128), jnp.float32), shape((rows, 128), jnp.float32), shape((rows, q_width), low),
            shape((rows, q_width), low), shape((rows, 128), low), shape((rows, 128), low),
            shape((width, q_width + 128), low), shape((width, q_width), low), shape((width, 3 * ff), low),
        ),
        in_specs=[vmem] * 6 + [hbm] * 3,
        out_specs=(vmem,) * 4 + (hbm,) * 9,
        scratch_shapes=line_scratch(chunks, rc, width) + [
            pltpu.VMEM((rows, width), low),
            pltpu.VMEM((rows, width), low),
            pltpu.VMEM((size, q_width + 128), jnp.float32),
            pltpu.VMEM((blocks, size, size), jnp.float32),
            pltpu.VMEM((blocks, size, 2 * size), jnp.float32),
            pltpu.VMEM((blocks, 128, size), low),
            pltpu.VMEM((m, 2, width), jnp.float32),
            pltpu.VMEM((rows, width), low),
            pltpu.VMEM((rows, 128), jnp.float32),
            pltpu.VMEM((rows, 128), jnp.float32),
            pltpu.VMEM((rows, q_width), low),
            pltpu.VMEM((rows, q_width), low),
            pltpu.VMEM((rows, 128), low),
            pltpu.VMEM((rows, 128), low),
            pltpu.VMEM((width, q_width + 128), low),
            pltpu.VMEM((width, q_width), low),
            pltpu.VMEM(gateup.shape, jnp.float32),
            pltpu.VMEM(down.shape, jnp.float32),
            pltpu.VMEM((share, 3 * ff), low),
            dma((m,)), dma((m,)), dma((2, chips)), dma((2, chips)), dma((2, m)), dma((2,)), dma, dma((8,)), dma,
            dma((chips, share // 32)), dma((chips, share // 32)), dma((m, share // 32)),
        ],
        compiler_params=pltpu.CompilerParams(collective_id=cid, has_side_effects=True, vmem_limit_bytes=56 << 20),
        cost_estimate=pl.CostEstimate(flops=20 * rows * width * q_width, bytes_accessed=rows * width * 170,
                                      transcendentals=rows * rows * pairs),
    )(gain_part, query, keyval, out, frequency, seg_row, x, gateup, down)


def back_kernel(n, m, chunks, lag, eps, size, pairs,
                feed_part, gain, lse_ref, seg_row_ref,
                low_hbm, q_hbm, k_hbm, v_hbm, mix_hbm, cos_hbm, sin_hbm, seg_hbm, out_hbm, x_hbm, qkv_hbm,
                branch_hbm, middle_hbm,
                layer_hbm, input_hbm, gain_out, reduced,
                got2, sa2, ra2, sg2, rg2, got4, sa4, ra4, sg4, rg4, feed_sum, part, grad_sum,
                grad_low, q_ref, k_ref, v_ref, mix_ref, cos_ref, sin_ref, seg_col_ref, out_w, x, qkv_w,
                normed, grad_mix, bias, k_turned, grad_k, grad_v, grad_qkv, send, recv,
                branch_stage, layer_stage, middle_stage, input_stage,
                w_sem, branch_sem, middle_sem, layer_sem, input_sem, send_sem, recv_sem):
    rows, width = feed_part.shape
    q_width = pairs * 128
    z = lax.axis_index("tensor")
    dp = lax.axis_index("dp")
    rc = rows // (2 * chunks)
    per = size // (2 * rc)
    hb = size // 2
    blocks = rows // size
    tile = 256
    wide = width // tile
    share = width // m
    owners = tile // share
    lead = 2 * lag * (n - 1)
    shift = chunks + per
    low_lanes, first_half = lane_tests(size)
    low_rows = lax.broadcasted_iota(jnp.int32, (128, size), 0) < 64

    def descending(stream, c):
        b = c // per
        return (blocks - 1 - b) * size + stream * hb + (c - b * per) * rc

    two = Line(n, chunks, rc, lag, feed_part, got2, feed_sum, (sa2, ra2, sg2, rg2))
    four = Line(n, chunks, rc, lag, part, got4, grad_sum, (sa4, ra4, sg4, rg4), descending)
    loads = [
        pltpu.make_async_copy(source, target, w_sem.at[k])
        for k, (source, target) in enumerate((
            (k_hbm, k_ref), (q_hbm, q_ref), (low_hbm, grad_low), (out_hbm, out_w), (v_hbm, v_ref), (mix_hbm, mix_ref),
            (cos_hbm, cos_ref), (sin_hbm, sin_ref), (seg_hbm, seg_col_ref), (x_hbm, x), (qkv_hbm, qkv_w)))
    ]
    for copy in loads:
        copy.start()

    def start(copies):
        for copy in copies:
            copy.start()

    def wait(copies):
        for copy in copies:
            copy.wait()

    def load_branch(d, slot):
        return [pltpu.make_async_copy(branch_hbm.at[two.rows(k, d)], branch_stage.at[slot, k], branch_sem.at[slot, k])
                for k in (0, 1)]

    def load_middle(d, slot):
        return [pltpu.make_async_copy(middle_hbm.at[four.rows(k, d)], middle_stage.at[slot, k], middle_sem.at[slot, k])
                for k in (0, 1)]

    def save_layer(d):
        return [pltpu.make_async_copy(layer_stage.at[k], layer_hbm.at[two.rows(k, d)], layer_sem.at[k]) for k in (0, 1)]

    def save_input(d):
        return [pltpu.make_async_copy(input_stage.at[k], input_hbm.at[four.rows(k, d)], input_sem.at[k]) for k in (0, 1)]

    def to_owner(w, o):
        owner = w * owners + o
        return pltpu.make_async_remote_copy(
            src_ref=send.at[w, pl.ds(o * share, share)], dst_ref=recv.at[dp], send_sem=send_sem.at[owner],
            recv_sem=recv_sem.at[dp], device_id={"dp": owner}, device_id_type=MESH)

    gain_out[...] = jnp.zeros_like(gain_out)

    def prepare(i, carry):
        at = pl.ds(pl.multiple_of(i * size, size), size)
        k_turned[i] = k_ref[at, :].astype(jnp.float32).T.astype(jnp.bfloat16)
        grad_k[i] = jnp.zeros((size, 128), jnp.float32)
        grad_v[i] = jnp.zeros((size, 128), jnp.float32)
        return carry

    barrier = pltpu.get_barrier_semaphore()

    @pl.when(z > 0)
    def _():
        pl.semaphore_signal(barrier, inc=1, device_id={"tensor": z - 1}, device_id_type=MESH)

    @pl.when(z < n - 1)
    def _():
        pl.semaphore_signal(barrier, inc=1, device_id={"tensor": z + 1}, device_id_type=MESH)

    for k in range(1, m):
        pl.semaphore_signal(barrier, inc=1, device_id={"dp": lax.rem(dp + k, m)}, device_id_type=MESH)

    @pl.when((z > 0) & (z < n - 1))
    def _():
        pl.semaphore_wait(barrier, m + 1)

    @pl.when((z == 0) | (z == n - 1))
    def _():
        pl.semaphore_wait(barrier, m)

    def unit_rows(where):
        values = x[where, :].astype(jnp.float32)
        inverse = lax.rsqrt(jnp.mean(values * values, axis=-1, keepdims=True) + eps)
        return values * inverse, inverse

    def attend(i, hp):
        at_rows = pl.ds(pl.multiple_of(i * size, size), size)
        columns = pl.ds(pl.multiple_of(hp * 128, 128), 128)
        stacked = stack_pair(q_ref[at_rows, columns], low_lanes)
        grad_pair = grad_mix[:, columns]
        grad_stacked = stack_pair(grad_pair, low_lanes)
        product = (grad_pair.astype(jnp.float32) * mix_ref[at_rows, columns].astype(jnp.float32)).T
        spread = jnp.concatenate([
            jnp.sum(product[:64], axis=0, keepdims=True), jnp.sum(product[64:], axis=0, keepdims=True)], axis=1)
        logsum = lse_ref[i, hp]

        def piece(j, acc):
            at = pl.ds(pl.multiple_of(j * size, size), size)
            b = bias[j]
            s = dot_t(k_ref[at, :], stacked) + jnp.concatenate([b, b], axis=1)
            p = jnp.exp(s - logsum)
            grad_p = dot_t(v_ref[at, :], grad_stacked)
            grad_s = (p * (grad_p - spread)).astype(jnp.bfloat16)
            grad_v[j] += dot_n(p.astype(jnp.bfloat16), grad_stacked)
            grad_k[j] += dot_n(grad_s, stacked)
            return acc + dot_n(k_turned[j], grad_s)

        acc = lax.fori_loop(0, i + 1, piece, jnp.zeros((128, 2 * size), jnp.float32))
        acc = jnp.where(low_rows, acc[:, :size], acc[:, size:]).T * 0.125
        turned = acc * cos_ref[at_rows, :] - swap_halves(acc, first_half) * sin_ref[at_rows, :]
        grad_qkv[at_rows, columns] = turned.astype(jnp.bfloat16)

    def finish(k, carry):
        owner = lax.rem(dp + k, m)
        w = owner // owners

        def copy(peer):
            return pltpu.make_async_remote_copy(
                src_ref=send.at[0, pl.ds(0, share)], dst_ref=recv.at[peer], send_sem=send_sem.at[peer],
                recv_sem=recv_sem.at[peer], device_id={"dp": peer}, device_id_type=MESH)

        copy(owner).wait_send()
        copy(owner).wait_recv()
        return carry

    def step(s, carry):
        two.step(s)
        four.step(s - shift)
        b = s // per
        hp = s - b * per
        i = blocks - 1 - b
        live = s < blocks * per
        at_rows = pl.ds(pl.multiple_of(i * size, size), size)

        @pl.when(s == 0)
        def _():
            wait(loads)
            lax.fori_loop(0, blocks, prepare, 0)

        @pl.when(live & (hp == 0))
        def _():
            grad_mix[...] = dot_n(grad_low[at_rows, :], out_w[...]).astype(jnp.bfloat16)

            def fill(j, c):
                bias[j] = block_bias(seg_col_ref, seg_row_ref, i, j, size)
                return c

            lax.fori_loop(0, i + 1, fill, 0)

        @pl.when(live)
        def _():
            def each(h, c):
                attend(i, h)
                return c

            lax.fori_loop(hp * pairs // per, (hp + 1) * pairs // per, each, 0)

            def some(r, c):
                at = pl.ds(pl.multiple_of(s * 2 * rc + r * rc, rc), rc)
                normed[at, :] = (unit_rows(at)[0] * gain[0:1, :]).astype(jnp.bfloat16)
                return c

            lax.fori_loop(0, 2, some, 0)

        @pl.when(live & (hp == per - 1))
        def _():
            cosines, sines = cos_ref[at_rows, :], sin_ref[at_rows, :]
            dk = grad_k[i] + pltpu.roll(grad_k[i], 64, 1)
            dk = dk * cosines - swap_halves(dk, first_half) * sines
            dv = grad_v[i] + pltpu.roll(grad_v[i], 64, 1)
            grad_qkv[at_rows, q_width:] = jnp.where(low_lanes, dk, dv).astype(jnp.bfloat16)

            def part_tile(t, c):
                at = pl.ds(pl.multiple_of(t * tile, tile), tile)
                part[at_rows, at] = dot_t(grad_qkv[at_rows, :], qkv_w[at, :]).astype(jnp.bfloat16)
                return c

            lax.fori_loop(0, wide, part_tile, 0)

        w = s - blocks * per

        @pl.when((w >= 0) & (w < wide))
        def _():
            columns = pl.ds(pl.multiple_of(w * tile, tile), tile)
            send[w, :, :q_width + 128] = dot_rows(normed[:, columns], grad_qkv[...]).astype(jnp.bfloat16)
            send[w, :, q_width + 128:] = dot_rows(grad_low[:, columns], mix_ref[...]).astype(jnp.bfloat16)
            for o in range(owners):
                owner = w * owners + o

                @pl.when(owner != dp)
                def _():
                    to_owner(w, o).start()

                @pl.when(owner == dp)
                def _():
                    recv[dp] = send[w, o * share:(o + 1) * share, :]

        @pl.when(s == shift + lead + per)
        def _():
            lax.fori_loop(1, m, finish, 0)
            reduced[...] = recv[0].astype(jnp.float32)

            def add(k, c):
                reduced[...] += recv[k].astype(jnp.float32)
                return c

            lax.fori_loop(1, m, add, 0)

        e = s - lead + 1

        @pl.when((e >= 0) & (e < chunks))
        def _():
            start(load_branch(e, e % 2))

        d = s - lead

        @pl.when((d >= 0) & (d < chunks))
        def _():
            wait(load_branch(d, d % 2))

            @pl.when(d > 0)
            def _():
                wait(save_layer(d - 1))
            for k in (0, 1):
                where = two.rows(k, d)
                layer_stage[k] = (
                    x[where, :].astype(jnp.float32) + branch_stage[d % 2, k].astype(jnp.float32)
                    + feed_sum[where, :].astype(jnp.float32)
                ).astype(jnp.bfloat16)
            start(save_layer(d))

        e4 = s - lead - shift + 1

        @pl.when((e4 >= 0) & (e4 < chunks))
        def _():
            start(load_middle(e4, e4 % 2))

        d4 = s - lead - shift

        @pl.when(d4 >= 0)
        def _():
            wait(load_middle(d4, d4 % 2))

            @pl.when(d4 > 0)
            def _():
                wait(save_input(d4 - 1))
            for k in (0, 1):
                where = four.rows(k, d4)
                unit, inverse = unit_rows(where)
                grad = grad_sum[where, :].astype(jnp.float32)
                scaled = grad * gain[0:1, :]
                inner = jnp.mean(scaled * unit, axis=-1, keepdims=True)
                input_stage[k] = middle_stage[d4 % 2, k] + inverse * (scaled - unit * inner)
                gain_out[...] += jnp.sum(grad * unit, axis=0, keepdims=True)
            start(save_input(d4))
        return carry

    lax.fori_loop(0, shift + four.steps, step, 0)
    two.drain()
    four.drain()
    wait(save_layer(chunks - 1))
    wait(save_input(chunks - 1))


def attention_back(feed_part, grad_low, gain, q, k, v, mix, lse, cosines, sines, seg_col, seg_row, out_w,
                   x, qkv_w, branch, grad_middle, n, m, cid, size, chunks=16, lag=2):
    rows, width = feed_part.shape
    q_width = q.shape[1]
    pairs = q_width // 128
    rc = rows // (2 * chunks)
    blocks = rows // size
    share = width // m
    cat = 2 * q_width + 128
    low = jnp.bfloat16
    vmem = pl.BlockSpec(memory_space=pltpu.VMEM)
    hbm = pl.BlockSpec(memory_space=pl.ANY)
    dma = pltpu.SemaphoreType.DMA
    shape = jax.ShapeDtypeStruct
    return pl.pallas_call(
        functools.partial(back_kernel, n, m, chunks, lag, norm_eps, size, pairs),
        out_shape=(
            shape((rows, width), low), shape((rows, width), jnp.float32), shape((1, width), jnp.float32),
            shape((share, cat), jnp.float32),
        ),
        in_specs=[vmem] * 4 + [hbm] * 13,
        out_specs=(hbm, hbm, vmem, vmem),
        scratch_shapes=line_scratch(chunks, rc, width) + line_scratch(chunks, rc, width) + [
            pltpu.VMEM((rows, width), low),
            pltpu.VMEM((rows, width), low),
            pltpu.VMEM((rows, width), low),
            pltpu.VMEM((rows, width), low),
            pltpu.VMEM((rows, q_width), low),
            pltpu.VMEM((rows, 128), low),
            pltpu.VMEM((rows, 128), low),
            pltpu.VMEM((rows, q_width), low),
            pltpu.VMEM((rows, 128), jnp.float32),
            pltpu.VMEM((rows, 128), jnp.float32),
            pltpu.VMEM((rows, 1), jnp.int32),
            pltpu.VMEM((width, q_width), low),
            pltpu.VMEM((rows, width), low),
            pltpu.VMEM((width, q_width + 128), low),
            pltpu.VMEM((rows, width), low),
            pltpu.VMEM((size, q_width), low),
            pltpu.VMEM((blocks, size, size), jnp.float32),
            pltpu.VMEM((blocks, 128, size), low),
            pltpu.VMEM((blocks, size, 128), jnp.float32),
            pltpu.VMEM((blocks, size, 128), jnp.float32),
            pltpu.VMEM((rows, q_width + 128), low),
            pltpu.VMEM((width // 256, 256, cat), low),
            pltpu.VMEM((m, share, cat), low),
            pltpu.VMEM((2, 2, rc, width), low),
            pltpu.VMEM((2, rc, width), low),
            pltpu.VMEM((2, 2, rc, width), jnp.float32),
            pltpu.VMEM((2, rc, width), jnp.float32),
            dma((11,)), dma((2, 2)), dma((2, 2)), dma((2,)), dma((2,)), dma((m,)), dma((m,)),
        ],
        compiler_params=pltpu.CompilerParams(collective_id=cid, has_side_effects=True, vmem_limit_bytes=63 << 20),
        cost_estimate=pl.CostEstimate(flops=40 * rows * width * q_width, bytes_accessed=rows * width * 260,
                                      transcendentals=rows * rows * pairs),
    )(feed_part, gain, lse, seg_row, grad_low, q, k, v, mix, cosines, sines, seg_col, out_w,
      x, qkv_w, branch, grad_middle)


def norm_kernel(n, m, count, gains_ref, ff_ref, head_ref, *refs):
    sources, (norm_ref, gain_ref), kept = refs[:count], refs[count:count + 2], refs[count + 2:2 * count + 2]
    norm_body(n, m, gains_ref, ff_ref, head_ref, sources, kept, norm_ref, gain_ref, *refs[2 * count + 2:])


def norm_body(n, m, gains_ref, ff_ref, head_ref, sources, kept, norm_ref, gain_ref, line, got_gains, got_line, got_plane, got_squares,
                send_squares, recv_squares, send_gains, recv_gains, send_line, recv_line, send_plane, recv_plane, fetch_sem):
    fetches = [pltpu.make_async_copy(a, b, fetch_sem.at[k]) for k, (a, b) in enumerate(zip(sources, kept))]
    for copy in fetches:
        copy.start()
    z = lax.axis_index("tensor")
    d = lax.axis_index("dp")
    share = head_ref.shape[0]

    barrier = pltpu.get_barrier_semaphore()
    for k in range(1, n):
        pl.semaphore_signal(barrier, inc=1, device_id={"tensor": lax.rem(z + k, n)}, device_id_type=MESH)
    for k in range(1, m):
        pl.semaphore_signal(barrier, inc=1, device_id={"dp": lax.rem(d + k, m)}, device_id_type=MESH)
    pl.semaphore_wait(barrier, n - 1 + m - 1)

    def gains_to(k, sender):
        peer = lax.rem(d + k, m)
        return pltpu.make_async_remote_copy(
            src_ref=gains_ref.at[peer], dst_ref=got_gains.at[sender], send_sem=send_gains.at[k],
            recv_sem=recv_gains.at[sender], device_id={"dp": peer}, device_id_type=MESH)

    def squares_to(k, sender):
        return pltpu.make_async_remote_copy(
            src_ref=line.at[2], dst_ref=got_squares.at[sender], send_sem=send_squares.at[k],
            recv_sem=recv_squares.at[sender], device_id={"dp": lax.rem(d + k, m)}, device_id_type=MESH)

    def along_line(k, sender):
        return pltpu.make_async_remote_copy(
            src_ref=line.at[0], dst_ref=got_line.at[sender], send_sem=send_line.at[k], recv_sem=recv_line.at[sender],
            device_id={"tensor": lax.rem(z + k, n)}, device_id_type=MESH)

    def over_plane(k, sender):
        return pltpu.make_async_remote_copy(
            src_ref=line.at[1], dst_ref=got_plane.at[sender], send_sem=send_plane.at[k], recv_sem=recv_plane.at[sender],
            device_id={"dp": lax.rem(d + k, m)}, device_id_type=MESH)

    def summed(ref, number):
        whole = ref[0]
        for k in range(1, number):
            whole = whole + ref[k]
        return whole

    def squares(value):
        return jnp.sum(jnp.sum(value * value, axis=0, keepdims=True), axis=1, keepdims=True)

    for k in range(1, m):
        gains_to(k, d).start()
    got_gains[d] = gains_ref[d]
    sub = 32

    def head_rows(r, acc):
        value = head_ref[pl.ds(pl.multiple_of(r * sub, sub), sub), :]
        return acc + squares(value)

    local = lax.fori_loop(0, share // sub, head_rows, jnp.zeros((1, 1), jnp.float32))

    def ff_rows(r, acc):
        value = ff_ref[pl.ds(pl.multiple_of(r * sub, sub), sub), :].astype(jnp.float32)
        return acc + squares(value)

    local = lax.fori_loop(0, share // sub, ff_rows, local)
    line[2] = jnp.broadcast_to(local, (8, 128))
    for k in range(1, m):
        squares_to(k, d).start()
    got_squares[d] = line[2]
    for k in range(1, m):
        gains_to(k, d).wait_send()
        gains_to(k, lax.rem(d + m - k, m)).wait_recv()
    for k in range(1, m):
        squares_to(k, d).wait_send()
        squares_to(k, lax.rem(d + m - k, m)).wait_recv()
    line[0] = summed(got_squares, m)
    gains = summed(got_gains, m)
    gain_ref[...] = gains
    line[1] = jnp.broadcast_to(squares(gains), (8, 128))
    for k in range(1, m):
        over_plane(k, d).start()
    got_plane[d] = line[1]
    for k in range(1, n):
        along_line(k, z).start()
    got_line[z] = line[0]
    for k in range(1, n):
        along_line(k, z).wait_send()
        along_line(k, lax.rem(z + n - k, n)).wait_recv()
    for k in range(1, m):
        over_plane(k, d).wait_send()
        over_plane(k, lax.rem(d + m - k, m)).wait_recv()
    norm_ref[...] = jnp.sqrt(summed(got_line, n) + summed(got_plane, m))
    for copy in fetches:
        copy.wait()


def adam_kernel(rates, kv_width, correct_ref, norm_ref, gain_ref, ff_hbm, head_hbm, layer_hbm, input_hbm, *refs):
    count = len(rates)
    params, refs = refs[:3 * count], refs[3 * count:]
    norm_out, layer_out, input_out, outs, refs = refs[0], refs[1], refs[2], refs[3:3 * count + 3], refs[3 * count + 3:]
    (ff_grad, head_ref, layer_held, input_held), held = refs[:4], refs[4:3 * count + 4]
    grad_sem, load_sem, save_sem, in_sem, back_sem = refs[3 * count + 4:]
    share = gain_ref.shape[1]
    q_width = outs[3].shape[1]
    ff = outs[12].shape[2]
    sub = 32

    saves = [pltpu.make_async_copy(held[k], outs[k], save_sem.at[k]) for k in range(3 * count)]
    grads = (
        pltpu.make_async_copy(head_hbm, head_ref, grad_sem.at[1]),
        pltpu.make_async_copy(ff_hbm, ff_grad, grad_sem.at[0]),
    )
    quarter = layer_hbm.shape[0] // 4
    arrive, depart = [], []
    for k in range(4):
        at = pl.ds(k * quarter, quarter)
        for t, (source, kept, target) in enumerate(
                ((layer_hbm, layer_held, layer_out), (input_hbm, input_held, input_out))):
            arrive.append(pltpu.make_async_copy(source.at[at], kept.at[at], in_sem.at[t, k]))
            depart.append(pltpu.make_async_copy(kept.at[at], target.at[at], back_sem.at[t, k]))
    loads = [pltpu.make_async_copy(params[k], held[k], load_sem.at[k]) for k in range(12)]
    for copy in grads:
        copy.start()
    for copy in loads:
        copy.start()
    for copy in arrive:
        copy.start()
    norm_out[0] = norm_ref[0, 0]
    factor = jnp.minimum(1.0, clip_limit / (norm_ref[:1, :1] + 1e-06))
    one, two = correct_ref[0], correct_ref[1]

    def update(which, where, gradient):
        rate, decay = rates[which]
        p, a, b = ((params if which > 3 else held)[3 * which + k] for k in range(3))
        p_new, a_new, b_new = (held[3 * which + k] for k in range(3))
        gradient = gradient * factor
        first = beta_first * a[where] + (1.0 - beta_first) * gradient
        second = beta_second * b[where] + (1.0 - beta_second) * gradient * gradient
        a_new[where] = first
        b_new[where] = second
        change = first / one / (jnp.sqrt(second / two) + adam_eps)
        old = p[where]
        p_new[where] = old - rate * (change + decay * old)

    def save(which):
        for k in range(3):
            saves[3 * which + k].start()

    def by_rows(which, body):
        lax.fori_loop(0, share // sub, lambda r, c: (body(pl.ds(pl.multiple_of(r * sub, sub), sub)), c)[1], 0)
        save(which)

    for copy in grads:
        copy.wait()
    for copy in loads:
        copy.wait()
    by_rows(1, lambda where: update(1, (where, slice(None)), head_ref[where, :q_width]))

    def out_tile(t, carry):
        at = pl.ds(pl.multiple_of(t * 128, 128), 128)
        source = pl.ds(pl.multiple_of(q_width + 2 * kv_width + t * 128, 128), 128)
        update(3, (at, slice(None)), head_ref[:, source].T)
        return carry

    lax.fori_loop(0, outs[9].shape[0] // 128, out_tile, 0)
    save(3)

    both = head_ref[:, q_width:q_width + 2 * kv_width].T
    for t in (0, 1):
        update(2, (t, slice(None), slice(None)), both[t * kv_width:(t + 1) * kv_width])
    save(2)

    def gateup_rows(where):
        for t in (0, 1):
            update(4, (t, where, slice(None)), ff_grad[where, t * ff:(t + 1) * ff].astype(jnp.float32))


    for came, left in zip(arrive, depart):
        came.wait()
        left.start()

    def down_tile(t, carry):
        at = pl.ds(pl.multiple_of(t * 128, 128), 128)
        source = pl.ds(pl.multiple_of(2 * ff + t * 128, 128), 128)
        update(5, (at, slice(None)), ff_grad[:, source].astype(jnp.float32).T)
        return carry

    lax.fori_loop(0, ff // 128, down_tile, 0)
    save(5)
    by_rows(4, gateup_rows)
    update(0, (slice(None), slice(None)), gain_ref[...])
    save(0)
    for copy in saves + depart:
        copy.wait()


def finish_step(gains, correct, ff_grad, head_grad, layer, grad_in, params, rates, kv_width, n, m, cid):
    share = gains.shape[1] // m
    parts = gains.reshape(2, m, share).transpose(1, 0, 2)
    vmem = pl.BlockSpec(memory_space=pltpu.VMEM)
    hbm = pl.BlockSpec(memory_space=pl.ANY)
    dma = pltpu.SemaphoreType.DMA
    shape = jax.ShapeDtypeStruct
    fetched = list(params[12:])
    norm, gain, *kept = pl.pallas_call(
        functools.partial(norm_kernel, n, m, len(fetched)),
        out_shape=(shape((8, 128), jnp.float32), shape((2, share), jnp.float32))
        + tuple(pltpu.VMEM(a.shape, a.dtype) for a in fetched),
        in_specs=[vmem, vmem, vmem] + [pl.BlockSpec(memory_space=pltpu.HBM)] * len(fetched),
        out_specs=(vmem,) * (2 + len(fetched)),
        scratch_shapes=[
            pltpu.VMEM((3, 8, 128), jnp.float32),
            pltpu.VMEM((m, 2, share), jnp.float32),
            pltpu.VMEM((n, 8, 128), jnp.float32),
            pltpu.VMEM((m, 8, 128), jnp.float32),
            pltpu.VMEM((m, 8, 128), jnp.float32),
            dma((m,)), dma((m,)), dma((m,)), dma((m,)), dma((n,)), dma((n,)), dma((m,)), dma((m,)),
            dma((len(fetched),)),
        ],
        compiler_params=pltpu.CompilerParams(collective_id=cid, has_side_effects=True, vmem_limit_bytes=40 << 20),
    )(parts, ff_grad, head_grad, *fetched)
    size = sum(p.size for p in params)
    norm, layer, grad_in, *outs = pl.pallas_call(
        functools.partial(adam_kernel, rates, kv_width),
        out_shape=(shape((1,), jnp.float32), shape(layer.shape, layer.dtype), shape(grad_in.shape, grad_in.dtype))
        + tuple(shape(p.shape, jnp.float32) for p in params),
        in_specs=[pl.BlockSpec(memory_space=pltpu.SMEM), vmem, vmem] + [hbm] * 16 + [vmem] * len(fetched),
        out_specs=(pl.BlockSpec(memory_space=pltpu.SMEM),) + (hbm,) * (2 + len(params)),
        scratch_shapes=[pltpu.VMEM(a.shape, a.dtype) for a in (ff_grad, head_grad, layer, grad_in)]
        + [pltpu.VMEM(p.shape, jnp.float32) for p in params]
        + [dma((2,)), dma((12,)), dma((len(params),)), dma((2, 4)), dma((2, 4))],
        compiler_params=pltpu.CompilerParams(vmem_limit_bytes=34 << 20),
        cost_estimate=pl.CostEstimate(flops=20 * size, bytes_accessed=24 * size, transcendentals=size),
    )(correct, norm, gain, ff_grad, head_grad, layer, grad_in, *params[:12], *kept)
    return norm, layer, grad_in, outs


norm_eps = 1e-05
beta_first = 0.9
beta_second = 0.95
adam_eps = 1e-08
weight_decay = 0.1
weight_rate = 0.02
out_rate = 0.1
gain_rate = 0.2
clip_limit = 1.0


def on_device(
    n,
    m,
    tokens,
    cotangent,
    segment_ids,
    step_count,
    norm_gains,
    gains_first,
    gains_second,
    w_query,
    query_first,
    query_second,
    w_keyval,
    keyval_first,
    keyval_second,
    w_out,
    out_first,
    out_second,
    w_gateup,
    gateup_first,
    gateup_second,
    w_down,
    down_first,
    down_second,
):
    low = jnp.bfloat16
    width = w_query.shape[1]
    kv_width = w_keyval.shape[2]
    share = norm_gains.shape[1]
    gain_part = lax.dynamic_update_slice(
        jnp.zeros((2, tokens.shape[1]), jnp.float32), norm_gains, (0, lax.axis_index("dp") * share)
    )
    length = tokens.shape[0]
    size = min(256, length)
    segment = segment_ids[0]
    seg_row = segment[None, :]
    lane = jnp.arange(128, dtype=jnp.int32) % (HD // 2)
    frequency = jnp.power(10000.0, -lane.astype(jnp.float32) * (2.0 / HD))[None, :]
    (branch, gain_values, lse, seg_col, cosines, sines, mixture, q, k, v, qkv_weight, out_weight, ff_weight) = attention_head(
        tokens, gain_part, w_query, w_keyval.swapaxes(1, 2), w_out, frequency, seg_row, w_gateup, w_down, n, m, 1, size
    )
    feed_part, grad_middle, grad_branch, gain_grad_two, grad_ff_weight = feed_forward(
        branch, gain_values, tokens, cotangent, ff_weight, n, 2
    )
    ff_reduced = lax.psum_scatter(grad_ff_weight, "dp", scatter_dimension=0, tiled=True)
    layer_out, input_grad, gain_grad_one, head_reduced = attention_back(
        feed_part, grad_branch, gain_values, q, k, v, mixture, lse, cosines, sines, seg_col, seg_row,
        out_weight, tokens, qkv_weight, branch, grad_middle, n, m, 3, size
    )
    gain_grads = jnp.concatenate([gain_grad_one, gain_grad_two])
    step_float = step_count[0].astype(jnp.float32)
    correct = jnp.stack([1.0 - jnp.power(beta_first, step_float), 1.0 - jnp.power(beta_second, step_float)])
    params = (
        (norm_gains, gains_first, gains_second),
        (w_query, query_first, query_second),
        tuple(a.swapaxes(1, 2) for a in (w_keyval, keyval_first, keyval_second)),
        (w_out, out_first, out_second),
        (w_gateup, gateup_first, gateup_second),
        (w_down, down_first, down_second),
    )
    rates = (
        (gain_rate, 0.0),
        (weight_rate, weight_decay),
        (weight_rate, weight_decay),
        (out_rate, weight_decay),
        (weight_rate, weight_decay),
        (weight_rate, weight_decay),
    )
    norm, layer_out, input_grad, updated = finish_step(
        gain_grads, correct, ff_reduced, head_reduced, layer_out, input_grad,
        [a for group in params for a in group], rates, kv_width, n, m, 4
    )
    results = []
    for k in range(len(params)):
        weight, first_state, second_state = updated[3 * k : 3 * k + 3]
        group = [first_state, second_state, weight]
        results += [a.swapaxes(1, 2) for a in group] if k == 2 else group
    return (layer_out, input_grad, norm, *results)


def solution(mesh):
    rows = P("dp", None)
    gains = P(None, "dp")
    query = P("dp", "tensor")
    stacked = P(None, "dp", "tensor")
    turned = P("tensor", "dp")
    states = (gains,) * 3 + (query,) * 3 + (stacked,) * 3 + (turned,) * 3 + (stacked,) * 3 + (turned,) * 3
    return jax.shard_map(
        functools.partial(on_device, mesh.shape["tensor"], mesh.shape["dp"]),
        mesh=mesh,
        in_specs=(rows, rows, rows, P()) + states,
        out_specs=(rows, rows, P()) + states,
        check_vma=False,
    )
```

```python
import functools

import jax
import jax.numpy as jnp
from jax import lax
from jax.experimental import pallas as pl
from jax.experimental.pallas import tpu as pltpu
from jax.sharding import PartitionSpec as P

HD = 64
MESH = pl.DeviceIdType.MESH


masked_value = -1e9


def dot_t(left, right):
    return lax.dot_general(left, right, (((1,), (1,)), ((), ())), preferred_element_type=jnp.float32)


def dot_n(left, right):
    return lax.dot_general(left, right, (((1,), (0,)), ((), ())), preferred_element_type=jnp.float32)


def swap_halves(values, first_half):
    return jnp.where(first_half, pltpu.roll(values, 96, 1), pltpu.roll(values, 32, 1))


def lane_tests(rows):
    lane = lax.broadcasted_iota(jnp.int32, (rows, 128), 1)
    return lane < 64, (lane % 64) < 32


def block_bias(seg_col_ref, seg_row_ref, i, j, size):
    keys = seg_col_ref[pl.ds(pl.multiple_of(j * size, size), size), :]
    rows = seg_row_ref[:, pl.ds(pl.multiple_of(i * size, size), size)]
    key_at = j * size + lax.broadcasted_iota(jnp.int32, (size, size), 0)
    row_at = i * size + lax.broadcasted_iota(jnp.int32, (size, size), 1)
    return jnp.where((keys == rows) & (key_at <= row_at), 0.0, masked_value)


def stack_pair(pair, low_lanes):
    zero = jnp.zeros_like(pair)
    return jnp.concatenate([jnp.where(low_lanes, pair, zero), jnp.where(low_lanes, zero, pair)], axis=0)


class Line:
    def __init__(self, n, chunks, rc, lag, part, got, out, sems, order=None):
        self.order = order
        self.n, self.chunks, self.rc, self.lag = n, chunks, rc, lag
        self.part, self.got, self.out = part, got, out
        self.send_a, self.recv_a, self.send_g, self.recv_g = sems
        self.me = lax.axis_index("tensor")
        self.steps = chunks + 2 * lag * (n - 1)

    def rows(self, stream, c):
        begin = (stream * self.chunks + c) * self.rc if self.order is None else self.order(stream, c)
        return pl.ds(pl.multiple_of(begin, self.rc), self.rc)

    def side(self, stream):
        pos = self.me if stream == 0 else self.n - 1 - self.me
        fwd = self.me + 1 if stream == 0 else self.me - 1
        bwd = self.me - 1 if stream == 0 else self.me + 1
        return pos, fwd, bwd

    def toward(self, stream, c, nxt, src):
        return pltpu.make_async_remote_copy(
            src_ref=src, dst_ref=self.got.at[stream, c],
            send_sem=self.send_a.at[stream, c], recv_sem=self.recv_a.at[stream, c],
            device_id={"tensor": nxt}, device_id_type=MESH)

    def back(self, stream, c, nxt):
        where = self.rows(stream, c)
        return pltpu.make_async_remote_copy(
            src_ref=self.out.at[where], dst_ref=self.out.at[where],
            send_sem=self.send_g.at[stream, c], recv_sem=self.recv_g.at[stream, c],
            device_id={"tensor": nxt}, device_id_type=MESH)

    def step(self, s):
        n, lag = self.n, self.lag
        for stream in (0, 1):
            pos, fwd, bwd = self.side(stream)
            c = s - lag * pos

            @pl.when((c >= 0) & (c < self.chunks))
            def _():
                where = self.rows(stream, c)
                slot = self.got.at[stream, c]

                def summed():
                    self.toward(stream, c, fwd, slot).wait_recv()
                    return (
                        self.part[where, :].astype(jnp.float32) + self.got[stream, c].astype(jnp.float32)
                    ).astype(self.out.dtype)

                @pl.when(pos == 0)
                def _():
                    self.toward(stream, c, fwd, self.part.at[where]).start()

                @pl.when((pos > 0) & (pos < n - 1))
                def _():
                    self.got[stream, c] = summed()
                    self.toward(stream, c, fwd, slot).start()

                @pl.when(pos == n - 1)
                def _():
                    self.out[where, :] = summed()
                    self.back(stream, c, bwd).start()
            d = s - lag * (n - 1) - lag * (n - 1 - pos)

            @pl.when((d >= 0) & (d < self.chunks) & (pos < n - 1))
            def _():
                self.back(stream, d, bwd).wait_recv()

                @pl.when(pos > 0)
                def _():
                    self.back(stream, d, bwd).start()

    def drain(self):
        def one(c, carry):
            for stream in (0, 1):
                pos, fwd, bwd = self.side(stream)

                @pl.when(pos < self.n - 1)
                def _():
                    self.toward(stream, c, fwd, self.got.at[stream, c]).wait_send()

                @pl.when(pos > 0)
                def _():
                    self.back(stream, c, bwd).wait_send()
            return carry

        lax.fori_loop(0, self.chunks, one, 0)


def greet(n):
    me = lax.axis_index("tensor")
    barrier = pltpu.get_barrier_semaphore()

    @pl.when(me > 0)
    def _():
        pl.semaphore_signal(barrier, inc=1, device_id={"tensor": me - 1}, device_id_type=MESH)

    @pl.when(me < n - 1)
    def _():
        pl.semaphore_signal(barrier, inc=1, device_id={"tensor": me + 1}, device_id_type=MESH)

    @pl.when((me > 0) & (me < n - 1))
    def _():
        pl.semaphore_wait(barrier, 2)

    @pl.when((me == 0) | (me == n - 1))
    def _():
        pl.semaphore_wait(barrier, 1)


def line_scratch(chunks, rc, width):
    return [pltpu.VMEM((2, chunks, rc, width), jnp.bfloat16)] + [pltpu.SemaphoreType.DMA((2, chunks))] * 4


def line_kernel(n, chunks, lag, count, *refs):
    parts, outs, scratch = refs[:count], refs[count:2 * count], refs[2 * count:]
    rc = parts[0].shape[0] // (2 * chunks)
    lines = [
        Line(n, chunks, rc, lag, parts[k], scratch[5 * k], outs[k], scratch[5 * k + 1:5 * k + 5])
        for k in range(count)
    ]
    greet(n)

    def step(s, carry):
        for k, line in enumerate(lines):
            line.step(s - k * chunks)
        return carry

    lax.fori_loop(0, lines[0].steps + (count - 1) * chunks, step, 0)
    for line in lines:
        line.drain()


def line_reduce(parts, n, chunks, cid, lag=2):
    rows, width = parts[0].shape
    count = len(parts)
    rc = rows // (2 * chunks)
    scratch = []
    for _ in parts:
        scratch += line_scratch(chunks, rc, width)
    vmem = pl.BlockSpec(memory_space=pltpu.VMEM)
    return pl.pallas_call(
        functools.partial(line_kernel, n, chunks, lag, count),
        out_shape=tuple(jax.ShapeDtypeStruct((rows, width), jnp.bfloat16) for _ in parts),
        in_specs=[vmem] * count,
        out_specs=(vmem,) * count,
        scratch_shapes=scratch,
        compiler_params=pltpu.CompilerParams(collective_id=cid, has_side_effects=True, vmem_limit_bytes=40 << 20),
        cost_estimate=pl.CostEstimate(flops=rows * width * 2 * count, bytes_accessed=rows * width * 120 * count,
                                      transcendentals=0),
    )(*parts)


def dot_rows(left, right):
    return lax.dot_general(left, right, (((0,), (0,)), ((), ())), preferred_element_type=jnp.float32)


def ff_kernel(n, chunks, lag, eps, branch, gain, x, cot_hbm, w_hbm,
              feed_hbm, middle_hbm, low_hbm, gain_out, grads_hbm,
              got, sa, ra, sg, rg, two_sum, two_part, weight, cot, normed, hidden, gg, feed,
              middle_stage, low_stage, unit_stage, w_sem, cot_sem, feed_sem, stage_sem, grad_sem):
    rows, width = branch.shape
    ff = hidden.shape[1]
    rc = rows // (2 * chunks)
    per = 8
    offset = per - 1
    half = rows // 2
    hb = per * rc
    block = 2 * hb
    blocks = chunks // per
    line = Line(n, chunks, rc, lag, two_part, got, two_sum, (sa, ra, sg, rg))
    landed = 2 * lag * (n - 1) + offset
    tile = 256
    full, rest = ff // tile, ff % tile
    wide = width // tile

    groups = []
    for g, (begin, end) in enumerate(((0, tile), (tile, 2 * tile), (2 * tile, ff))):
        groups.append([
            pltpu.make_async_copy(w_hbm.at[:, pl.ds(t * ff + begin, end - begin)],
                                  weight.at[:, pl.ds(t * ff + begin, end - begin)], w_sem.at[g, t])
            for t in range(3)
        ])
    for copy in sum(groups, []):
        copy.start()

    def natural(k, b):
        return pl.ds(pl.multiple_of(k * half + b * hb, hb), hb)

    def blocked(k, b):
        return pl.ds(pl.multiple_of(b * block + k * hb, hb), hb)

    def load_cot(b):
        return [pltpu.make_async_copy(cot_hbm.at[natural(k, b)], cot.at[blocked(k, b)], cot_sem.at[b, k])
                for k in (0, 1)]

    def save_feed(b):
        return [pltpu.make_async_copy(feed.at[pl.ds(k * hb, hb)], feed_hbm.at[natural(k, b)], feed_sem.at[k])
                for k in (0, 1)]

    def save_rows(d):
        copies = []
        for k in (0, 1):
            where = line.rows(k, d)
            copies.append(pltpu.make_async_copy(middle_stage.at[k], middle_hbm.at[where], stage_sem.at[0, k]))
            copies.append(pltpu.make_async_copy(low_stage.at[k], low_hbm.at[where], stage_sem.at[1, k]))
        return copies

    def save_units(w):
        return [pltpu.make_async_copy(unit_stage, grads_hbm.at[pl.ds(pl.multiple_of(w * tile, tile), tile)], grad_sem.at[0])]

    def start(copies):
        for copy in copies:
            copy.start()

    def wait(copies):
        for copy in copies:
            copy.wait()

    for b in range(blocks):
        start(load_cot(b))
    gain_out[...] = jnp.zeros_like(gain_out)
    greet(n)

    def unit_rows(where):
        middle = x[where, :].astype(jnp.float32) + branch[where, :].astype(jnp.float32)
        inverse = lax.rsqrt(jnp.mean(middle * middle, axis=-1, keepdims=True) + eps)
        return middle * inverse, inverse

    def normalize(b):
        def some(r, carry):
            for k in (0, 1):
                where = pl.ds(pl.multiple_of(k * half + b * hb + r * rc, rc), rc)
                at = pl.ds(pl.multiple_of(b * block + k * hb + r * rc, rc), rc)
                normed[at, :] = (unit_rows(where)[0] * gain[1:2, :]).astype(jnp.bfloat16)
            return carry

        lax.fori_loop(0, per, some, 0)

    def step(s, carry):
        line.step(s - offset)
        b = s // per
        phase = s - b * per
        live = s < chunks
        mine = pl.ds(pl.multiple_of(b * block, block), block)

        def units(at, count):
            columns = pl.ds(at, count)
            second = pl.ds(pl.multiple_of(ff + at, 128), count)
            third = pl.ds(pl.multiple_of(2 * ff + at, 128), count)
            gate = dot_n(normed[mine, :], weight[:, columns])
            up = dot_n(normed[mine, :], weight[:, second])
            grad_hidden = dot_n(cot[mine, :], weight[:, third])
            sg_gate = 1.0 / (1.0 + jnp.exp(-gate))
            silu = gate * sg_gate
            hidden[mine, columns] = (silu * up).astype(jnp.bfloat16)
            gg[mine, columns] = (grad_hidden * up * sg_gate * (1.0 + gate * (1.0 - sg_gate))).astype(jnp.bfloat16)
            gg[mine, second] = (grad_hidden * silu).astype(jnp.bfloat16)

        def unit_tile(t, c):
            for g in range(3):
                @pl.when((b == 0) & (t == g))
                def _():
                    wait(groups[g])
            units(pl.multiple_of(t * tile, tile), tile)
            return c

        @pl.when(live & (phase == 0))
        def _():
            normalize(b)
            wait(load_cot(b))

        @pl.when(live & (phase < 3))
        def _():
            lax.fori_loop(jnp.maximum(2 * phase - 1, 0), jnp.minimum(2 * phase + 1, full), unit_tile, 0)

        @pl.when(live & (phase == 3))
        def _():
            if rest:
                units(full * tile, rest)

            @pl.when(b > 0)
            def _():
                wait(save_feed(b - 1))

        @pl.when(live & ((phase == 3) | (phase == 4)))
        def _():
            def feed_tile(t, c):
                columns = pl.ds(pl.multiple_of(t * 2 * tile, 2 * tile), 2 * tile)
                feed[:, columns] = dot_t(hidden[mine, :], weight[columns, 2 * ff:]).astype(jnp.bfloat16)
                return c

            lax.fori_loop((phase - 3) * (wide // 4), (phase - 2) * (wide // 4), feed_tile, 0)

            @pl.when(phase == 4)
            def _():
                start(save_feed(b))

        @pl.when(live & ((phase == 5) | (phase == 6)))
        def _():
            def two_tile(t, c):
                at = pl.ds(pl.multiple_of(t * 2 * tile, 2 * tile), 2 * tile)
                value = dot_t(gg[mine, :], weight[at, :2 * ff]).astype(jnp.bfloat16)
                for k in (0, 1):
                    two_part[natural(k, b), at] = value[k * hb:(k + 1) * hb]
                return c

            lax.fori_loop((phase - 5) * (wide // 4), (phase - 4) * (wide // 4), two_tile, 0)

        d = s - landed

        @pl.when(d >= 0)
        def _():
            @pl.when(d > 0)
            def _():
                wait(save_rows(d - 1))
            for k in (0, 1):
                where = line.rows(k, d)
                at = pl.ds(pl.multiple_of((d // per) * block + k * hb + (d - (d // per) * per) * rc, rc), rc)
                pieces = [pl.ds(c * tile, tile) for c in range(wide)]

                def middle_at(c):
                    return x[where, c].astype(jnp.float32) + branch[where, c].astype(jnp.float32)

                def folded(value):
                    return value[:, :128] + value[:, 128:]

                total = jnp.zeros((rc, 128), jnp.float32)
                for c in pieces:
                    middle = middle_at(c)
                    total = total + folded(middle * middle)
                inverse = lax.rsqrt(jnp.sum(total, axis=-1, keepdims=True) * (1.0 / width) + eps)
                total = jnp.zeros((rc, 128), jnp.float32)
                for c in pieces:
                    product = two_sum[where, c].astype(jnp.float32) * (middle_at(c) * inverse)
                    gain_out[:, c] += jnp.sum(product, axis=0, keepdims=True)
                    total = total + folded(product * gain[1:2, c])
                inner = jnp.sum(total, axis=-1, keepdims=True) * (1.0 / width)
                for c in pieces:
                    scaled = two_sum[where, c].astype(jnp.float32) * gain[1:2, c]
                    value = cot[at, c].astype(jnp.float32) + inverse * (scaled - middle_at(c) * inverse * inner)
                    middle_stage[k, :, c] = value
                    low_stage[k, :, c] = value.astype(jnp.bfloat16)
            start(save_rows(d))

        late = s - chunks
        w = late // 2

        @pl.when((late >= 0) & (late == 2 * w) & (w < wide))
        def _():
            @pl.when(w > 0)
            def _():
                wait(save_units(w - 1))
            columns = pl.ds(pl.multiple_of(w * tile, tile), tile)
            left = normed[:, columns]
            for t in (0, 1):
                unit_stage[:, t * ff:(t + 1) * ff] = dot_rows(left, gg[:, t * ff:(t + 1) * ff]).astype(jnp.bfloat16)
            unit_stage[:, 2 * ff:] = dot_rows(cot[:, columns], hidden[...]).astype(jnp.bfloat16)
            start(save_units(w))
        return carry

    lax.fori_loop(0, offset + line.steps, step, 0)
    line.drain()
    wait(save_feed(blocks - 1))
    wait(save_rows(chunks - 1))
    wait(save_units(wide - 1))


def feed_forward(branch, gain, x, cot, weight, n, cid, chunks=32, lag=2):
    rows, width = branch.shape
    ff = weight.shape[1] // 3
    rc = rows // (2 * chunks)
    block = 16 * rc
    blocks = chunks // 8
    low = jnp.bfloat16
    vmem = pl.BlockSpec(memory_space=pltpu.VMEM)
    hbm = pl.BlockSpec(memory_space=pl.ANY)
    dma = pltpu.SemaphoreType.DMA
    shape = jax.ShapeDtypeStruct
    return pl.pallas_call(
        functools.partial(ff_kernel, n, chunks, lag, norm_eps),
        out_shape=(
            shape((rows, width), low), shape((rows, width), jnp.float32), shape((rows, width), low),
            shape((1, width), jnp.float32), shape((width, 3 * ff), low),
        ),
        in_specs=[vmem, vmem, vmem, hbm, hbm],
        out_specs=(hbm, hbm, hbm, vmem, hbm),
        scratch_shapes=line_scratch(chunks, rc, width) + [
            pltpu.VMEM((rows, width), low),
            pltpu.VMEM((rows, width), low),
            pltpu.VMEM((width, 3 * ff), low),
            pltpu.VMEM((rows, width), low),
            pltpu.VMEM((rows, width), low),
            pltpu.VMEM((rows, ff), low),
            pltpu.VMEM((rows, 2 * ff), low),
            pltpu.VMEM((block, width), low),
            pltpu.VMEM((2, rc, width), jnp.float32),
            pltpu.VMEM((2, rc, width), low),
            pltpu.VMEM((256, 3 * ff), low),
            dma((3, 3)), dma((blocks, 2)), dma((2,)), dma((2, 2)), dma((1,)),
        ],
        compiler_params=pltpu.CompilerParams(collective_id=cid, has_side_effects=True, vmem_limit_bytes=63 << 20),
        cost_estimate=pl.CostEstimate(flops=18 * rows * width * ff, bytes_accessed=rows * width * 150,
                                      transcendentals=rows * ff),
    )(branch, gain, x, cot, weight)


def head_kernel(n, m, chunks, lag, eps, size, pairs,
                gain_part, query_own, keyval_own, out_own, frequency, seg_row_ref,
                x_hbm, gateup_hbm, down_hbm,
                branch, gain, lse_ref, seg_col_ref, cos_hbm, sin_hbm, mix_hbm, q_hbm, k_hbm, v_hbm, qkv_hbm, out_hbm, ff_hbm,
                got, sa, ra, sg, rg, part, normed, raw, bias, scores, v_turned, got_gain,
                x, cos_ref, sin_ref, mix_ref, q_ref, k_ref, v_ref, qkv_w, out_w, gateup_own, down_own, ff_own,
                send_gain, recv_gain, send_direct, send_forward, recv_w, own_sem, save_sem, result_sem, x_sem,
                send_ff, pass_ff, recv_ff):
    rows, width = branch.shape
    q_width = pairs * 128
    x_load = pltpu.make_async_copy(x_hbm, x, x_sem)
    x_load.start()
    results = [
        pltpu.make_async_copy(source, target, result_sem.at[k])
        for k, (source, target) in enumerate((
            (q_ref, q_hbm), (k_ref, k_hbm), (v_ref, v_hbm), (cos_ref, cos_hbm), (sin_ref, sin_hbm),
            (qkv_w, qkv_hbm), (out_w, out_hbm), (mix_ref, mix_hbm)))
    ]
    z = lax.axis_index("tensor")
    dp = lax.axis_index("dp")
    share = width // m
    chips = m // 2
    chip, core = dp // 2, dp % 2
    rc = rows // (2 * chunks)
    per = size // (2 * rc)
    hb = size // 2
    blocks = rows // size
    tile = 256
    wide = width // tile
    low_lanes, first_half = lane_tests(size)
    low_rows = lax.broadcasted_iota(jnp.int32, (128, size), 0) < 64
    wholes = (qkv_w, out_w)
    ff = down_own.shape[0]
    piece = 32
    pieces = share // piece
    spacing = 40 // pieces
    owned = (
        pltpu.make_async_copy(gateup_hbm, gateup_own, own_sem.at[0]),
        pltpu.make_async_copy(down_hbm, down_own, own_sem.at[1]),
    )
    for copy in owned:
        copy.start()

    def ascending(stream, c):
        b = c // per
        return b * size + stream * hb + (c - b * per) * rc

    line = Line(n, chunks, rc, lag, part, got, branch, (sa, ra, sg, rg), ascending)

    def shard_rows(s):
        return pl.ds(pl.multiple_of(s * share, share), share)

    def direct(kind, k):
        peer = 2 * lax.rem(chip + k, chips) + core
        return pltpu.make_async_remote_copy(
            src_ref=wholes[kind].at[shard_rows(dp)], dst_ref=wholes[kind].at[shard_rows(dp)], send_sem=send_direct.at[kind, k],
            recv_sem=recv_w.at[kind, dp], device_id={"dp": peer}, device_id_type=MESH)

    def forward(kind, c, side):
        shard = 2 * c + side
        where = shard_rows(shard)
        return pltpu.make_async_remote_copy(
            src_ref=wholes[kind].at[where], dst_ref=wholes[kind].at[where], send_sem=send_forward.at[kind, c],
            recv_sem=recv_w.at[kind, shard], device_id={"dp": 2 * chip + 1 - core}, device_id_type=MESH)

    def piece_rows(shard, p):
        return pl.ds(pl.multiple_of(shard * share + p * piece, piece), piece)

    def own_piece(p):
        return ff_own.at[pl.ds(pl.multiple_of(p * piece, piece), piece)]

    def send_piece(k, p):
        peer = 2 * lax.rem(chip + k, chips) + core
        return pltpu.make_async_remote_copy(
            src_ref=own_piece(p), dst_ref=ff_hbm.at[piece_rows(dp, p)], send_sem=send_ff.at[k, p],
            recv_sem=recv_ff.at[dp, p], device_id={"dp": peer}, device_id_type=MESH)

    def pass_piece(c, side, p, src=None):
        shard = 2 * c + side
        where = ff_hbm.at[piece_rows(shard, p)]
        return pltpu.make_async_remote_copy(
            src_ref=where if src is None else src, dst_ref=where, send_sem=pass_ff.at[c, p],
            recv_sem=recv_ff.at[shard, p], device_id={"dp": 2 * chip + 1 - core}, device_id_type=MESH)

    def save_own():
        return pltpu.make_async_copy(ff_own, ff_hbm.at[shard_rows(dp)], save_sem)

    def send_gains(k, sender):
        return pltpu.make_async_remote_copy(
            src_ref=gain_part, dst_ref=got_gain.at[sender], send_sem=send_gain.at[k], recv_sem=recv_gain.at[sender],
            device_id={"dp": lax.rem(dp + k, m)}, device_id_type=MESH)

    barrier = pltpu.get_barrier_semaphore()

    @pl.when(z > 0)
    def _():
        pl.semaphore_signal(barrier, inc=1, device_id={"tensor": z - 1}, device_id_type=MESH)

    @pl.when(z < n - 1)
    def _():
        pl.semaphore_signal(barrier, inc=1, device_id={"tensor": z + 1}, device_id_type=MESH)

    for k in range(1, m):
        pl.semaphore_signal(barrier, inc=1, device_id={"dp": lax.rem(dp + k, m)}, device_id_type=MESH)

    qkv_w[shard_rows(dp), :q_width] = query_own[...].astype(jnp.bfloat16)
    both_own = jnp.concatenate([keyval_own[0], keyval_own[1]], axis=0)
    qkv_w[shard_rows(dp), q_width:] = both_own.T.astype(jnp.bfloat16)
    for t in range(q_width // 128):
        out_w[shard_rows(dp), t * 128:(t + 1) * 128] = out_own[t * 128:(t + 1) * 128, :].T.astype(jnp.bfloat16)
    got_gain[dp] = gain_part[...]

    @pl.when((z > 0) & (z < n - 1))
    def _():
        pl.semaphore_wait(barrier, m + 1)

    @pl.when((z == 0) | (z == n - 1))
    def _():
        pl.semaphore_wait(barrier, m)

    for k in range(1, m):
        send_gains(k, dp).start()
    for kind in (0, 1):
        for k in range(1, chips):
            direct(kind, k).start()
        forward(kind, chip, core).start()
    for k in range(1, m):
        send_gains(k, lax.rem(dp + m - k, m)).wait_recv()
    whole = got_gain[0]
    for k in range(1, m):
        whole = whole + got_gain[k]
    gain[...] = whole.astype(jnp.bfloat16).astype(jnp.float32)

    x_load.wait()

    def norm_rows(r, carry):
        where = pl.ds(pl.multiple_of(r * rc, rc), rc)
        values = x[where, :].astype(jnp.float32)
        inverse = lax.rsqrt(jnp.mean(values * values, axis=-1, keepdims=True) + eps)
        normed[where, :] = (values * inverse * gain[0:1, :]).astype(jnp.bfloat16)
        return carry

    lax.fori_loop(0, rows // rc, norm_rows, 0)
    def tables(i, carry):
        where = pl.ds(pl.multiple_of(i * size, size), size)
        ids = jnp.broadcast_to(seg_row_ref[:, where].astype(jnp.float32), (128, size)).T[:, :1]
        seg_col_ref[where, :] = ids.astype(jnp.int32)
        earlier = jnp.where(seg_row_ref[...].astype(jnp.float32) < ids, 1.0, 0.0)
        place = (i * size + lax.broadcasted_iota(jnp.int32, (size, 1), 0)).astype(jnp.float32) - jnp.sum(
            earlier, axis=1, keepdims=True)
        angles = place * frequency[...]
        sines = jnp.sin(angles)
        cos_ref[where, :] = jnp.cos(angles)
        sin_ref[where, :] = jnp.where(first_half, -sines, sines)
        return carry

    lax.fori_loop(0, blocks, tables, 0)
    for copy in owned:
        copy.wait()

    def own_rows(r, carry):
        where = pl.ds(pl.multiple_of(r * piece, piece), piece)
        for t in (0, 1):
            ff_own[where, t * ff:(t + 1) * ff] = gateup_own[t, where, :].astype(jnp.bfloat16)
        return carry

    lax.fori_loop(0, pieces, own_rows, 0)

    def own_columns(t, carry):
        at = pl.ds(pl.multiple_of(2 * ff + t * 128, 128), 128)
        ff_own[:, at] = down_own[pl.ds(pl.multiple_of(t * 128, 128), 128), :].T.astype(jnp.bfloat16)
        return carry

    lax.fori_loop(0, ff // 128, own_columns, 0)
    save_own().start()

    def pass_on(kind):
        for k in range(1, chips):
            c = lax.rem(chip + chips - k, chips)
            forward(kind, c, core).wait_recv()
            forward(kind, c, core).start()

    def receive(kind):
        for c in range(chips):
            forward(kind, c, 1 - core).wait_recv()

    pass_on(0)
    receive(0)
    for p in range(min(2, pieces)):
        for k in range(1, chips):
            send_piece(k, p).start()

    def prepare(i, carry):
        where = pl.ds(pl.multiple_of(i * size, size), size)
        raw[...] = dot_n(normed[where, :], qkv_w[...])
        cosines, sines = cos_ref[where, :], sin_ref[where, :]
        for hp in range(pairs):
            values = raw[:, hp * 128:(hp + 1) * 128]
            turned = values * cosines + swap_halves(values, first_half) * sines
            q_ref[where, hp * 128:(hp + 1) * 128] = (
                turned.astype(jnp.bfloat16).astype(jnp.float32) * 0.125).astype(jnp.bfloat16)
        both = raw[:, q_width:q_width + 128]
        other = pltpu.roll(both, 64, 1)
        keys = jnp.where(low_lanes, both, other)
        k_ref[where, :] = (keys * cosines + swap_halves(keys, first_half) * sines).astype(jnp.bfloat16)
        values = jnp.where(low_lanes, other, both)
        v_ref[where, :] = values.astype(jnp.bfloat16)
        v_turned[i] = values.T.astype(jnp.bfloat16)
        return carry

    lax.fori_loop(0, blocks, prepare, 0)
    for copy in results[:5]:
        copy.start()
    pass_on(1)

    def attend(i, hp):
        where = pl.ds(pl.multiple_of(i * size, size), size)
        columns = pl.ds(pl.multiple_of(hp * 128, 128), 128)
        stacked = stack_pair(q_ref[where, columns], low_lanes)

        def score(j, top):
            keys = k_ref[pl.ds(pl.multiple_of(j * size, size), size), :]
            b = bias[j]
            s = dot_t(keys, stacked) + jnp.concatenate([b, b], axis=1)
            scores[j] = s
            return jnp.maximum(top, jnp.max(s, axis=0, keepdims=True))

        top = lax.fori_loop(0, i + 1, score, jnp.full((1, 2 * size), -jnp.inf, jnp.float32))

        def mix(j, c):
            total, acc = c
            p = jnp.exp(scores[j] - top)
            total = total + jnp.sum(p, axis=0, keepdims=True)
            return total, acc + dot_n(v_turned[j], p.astype(jnp.bfloat16))

        total, acc = lax.fori_loop(0, i + 1, mix, (
            jnp.zeros((1, 2 * size), jnp.float32), jnp.zeros((128, 2 * size), jnp.float32)))
        lse_ref[i, hp] = top + jnp.log(total)
        acc = acc / total
        acc = jnp.where(low_rows, acc[:, :size], acc[:, size:])
        mix_ref[where, columns] = acc.T.astype(jnp.bfloat16)

    def step(s, carry):
        line.step(s - per)
        p_send = (s - 1) // spacing + 2
        p_pass = (s - 12) // spacing

        @pl.when((s >= 1) & ((p_send - 2) * spacing == s - 1) & (p_send < pieces))
        def _():
            for k in range(1, chips):
                send_piece(k, p_send).start()

        @pl.when((s >= 12) & (p_pass * spacing == s - 12) & (p_pass < pieces))
        def _():
            pass_piece(chip, core, p_pass, own_piece(p_pass)).start()
            for k in range(1, chips):
                c = lax.rem(chip + chips - k, chips)
                pass_piece(c, core, p_pass).wait_recv()
                pass_piece(c, core, p_pass).start()

        i = s // per
        hp = s - i * per
        live = s < blocks * per

        @pl.when(live & (hp == 0))
        def _():
            def fill(j, c):
                bias[j] = block_bias(seg_col_ref, seg_row_ref, i, j, size)
                return c

            lax.fori_loop(0, i + 1, fill, 0)

        @pl.when(live)
        def _():
            def each(h, c):
                attend(i, h)
                return c

            lax.fori_loop(hp * pairs // per, (hp + 1) * pairs // per, each, 0)

        @pl.when(s == per - 1)
        def _():
            receive(1)
            for copy in results[5:7]:
                copy.start()

        @pl.when(s == blocks * per)
        def _():
            results[7].start()

        @pl.when(live & (hp == per - 1))
        def _():
            where = pl.ds(pl.multiple_of(i * size, size), size)

            def part_tile(t, c):
                at = pl.ds(pl.multiple_of(t * tile, tile), tile)
                part[where, at] = dot_t(mix_ref[where, :], out_w[at, :]).astype(jnp.bfloat16)
                return c

            lax.fori_loop(0, wide, part_tile, 0)
        return carry

    lax.fori_loop(0, per + line.steps, step, 0)
    line.drain()
    save_own().wait()
    for copy in results:
        copy.wait()

    def settle(p, carry):
        for k in range(1, chips):
            send_piece(k, p).wait_send()
        for c in range(chips):
            pass_piece(c, core, p).wait_send()
            pass_piece(c, 1 - core, p).wait_recv()
        return carry

    lax.fori_loop(0, pieces, settle, 0)
    for k in range(1, m):
        send_gains(k, dp).wait_send()
    for kind in (0, 1):
        for k in range(1, chips):
            direct(kind, k).wait_send()
        for c in range(chips):
            forward(kind, c, core).wait_send()


def attention_head(x, gain_part, query, keyval, out, frequency, seg_row, gateup, down, n, m, cid, size,
                   chunks=32, lag=2):
    rows, width = x.shape
    q_width = query.shape[1]
    share, ff = width // m, down.shape[0]
    pairs = q_width // 128
    rc = rows // (2 * chunks)
    blocks = rows // size
    chips = m // 2
    low = jnp.bfloat16
    vmem = pl.BlockSpec(memory_space=pltpu.VMEM)
    hbm = pl.BlockSpec(memory_space=pl.ANY)
    dma = pltpu.SemaphoreType.DMA
    shape = jax.ShapeDtypeStruct
    return pl.pallas_call(
        functools.partial(head_kernel, n, m, chunks, lag, norm_eps, size, pairs),
        out_shape=(
            shape((rows, width), low), shape((2, width), jnp.float32),
            shape((blocks, pairs, 1, 2 * size), jnp.float32), shape((rows, 1), jnp.int32),
            shape((rows, 128), jnp.float32), shape((rows, 128), jnp.float32), shape((rows, q_width), low),
            shape((rows, q_width), low), shape((rows, 128), low), shape((rows, 128), low),
            shape((width, q_width + 128), low), shape((width, q_width), low), shape((width, 3 * ff), low),
        ),
        in_specs=[vmem] * 6 + [hbm] * 3,
        out_specs=(vmem,) * 4 + (hbm,) * 9,
        scratch_shapes=line_scratch(chunks, rc, width) + [
            pltpu.VMEM((rows, width), low),
            pltpu.VMEM((rows, width), low),
            pltpu.VMEM((size, q_width + 128), jnp.float32),
            pltpu.VMEM((blocks, size, size), jnp.float32),
            pltpu.VMEM((blocks, size, 2 * size), jnp.float32),
            pltpu.VMEM((blocks, 128, size), low),
            pltpu.VMEM((m, 2, width), jnp.float32),
            pltpu.VMEM((rows, width), low),
            pltpu.VMEM((rows, 128), jnp.float32),
            pltpu.VMEM((rows, 128), jnp.float32),
            pltpu.VMEM((rows, q_width), low),
            pltpu.VMEM((rows, q_width), low),
            pltpu.VMEM((rows, 128), low),
            pltpu.VMEM((rows, 128), low),
            pltpu.VMEM((width, q_width + 128), low),
            pltpu.VMEM((width, q_width), low),
            pltpu.VMEM(gateup.shape, jnp.float32),
            pltpu.VMEM(down.shape, jnp.float32),
            pltpu.VMEM((share, 3 * ff), low),
            dma((m,)), dma((m,)), dma((2, chips)), dma((2, chips)), dma((2, m)), dma((2,)), dma, dma((8,)), dma,
            dma((chips, share // 32)), dma((chips, share // 32)), dma((m, share // 32)),
        ],
        compiler_params=pltpu.CompilerParams(collective_id=cid, has_side_effects=True, vmem_limit_bytes=56 << 20),
        cost_estimate=pl.CostEstimate(flops=20 * rows * width * q_width, bytes_accessed=rows * width * 170,
                                      transcendentals=rows * rows * pairs),
    )(gain_part, query, keyval, out, frequency, seg_row, x, gateup, down)


def back_kernel(n, m, chunks, lag, eps, size, pairs,
                feed_part, gain, lse_ref, seg_row_ref,
                low_hbm, q_hbm, k_hbm, v_hbm, mix_hbm, cos_hbm, sin_hbm, seg_hbm, out_hbm, x_hbm, qkv_hbm,
                branch_hbm, middle_hbm,
                layer_hbm, input_hbm, gain_out, reduced,
                got2, sa2, ra2, sg2, rg2, got4, sa4, ra4, sg4, rg4, feed_sum, part, grad_sum,
                grad_low, q_ref, k_ref, v_ref, mix_ref, cos_ref, sin_ref, seg_col_ref, out_w, x, qkv_w,
                normed, grad_mix, bias, k_turned, grad_k, grad_v, grad_qkv, send, recv,
                branch_stage, layer_stage, middle_stage, input_stage,
                w_sem, branch_sem, middle_sem, layer_sem, input_sem, send_sem, recv_sem):
    rows, width = feed_part.shape
    q_width = pairs * 128
    z = lax.axis_index("tensor")
    dp = lax.axis_index("dp")
    rc = rows // (2 * chunks)
    per = size // (2 * rc)
    hb = size // 2
    blocks = rows // size
    tile = 256
    wide = width // tile
    share = width // m
    owners = tile // share
    lead = 2 * lag * (n - 1)
    shift = chunks + per
    low_lanes, first_half = lane_tests(size)
    low_rows = lax.broadcasted_iota(jnp.int32, (128, size), 0) < 64

    def descending(stream, c):
        b = c // per
        return (blocks - 1 - b) * size + stream * hb + (c - b * per) * rc

    two = Line(n, chunks, rc, lag, feed_part, got2, feed_sum, (sa2, ra2, sg2, rg2))
    four = Line(n, chunks, rc, lag, part, got4, grad_sum, (sa4, ra4, sg4, rg4), descending)
    loads = [
        pltpu.make_async_copy(source, target, w_sem.at[k])
        for k, (source, target) in enumerate((
            (k_hbm, k_ref), (q_hbm, q_ref), (low_hbm, grad_low), (out_hbm, out_w), (v_hbm, v_ref), (mix_hbm, mix_ref),
            (cos_hbm, cos_ref), (sin_hbm, sin_ref), (seg_hbm, seg_col_ref), (x_hbm, x), (qkv_hbm, qkv_w)))
    ]
    for copy in loads:
        copy.start()

    def start(copies):
        for copy in copies:
            copy.start()

    def wait(copies):
        for copy in copies:
            copy.wait()

    def load_branch(d, slot):
        return [pltpu.make_async_copy(branch_hbm.at[two.rows(k, d)], branch_stage.at[slot, k], branch_sem.at[slot, k])
                for k in (0, 1)]

    def load_middle(d, slot):
        return [pltpu.make_async_copy(middle_hbm.at[four.rows(k, d)], middle_stage.at[slot, k], middle_sem.at[slot, k])
                for k in (0, 1)]

    def save_layer(d):
        return [pltpu.make_async_copy(layer_stage.at[k], layer_hbm.at[two.rows(k, d)], layer_sem.at[k]) for k in (0, 1)]

    def save_input(d):
        return [pltpu.make_async_copy(input_stage.at[k], input_hbm.at[four.rows(k, d)], input_sem.at[k]) for k in (0, 1)]

    def to_owner(w, o):
        owner = w * owners + o
        return pltpu.make_async_remote_copy(
            src_ref=send.at[w, pl.ds(o * share, share)], dst_ref=recv.at[dp], send_sem=send_sem.at[owner],
            recv_sem=recv_sem.at[dp], device_id={"dp": owner}, device_id_type=MESH)

    gain_out[...] = jnp.zeros_like(gain_out)

    def prepare(i, carry):
        at = pl.ds(pl.multiple_of(i * size, size), size)
        k_turned[i] = k_ref[at, :].astype(jnp.float32).T.astype(jnp.bfloat16)
        grad_k[i] = jnp.zeros((size, 128), jnp.float32)
        grad_v[i] = jnp.zeros((size, 128), jnp.float32)
        return carry

    barrier = pltpu.get_barrier_semaphore()

    @pl.when(z > 0)
    def _():
        pl.semaphore_signal(barrier, inc=1, device_id={"tensor": z - 1}, device_id_type=MESH)

    @pl.when(z < n - 1)
    def _():
        pl.semaphore_signal(barrier, inc=1, device_id={"tensor": z + 1}, device_id_type=MESH)

    for k in range(1, m):
        pl.semaphore_signal(barrier, inc=1, device_id={"dp": lax.rem(dp + k, m)}, device_id_type=MESH)

    @pl.when((z > 0) & (z < n - 1))
    def _():
        pl.semaphore_wait(barrier, m + 1)

    @pl.when((z == 0) | (z == n - 1))
    def _():
        pl.semaphore_wait(barrier, m)

    def unit_rows(where):
        values = x[where, :].astype(jnp.float32)
        inverse = lax.rsqrt(jnp.mean(values * values, axis=-1, keepdims=True) + eps)
        return values * inverse, inverse

    def attend(i, hp):
        at_rows = pl.ds(pl.multiple_of(i * size, size), size)
        columns = pl.ds(pl.multiple_of(hp * 128, 128), 128)
        stacked = stack_pair(q_ref[at_rows, columns], low_lanes)
        grad_pair = grad_mix[:, columns]
        grad_stacked = stack_pair(grad_pair, low_lanes)
        product = (grad_pair.astype(jnp.float32) * mix_ref[at_rows, columns].astype(jnp.float32)).T
        spread = jnp.concatenate([
            jnp.sum(product[:64], axis=0, keepdims=True), jnp.sum(product[64:], axis=0, keepdims=True)], axis=1)
        logsum = lse_ref[i, hp]

        def piece(j, acc):
            at = pl.ds(pl.multiple_of(j * size, size), size)
            b = bias[j]
            s = dot_t(k_ref[at, :], stacked) + jnp.concatenate([b, b], axis=1)
            p = jnp.exp(s - logsum)
            grad_p = dot_t(v_ref[at, :], grad_stacked)
            grad_s = (p * (grad_p - spread)).astype(jnp.bfloat16)
            grad_v[j] += dot_n(p.astype(jnp.bfloat16), grad_stacked)
            grad_k[j] += dot_n(grad_s, stacked)
            return acc + dot_n(k_turned[j], grad_s)

        acc = lax.fori_loop(0, i + 1, piece, jnp.zeros((128, 2 * size), jnp.float32))
        acc = jnp.where(low_rows, acc[:, :size], acc[:, size:]).T * 0.125
        turned = acc * cos_ref[at_rows, :] - swap_halves(acc, first_half) * sin_ref[at_rows, :]
        grad_qkv[at_rows, columns] = turned.astype(jnp.bfloat16)

    def finish(k, carry):
        owner = lax.rem(dp + k, m)
        w = owner // owners

        def copy(peer):
            return pltpu.make_async_remote_copy(
                src_ref=send.at[0, pl.ds(0, share)], dst_ref=recv.at[peer], send_sem=send_sem.at[peer],
                recv_sem=recv_sem.at[peer], device_id={"dp": peer}, device_id_type=MESH)

        copy(owner).wait_send()
        copy(owner).wait_recv()
        return carry

    def step(s, carry):
        two.step(s)
        four.step(s - shift)
        b = s // per
        hp = s - b * per
        i = blocks - 1 - b
        live = s < blocks * per
        at_rows = pl.ds(pl.multiple_of(i * size, size), size)

        @pl.when(s == 0)
        def _():
            wait(loads)
            lax.fori_loop(0, blocks, prepare, 0)

        @pl.when(live & (hp == 0))
        def _():
            grad_mix[...] = dot_n(grad_low[at_rows, :], out_w[...]).astype(jnp.bfloat16)

            def fill(j, c):
                bias[j] = block_bias(seg_col_ref, seg_row_ref, i, j, size)
                return c

            lax.fori_loop(0, i + 1, fill, 0)

        @pl.when(live)
        def _():
            def each(h, c):
                attend(i, h)
                return c

            lax.fori_loop(hp * pairs // per, (hp + 1) * pairs // per, each, 0)

            def some(r, c):
                at = pl.ds(pl.multiple_of(s * 2 * rc + r * rc, rc), rc)
                normed[at, :] = (unit_rows(at)[0] * gain[0:1, :]).astype(jnp.bfloat16)
                return c

            lax.fori_loop(0, 2, some, 0)

        @pl.when(live & (hp == per - 1))
        def _():
            cosines, sines = cos_ref[at_rows, :], sin_ref[at_rows, :]
            dk = grad_k[i] + pltpu.roll(grad_k[i], 64, 1)
            dk = dk * cosines - swap_halves(dk, first_half) * sines
            dv = grad_v[i] + pltpu.roll(grad_v[i], 64, 1)
            grad_qkv[at_rows, q_width:] = jnp.where(low_lanes, dk, dv).astype(jnp.bfloat16)

            def part_tile(t, c):
                at = pl.ds(pl.multiple_of(t * tile, tile), tile)
                part[at_rows, at] = dot_t(grad_qkv[at_rows, :], qkv_w[at, :]).astype(jnp.bfloat16)
                return c

            lax.fori_loop(0, wide, part_tile, 0)

        w = s - blocks * per

        @pl.when((w >= 0) & (w < wide))
        def _():
            columns = pl.ds(pl.multiple_of(w * tile, tile), tile)
            send[w, :, :q_width + 128] = dot_rows(normed[:, columns], grad_qkv[...]).astype(jnp.bfloat16)
            send[w, :, q_width + 128:] = dot_rows(grad_low[:, columns], mix_ref[...]).astype(jnp.bfloat16)
            for o in range(owners):
                owner = w * owners + o

                @pl.when(owner != dp)
                def _():
                    to_owner(w, o).start()

                @pl.when(owner == dp)
                def _():
                    recv[dp] = send[w, o * share:(o + 1) * share, :]

        @pl.when(s == shift + lead + per)
        def _():
            lax.fori_loop(1, m, finish, 0)
            reduced[...] = recv[0].astype(jnp.float32)

            def add(k, c):
                reduced[...] += recv[k].astype(jnp.float32)
                return c

            lax.fori_loop(1, m, add, 0)

        e = s - lead + 1

        @pl.when((e >= 0) & (e < chunks))
        def _():
            start(load_branch(e, e % 2))

        d = s - lead

        @pl.when((d >= 0) & (d < chunks))
        def _():
            wait(load_branch(d, d % 2))

            @pl.when(d > 0)
            def _():
                wait(save_layer(d - 1))
            for k in (0, 1):
                where = two.rows(k, d)
                layer_stage[k] = (
                    x[where, :].astype(jnp.float32) + branch_stage[d % 2, k].astype(jnp.float32)
                    + feed_sum[where, :].astype(jnp.float32)
                ).astype(jnp.bfloat16)
            start(save_layer(d))

        e4 = s - lead - shift + 1

        @pl.when((e4 >= 0) & (e4 < chunks))
        def _():
            start(load_middle(e4, e4 % 2))

        d4 = s - lead - shift

        @pl.when(d4 >= 0)
        def _():
            wait(load_middle(d4, d4 % 2))

            @pl.when(d4 > 0)
            def _():
                wait(save_input(d4 - 1))
            for k in (0, 1):
                where = four.rows(k, d4)
                unit, inverse = unit_rows(where)
                grad = grad_sum[where, :].astype(jnp.float32)
                scaled = grad * gain[0:1, :]
                inner = jnp.mean(scaled * unit, axis=-1, keepdims=True)
                input_stage[k] = middle_stage[d4 % 2, k] + inverse * (scaled - unit * inner)
                gain_out[...] += jnp.sum(grad * unit, axis=0, keepdims=True)
            start(save_input(d4))
        return carry

    lax.fori_loop(0, shift + four.steps, step, 0)
    two.drain()
    four.drain()
    wait(save_layer(chunks - 1))
    wait(save_input(chunks - 1))


def attention_back(feed_part, grad_low, gain, q, k, v, mix, lse, cosines, sines, seg_col, seg_row, out_w,
                   x, qkv_w, branch, grad_middle, n, m, cid, size, chunks=16, lag=2):
    rows, width = feed_part.shape
    q_width = q.shape[1]
    pairs = q_width // 128
    rc = rows // (2 * chunks)
    blocks = rows // size
    share = width // m
    cat = 2 * q_width + 128
    low = jnp.bfloat16
    vmem = pl.BlockSpec(memory_space=pltpu.VMEM)
    hbm = pl.BlockSpec(memory_space=pl.ANY)
    dma = pltpu.SemaphoreType.DMA
    shape = jax.ShapeDtypeStruct
    return pl.pallas_call(
        functools.partial(back_kernel, n, m, chunks, lag, norm_eps, size, pairs),
        out_shape=(
            shape((rows, width), low), shape((rows, width), jnp.float32), shape((1, width), jnp.float32),
            shape((share, cat), jnp.float32),
        ),
        in_specs=[vmem] * 4 + [hbm] * 13,
        out_specs=(hbm, hbm, vmem, vmem),
        scratch_shapes=line_scratch(chunks, rc, width) + line_scratch(chunks, rc, width) + [
            pltpu.VMEM((rows, width), low),
            pltpu.VMEM((rows, width), low),
            pltpu.VMEM((rows, width), low),
            pltpu.VMEM((rows, width), low),
            pltpu.VMEM((rows, q_width), low),
            pltpu.VMEM((rows, 128), low),
            pltpu.VMEM((rows, 128), low),
            pltpu.VMEM((rows, q_width), low),
            pltpu.VMEM((rows, 128), jnp.float32),
            pltpu.VMEM((rows, 128), jnp.float32),
            pltpu.VMEM((rows, 1), jnp.int32),
            pltpu.VMEM((width, q_width), low),
            pltpu.VMEM((rows, width), low),
            pltpu.VMEM((width, q_width + 128), low),
            pltpu.VMEM((rows, width), low),
            pltpu.VMEM((size, q_width), low),
            pltpu.VMEM((blocks, size, size), jnp.float32),
            pltpu.VMEM((blocks, 128, size), low),
            pltpu.VMEM((blocks, size, 128), jnp.float32),
            pltpu.VMEM((blocks, size, 128), jnp.float32),
            pltpu.VMEM((rows, q_width + 128), low),
            pltpu.VMEM((width // 256, 256, cat), low),
            pltpu.VMEM((m, share, cat), low),
            pltpu.VMEM((2, 2, rc, width), low),
            pltpu.VMEM((2, rc, width), low),
            pltpu.VMEM((2, 2, rc, width), jnp.float32),
            pltpu.VMEM((2, rc, width), jnp.float32),
            dma((11,)), dma((2, 2)), dma((2, 2)), dma((2,)), dma((2,)), dma((m,)), dma((m,)),
        ],
        compiler_params=pltpu.CompilerParams(collective_id=cid, has_side_effects=True, vmem_limit_bytes=63 << 20),
        cost_estimate=pl.CostEstimate(flops=40 * rows * width * q_width, bytes_accessed=rows * width * 260,
                                      transcendentals=rows * rows * pairs),
    )(feed_part, gain, lse, seg_row, grad_low, q, k, v, mix, cosines, sines, seg_col, out_w,
      x, qkv_w, branch, grad_middle)


def norm_kernel(n, m, count, gains_ref, ff_ref, head_ref, *refs):
    sources, (norm_ref, gain_ref), kept = refs[:count], refs[count:count + 2], refs[count + 2:2 * count + 2]
    norm_body(n, m, gains_ref, ff_ref, head_ref, sources, kept, norm_ref, gain_ref, *refs[2 * count + 2:])


def norm_body(n, m, gains_ref, ff_ref, head_ref, sources, kept, norm_ref, gain_ref, line, got_gains, got_line, got_plane, got_squares,
                send_squares, recv_squares, send_gains, recv_gains, send_line, recv_line, send_plane, recv_plane, fetch_sem):
    fetches = [pltpu.make_async_copy(a, b, fetch_sem.at[k]) for k, (a, b) in enumerate(zip(sources, kept))]
    for copy in fetches:
        copy.start()
    z = lax.axis_index("tensor")
    d = lax.axis_index("dp")
    share = head_ref.shape[0]

    barrier = pltpu.get_barrier_semaphore()
    for k in range(1, n):
        pl.semaphore_signal(barrier, inc=1, device_id={"tensor": lax.rem(z + k, n)}, device_id_type=MESH)
    for k in range(1, m):
        pl.semaphore_signal(barrier, inc=1, device_id={"dp": lax.rem(d + k, m)}, device_id_type=MESH)
    pl.semaphore_wait(barrier, n - 1 + m - 1)

    def gains_to(k, sender):
        peer = lax.rem(d + k, m)
        return pltpu.make_async_remote_copy(
            src_ref=gains_ref.at[peer], dst_ref=got_gains.at[sender], send_sem=send_gains.at[k],
            recv_sem=recv_gains.at[sender], device_id={"dp": peer}, device_id_type=MESH)

    def squares_to(k, sender):
        return pltpu.make_async_remote_copy(
            src_ref=line.at[2], dst_ref=got_squares.at[sender], send_sem=send_squares.at[k],
            recv_sem=recv_squares.at[sender], device_id={"dp": lax.rem(d + k, m)}, device_id_type=MESH)

    def along_line(k, sender):
        return pltpu.make_async_remote_copy(
            src_ref=line.at[0], dst_ref=got_line.at[sender], send_sem=send_line.at[k], recv_sem=recv_line.at[sender],
            device_id={"tensor": lax.rem(z + k, n)}, device_id_type=MESH)

    def over_plane(k, sender):
        return pltpu.make_async_remote_copy(
            src_ref=line.at[1], dst_ref=got_plane.at[sender], send_sem=send_plane.at[k], recv_sem=recv_plane.at[sender],
            device_id={"dp": lax.rem(d + k, m)}, device_id_type=MESH)

    def summed(ref, number):
        whole = ref[0]
        for k in range(1, number):
            whole = whole + ref[k]
        return whole

    def squares(value):
        return jnp.sum(jnp.sum(value * value, axis=0, keepdims=True), axis=1, keepdims=True)

    for k in range(1, m):
        gains_to(k, d).start()
    got_gains[d] = gains_ref[d]
    sub = 32

    def head_rows(r, acc):
        value = head_ref[pl.ds(pl.multiple_of(r * sub, sub), sub), :]
        return acc + squares(value)

    local = lax.fori_loop(0, share // sub, head_rows, jnp.zeros((1, 1), jnp.float32))

    def ff_rows(r, acc):
        value = ff_ref[pl.ds(pl.multiple_of(r * sub, sub), sub), :].astype(jnp.float32)
        return acc + squares(value)

    local = lax.fori_loop(0, share // sub, ff_rows, local)
    line[2] = jnp.broadcast_to(local, (8, 128))
    for k in range(1, m):
        squares_to(k, d).start()
    got_squares[d] = line[2]
    for k in range(1, m):
        gains_to(k, d).wait_send()
        gains_to(k, lax.rem(d + m - k, m)).wait_recv()
    for k in range(1, m):
        squares_to(k, d).wait_send()
        squares_to(k, lax.rem(d + m - k, m)).wait_recv()
    line[0] = summed(got_squares, m)
    gains = summed(got_gains, m)
    gain_ref[...] = gains
    line[1] = jnp.broadcast_to(squares(gains), (8, 128))
    for k in range(1, m):
        over_plane(k, d).start()
    got_plane[d] = line[1]
    for k in range(1, n):
        along_line(k, z).start()
    got_line[z] = line[0]
    for k in range(1, n):
        along_line(k, z).wait_send()
        along_line(k, lax.rem(z + n - k, n)).wait_recv()
    for k in range(1, m):
        over_plane(k, d).wait_send()
        over_plane(k, lax.rem(d + m - k, m)).wait_recv()
    norm_ref[...] = jnp.sqrt(summed(got_line, n) + summed(got_plane, m))
    for copy in fetches:
        copy.wait()


def adam_kernel(rates, kv_width, correct_ref, norm_ref, gain_ref, ff_hbm, head_hbm, layer_hbm, input_hbm, *refs):
    count = len(rates)
    params, refs = refs[:3 * count], refs[3 * count:]
    norm_out, layer_out, input_out, outs, refs = refs[0], refs[1], refs[2], refs[3:3 * count + 3], refs[3 * count + 3:]
    (ff_grad, head_ref, layer_held, input_held), held = refs[:4], refs[4:3 * count + 4]
    grad_sem, load_sem, save_sem, in_sem, back_sem = refs[3 * count + 4:]
    share = gain_ref.shape[1]
    q_width = outs[3].shape[1]
    ff = outs[12].shape[2]
    sub = 32

    saves = [pltpu.make_async_copy(held[k], outs[k], save_sem.at[k]) for k in range(3 * count)]
    grads = (
        pltpu.make_async_copy(head_hbm, head_ref, grad_sem.at[1]),
        pltpu.make_async_copy(ff_hbm, ff_grad, grad_sem.at[0]),
    )
    quarter = layer_hbm.shape[0] // 4
    arrive, depart = [], []
    for k in range(4):
        at = pl.ds(k * quarter, quarter)
        for t, (source, kept, target) in enumerate(
                ((layer_hbm, layer_held, layer_out), (input_hbm, input_held, input_out))):
            arrive.append(pltpu.make_async_copy(source.at[at], kept.at[at], in_sem.at[t, k]))
            depart.append(pltpu.make_async_copy(kept.at[at], target.at[at], back_sem.at[t, k]))
    loads = [pltpu.make_async_copy(params[k], held[k], load_sem.at[k]) for k in range(12)]
    for copy in grads:
        copy.start()
    for copy in loads:
        copy.start()
    for copy in arrive:
        copy.start()
    norm_out[0] = norm_ref[0, 0]
    factor = jnp.minimum(1.0, clip_limit / (norm_ref[:1, :1] + 1e-06))
    one, two = correct_ref[0], correct_ref[1]

    def update(which, where, gradient):
        rate, decay = rates[which]
        p, a, b = ((params if which > 3 else held)[3 * which + k] for k in range(3))
        p_new, a_new, b_new = (held[3 * which + k] for k in range(3))
        gradient = gradient * factor
        first = beta_first * a[where] + (1.0 - beta_first) * gradient
        second = beta_second * b[where] + (1.0 - beta_second) * gradient * gradient
        a_new[where] = first
        b_new[where] = second
        change = first * one / (jnp.sqrt(second * two) + adam_eps)
        old = p[where]
        p_new[where] = old - rate * (change + decay * old)

    def save(which):
        for k in range(3):
            saves[3 * which + k].start()

    def by_rows(which, body):
        lax.fori_loop(0, share // sub, lambda r, c: (body(pl.ds(pl.multiple_of(r * sub, sub), sub)), c)[1], 0)
        save(which)

    for copy in grads:
        copy.wait()

    def gateup_rows(where):
        for t in (0, 1):
            update(4, (t, where, slice(None)), ff_grad[where, t * ff:(t + 1) * ff].astype(jnp.float32))

    by_rows(4, gateup_rows)

    def pass_on(begin, end):
        for came, left in zip(arrive[begin:end], depart[begin:end]):
            came.wait()
            left.start()

    pass_on(0, 4)

    def down_tile(t, carry):
        at = pl.ds(pl.multiple_of(t * 128, 128), 128)
        source = pl.ds(pl.multiple_of(2 * ff + t * 128, 128), 128)
        update(5, (at, slice(None)), ff_grad[:, source].astype(jnp.float32).T)
        return carry

    lax.fori_loop(0, ff // 128, down_tile, 0)
    save(5)
    pass_on(4, 8)
    for copy in loads:
        copy.wait()
    by_rows(1, lambda where: update(1, (where, slice(None)), head_ref[where, :q_width]))

    def out_tile(t, carry):
        at = pl.ds(pl.multiple_of(t * 128, 128), 128)
        source = pl.ds(pl.multiple_of(q_width + 2 * kv_width + t * 128, 128), 128)
        update(3, (at, slice(None)), head_ref[:, source].T)
        return carry

    lax.fori_loop(0, outs[9].shape[0] // 128, out_tile, 0)
    save(3)

    both = head_ref[:, q_width:q_width + 2 * kv_width].T
    for t in (0, 1):
        update(2, (t, slice(None), slice(None)), both[t * kv_width:(t + 1) * kv_width])
    save(2)
    update(0, (slice(None), slice(None)), gain_ref[...])
    save(0)
    for copy in saves + depart:
        copy.wait()


def finish_step(gains, correct, ff_grad, head_grad, layer, grad_in, params, rates, kv_width, n, m, cid):
    share = gains.shape[1] // m
    parts = gains.reshape(2, m, share).transpose(1, 0, 2)
    vmem = pl.BlockSpec(memory_space=pltpu.VMEM)
    hbm = pl.BlockSpec(memory_space=pl.ANY)
    dma = pltpu.SemaphoreType.DMA
    shape = jax.ShapeDtypeStruct
    fetched = list(params[12:])
    norm, gain, *kept = pl.pallas_call(
        functools.partial(norm_kernel, n, m, len(fetched)),
        out_shape=(shape((8, 128), jnp.float32), shape((2, share), jnp.float32))
        + tuple(pltpu.VMEM(a.shape, a.dtype) for a in fetched),
        in_specs=[vmem, vmem, vmem] + [pl.BlockSpec(memory_space=pltpu.HBM)] * len(fetched),
        out_specs=(vmem,) * (2 + len(fetched)),
        scratch_shapes=[
            pltpu.VMEM((3, 8, 128), jnp.float32),
            pltpu.VMEM((m, 2, share), jnp.float32),
            pltpu.VMEM((n, 8, 128), jnp.float32),
            pltpu.VMEM((m, 8, 128), jnp.float32),
            pltpu.VMEM((m, 8, 128), jnp.float32),
            dma((m,)), dma((m,)), dma((m,)), dma((m,)), dma((n,)), dma((n,)), dma((m,)), dma((m,)),
            dma((len(fetched),)),
        ],
        compiler_params=pltpu.CompilerParams(collective_id=cid, has_side_effects=True, vmem_limit_bytes=40 << 20),
    )(parts, ff_grad, head_grad, *fetched)
    size = sum(p.size for p in params)
    norm, layer, grad_in, *outs = pl.pallas_call(
        functools.partial(adam_kernel, rates, kv_width),
        out_shape=(shape((1,), jnp.float32), shape(layer.shape, layer.dtype), shape(grad_in.shape, grad_in.dtype))
        + tuple(shape(p.shape, jnp.float32) for p in params),
        in_specs=[pl.BlockSpec(memory_space=pltpu.SMEM), vmem, vmem] + [hbm] * 16 + [vmem] * len(fetched),
        out_specs=(pl.BlockSpec(memory_space=pltpu.SMEM),) + (hbm,) * (2 + len(params)),
        scratch_shapes=[pltpu.VMEM(a.shape, a.dtype) for a in (ff_grad, head_grad, layer, grad_in)]
        + [pltpu.VMEM(p.shape, jnp.float32) for p in params]
        + [dma((2,)), dma((12,)), dma((len(params),)), dma((2, 4)), dma((2, 4))],
        compiler_params=pltpu.CompilerParams(vmem_limit_bytes=34 << 20),
        cost_estimate=pl.CostEstimate(flops=20 * size, bytes_accessed=24 * size, transcendentals=size),
    )(correct, norm, gain, ff_grad, head_grad, layer, grad_in, *params[:12], *kept)
    return norm, layer, grad_in, outs


norm_eps = 1e-05
beta_first = 0.9
beta_second = 0.95
adam_eps = 1e-08
weight_decay = 0.1
weight_rate = 0.02
out_rate = 0.1
gain_rate = 0.2
clip_limit = 1.0


def on_device(
    n,
    m,
    tokens,
    cotangent,
    segment_ids,
    step_count,
    norm_gains,
    gains_first,
    gains_second,
    w_query,
    query_first,
    query_second,
    w_keyval,
    keyval_first,
    keyval_second,
    w_out,
    out_first,
    out_second,
    w_gateup,
    gateup_first,
    gateup_second,
    w_down,
    down_first,
    down_second,
):
    low = jnp.bfloat16
    width = w_query.shape[1]
    kv_width = w_keyval.shape[2]
    share = norm_gains.shape[1]
    gain_part = lax.dynamic_update_slice(
        jnp.zeros((2, tokens.shape[1]), jnp.float32), norm_gains, (0, lax.axis_index("dp") * share)
    )
    length = tokens.shape[0]
    size = min(256, length)
    segment = segment_ids[0]
    seg_row = segment[None, :]
    lane = jnp.arange(128, dtype=jnp.int32) % (HD // 2)
    frequency = jnp.power(10000.0, -lane.astype(jnp.float32) * (2.0 / HD))[None, :]
    (branch, gain_values, lse, seg_col, cosines, sines, mixture, q, k, v, qkv_weight, out_weight, ff_weight) = attention_head(
        tokens, gain_part, w_query, w_keyval.swapaxes(1, 2), w_out, frequency, seg_row, w_gateup, w_down, n, m, 1, size
    )
    feed_part, grad_middle, grad_branch, gain_grad_two, grad_ff_weight = feed_forward(
        branch, gain_values, tokens, cotangent, ff_weight, n, 2
    )
    ff_reduced = lax.psum_scatter(grad_ff_weight, "dp", scatter_dimension=0, tiled=True)
    layer_out, input_grad, gain_grad_one, head_reduced = attention_back(
        feed_part, grad_branch, gain_values, q, k, v, mixture, lse, cosines, sines, seg_col, seg_row,
        out_weight, tokens, qkv_weight, branch, grad_middle, n, m, 3, size
    )
    gain_grads = jnp.concatenate([gain_grad_one, gain_grad_two])
    step_float = step_count[0].astype(jnp.float32)
    correct = 1.0 / jnp.stack([1.0 - jnp.power(beta_first, step_float), 1.0 - jnp.power(beta_second, step_float)])
    params = (
        (norm_gains, gains_first, gains_second),
        (w_query, query_first, query_second),
        tuple(a.swapaxes(1, 2) for a in (w_keyval, keyval_first, keyval_second)),
        (w_out, out_first, out_second),
        (w_gateup, gateup_first, gateup_second),
        (w_down, down_first, down_second),
    )
    rates = (
        (gain_rate, 0.0),
        (weight_rate, weight_decay),
        (weight_rate, weight_decay),
        (out_rate, weight_decay),
        (weight_rate, weight_decay),
        (weight_rate, weight_decay),
    )
    norm, layer_out, input_grad, updated = finish_step(
        gain_grads, correct, ff_reduced, head_reduced, layer_out, input_grad,
        [a for group in params for a in group], rates, kv_width, n, m, 4
    )
    results = []
    for k in range(len(params)):
        weight, first_state, second_state = updated[3 * k : 3 * k + 3]
        group = [first_state, second_state, weight]
        results += [a.swapaxes(1, 2) for a in group] if k == 2 else group
    return (layer_out, input_grad, norm, *results)


def solution(mesh):
    rows = P("dp", None)
    gains = P(None, "dp")
    query = P("dp", "tensor")
    stacked = P(None, "dp", "tensor")
    turned = P("tensor", "dp")
    states = (gains,) * 3 + (query,) * 3 + (stacked,) * 3 + (turned,) * 3 + (stacked,) * 3 + (turned,) * 3
    return jax.shard_map(
        functools.partial(on_device, mesh.shape["tensor"], mesh.shape["dp"]),
        mesh=mesh,
        in_specs=(rows, rows, rows, P()) + states,
        out_specs=(rows, rows, P()) + states,
        check_vma=False,
    )
```

```python
import functools

import jax
import jax.numpy as jnp
from jax import lax
from jax.experimental import pallas as pl
from jax.experimental.pallas import tpu as pltpu
from jax.sharding import PartitionSpec as P

HD = 64
MESH = pl.DeviceIdType.MESH


masked_value = -1e9


def dot_t(left, right):
    return lax.dot_general(left, right, (((1,), (1,)), ((), ())), preferred_element_type=jnp.float32)


def dot_n(left, right):
    return lax.dot_general(left, right, (((1,), (0,)), ((), ())), preferred_element_type=jnp.float32)


def swap_halves(values, first_half):
    return jnp.where(first_half, pltpu.roll(values, 96, 1), pltpu.roll(values, 32, 1))


def lane_tests(rows):
    lane = lax.broadcasted_iota(jnp.int32, (rows, 128), 1)
    return lane < 64, (lane % 64) < 32


def block_bias(seg_col_ref, seg_row_ref, i, j, size):
    keys = seg_col_ref[pl.ds(pl.multiple_of(j * size, size), size), :]
    rows = seg_row_ref[:, pl.ds(pl.multiple_of(i * size, size), size)]
    key_at = j * size + lax.broadcasted_iota(jnp.int32, (size, size), 0)
    row_at = i * size + lax.broadcasted_iota(jnp.int32, (size, size), 1)
    return jnp.where((keys == rows) & (key_at <= row_at), 0.0, masked_value)


def stack_pair(pair, low_lanes):
    zero = jnp.zeros_like(pair)
    return jnp.concatenate([jnp.where(low_lanes, pair, zero), jnp.where(low_lanes, zero, pair)], axis=0)


class Line:
    def __init__(self, n, chunks, rc, lag, part, got, out, sems, order=None):
        self.order = order
        self.n, self.chunks, self.rc, self.lag = n, chunks, rc, lag
        self.part, self.got, self.out = part, got, out
        self.send_a, self.recv_a, self.send_g, self.recv_g = sems
        self.me = lax.axis_index("tensor")
        self.steps = chunks + 2 * lag * (n - 1)

    def rows(self, stream, c):
        begin = (stream * self.chunks + c) * self.rc if self.order is None else self.order(stream, c)
        return pl.ds(pl.multiple_of(begin, self.rc), self.rc)

    def side(self, stream):
        pos = self.me if stream == 0 else self.n - 1 - self.me
        fwd = self.me + 1 if stream == 0 else self.me - 1
        bwd = self.me - 1 if stream == 0 else self.me + 1
        return pos, fwd, bwd

    def toward(self, stream, c, nxt, src):
        return pltpu.make_async_remote_copy(
            src_ref=src, dst_ref=self.got.at[stream, c],
            send_sem=self.send_a.at[stream, c], recv_sem=self.recv_a.at[stream, c],
            device_id={"tensor": nxt}, device_id_type=MESH)

    def back(self, stream, c, nxt):
        where = self.rows(stream, c)
        return pltpu.make_async_remote_copy(
            src_ref=self.out.at[where], dst_ref=self.out.at[where],
            send_sem=self.send_g.at[stream, c], recv_sem=self.recv_g.at[stream, c],
            device_id={"tensor": nxt}, device_id_type=MESH)

    def step(self, s):
        n, lag = self.n, self.lag
        for stream in (0, 1):
            pos, fwd, bwd = self.side(stream)
            c = s - lag * pos

            @pl.when((c >= 0) & (c < self.chunks))
            def _():
                where = self.rows(stream, c)
                slot = self.got.at[stream, c]

                def summed():
                    self.toward(stream, c, fwd, slot).wait_recv()
                    return (
                        self.part[where, :].astype(jnp.float32) + self.got[stream, c].astype(jnp.float32)
                    ).astype(self.out.dtype)

                @pl.when(pos == 0)
                def _():
                    self.toward(stream, c, fwd, self.part.at[where]).start()

                @pl.when((pos > 0) & (pos < n - 1))
                def _():
                    self.got[stream, c] = summed()
                    self.toward(stream, c, fwd, slot).start()

                @pl.when(pos == n - 1)
                def _():
                    self.out[where, :] = summed()
                    self.back(stream, c, bwd).start()
            d = s - lag * (n - 1) - lag * (n - 1 - pos)

            @pl.when((d >= 0) & (d < self.chunks) & (pos < n - 1))
            def _():
                self.back(stream, d, bwd).wait_recv()

                @pl.when(pos > 0)
                def _():
                    self.back(stream, d, bwd).start()

    def drain(self):
        def one(c, carry):
            for stream in (0, 1):
                pos, fwd, bwd = self.side(stream)

                @pl.when(pos < self.n - 1)
                def _():
                    self.toward(stream, c, fwd, self.got.at[stream, c]).wait_send()

                @pl.when(pos > 0)
                def _():
                    self.back(stream, c, bwd).wait_send()
            return carry

        lax.fori_loop(0, self.chunks, one, 0)


def greet(n):
    me = lax.axis_index("tensor")
    barrier = pltpu.get_barrier_semaphore()

    @pl.when(me > 0)
    def _():
        pl.semaphore_signal(barrier, inc=1, device_id={"tensor": me - 1}, device_id_type=MESH)

    @pl.when(me < n - 1)
    def _():
        pl.semaphore_signal(barrier, inc=1, device_id={"tensor": me + 1}, device_id_type=MESH)

    @pl.when((me > 0) & (me < n - 1))
    def _():
        pl.semaphore_wait(barrier, 2)

    @pl.when((me == 0) | (me == n - 1))
    def _():
        pl.semaphore_wait(barrier, 1)


def line_scratch(chunks, rc, width):
    return [pltpu.VMEM((2, chunks, rc, width), jnp.bfloat16)] + [pltpu.SemaphoreType.DMA((2, chunks))] * 4


def line_kernel(n, chunks, lag, count, *refs):
    parts, outs, scratch = refs[:count], refs[count:2 * count], refs[2 * count:]
    rc = parts[0].shape[0] // (2 * chunks)
    lines = [
        Line(n, chunks, rc, lag, parts[k], scratch[5 * k], outs[k], scratch[5 * k + 1:5 * k + 5])
        for k in range(count)
    ]
    greet(n)

    def step(s, carry):
        for k, line in enumerate(lines):
            line.step(s - k * chunks)
        return carry

    lax.fori_loop(0, lines[0].steps + (count - 1) * chunks, step, 0)
    for line in lines:
        line.drain()


def line_reduce(parts, n, chunks, cid, lag=2):
    rows, width = parts[0].shape
    count = len(parts)
    rc = rows // (2 * chunks)
    scratch = []
    for _ in parts:
        scratch += line_scratch(chunks, rc, width)
    vmem = pl.BlockSpec(memory_space=pltpu.VMEM)
    return pl.pallas_call(
        functools.partial(line_kernel, n, chunks, lag, count),
        out_shape=tuple(jax.ShapeDtypeStruct((rows, width), jnp.bfloat16) for _ in parts),
        in_specs=[vmem] * count,
        out_specs=(vmem,) * count,
        scratch_shapes=scratch,
        compiler_params=pltpu.CompilerParams(collective_id=cid, has_side_effects=True, vmem_limit_bytes=40 << 20),
        cost_estimate=pl.CostEstimate(flops=rows * width * 2 * count, bytes_accessed=rows * width * 120 * count,
                                      transcendentals=0),
    )(*parts)


def dot_rows(left, right):
    return lax.dot_general(left, right, (((0,), (0,)), ((), ())), preferred_element_type=jnp.float32)


def ff_kernel(n, chunks, lag, eps, gain, branch_hbm, x_hbm, cot_hbm, w_hbm,
              feed_hbm, middle_hbm, low_hbm, gain_out, grads_hbm,
              got, sa, ra, sg, rg, two_sum, two_part, branch, x, weight, cot, normed, hidden, gg, feed,
              middle_stage, low_stage, unit_stage, w_sem, rows_sem, cot_sem, feed_sem, stage_sem, grad_sem):
    rows, width = branch.shape
    ff = hidden.shape[1]
    rc = rows // (2 * chunks)
    per = 8
    offset = per - 1
    half = rows // 2
    hb = per * rc
    block = 2 * hb
    blocks = chunks // per
    line = Line(n, chunks, rc, lag, two_part, got, two_sum, (sa, ra, sg, rg))
    landed = 2 * lag * (n - 1) + offset
    tile = 256
    full, rest = ff // tile, ff % tile
    wide = width // tile

    whole_rows = (
        pltpu.make_async_copy(branch_hbm, branch, rows_sem.at[0]),
        pltpu.make_async_copy(x_hbm, x, rows_sem.at[1]),
    )
    for copy in whole_rows:
        copy.start()
    groups = []
    for g, (begin, end) in enumerate(((0, tile), (tile, 2 * tile), (2 * tile, ff))):
        groups.append([
            pltpu.make_async_copy(w_hbm.at[:, pl.ds(t * ff + begin, end - begin)],
                                  weight.at[:, pl.ds(t * ff + begin, end - begin)], w_sem.at[g, t])
            for t in range(3)
        ])
    for copy in sum(groups, []):
        copy.start()

    def natural(k, b):
        return pl.ds(pl.multiple_of(k * half + b * hb, hb), hb)

    def blocked(k, b):
        return pl.ds(pl.multiple_of(b * block + k * hb, hb), hb)

    def load_cot(b):
        return [pltpu.make_async_copy(cot_hbm.at[natural(k, b)], cot.at[blocked(k, b)], cot_sem.at[b, k])
                for k in (0, 1)]

    def save_feed(b):
        return [pltpu.make_async_copy(feed.at[pl.ds(k * hb, hb)], feed_hbm.at[natural(k, b)], feed_sem.at[k])
                for k in (0, 1)]

    def save_rows(d):
        copies = []
        for k in (0, 1):
            where = line.rows(k, d)
            copies.append(pltpu.make_async_copy(middle_stage.at[k], middle_hbm.at[where], stage_sem.at[0, k]))
            copies.append(pltpu.make_async_copy(low_stage.at[k], low_hbm.at[where], stage_sem.at[1, k]))
        return copies

    def save_units(w):
        return [pltpu.make_async_copy(unit_stage, grads_hbm.at[pl.ds(pl.multiple_of(w * tile, tile), tile)], grad_sem.at[0])]

    def start(copies):
        for copy in copies:
            copy.start()

    def wait(copies):
        for copy in copies:
            copy.wait()

    for b in range(blocks):
        start(load_cot(b))
    gain_out[...] = jnp.zeros_like(gain_out)
    greet(n)

    def unit_rows(where):
        middle = x[where, :].astype(jnp.float32) + branch[where, :].astype(jnp.float32)
        inverse = lax.rsqrt(jnp.mean(middle * middle, axis=-1, keepdims=True) + eps)
        return middle * inverse, inverse

    def normalize(b):
        def some(r, carry):
            for k in (0, 1):
                where = pl.ds(pl.multiple_of(k * half + b * hb + r * rc, rc), rc)
                at = pl.ds(pl.multiple_of(b * block + k * hb + r * rc, rc), rc)
                normed[at, :] = (unit_rows(where)[0] * gain[1:2, :]).astype(jnp.bfloat16)
            return carry

        lax.fori_loop(0, per, some, 0)

    def step(s, carry):
        line.step(s - offset)
        b = s // per
        phase = s - b * per
        live = s < chunks
        mine = pl.ds(pl.multiple_of(b * block, block), block)

        def units(at, count):
            columns = pl.ds(at, count)
            second = pl.ds(pl.multiple_of(ff + at, 128), count)
            third = pl.ds(pl.multiple_of(2 * ff + at, 128), count)
            gate = dot_n(normed[mine, :], weight[:, columns])
            up = dot_n(normed[mine, :], weight[:, second])
            grad_hidden = dot_n(cot[mine, :], weight[:, third])
            sg_gate = 1.0 / (1.0 + jnp.exp(-gate))
            silu = gate * sg_gate
            hidden[mine, columns] = (silu * up).astype(jnp.bfloat16)
            gg[mine, columns] = (grad_hidden * up * sg_gate * (1.0 + gate * (1.0 - sg_gate))).astype(jnp.bfloat16)
            gg[mine, second] = (grad_hidden * silu).astype(jnp.bfloat16)

        def unit_tile(t, c):
            for g in range(3):
                @pl.when((b == 0) & (t == g))
                def _():
                    wait(groups[g])
            units(pl.multiple_of(t * tile, tile), tile)
            return c

        @pl.when(live & (phase == 0))
        def _():
            @pl.when(b == 0)
            def _():
                wait(whole_rows)
            normalize(b)
            wait(load_cot(b))

        @pl.when(live & (phase < 3))
        def _():
            lax.fori_loop(jnp.maximum(2 * phase - 1, 0), jnp.minimum(2 * phase + 1, full), unit_tile, 0)

        @pl.when(live & (phase == 3))
        def _():
            if rest:
                units(full * tile, rest)

            @pl.when(b > 0)
            def _():
                wait(save_feed(b - 1))

        @pl.when(live & ((phase == 3) | (phase == 4)))
        def _():
            def feed_tile(t, c):
                columns = pl.ds(pl.multiple_of(t * 2 * tile, 2 * tile), 2 * tile)
                feed[:, columns] = dot_t(hidden[mine, :], weight[columns, 2 * ff:]).astype(jnp.bfloat16)
                return c

            lax.fori_loop((phase - 3) * (wide // 4), (phase - 2) * (wide // 4), feed_tile, 0)

            @pl.when(phase == 4)
            def _():
                start(save_feed(b))

        @pl.when(live & ((phase == 5) | (phase == 6)))
        def _():
            def two_tile(t, c):
                at = pl.ds(pl.multiple_of(t * 2 * tile, 2 * tile), 2 * tile)
                value = dot_t(gg[mine, :], weight[at, :2 * ff]).astype(jnp.bfloat16)
                for k in (0, 1):
                    two_part[natural(k, b), at] = value[k * hb:(k + 1) * hb]
                return c

            lax.fori_loop((phase - 5) * (wide // 4), (phase - 4) * (wide // 4), two_tile, 0)

        d = s - landed

        @pl.when(d >= 0)
        def _():
            @pl.when(d > 0)
            def _():
                wait(save_rows(d - 1))
            for k in (0, 1):
                where = line.rows(k, d)
                at = pl.ds(pl.multiple_of((d // per) * block + k * hb + (d - (d // per) * per) * rc, rc), rc)
                pieces = [pl.ds(c * tile, tile) for c in range(wide)]

                def middle_at(c):
                    return x[where, c].astype(jnp.float32) + branch[where, c].astype(jnp.float32)

                def folded(value):
                    return value[:, :128] + value[:, 128:]

                total = jnp.zeros((rc, 128), jnp.float32)
                for c in pieces:
                    middle = middle_at(c)
                    total = total + folded(middle * middle)
                inverse = lax.rsqrt(jnp.sum(total, axis=-1, keepdims=True) * (1.0 / width) + eps)
                total = jnp.zeros((rc, 128), jnp.float32)
                for c in pieces:
                    product = two_sum[where, c].astype(jnp.float32) * (middle_at(c) * inverse)
                    gain_out[:, c] += jnp.sum(product, axis=0, keepdims=True)
                    total = total + folded(product * gain[1:2, c])
                inner = jnp.sum(total, axis=-1, keepdims=True) * (1.0 / width)
                for c in pieces:
                    scaled = two_sum[where, c].astype(jnp.float32) * gain[1:2, c]
                    value = cot[at, c].astype(jnp.float32) + inverse * (scaled - middle_at(c) * inverse * inner)
                    middle_stage[k, :, c] = value
                    low_stage[k, :, c] = value.astype(jnp.bfloat16)
            start(save_rows(d))

        late = s - chunks
        w = late // 2

        @pl.when((late >= 0) & (late == 2 * w) & (w < wide))
        def _():
            @pl.when(w > 0)
            def _():
                wait(save_units(w - 1))
            columns = pl.ds(pl.multiple_of(w * tile, tile), tile)
            left = normed[:, columns]
            for t in (0, 1):
                unit_stage[:, t * ff:(t + 1) * ff] = dot_rows(left, gg[:, t * ff:(t + 1) * ff]).astype(jnp.bfloat16)
            unit_stage[:, 2 * ff:] = dot_rows(cot[:, columns], hidden[...]).astype(jnp.bfloat16)
            start(save_units(w))
        return carry

    lax.fori_loop(0, offset + line.steps, step, 0)
    line.drain()
    wait(save_feed(blocks - 1))
    wait(save_rows(chunks - 1))
    wait(save_units(wide - 1))


def feed_forward(branch, gain, x, cot, weight, n, cid, chunks=32, lag=2):
    rows, width = branch.shape
    ff = weight.shape[1] // 3
    rc = rows // (2 * chunks)
    block = 16 * rc
    blocks = chunks // 8
    low = jnp.bfloat16
    vmem = pl.BlockSpec(memory_space=pltpu.VMEM)
    hbm = pl.BlockSpec(memory_space=pl.ANY)
    dma = pltpu.SemaphoreType.DMA
    shape = jax.ShapeDtypeStruct
    return pl.pallas_call(
        functools.partial(ff_kernel, n, chunks, lag, norm_eps),
        out_shape=(
            shape((rows, width), low), shape((rows, width), jnp.float32), shape((rows, width), low),
            shape((1, width), jnp.float32), shape((width, 3 * ff), low),
        ),
        in_specs=[vmem] + [hbm] * 4,
        out_specs=(hbm, hbm, hbm, vmem, hbm),
        scratch_shapes=line_scratch(chunks, rc, width) + [
            pltpu.VMEM((rows, width), low),
            pltpu.VMEM((rows, width), low),
            pltpu.VMEM((rows, width), low),
            pltpu.VMEM((rows, width), low),
            pltpu.VMEM((width, 3 * ff), low),
            pltpu.VMEM((rows, width), low),
            pltpu.VMEM((rows, width), low),
            pltpu.VMEM((rows, ff), low),
            pltpu.VMEM((rows, 2 * ff), low),
            pltpu.VMEM((block, width), low),
            pltpu.VMEM((2, rc, width), jnp.float32),
            pltpu.VMEM((2, rc, width), low),
            pltpu.VMEM((256, 3 * ff), low),
            dma((3, 3)), dma((2,)), dma((blocks, 2)), dma((2,)), dma((2, 2)), dma((1,)),
        ],
        compiler_params=pltpu.CompilerParams(collective_id=cid, has_side_effects=True, vmem_limit_bytes=63 << 20),
        cost_estimate=pl.CostEstimate(flops=18 * rows * width * ff, bytes_accessed=rows * width * 150,
                                      transcendentals=rows * ff),
    )(gain, branch, x, cot, weight)


def head_kernel(n, m, chunks, lag, eps, size, pairs,
                gain_part, query_own, keyval_own, out_own, frequency, seg_row_ref,
                x_hbm, gateup_hbm, down_hbm,
                branch, gain, lse_ref, seg_col_ref, cos_hbm, sin_hbm, mix_hbm, q_hbm, k_hbm, v_hbm, qkv_hbm, out_hbm, ff_hbm,
                got, sa, ra, sg, rg, part, normed, raw, bias, scores, v_turned, got_gain,
                x, cos_ref, sin_ref, mix_ref, q_ref, k_ref, v_ref, qkv_w, out_w, gateup_own, down_own, ff_own,
                send_gain, recv_gain, send_direct, send_forward, recv_w, own_sem, save_sem, result_sem, x_sem,
                send_ff, pass_ff, recv_ff):
    rows, width = branch.shape
    q_width = pairs * 128
    x_load = pltpu.make_async_copy(x_hbm, x, x_sem)
    x_load.start()
    results = [
        pltpu.make_async_copy(source, target, result_sem.at[k])
        for k, (source, target) in enumerate((
            (q_ref, q_hbm), (k_ref, k_hbm), (v_ref, v_hbm), (cos_ref, cos_hbm), (sin_ref, sin_hbm),
            (qkv_w, qkv_hbm), (out_w, out_hbm), (mix_ref, mix_hbm)))
    ]
    z = lax.axis_index("tensor")
    dp = lax.axis_index("dp")
    share = width // m
    chips = m // 2
    chip, core = dp // 2, dp % 2
    rc = rows // (2 * chunks)
    per = size // (2 * rc)
    hb = size // 2
    blocks = rows // size
    tile = 256
    wide = width // tile
    low_lanes, first_half = lane_tests(size)
    low_rows = lax.broadcasted_iota(jnp.int32, (128, size), 0) < 64
    wholes = (qkv_w, out_w)
    ff = down_own.shape[0]
    piece = 32
    pieces = share // piece
    spacing = 40 // pieces
    owned = (
        pltpu.make_async_copy(gateup_hbm, gateup_own, own_sem.at[0]),
        pltpu.make_async_copy(down_hbm, down_own, own_sem.at[1]),
    )
    for copy in owned:
        copy.start()

    def ascending(stream, c):
        b = c // per
        return b * size + stream * hb + (c - b * per) * rc

    line = Line(n, chunks, rc, lag, part, got, branch, (sa, ra, sg, rg), ascending)

    def shard_rows(s):
        return pl.ds(pl.multiple_of(s * share, share), share)

    def direct(kind, k):
        peer = 2 * lax.rem(chip + k, chips) + core
        return pltpu.make_async_remote_copy(
            src_ref=wholes[kind].at[shard_rows(dp)], dst_ref=wholes[kind].at[shard_rows(dp)], send_sem=send_direct.at[kind, k],
            recv_sem=recv_w.at[kind, dp], device_id={"dp": peer}, device_id_type=MESH)

    def forward(kind, c, side):
        shard = 2 * c + side
        where = shard_rows(shard)
        return pltpu.make_async_remote_copy(
            src_ref=wholes[kind].at[where], dst_ref=wholes[kind].at[where], send_sem=send_forward.at[kind, c],
            recv_sem=recv_w.at[kind, shard], device_id={"dp": 2 * chip + 1 - core}, device_id_type=MESH)

    def piece_rows(shard, p):
        return pl.ds(pl.multiple_of(shard * share + p * piece, piece), piece)

    def own_piece(p):
        return ff_own.at[pl.ds(pl.multiple_of(p * piece, piece), piece)]

    def send_piece(k, p):
        peer = 2 * lax.rem(chip + k, chips) + core
        return pltpu.make_async_remote_copy(
            src_ref=own_piece(p), dst_ref=ff_hbm.at[piece_rows(dp, p)], send_sem=send_ff.at[k, p],
            recv_sem=recv_ff.at[dp, p], device_id={"dp": peer}, device_id_type=MESH)

    def pass_piece(c, side, p, src=None):
        shard = 2 * c + side
        where = ff_hbm.at[piece_rows(shard, p)]
        return pltpu.make_async_remote_copy(
            src_ref=where if src is None else src, dst_ref=where, send_sem=pass_ff.at[c, p],
            recv_sem=recv_ff.at[shard, p], device_id={"dp": 2 * chip + 1 - core}, device_id_type=MESH)

    def save_own():
        return pltpu.make_async_copy(ff_own, ff_hbm.at[shard_rows(dp)], save_sem)

    def send_gains(k, sender):
        return pltpu.make_async_remote_copy(
            src_ref=gain_part, dst_ref=got_gain.at[sender], send_sem=send_gain.at[k], recv_sem=recv_gain.at[sender],
            device_id={"dp": lax.rem(dp + k, m)}, device_id_type=MESH)

    barrier = pltpu.get_barrier_semaphore()

    @pl.when(z > 0)
    def _():
        pl.semaphore_signal(barrier, inc=1, device_id={"tensor": z - 1}, device_id_type=MESH)

    @pl.when(z < n - 1)
    def _():
        pl.semaphore_signal(barrier, inc=1, device_id={"tensor": z + 1}, device_id_type=MESH)

    for k in range(1, m):
        pl.semaphore_signal(barrier, inc=1, device_id={"dp": lax.rem(dp + k, m)}, device_id_type=MESH)

    qkv_w[shard_rows(dp), :q_width] = query_own[...].astype(jnp.bfloat16)
    both_own = jnp.concatenate([keyval_own[0], keyval_own[1]], axis=0)
    qkv_w[shard_rows(dp), q_width:] = both_own.T.astype(jnp.bfloat16)
    for t in range(q_width // 128):
        out_w[shard_rows(dp), t * 128:(t + 1) * 128] = out_own[t * 128:(t + 1) * 128, :].T.astype(jnp.bfloat16)
    got_gain[dp] = gain_part[...]

    @pl.when((z > 0) & (z < n - 1))
    def _():
        pl.semaphore_wait(barrier, m + 1)

    @pl.when((z == 0) | (z == n - 1))
    def _():
        pl.semaphore_wait(barrier, m)

    for k in range(1, m):
        send_gains(k, dp).start()
    for kind in (0, 1):
        for k in range(1, chips):
            direct(kind, k).start()
        forward(kind, chip, core).start()
    for k in range(1, m):
        send_gains(k, lax.rem(dp + m - k, m)).wait_recv()
    whole = got_gain[0]
    for k in range(1, m):
        whole = whole + got_gain[k]
    gain[...] = whole.astype(jnp.bfloat16).astype(jnp.float32)

    x_load.wait()

    def norm_rows(r, carry):
        where = pl.ds(pl.multiple_of(r * rc, rc), rc)
        values = x[where, :].astype(jnp.float32)
        inverse = lax.rsqrt(jnp.mean(values * values, axis=-1, keepdims=True) + eps)
        normed[where, :] = (values * inverse * gain[0:1, :]).astype(jnp.bfloat16)
        return carry

    lax.fori_loop(0, rows // rc, norm_rows, 0)
    def tables(i, carry):
        where = pl.ds(pl.multiple_of(i * size, size), size)
        ids = jnp.broadcast_to(seg_row_ref[:, where].astype(jnp.float32), (128, size)).T[:, :1]
        seg_col_ref[where, :] = ids.astype(jnp.int32)
        earlier = jnp.where(seg_row_ref[...].astype(jnp.float32) < ids, 1.0, 0.0)
        place = (i * size + lax.broadcasted_iota(jnp.int32, (size, 1), 0)).astype(jnp.float32) - jnp.sum(
            earlier, axis=1, keepdims=True)
        angles = place * frequency[...]
        sines = jnp.sin(angles)
        cos_ref[where, :] = jnp.cos(angles)
        sin_ref[where, :] = jnp.where(first_half, -sines, sines)
        return carry

    lax.fori_loop(0, blocks, tables, 0)
    for copy in owned:
        copy.wait()

    def own_rows(r, carry):
        where = pl.ds(pl.multiple_of(r * piece, piece), piece)
        for t in (0, 1):
            ff_own[where, t * ff:(t + 1) * ff] = gateup_own[t, where, :].astype(jnp.bfloat16)
        return carry

    lax.fori_loop(0, pieces, own_rows, 0)

    def own_columns(t, carry):
        at = pl.ds(pl.multiple_of(2 * ff + t * 128, 128), 128)
        ff_own[:, at] = down_own[pl.ds(pl.multiple_of(t * 128, 128), 128), :].T.astype(jnp.bfloat16)
        return carry

    lax.fori_loop(0, ff // 128, own_columns, 0)
    save_own().start()

    def pass_on(kind):
        for k in range(1, chips):
            c = lax.rem(chip + chips - k, chips)
            forward(kind, c, core).wait_recv()
            forward(kind, c, core).start()

    def receive(kind):
        for c in range(chips):
            forward(kind, c, 1 - core).wait_recv()

    pass_on(0)
    receive(0)
    for p in range(min(2, pieces)):
        for k in range(1, chips):
            send_piece(k, p).start()

    def prepare(i, carry):
        where = pl.ds(pl.multiple_of(i * size, size), size)
        raw[...] = dot_n(normed[where, :], qkv_w[...])
        cosines, sines = cos_ref[where, :], sin_ref[where, :]
        for hp in range(pairs):
            values = raw[:, hp * 128:(hp + 1) * 128]
            turned = values * cosines + swap_halves(values, first_half) * sines
            q_ref[where, hp * 128:(hp + 1) * 128] = (
                turned.astype(jnp.bfloat16).astype(jnp.float32) * 0.125).astype(jnp.bfloat16)
        both = raw[:, q_width:q_width + 128]
        other = pltpu.roll(both, 64, 1)
        keys = jnp.where(low_lanes, both, other)
        k_ref[where, :] = (keys * cosines + swap_halves(keys, first_half) * sines).astype(jnp.bfloat16)
        values = jnp.where(low_lanes, other, both)
        v_ref[where, :] = values.astype(jnp.bfloat16)
        v_turned[i] = values.T.astype(jnp.bfloat16)
        return carry

    lax.fori_loop(0, blocks, prepare, 0)
    for copy in results[:5]:
        copy.start()
    pass_on(1)

    def attend(i, hp):
        where = pl.ds(pl.multiple_of(i * size, size), size)
        columns = pl.ds(pl.multiple_of(hp * 128, 128), 128)
        stacked = stack_pair(q_ref[where, columns], low_lanes)

        def score(j, top):
            keys = k_ref[pl.ds(pl.multiple_of(j * size, size), size), :]
            b = bias[j]
            s = dot_t(keys, stacked) + jnp.concatenate([b, b], axis=1)
            scores[j] = s
            return jnp.maximum(top, jnp.max(s, axis=0, keepdims=True))

        top = lax.fori_loop(0, i + 1, score, jnp.full((1, 2 * size), -jnp.inf, jnp.float32))

        def mix(j, c):
            total, acc = c
            p = jnp.exp(scores[j] - top)
            total = total + jnp.sum(p, axis=0, keepdims=True)
            return total, acc + dot_n(v_turned[j], p.astype(jnp.bfloat16))

        total, acc = lax.fori_loop(0, i + 1, mix, (
            jnp.zeros((1, 2 * size), jnp.float32), jnp.zeros((128, 2 * size), jnp.float32)))
        lse_ref[i, hp] = top + jnp.log(total)
        acc = acc / total
        acc = jnp.where(low_rows, acc[:, :size], acc[:, size:])
        mix_ref[where, columns] = acc.T.astype(jnp.bfloat16)

    def step(s, carry):
        line.step(s - per)
        p_send = (s - 1) // spacing + 2
        p_pass = (s - 12) // spacing

        @pl.when((s >= 1) & ((p_send - 2) * spacing == s - 1) & (p_send < pieces))
        def _():
            for k in range(1, chips):
                send_piece(k, p_send).start()

        @pl.when((s >= 12) & (p_pass * spacing == s - 12) & (p_pass < pieces))
        def _():
            pass_piece(chip, core, p_pass, own_piece(p_pass)).start()
            for k in range(1, chips):
                c = lax.rem(chip + chips - k, chips)
                pass_piece(c, core, p_pass).wait_recv()
                pass_piece(c, core, p_pass).start()

        i = s // per
        hp = s - i * per
        live = s < blocks * per

        @pl.when(live & (hp == 0))
        def _():
            def fill(j, c):
                bias[j] = block_bias(seg_col_ref, seg_row_ref, i, j, size)
                return c

            lax.fori_loop(0, i + 1, fill, 0)

        @pl.when(live)
        def _():
            def each(h, c):
                attend(i, h)
                return c

            lax.fori_loop(hp * pairs // per, (hp + 1) * pairs // per, each, 0)

        @pl.when(s == per - 1)
        def _():
            receive(1)
            for copy in results[5:7]:
                copy.start()

        @pl.when(s == blocks * per)
        def _():
            results[7].start()

        @pl.when(live & (hp == per - 1))
        def _():
            where = pl.ds(pl.multiple_of(i * size, size), size)

            def part_tile(t, c):
                at = pl.ds(pl.multiple_of(t * tile, tile), tile)
                part[where, at] = dot_t(mix_ref[where, :], out_w[at, :]).astype(jnp.bfloat16)
                return c

            lax.fori_loop(0, wide, part_tile, 0)
        return carry

    lax.fori_loop(0, per + line.steps, step, 0)
    line.drain()
    save_own().wait()
    for copy in results:
        copy.wait()

    def settle(p, carry):
        for k in range(1, chips):
            send_piece(k, p).wait_send()
        for c in range(chips):
            pass_piece(c, core, p).wait_send()
            pass_piece(c, 1 - core, p).wait_recv()
        return carry

    lax.fori_loop(0, pieces, settle, 0)
    for k in range(1, m):
        send_gains(k, dp).wait_send()
    for kind in (0, 1):
        for k in range(1, chips):
            direct(kind, k).wait_send()
        for c in range(chips):
            forward(kind, c, core).wait_send()


def attention_head(x, gain_part, query, keyval, out, frequency, seg_row, gateup, down, n, m, cid, size,
                   chunks=32, lag=2):
    rows, width = x.shape
    q_width = query.shape[1]
    share, ff = width // m, down.shape[0]
    pairs = q_width // 128
    rc = rows // (2 * chunks)
    blocks = rows // size
    chips = m // 2
    low = jnp.bfloat16
    vmem = pl.BlockSpec(memory_space=pltpu.VMEM)
    hbm = pl.BlockSpec(memory_space=pl.ANY)
    dma = pltpu.SemaphoreType.DMA
    shape = jax.ShapeDtypeStruct
    return pl.pallas_call(
        functools.partial(head_kernel, n, m, chunks, lag, norm_eps, size, pairs),
        out_shape=(
            shape((rows, width), low), shape((2, width), jnp.float32),
            shape((blocks, pairs, 1, 2 * size), jnp.float32), shape((rows, 1), jnp.int32),
            shape((rows, 128), jnp.float32), shape((rows, 128), jnp.float32), shape((rows, q_width), low),
            shape((rows, q_width), low), shape((rows, 128), low), shape((rows, 128), low),
            shape((width, q_width + 128), low), shape((width, q_width), low), shape((width, 3 * ff), low),
        ),
        in_specs=[vmem] * 6 + [hbm] * 3,
        out_specs=(vmem,) * 4 + (hbm,) * 9,
        scratch_shapes=line_scratch(chunks, rc, width) + [
            pltpu.VMEM((rows, width), low),
            pltpu.VMEM((rows, width), low),
            pltpu.VMEM((size, q_width + 128), jnp.float32),
            pltpu.VMEM((blocks, size, size), jnp.float32),
            pltpu.VMEM((blocks, size, 2 * size), jnp.float32),
            pltpu.VMEM((blocks, 128, size), low),
            pltpu.VMEM((m, 2, width), jnp.float32),
            pltpu.VMEM((rows, width), low),
            pltpu.VMEM((rows, 128), jnp.float32),
            pltpu.VMEM((rows, 128), jnp.float32),
            pltpu.VMEM((rows, q_width), low),
            pltpu.VMEM((rows, q_width), low),
            pltpu.VMEM((rows, 128), low),
            pltpu.VMEM((rows, 128), low),
            pltpu.VMEM((width, q_width + 128), low),
            pltpu.VMEM((width, q_width), low),
            pltpu.VMEM(gateup.shape, jnp.float32),
            pltpu.VMEM(down.shape, jnp.float32),
            pltpu.VMEM((share, 3 * ff), low),
            dma((m,)), dma((m,)), dma((2, chips)), dma((2, chips)), dma((2, m)), dma((2,)), dma, dma((8,)), dma,
            dma((chips, share // 32)), dma((chips, share // 32)), dma((m, share // 32)),
        ],
        compiler_params=pltpu.CompilerParams(collective_id=cid, has_side_effects=True, vmem_limit_bytes=56 << 20),
        cost_estimate=pl.CostEstimate(flops=20 * rows * width * q_width, bytes_accessed=rows * width * 170,
                                      transcendentals=rows * rows * pairs),
    )(gain_part, query, keyval, out, frequency, seg_row, x, gateup, down)


def back_kernel(n, m, chunks, lag, eps, size, pairs,
                feed_part, gain, lse_ref, seg_row_ref,
                low_hbm, q_hbm, k_hbm, v_hbm, mix_hbm, cos_hbm, sin_hbm, seg_hbm, out_hbm, x_hbm, qkv_hbm,
                branch_hbm, middle_hbm,
                layer_hbm, input_hbm, gain_out, reduced,
                got2, sa2, ra2, sg2, rg2, got4, sa4, ra4, sg4, rg4, feed_sum, part, grad_sum,
                grad_low, q_ref, k_ref, v_ref, mix_ref, cos_ref, sin_ref, seg_col_ref, out_w, x, qkv_w,
                normed, grad_mix, bias, k_turned, grad_k, grad_v, grad_qkv, send, recv,
                branch_stage, layer_stage, middle_stage, input_stage,
                w_sem, branch_sem, middle_sem, layer_sem, input_sem, send_sem, recv_sem):
    rows, width = feed_part.shape
    q_width = pairs * 128
    z = lax.axis_index("tensor")
    dp = lax.axis_index("dp")
    rc = rows // (2 * chunks)
    per = size // (2 * rc)
    hb = size // 2
    blocks = rows // size
    tile = 256
    wide = width // tile
    share = width // m
    owners = tile // share
    lead = 2 * lag * (n - 1)
    shift = chunks + per
    low_lanes, first_half = lane_tests(size)
    low_rows = lax.broadcasted_iota(jnp.int32, (128, size), 0) < 64

    def descending(stream, c):
        b = c // per
        return (blocks - 1 - b) * size + stream * hb + (c - b * per) * rc

    two = Line(n, chunks, rc, lag, feed_part, got2, feed_sum, (sa2, ra2, sg2, rg2))
    four = Line(n, chunks, rc, lag, part, got4, grad_sum, (sa4, ra4, sg4, rg4), descending)
    loads = [
        pltpu.make_async_copy(source, target, w_sem.at[k])
        for k, (source, target) in enumerate((
            (k_hbm, k_ref), (q_hbm, q_ref), (low_hbm, grad_low), (out_hbm, out_w), (v_hbm, v_ref), (mix_hbm, mix_ref),
            (cos_hbm, cos_ref), (sin_hbm, sin_ref), (seg_hbm, seg_col_ref), (x_hbm, x), (qkv_hbm, qkv_w)))
    ]
    for copy in loads:
        copy.start()

    def start(copies):
        for copy in copies:
            copy.start()

    def wait(copies):
        for copy in copies:
            copy.wait()

    def load_branch(d, slot):
        return [pltpu.make_async_copy(branch_hbm.at[two.rows(k, d)], branch_stage.at[slot, k], branch_sem.at[slot, k])
                for k in (0, 1)]

    def load_middle(d, slot):
        return [pltpu.make_async_copy(middle_hbm.at[four.rows(k, d)], middle_stage.at[slot, k], middle_sem.at[slot, k])
                for k in (0, 1)]

    def save_layer(d):
        return [pltpu.make_async_copy(layer_stage.at[k], layer_hbm.at[two.rows(k, d)], layer_sem.at[k]) for k in (0, 1)]

    def save_input(d):
        return [pltpu.make_async_copy(input_stage.at[k], input_hbm.at[four.rows(k, d)], input_sem.at[k]) for k in (0, 1)]

    def to_owner(w, o):
        owner = w * owners + o
        return pltpu.make_async_remote_copy(
            src_ref=send.at[w, pl.ds(o * share, share)], dst_ref=recv.at[dp], send_sem=send_sem.at[owner],
            recv_sem=recv_sem.at[dp], device_id={"dp": owner}, device_id_type=MESH)

    gain_out[...] = jnp.zeros_like(gain_out)

    def prepare(i, carry):
        at = pl.ds(pl.multiple_of(i * size, size), size)
        k_turned[i] = k_ref[at, :].astype(jnp.float32).T.astype(jnp.bfloat16)
        grad_k[i] = jnp.zeros((size, 128), jnp.float32)
        grad_v[i] = jnp.zeros((size, 128), jnp.float32)
        return carry

    barrier = pltpu.get_barrier_semaphore()

    @pl.when(z > 0)
    def _():
        pl.semaphore_signal(barrier, inc=1, device_id={"tensor": z - 1}, device_id_type=MESH)

    @pl.when(z < n - 1)
    def _():
        pl.semaphore_signal(barrier, inc=1, device_id={"tensor": z + 1}, device_id_type=MESH)

    for k in range(1, m):
        pl.semaphore_signal(barrier, inc=1, device_id={"dp": lax.rem(dp + k, m)}, device_id_type=MESH)

    @pl.when((z > 0) & (z < n - 1))
    def _():
        pl.semaphore_wait(barrier, m + 1)

    @pl.when((z == 0) | (z == n - 1))
    def _():
        pl.semaphore_wait(barrier, m)

    def unit_rows(where):
        values = x[where, :].astype(jnp.float32)
        inverse = lax.rsqrt(jnp.mean(values * values, axis=-1, keepdims=True) + eps)
        return values * inverse, inverse

    def attend(i, hp):
        at_rows = pl.ds(pl.multiple_of(i * size, size), size)
        columns = pl.ds(pl.multiple_of(hp * 128, 128), 128)
        stacked = stack_pair(q_ref[at_rows, columns], low_lanes)
        grad_pair = grad_mix[:, columns]
        grad_stacked = stack_pair(grad_pair, low_lanes)
        product = (grad_pair.astype(jnp.float32) * mix_ref[at_rows, columns].astype(jnp.float32)).T
        spread = jnp.concatenate([
            jnp.sum(product[:64], axis=0, keepdims=True), jnp.sum(product[64:], axis=0, keepdims=True)], axis=1)
        logsum = lse_ref[i, hp]

        def piece(j, acc):
            at = pl.ds(pl.multiple_of(j * size, size), size)
            b = bias[j]
            s = dot_t(k_ref[at, :], stacked) + jnp.concatenate([b, b], axis=1)
            p = jnp.exp(s - logsum)
            grad_p = dot_t(v_ref[at, :], grad_stacked)
            grad_s = (p * (grad_p - spread)).astype(jnp.bfloat16)
            grad_v[j] += dot_n(p.astype(jnp.bfloat16), grad_stacked)
            grad_k[j] += dot_n(grad_s, stacked)
            return acc + dot_n(k_turned[j], grad_s)

        acc = lax.fori_loop(0, i + 1, piece, jnp.zeros((128, 2 * size), jnp.float32))
        acc = jnp.where(low_rows, acc[:, :size], acc[:, size:]).T * 0.125
        turned = acc * cos_ref[at_rows, :] - swap_halves(acc, first_half) * sin_ref[at_rows, :]
        grad_qkv[at_rows, columns] = turned.astype(jnp.bfloat16)

    def finish(k, carry):
        owner = lax.rem(dp + k, m)
        w = owner // owners

        def copy(peer):
            return pltpu.make_async_remote_copy(
                src_ref=send.at[0, pl.ds(0, share)], dst_ref=recv.at[peer], send_sem=send_sem.at[peer],
                recv_sem=recv_sem.at[peer], device_id={"dp": peer}, device_id_type=MESH)

        copy(owner).wait_send()
        copy(owner).wait_recv()
        return carry

    def step(s, carry):
        two.step(s)
        four.step(s - shift)
        b = s // per
        hp = s - b * per
        i = blocks - 1 - b
        live = s < blocks * per
        at_rows = pl.ds(pl.multiple_of(i * size, size), size)

        @pl.when(s == 0)
        def _():
            wait(loads)
            lax.fori_loop(0, blocks, prepare, 0)

        @pl.when(live & (hp == 0))
        def _():
            grad_mix[...] = dot_n(grad_low[at_rows, :], out_w[...]).astype(jnp.bfloat16)

            def fill(j, c):
                bias[j] = block_bias(seg_col_ref, seg_row_ref, i, j, size)
                return c

            lax.fori_loop(0, i + 1, fill, 0)

        @pl.when(live)
        def _():
            def each(h, c):
                attend(i, h)
                return c

            lax.fori_loop(hp * pairs // per, (hp + 1) * pairs // per, each, 0)

            def some(r, c):
                at = pl.ds(pl.multiple_of(s * 2 * rc + r * rc, rc), rc)
                normed[at, :] = (unit_rows(at)[0] * gain[0:1, :]).astype(jnp.bfloat16)
                return c

            lax.fori_loop(0, 2, some, 0)

        @pl.when(live & (hp == per - 1))
        def _():
            cosines, sines = cos_ref[at_rows, :], sin_ref[at_rows, :]
            dk = grad_k[i] + pltpu.roll(grad_k[i], 64, 1)
            dk = dk * cosines - swap_halves(dk, first_half) * sines
            dv = grad_v[i] + pltpu.roll(grad_v[i], 64, 1)
            grad_qkv[at_rows, q_width:] = jnp.where(low_lanes, dk, dv).astype(jnp.bfloat16)

            def part_tile(t, c):
                at = pl.ds(pl.multiple_of(t * tile, tile), tile)
                part[at_rows, at] = dot_t(grad_qkv[at_rows, :], qkv_w[at, :]).astype(jnp.bfloat16)
                return c

            lax.fori_loop(0, wide, part_tile, 0)

        w = s - blocks * per

        @pl.when((w >= 0) & (w < wide))
        def _():
            columns = pl.ds(pl.multiple_of(w * tile, tile), tile)
            send[w, :, :q_width + 128] = dot_rows(normed[:, columns], grad_qkv[...]).astype(jnp.bfloat16)
            send[w, :, q_width + 128:] = dot_rows(grad_low[:, columns], mix_ref[...]).astype(jnp.bfloat16)
            for o in range(owners):
                owner = w * owners + o

                @pl.when(owner != dp)
                def _():
                    to_owner(w, o).start()

                @pl.when(owner == dp)
                def _():
                    recv[dp] = send[w, o * share:(o + 1) * share, :]

        @pl.when(s == shift + lead + per)
        def _():
            lax.fori_loop(1, m, finish, 0)
            reduced[...] = recv[0].astype(jnp.float32)

            def add(k, c):
                reduced[...] += recv[k].astype(jnp.float32)
                return c

            lax.fori_loop(1, m, add, 0)

        e = s - lead + 1

        @pl.when((e >= 0) & (e < chunks))
        def _():
            start(load_branch(e, e % 2))

        d = s - lead

        @pl.when((d >= 0) & (d < chunks))
        def _():
            wait(load_branch(d, d % 2))

            @pl.when(d > 0)
            def _():
                wait(save_layer(d - 1))
            for k in (0, 1):
                where = two.rows(k, d)
                layer_stage[k] = (
                    x[where, :].astype(jnp.float32) + branch_stage[d % 2, k].astype(jnp.float32)
                    + feed_sum[where, :].astype(jnp.float32)
                ).astype(jnp.bfloat16)
            start(save_layer(d))

        e4 = s - lead - shift + 1

        @pl.when((e4 >= 0) & (e4 < chunks))
        def _():
            start(load_middle(e4, e4 % 2))

        d4 = s - lead - shift

        @pl.when(d4 >= 0)
        def _():
            wait(load_middle(d4, d4 % 2))

            @pl.when(d4 > 0)
            def _():
                wait(save_input(d4 - 1))
            for k in (0, 1):
                where = four.rows(k, d4)
                unit, inverse = unit_rows(where)
                grad = grad_sum[where, :].astype(jnp.float32)
                scaled = grad * gain[0:1, :]
                inner = jnp.mean(scaled * unit, axis=-1, keepdims=True)
                input_stage[k] = middle_stage[d4 % 2, k] + inverse * (scaled - unit * inner)
                gain_out[...] += jnp.sum(grad * unit, axis=0, keepdims=True)
            start(save_input(d4))
        return carry

    lax.fori_loop(0, shift + four.steps, step, 0)
    two.drain()
    four.drain()
    wait(save_layer(chunks - 1))
    wait(save_input(chunks - 1))


def attention_back(feed_part, grad_low, gain, q, k, v, mix, lse, cosines, sines, seg_col, seg_row, out_w,
                   x, qkv_w, branch, grad_middle, n, m, cid, size, chunks=16, lag=2):
    rows, width = feed_part.shape
    q_width = q.shape[1]
    pairs = q_width // 128
    rc = rows // (2 * chunks)
    blocks = rows // size
    share = width // m
    cat = 2 * q_width + 128
    low = jnp.bfloat16
    vmem = pl.BlockSpec(memory_space=pltpu.VMEM)
    hbm = pl.BlockSpec(memory_space=pl.ANY)
    dma = pltpu.SemaphoreType.DMA
    shape = jax.ShapeDtypeStruct
    return pl.pallas_call(
        functools.partial(back_kernel, n, m, chunks, lag, norm_eps, size, pairs),
        out_shape=(
            shape((rows, width), low), shape((rows, width), jnp.float32), shape((1, width), jnp.float32),
            shape((share, cat), jnp.float32),
        ),
        in_specs=[vmem] * 4 + [hbm] * 13,
        out_specs=(hbm, hbm, vmem, vmem),
        scratch_shapes=line_scratch(chunks, rc, width) + line_scratch(chunks, rc, width) + [
            pltpu.VMEM((rows, width), low),
            pltpu.VMEM((rows, width), low),
            pltpu.VMEM((rows, width), low),
            pltpu.VMEM((rows, width), low),
            pltpu.VMEM((rows, q_width), low),
            pltpu.VMEM((rows, 128), low),
            pltpu.VMEM((rows, 128), low),
            pltpu.VMEM((rows, q_width), low),
            pltpu.VMEM((rows, 128), jnp.float32),
            pltpu.VMEM((rows, 128), jnp.float32),
            pltpu.VMEM((rows, 1), jnp.int32),
            pltpu.VMEM((width, q_width), low),
            pltpu.VMEM((rows, width), low),
            pltpu.VMEM((width, q_width + 128), low),
            pltpu.VMEM((rows, width), low),
            pltpu.VMEM((size, q_width), low),
            pltpu.VMEM((blocks, size, size), jnp.float32),
            pltpu.VMEM((blocks, 128, size), low),
            pltpu.VMEM((blocks, size, 128), jnp.float32),
            pltpu.VMEM((blocks, size, 128), jnp.float32),
            pltpu.VMEM((rows, q_width + 128), low),
            pltpu.VMEM((width // 256, 256, cat), low),
            pltpu.VMEM((m, share, cat), low),
            pltpu.VMEM((2, 2, rc, width), low),
            pltpu.VMEM((2, rc, width), low),
            pltpu.VMEM((2, 2, rc, width), jnp.float32),
            pltpu.VMEM((2, rc, width), jnp.float32),
            dma((11,)), dma((2, 2)), dma((2, 2)), dma((2,)), dma((2,)), dma((m,)), dma((m,)),
        ],
        compiler_params=pltpu.CompilerParams(collective_id=cid, has_side_effects=True, vmem_limit_bytes=63 << 20),
        cost_estimate=pl.CostEstimate(flops=40 * rows * width * q_width, bytes_accessed=rows * width * 260,
                                      transcendentals=rows * rows * pairs),
    )(feed_part, gain, lse, seg_row, grad_low, q, k, v, mix, cosines, sines, seg_col, out_w,
      x, qkv_w, branch, grad_middle)


def norm_kernel(n, m, count, gains_ref, ff_ref, head_ref, *refs):
    sources, (norm_ref, gain_ref), kept = refs[:count], refs[count:count + 2], refs[count + 2:2 * count + 2]
    norm_body(n, m, gains_ref, ff_ref, head_ref, sources, kept, norm_ref, gain_ref, *refs[2 * count + 2:])


def norm_body(n, m, gains_ref, ff_ref, head_ref, sources, kept, norm_ref, gain_ref, line, got_gains, got_line, got_plane, got_squares,
                send_squares, recv_squares, send_gains, recv_gains, send_line, recv_line, send_plane, recv_plane, fetch_sem):
    fetches = [pltpu.make_async_copy(a, b, fetch_sem.at[k]) for k, (a, b) in enumerate(zip(sources, kept))]
    for copy in fetches:
        copy.start()
    z = lax.axis_index("tensor")
    d = lax.axis_index("dp")
    share = head_ref.shape[0]

    barrier = pltpu.get_barrier_semaphore()
    for k in range(1, n):
        pl.semaphore_signal(barrier, inc=1, device_id={"tensor": lax.rem(z + k, n)}, device_id_type=MESH)
    for k in range(1, m):
        pl.semaphore_signal(barrier, inc=1, device_id={"dp": lax.rem(d + k, m)}, device_id_type=MESH)
    pl.semaphore_wait(barrier, n - 1 + m - 1)

    def gains_to(k, sender):
        peer = lax.rem(d + k, m)
        return pltpu.make_async_remote_copy(
            src_ref=gains_ref.at[peer], dst_ref=got_gains.at[sender], send_sem=send_gains.at[k],
            recv_sem=recv_gains.at[sender], device_id={"dp": peer}, device_id_type=MESH)

    def squares_to(k, sender):
        return pltpu.make_async_remote_copy(
            src_ref=line.at[2], dst_ref=got_squares.at[sender], send_sem=send_squares.at[k],
            recv_sem=recv_squares.at[sender], device_id={"dp": lax.rem(d + k, m)}, device_id_type=MESH)

    def along_line(k, sender):
        return pltpu.make_async_remote_copy(
            src_ref=line.at[0], dst_ref=got_line.at[sender], send_sem=send_line.at[k], recv_sem=recv_line.at[sender],
            device_id={"tensor": lax.rem(z + k, n)}, device_id_type=MESH)

    def over_plane(k, sender):
        return pltpu.make_async_remote_copy(
            src_ref=line.at[1], dst_ref=got_plane.at[sender], send_sem=send_plane.at[k], recv_sem=recv_plane.at[sender],
            device_id={"dp": lax.rem(d + k, m)}, device_id_type=MESH)

    def summed(ref, number):
        whole = ref[0]
        for k in range(1, number):
            whole = whole + ref[k]
        return whole

    def squares(value):
        return jnp.sum(jnp.sum(value * value, axis=0, keepdims=True), axis=1, keepdims=True)

    for k in range(1, m):
        gains_to(k, d).start()
    got_gains[d] = gains_ref[d]
    sub = 32

    def head_rows(r, acc):
        value = head_ref[pl.ds(pl.multiple_of(r * sub, sub), sub), :]
        return acc + squares(value)

    local = lax.fori_loop(0, share // sub, head_rows, jnp.zeros((1, 1), jnp.float32))

    def ff_rows(r, acc):
        value = ff_ref[pl.ds(pl.multiple_of(r * sub, sub), sub), :].astype(jnp.float32)
        return acc + squares(value)

    local = lax.fori_loop(0, share // sub, ff_rows, local)
    line[2] = jnp.broadcast_to(local, (8, 128))
    for k in range(1, m):
        squares_to(k, d).start()
    got_squares[d] = line[2]
    for k in range(1, m):
        gains_to(k, d).wait_send()
        gains_to(k, lax.rem(d + m - k, m)).wait_recv()
    for k in range(1, m):
        squares_to(k, d).wait_send()
        squares_to(k, lax.rem(d + m - k, m)).wait_recv()
    line[0] = summed(got_squares, m)
    gains = summed(got_gains, m)
    gain_ref[...] = gains
    line[1] = jnp.broadcast_to(squares(gains), (8, 128))
    for k in range(1, m):
        over_plane(k, d).start()
    got_plane[d] = line[1]
    for k in range(1, n):
        along_line(k, z).start()
    got_line[z] = line[0]
    for k in range(1, n):
        along_line(k, z).wait_send()
        along_line(k, lax.rem(z + n - k, n)).wait_recv()
    for k in range(1, m):
        over_plane(k, d).wait_send()
        over_plane(k, lax.rem(d + m - k, m)).wait_recv()
    norm_ref[...] = jnp.sqrt(summed(got_line, n) + summed(got_plane, m))
    for copy in fetches:
        copy.wait()


def adam_kernel(rates, kv_width, correct_ref, norm_ref, gain_ref, ff_hbm, head_hbm, layer_hbm, input_hbm, *refs):
    count = len(rates)
    params, refs = refs[:3 * count], refs[3 * count:]
    norm_out, layer_out, input_out, outs, refs = refs[0], refs[1], refs[2], refs[3:3 * count + 3], refs[3 * count + 3:]
    (ff_grad, head_ref, layer_held, input_held), held = refs[:4], refs[4:3 * count + 4]
    grad_sem, load_sem, save_sem, in_sem, back_sem = refs[3 * count + 4:]
    share = gain_ref.shape[1]
    q_width = outs[3].shape[1]
    ff = outs[12].shape[2]
    sub = 32

    saves = [pltpu.make_async_copy(held[k], outs[k], save_sem.at[k]) for k in range(3 * count)]
    grads = (
        pltpu.make_async_copy(head_hbm, head_ref, grad_sem.at[1]),
        pltpu.make_async_copy(ff_hbm, ff_grad, grad_sem.at[0]),
    )
    quarter = layer_hbm.shape[0] // 4
    arrive, depart = [], []
    for k in range(4):
        at = pl.ds(k * quarter, quarter)
        for t, (source, kept, target) in enumerate(
                ((layer_hbm, layer_held, layer_out), (input_hbm, input_held, input_out))):
            arrive.append(pltpu.make_async_copy(source.at[at], kept.at[at], in_sem.at[t, k]))
            depart.append(pltpu.make_async_copy(kept.at[at], target.at[at], back_sem.at[t, k]))
    loads = [pltpu.make_async_copy(params[k], held[k], load_sem.at[k]) for k in range(12)]
    for copy in grads:
        copy.start()
    for copy in loads:
        copy.start()
    for copy in arrive:
        copy.start()
    norm_out[0] = norm_ref[0, 0]
    factor = jnp.minimum(1.0, clip_limit / (norm_ref[:1, :1] + 1e-06))
    one, two = correct_ref[0], correct_ref[1]

    def update(which, where, gradient):
        rate, decay = rates[which]
        p, a, b = ((params if which > 3 else held)[3 * which + k] for k in range(3))
        p_new, a_new, b_new = (held[3 * which + k] for k in range(3))
        gradient = gradient * factor
        first = beta_first * a[where] + (1.0 - beta_first) * gradient
        second = beta_second * b[where] + (1.0 - beta_second) * gradient * gradient
        a_new[where] = first
        b_new[where] = second
        change = first * one / (jnp.sqrt(second * two) + adam_eps)
        old = p[where]
        p_new[where] = old - rate * (change + decay * old)

    def save(which):
        for k in range(3):
            saves[3 * which + k].start()

    def by_rows(which, body):
        lax.fori_loop(0, share // sub, lambda r, c: (body(pl.ds(pl.multiple_of(r * sub, sub), sub)), c)[1], 0)
        save(which)

    for copy in grads:
        copy.wait()

    def gateup_rows(where):
        for t in (0, 1):
            update(4, (t, where, slice(None)), ff_grad[where, t * ff:(t + 1) * ff].astype(jnp.float32))

    by_rows(4, gateup_rows)

    def pass_on(begin, end):
        for came, left in zip(arrive[begin:end], depart[begin:end]):
            came.wait()
            left.start()

    pass_on(0, 4)

    def down_tile(t, carry):
        at = pl.ds(pl.multiple_of(t * 128, 128), 128)
        source = pl.ds(pl.multiple_of(2 * ff + t * 128, 128), 128)
        update(5, (at, slice(None)), ff_grad[:, source].astype(jnp.float32).T)
        return carry

    lax.fori_loop(0, ff // 128, down_tile, 0)
    save(5)
    pass_on(4, 8)
    for copy in loads:
        copy.wait()
    by_rows(1, lambda where: update(1, (where, slice(None)), head_ref[where, :q_width]))

    def out_tile(t, carry):
        at = pl.ds(pl.multiple_of(t * 128, 128), 128)
        source = pl.ds(pl.multiple_of(q_width + 2 * kv_width + t * 128, 128), 128)
        update(3, (at, slice(None)), head_ref[:, source].T)
        return carry

    lax.fori_loop(0, outs[9].shape[0] // 128, out_tile, 0)
    save(3)

    both = head_ref[:, q_width:q_width + 2 * kv_width].T
    for t in (0, 1):
        update(2, (t, slice(None), slice(None)), both[t * kv_width:(t + 1) * kv_width])
    save(2)
    update(0, (slice(None), slice(None)), gain_ref[...])
    save(0)
    for copy in saves + depart:
        copy.wait()


def finish_step(gains, correct, ff_grad, head_grad, layer, grad_in, params, rates, kv_width, n, m, cid):
    share = gains.shape[1] // m
    parts = gains.reshape(2, m, share).transpose(1, 0, 2)
    vmem = pl.BlockSpec(memory_space=pltpu.VMEM)
    hbm = pl.BlockSpec(memory_space=pl.ANY)
    dma = pltpu.SemaphoreType.DMA
    shape = jax.ShapeDtypeStruct
    fetched = list(params[12:])
    norm, gain, *kept = pl.pallas_call(
        functools.partial(norm_kernel, n, m, len(fetched)),
        out_shape=(shape((8, 128), jnp.float32), shape((2, share), jnp.float32))
        + tuple(pltpu.VMEM(a.shape, a.dtype) for a in fetched),
        in_specs=[vmem, vmem, vmem] + [pl.BlockSpec(memory_space=pltpu.HBM)] * len(fetched),
        out_specs=(vmem,) * (2 + len(fetched)),
        scratch_shapes=[
            pltpu.VMEM((3, 8, 128), jnp.float32),
            pltpu.VMEM((m, 2, share), jnp.float32),
            pltpu.VMEM((n, 8, 128), jnp.float32),
            pltpu.VMEM((m, 8, 128), jnp.float32),
            pltpu.VMEM((m, 8, 128), jnp.float32),
            dma((m,)), dma((m,)), dma((m,)), dma((m,)), dma((n,)), dma((n,)), dma((m,)), dma((m,)),
            dma((len(fetched),)),
        ],
        compiler_params=pltpu.CompilerParams(collective_id=cid, has_side_effects=True, vmem_limit_bytes=40 << 20),
    )(parts, ff_grad, head_grad, *fetched)
    size = sum(p.size for p in params)
    norm, layer, grad_in, *outs = pl.pallas_call(
        functools.partial(adam_kernel, rates, kv_width),
        out_shape=(shape((1,), jnp.float32), shape(layer.shape, layer.dtype), shape(grad_in.shape, grad_in.dtype))
        + tuple(shape(p.shape, jnp.float32) for p in params),
        in_specs=[pl.BlockSpec(memory_space=pltpu.SMEM), vmem, vmem] + [hbm] * 16 + [vmem] * len(fetched),
        out_specs=(pl.BlockSpec(memory_space=pltpu.SMEM),) + (hbm,) * (2 + len(params)),
        scratch_shapes=[pltpu.VMEM(a.shape, a.dtype) for a in (ff_grad, head_grad, layer, grad_in)]
        + [pltpu.VMEM(p.shape, jnp.float32) for p in params]
        + [dma((2,)), dma((12,)), dma((len(params),)), dma((2, 4)), dma((2, 4))],
        compiler_params=pltpu.CompilerParams(vmem_limit_bytes=34 << 20),
        cost_estimate=pl.CostEstimate(flops=20 * size, bytes_accessed=24 * size, transcendentals=size),
    )(correct, norm, gain, ff_grad, head_grad, layer, grad_in, *params[:12], *kept)
    return norm, layer, grad_in, outs


norm_eps = 1e-05
beta_first = 0.9
beta_second = 0.95
adam_eps = 1e-08
weight_decay = 0.1
weight_rate = 0.02
out_rate = 0.1
gain_rate = 0.2
clip_limit = 1.0


def on_device(
    n,
    m,
    tokens,
    cotangent,
    segment_ids,
    step_count,
    norm_gains,
    gains_first,
    gains_second,
    w_query,
    query_first,
    query_second,
    w_keyval,
    keyval_first,
    keyval_second,
    w_out,
    out_first,
    out_second,
    w_gateup,
    gateup_first,
    gateup_second,
    w_down,
    down_first,
    down_second,
):
    low = jnp.bfloat16
    width = w_query.shape[1]
    kv_width = w_keyval.shape[2]
    share = norm_gains.shape[1]
    gain_part = lax.dynamic_update_slice(
        jnp.zeros((2, tokens.shape[1]), jnp.float32), norm_gains, (0, lax.axis_index("dp") * share)
    )
    length = tokens.shape[0]
    size = min(256, length)
    segment = segment_ids[0]
    seg_row = segment[None, :]
    lane = jnp.arange(128, dtype=jnp.int32) % (HD // 2)
    frequency = jnp.power(10000.0, -lane.astype(jnp.float32) * (2.0 / HD))[None, :]
    (branch, gain_values, lse, seg_col, cosines, sines, mixture, q, k, v, qkv_weight, out_weight, ff_weight) = attention_head(
        tokens, gain_part, w_query, w_keyval.swapaxes(1, 2), w_out, frequency, seg_row, w_gateup, w_down, n, m, 1, size
    )
    feed_part, grad_middle, grad_branch, gain_grad_two, grad_ff_weight = feed_forward(
        branch, gain_values, tokens, cotangent, ff_weight, n, 2
    )
    ff_reduced = lax.psum_scatter(grad_ff_weight, "dp", scatter_dimension=0, tiled=True)
    layer_out, input_grad, gain_grad_one, head_reduced = attention_back(
        feed_part, grad_branch, gain_values, q, k, v, mixture, lse, cosines, sines, seg_col, seg_row,
        out_weight, tokens, qkv_weight, branch, grad_middle, n, m, 3, size
    )
    gain_grads = jnp.concatenate([gain_grad_one, gain_grad_two])
    step_float = step_count[0].astype(jnp.float32)
    correct = 1.0 / jnp.stack([1.0 - jnp.power(beta_first, step_float), 1.0 - jnp.power(beta_second, step_float)])
    params = (
        (norm_gains, gains_first, gains_second),
        (w_query, query_first, query_second),
        tuple(a.swapaxes(1, 2) for a in (w_keyval, keyval_first, keyval_second)),
        (w_out, out_first, out_second),
        (w_gateup, gateup_first, gateup_second),
        (w_down, down_first, down_second),
    )
    rates = (
        (gain_rate, 0.0),
        (weight_rate, weight_decay),
        (weight_rate, weight_decay),
        (out_rate, weight_decay),
        (weight_rate, weight_decay),
        (weight_rate, weight_decay),
    )
    norm, layer_out, input_grad, updated = finish_step(
        gain_grads, correct, ff_reduced, head_reduced, layer_out, input_grad,
        [a for group in params for a in group], rates, kv_width, n, m, 4
    )
    results = []
    for k in range(len(params)):
        weight, first_state, second_state = updated[3 * k : 3 * k + 3]
        group = [first_state, second_state, weight]
        results += [a.swapaxes(1, 2) for a in group] if k == 2 else group
    return (layer_out, input_grad, norm, *results)


def solution(mesh):
    rows = P("dp", None)
    gains = P(None, "dp")
    query = P("dp", "tensor")
    stacked = P(None, "dp", "tensor")
    turned = P("tensor", "dp")
    states = (gains,) * 3 + (query,) * 3 + (stacked,) * 3 + (turned,) * 3 + (stacked,) * 3 + (turned,) * 3
    return jax.shard_map(
        functools.partial(on_device, mesh.shape["tensor"], mesh.shape["dp"]),
        mesh=mesh,
        in_specs=(rows, rows, rows, P()) + states,
        out_specs=(rows, rows, P()) + states,
        check_vma=False,
    )
```
